32 devices in a mesh: batch: 4 (over z), seq: 8 (over y, x, core).
Axes of the slice: x: 2, y: 2, z: 4, core: 2. Of those that a mesh axis runs over, the one named last changes fastest.
Arguments:
- tokens: bfloat16 [48, 1024, 768], P('batch', 'seq'), may hold values from -6 to 6
- attend_weight: bfloat16 [768, 2304], P('batch'), may hold values from -0.3125 to 0.3125
- query_bias: bfloat16 [768], P('batch'), may hold values from -3 to 3
- value_bias: bfloat16 [768], P('batch'), may hold values from -3 to 3
- output_weight: bfloat16 [768, 768], P('batch'), may hold values from -0.625 to 0.625
- output_bias: bfloat16 [768], P('batch'), may hold values from -3 to 3
- first_gain: bfloat16 [768], P('batch'), may hold values from 0.5 to 1.5
- first_shift: bfloat16 [768], P('batch'), may hold values from -3 to 3
- expand_weight: bfloat16 [768, 3072], P('batch'), may hold values from -0.21875 to 0.21875
- expand_bias: bfloat16 [3072], P('batch'), may hold values from -3 to 3
- reduce_weight: bfloat16 [3072, 768], P('batch'), may hold values from -0.109375 to 0.109375
- reduce_bias: bfloat16 [768], P('batch'), may hold values from -3 to 3
- second_gain: bfloat16 [768], P('batch'), may hold values from 0.5 to 1.5
- second_shift: bfloat16 [768], P('batch'), may hold values from -3 to 3
- query_rank: int32 [48, 12, 1024], P('batch', None, 'seq'), may hold values from 0 to 1023, as said below
- key_rank: int32 [48, 12, 1024], P('batch', None, 'seq'), may hold values from 0 to 1023, as said below
- cotangent: bfloat16 [48, 1024, 768], P('batch', 'seq'), may hold values from -6 to 6
Outputs:
- layer_out: bfloat16 [48, 1024, 768], P('batch', 'seq')
- token_grad: bfloat16 [48, 1024, 768], P('batch', 'seq')
- attend_weight_grad: float32 [768, 2304], P('batch')
- query_bias_grad: float32 [768], P('batch')
- value_bias_grad: float32 [768], P('batch')
- output_weight_grad: float32 [768, 768], P('batch')
- output_bias_grad: float32 [768], P('batch')
- first_gain_grad: float32 [768], P('batch')
- first_shift_grad: float32 [768], P('batch')
- expand_weight_grad: float32 [768, 3072], P('batch')
- expand_bias_grad: float32 [3072], P('batch')
- reduce_weight_grad: float32 [3072, 768], P('batch')
- reduce_bias_grad: float32 [768], P('batch')
- second_gain_grad: float32 [768], P('batch')
- second_shift_grad: float32 [768], P('batch')
The draws below stay inside these ranges and needn't reach their ends.
Inputs may be any that keep to these rules, and one draw needn't show every extreme that they name: `query_rank`: for each sequence and head a permutation of the token places; place p lies in cluster p // 128. Of the 128 tokens of each aligned block j * 128 to (j + 1) * 128 - 1 of a sequence, exactly 16 lie in each cluster. `key_rank`: drawn independently of query_rank under the same rules.
All inputs are finite; a program needn't handle non-finite values.
Results may differ from the reference program's by a relative error of at most 0.02.
Values may be sent and summed in bfloat16 or wider, within the bound.
A program may use at most 256 MiB of HBM per device.

```python
import jax
import jax.numpy as jnp
from jax import lax

D = 768
H = 12
HD = 64
FF = 3072
CLUSTER = 128
SEQS = 48
LENGTH = 1024
CLUSTERS = 8
SHARE = 16


def cluster_ranks(key):
    count = SEQS * H * CLUSTERS
    source_keys = jax.random.split(jax.random.fold_in(key, 11), count)
    target_keys = jax.random.split(jax.random.fold_in(key, 23), count)
    shuffle = jax.vmap(lambda part_key: jax.random.permutation(part_key, CLUSTER))
    local = shuffle(source_keys).astype(jnp.int32).reshape(SEQS, H, CLUSTERS, CLUSTER)
    inside = shuffle(target_keys).astype(jnp.int32).reshape(SEQS, H, CLUSTERS * CLUSTER)
    target = local // SHARE
    anchor = jnp.arange(CLUSTERS, dtype=jnp.int32).reshape(1, 1, CLUSTERS, 1)
    slot = anchor * SHARE + local % SHARE
    index = (target * CLUSTER + slot).reshape(SEQS, H, CLUSTERS * CLUSTER)
    placed = jnp.take_along_axis(inside, index, axis=2)
    return (target.reshape(SEQS, H, CLUSTERS * CLUSTER) * CLUSTER + placed).astype(jnp.int32)


def draw_query_rank(key, part):
    return cluster_ranks(jax.random.fold_in(key, 1))


def draw_key_rank(key, part):
    return cluster_ranks(jax.random.fold_in(key, 2))


def block_levels(rng, extent, cuts, smallest, top_value):
    def one(axis_at, blocks):
        draws = jax.random.uniform(jax.random.fold_in(jax.random.fold_in(rng, 6), axis_at), (blocks,), jnp.float32, smallest / len(cuts), top_value / len(cuts))
        return jnp.repeat(jnp.exp(draws), extent[axis_at] // blocks).reshape((-1,) + (1,) * (len(extent) - axis_at - 1))

    level = one(*cuts[0])
    for cut in cuts[1:]:
        level = level * one(*cut)
    return level


def noise(key, dims, deviation, limit, cuts=(), kind=jnp.bfloat16):
    drawn = deviation * jax.random.normal(key, dims, jnp.float32)
    if cuts:
        drawn = drawn * block_levels(key, dims, cuts, -0.22, 0.18)
    return jnp.clip(drawn, -limit, limit).astype(kind)


def setup_inputs(seed: int = 0) -> dict:
    seeds = jax.random.split(jax.random.key(seed), 18)
    tokens = noise(seeds[0], (SEQS, LENGTH, D), 1.0, 6.0, ((0, 4), (1, 8)))
    attend_weight = noise(seeds[1], (D, 3 * D), (D // 2) ** -0.5, 0.3125, ((0, 4),))
    query_bias = noise(seeds[2], (D,), 0.5, 3.0, ((0, 4),))
    value_bias = noise(seeds[3], (D,), 0.5, 3.0, ((0, 4),))
    output_weight = noise(seeds[4], (D, D), (D // 8) ** -0.5, 0.625, ((0, 4),))
    output_bias = noise(seeds[5], (D,), 0.5, 3.0, ((0, 4),))
    first_gain = jnp.clip(1.0 + 0.1 * jax.random.normal(seeds[6], (D,), jnp.float32), 0.5, 1.5).astype(jnp.bfloat16)
    first_shift = noise(seeds[7], (D,), 0.5, 3.0, ((0, 4),))
    expand_weight = noise(seeds[8], (D, FF), D ** -0.5, 0.21875, ((0, 4),))
    expand_bias = noise(seeds[9], (FF,), 0.5, 3.0, ((0, 4),))
    reduce_weight = noise(seeds[10], (FF, D), FF ** -0.5, 0.109375, ((0, 4),))
    reduce_bias = noise(seeds[11], (D,), 0.5, 3.0, ((0, 4),))
    second_gain = jnp.clip(1.0 + 0.1 * jax.random.normal(seeds[12], (D,), jnp.float32), 0.5, 1.5).astype(jnp.bfloat16)
    second_shift = noise(seeds[13], (D,), 0.5, 3.0, ((0, 4),))
    query_rank = draw_query_rank(jax.random.fold_in(seeds[17], 71), 0)
    key_rank = draw_key_rank(jax.random.fold_in(seeds[17], 71), 0)
    cotangent = noise(seeds[16], (SEQS, LENGTH, D), 1.0, 6.0, ((0, 4), (1, 8)))
    return {"tokens": tokens, "attend_weight": attend_weight, "query_bias": query_bias, "value_bias": value_bias, "output_weight": output_weight, "output_bias": output_bias, "first_gain": first_gain, "first_shift": first_shift, "expand_weight": expand_weight, "expand_bias": expand_bias, "reduce_weight": reduce_weight, "reduce_bias": reduce_bias, "second_gain": second_gain, "second_shift": second_shift, "query_rank": query_rank, "key_rank": key_rank, "cotangent": cotangent}


epsilon = 1e-05

@jax.custom_vjp
def low(v):
    return lax.optimization_barrier(v.astype(jnp.bfloat16)).astype(jnp.float32)

@jax.custom_vjp
def low_back(v):
    return v

def low_keep(v):
    return (low(v), None)

def low_pass(kept, grad):
    return (grad,)

def back_keep(v):
    return (v, None)

def back_low(kept, grad):
    return (low(grad),)
low.defvjp(low_keep, low_pass)
low_back.defvjp(back_keep, back_low)

def normalize(resid, gain, shift):
    center = lax.optimization_barrier(jnp.mean(resid, axis=-1, keepdims=True))
    centered = resid - center
    spread = lax.optimization_barrier(jnp.mean(centered * centered, axis=-1, keepdims=True))
    return centered * lax.rsqrt(spread + epsilon) * gain + shift

def arrange(rows, order):
    split = jnp.transpose(rows.reshape(LENGTH, H, HD), (1, 0, 2))
    return jnp.take_along_axis(split, order[:, :, None], axis=1)

def sequence_layer(params, tokens, query_rank, key_rank):
    attend_weight, query_bias, value_bias, output_weight, output_bias, first_gain, first_shift, expand_weight, expand_bias, reduce_weight, reduce_bias, second_gain, second_shift = params
    highest = lax.Precision.HIGHEST
    mixed = jnp.dot(tokens, attend_weight, precision=highest, preferred_element_type=jnp.float32)
    queries = low(low_back(mixed[:, :D] + query_bias))
    keys_rows = low(low_back(mixed[:, D:2 * D]))
    values_rows = low(low_back(mixed[:, 2 * D:] + value_bias))
    query_order = jnp.argsort(query_rank, axis=-1).astype(jnp.int32)
    key_order = jnp.argsort(key_rank, axis=-1).astype(jnp.int32)
    clusters = LENGTH // CLUSTER
    query_group = arrange(queries, query_order).reshape(H, clusters, CLUSTER, HD)
    key_group = arrange(keys_rows, key_order).reshape(H, clusters, CLUSTER, HD)
    value_group = arrange(values_rows, key_order).reshape(H, clusters, CLUSTER, HD)
    scores = jnp.einsum('hcqd,hckd->hcqk', query_group, key_group, precision=highest) * HD ** (-0.5)
    probs = low(jax.nn.softmax(low_back(scores), axis=-1))
    grouped = jnp.einsum('hcqk,hckd->hcqd', probs, value_group, precision=highest).reshape(H, LENGTH, HD)
    placed = jnp.take_along_axis(grouped, query_rank.astype(jnp.int32)[:, :, None], axis=1)
    context = low(low_back(jnp.transpose(placed, (1, 0, 2)).reshape(LENGTH, D)))
    branch_one = low_back(jnp.dot(context, output_weight, precision=highest, preferred_element_type=jnp.float32) + output_bias)
    middle = normalize(tokens + branch_one, first_gain, first_shift)
    pre = low_back(jnp.dot(low(middle), expand_weight, precision=highest, preferred_element_type=jnp.float32) + expand_bias)
    hidden = low(jax.nn.gelu(pre, approximate=False))
    branch_two = low_back(jnp.dot(hidden, reduce_weight, precision=highest, preferred_element_type=jnp.float32) + reduce_bias)
    return normalize(middle + branch_two, second_gain, second_shift)

def reference(tokens, attend_weight, query_bias, value_bias, output_weight, output_bias, first_gain, first_shift, expand_weight, expand_bias, reduce_weight, reduce_bias, second_gain, second_shift, query_rank, key_rank, cotangent):
    params = tuple((weight.astype(jnp.float32) for weight in (attend_weight, query_bias, value_bias, output_weight, output_bias, first_gain, first_shift, expand_weight, expand_bias, reduce_weight, reduce_bias, second_gain, second_shift)))
    inputs = tokens.astype(jnp.float32)
    layer_step = jax.checkpoint(sequence_layer)

    def whole(inputs, params):
        return lax.map(lambda item: layer_step(params, item[0], item[1], item[2]), (inputs, query_rank, key_rank))
    result, pullback = jax.vjp(whole, inputs, params)
    input_grad, grads = pullback(cotangent.astype(jnp.float32))
    return (result.astype(jnp.bfloat16), input_grad.astype(jnp.bfloat16), grads[0], grads[1], grads[2], grads[3], grads[4], grads[5], grads[6], grads[7], grads[8], grads[9], grads[10], grads[11], grads[12])
```

```python
import functools
import math

import jax
import jax.numpy as jnp
from jax import lax
from jax.experimental import pallas as pl
from jax.experimental.pallas import tpu as pltpu
from jax.sharding import PartitionSpec as P

epsilon = 1e-05


def layer_norm(resid, gain, shift):
    center = jnp.mean(resid, axis=-1, keepdims=True)
    centered = resid - center
    spread = jnp.mean(centered * centered, axis=-1, keepdims=True)
    inverse = lax.rsqrt(spread + epsilon)
    normed = centered * inverse
    return (normed * gain + shift, normed, inverse)


def norm_back(upstream, normed, inverse, gain):
    scaled = upstream * gain
    first_mean = jnp.mean(scaled, axis=-1, keepdims=True)
    second_mean = jnp.mean(scaled * normed, axis=-1, keepdims=True)
    return inverse * (scaled - first_mean - normed * second_mean)


def gelu_slope(value):
    cumulative = 0.5 * (1.0 + lax.erf(value * 0.5**0.5))
    density = jnp.exp(-0.5 * value * value) * (2.0 * math.pi) ** (-0.5)
    return cumulative + value * density


def transpose_left(first, second):
    return lax.dot_general(
        first, second, (((0,), (0,)), ((), ())), preferred_element_type=jnp.float32
    )


def transpose_right(first, second):
    return lax.dot_general(
        first, second, (((1,), (1,)), ((), ())), preferred_element_type=jnp.float32
    )


def group_table(rank, cluster, owners):
    share = cluster // owners
    target = rank // cluster
    length = rank.shape[-1]
    places = lax.broadcasted_iota(jnp.int32, (length, length), 0)
    later = lax.broadcasted_iota(jnp.int32, (length, length), 1)
    before = (places < later)[None, None]
    same = target[..., :, None] == target[..., None, :]
    earlier = jnp.sum((same & before).astype(jnp.int32), axis=-2)
    position = target * share + earlier
    slots = lax.broadcasted_iota(jnp.int32, position.shape + (length,), 3)
    return (position[..., None] == slots).astype(jnp.bfloat16)


def sort_heads(rows, table, heads):
    seqs, length, width = rows.shape
    split = rows.reshape(seqs, length, heads, width // heads)
    moved = jnp.einsum("shtp,sthd->sphd", table, split, preferred_element_type=jnp.float32)
    return moved.astype(rows.dtype).reshape(seqs, length, width)


def unsort_heads(rows, table, heads):
    seqs, length, width = rows.shape
    split = rows.reshape(seqs, length, heads, width // heads)
    moved = jnp.einsum("shtp,sphd->sthd", table, split, preferred_element_type=jnp.float32)
    return moved.astype(rows.dtype).reshape(seqs, length, width)


def cluster_scores(queries, keys_rows, heads):
    items, length, width = queries.shape
    size = width // heads
    query_split = queries.reshape(items, length, heads, size)
    key_split = keys_rows.reshape(items, length, heads, size)
    scores = jnp.einsum(
        "sqhd,skhd->shqk", query_split, key_split, preferred_element_type=jnp.float32
    )
    return scores * size ** (-0.5)


def cluster_forward(queries, keys_rows, values_rows, heads):
    items, length, width = queries.shape
    scores = cluster_scores(queries, keys_rows, heads)
    top = jnp.max(scores, axis=-1, keepdims=True)
    weights = jnp.exp(scores - top)
    total = jnp.sum(weights, axis=-1, keepdims=True)
    probs = (weights / total).astype(jnp.bfloat16)
    value_split = values_rows.reshape(items, length, heads, width // heads)
    context = jnp.einsum("shqk,skhd->sqhd", probs, value_split, preferred_element_type=jnp.float32)
    return (
        context.reshape(items, length, width).astype(jnp.bfloat16),
        (top + jnp.log(total))[..., 0],
    )


def cluster_backward(scores, log_total, queries, keys_rows, values_rows, grad_context, heads):
    items, length, width = queries.shape
    size = width // heads
    query_split = queries.reshape(items, length, heads, size)
    key_split = keys_rows.reshape(items, length, heads, size)
    value_split = values_rows.reshape(items, length, heads, size)
    grad_split = grad_context.reshape(items, length, heads, size)
    probs = jnp.exp(scores - log_total[..., None])
    grad_probs = jnp.einsum(
        "sqhd,skhd->shqk", grad_split, value_split, preferred_element_type=jnp.float32
    )
    inner = jnp.sum(probs * grad_probs, axis=-1, keepdims=True)
    grad_scores = (probs * (grad_probs - inner)).astype(jnp.bfloat16)
    scale = size ** (-0.5)
    grad_query = (
        jnp.einsum("shqk,skhd->sqhd", grad_scores, key_split, preferred_element_type=jnp.float32)
        * scale
    )
    grad_key = (
        jnp.einsum("shqk,sqhd->skhd", grad_scores, query_split, preferred_element_type=jnp.float32)
        * scale
    )
    grad_value = jnp.einsum(
        "shqk,sqhd->skhd",
        probs.astype(jnp.bfloat16),
        grad_split,
        preferred_element_type=jnp.float32,
    )
    shape = (items, length, width)
    return (
        grad_query.reshape(shape).astype(jnp.bfloat16),
        grad_key.reshape(shape).astype(jnp.bfloat16),
        grad_value.reshape(shape).astype(jnp.bfloat16),
    )


def send_context(context):
    return lax.all_to_all(context, "seq", split_axis=1, concat_axis=1, tiled=True)


def send_grads(grads):
    return (
        lax.all_to_all(grads[0], "seq", split_axis=1, concat_axis=1, tiled=True),
        lax.all_to_all(grads[1], "seq", split_axis=1, concat_axis=1, tiled=True),
        lax.all_to_all(grads[2], "seq", split_axis=1, concat_axis=1, tiled=True),
    )


def make_step(left, pieces):
    total = jnp.dot(left, pieces[0], preferred_element_type=jnp.float32)
    stored = tuple(pieces[1:]) + ()
    placed = tuple((piece for piece in stored))
    return (total,) + placed


def make_hidden_step(before, pieces):
    section = before + pieces[1].astype(jnp.float32)
    activated = jax.nn.gelu(section, approximate=False).astype(jnp.bfloat16)
    total = jnp.dot(activated, pieces[0], preferred_element_type=jnp.float32)
    stored = ()
    return (total, section, activated) + stored


def per_device(
    tokens,
    attend_weight,
    query_bias,
    value_bias,
    output_weight,
    output_bias,
    first_gain,
    first_shift,
    expand_weight,
    expand_bias,
    reduce_weight,
    reduce_bias,
    second_gain,
    second_shift,
    query_rank,
    key_rank,
    cotangent,
):
    seqs, cluster, width = tokens.shape
    heads = query_rank.shape[1]
    rows = seqs * cluster
    owners = lax.axis_size("seq")
    flat = tokens.reshape(rows, width)
    attend_out = make_step(
        flat,
        (
            lax.all_gather(attend_weight, "batch", axis=0, tiled=True),
            lax.all_gather(query_bias, "batch", axis=0, tiled=True),
            lax.all_gather(value_bias, "batch", axis=0, tiled=True),
        ),
    )
    summed = attend_out[0]
    queries = (summed[:, :width] + attend_out[1].astype(jnp.float32)).astype(jnp.bfloat16)
    keys_rows = summed[:, width : 2 * width].astype(jnp.bfloat16)
    values_rows = (summed[:, 2 * width :] + attend_out[2].astype(jnp.float32)).astype(jnp.bfloat16)
    query_table = group_table(query_rank, cluster, owners)
    key_table = group_table(key_rank, cluster, owners)
    query_sorted = sort_heads(queries.reshape(seqs, cluster, width), query_table, heads)
    key_sorted = sort_heads(keys_rows.reshape(seqs, cluster, width), key_table, heads)
    value_sorted = sort_heads(values_rows.reshape(seqs, cluster, width), key_table, heads)
    received = (
        lax.all_to_all(query_sorted, "seq", split_axis=1, concat_axis=1, tiled=True),
        lax.all_to_all(key_sorted, "seq", split_axis=1, concat_axis=1, tiled=True),
        lax.all_to_all(value_sorted, "seq", split_axis=1, concat_axis=1, tiled=True),
    )
    context, log_total = cluster_forward(received[0], received[1], received[2], heads)
    forward_out = (send_context(context), log_total, received[0], received[1], received[2])
    context_rows = unsort_heads(forward_out[0], query_table, heads).reshape(rows, width)
    output_out = make_step(
        context_rows,
        (
            lax.all_gather(output_weight, "batch", axis=0, tiled=True),
            lax.all_gather(output_bias, "batch", axis=0, tiled=True),
            lax.all_gather(first_gain, "batch", axis=0, tiled=True),
            lax.all_gather(first_shift, "batch", axis=0, tiled=True),
        ),
    )
    resid_one = flat.astype(jnp.float32) + output_out[0] + output_out[1].astype(jnp.float32)
    gain_one = output_out[2].astype(jnp.float32)
    middle, normed_one, inverse_one = layer_norm(
        resid_one, gain_one, output_out[3].astype(jnp.float32)
    )
    middle_low = middle.astype(jnp.bfloat16)
    expand_out = make_step(
        middle_low,
        (
            lax.all_gather(expand_weight, "batch", axis=0, tiled=True),
            lax.all_gather(reduce_bias, "batch", axis=0, tiled=True),
            lax.all_gather(second_gain, "batch", axis=0, tiled=True),
            lax.all_gather(second_shift, "batch", axis=0, tiled=True),
        ),
    )
    hidden_out = make_hidden_step(
        expand_out[0],
        (
            lax.all_gather(reduce_weight, "batch", axis=0, tiled=True),
            lax.all_gather(expand_bias, "batch", axis=0, tiled=True),
        ),
    )
    pre_full, hidden_full = (hidden_out[1], hidden_out[2])
    resid_two = middle + hidden_out[0] + expand_out[1].astype(jnp.float32)
    gain_two = expand_out[2].astype(jnp.float32)
    final, normed_two, inverse_two = layer_norm(
        resid_two, gain_two, expand_out[3].astype(jnp.float32)
    )
    layer_out = final.astype(jnp.bfloat16).reshape(seqs, cluster, width)
    attend_full, output_full, expand_full, reduce_full = (
        lax.all_gather(attend_weight, "batch", axis=0, tiled=True),
        lax.all_gather(output_weight, "batch", axis=0, tiled=True),
        lax.all_gather(expand_weight, "batch", axis=0, tiled=True),
        lax.all_gather(reduce_weight, "batch", axis=0, tiled=True),
    )
    upstream = cotangent.reshape(rows, width).astype(jnp.float32)
    grad_second_gain = jnp.sum(upstream * normed_two, axis=0)
    grad_second_shift = jnp.sum(upstream, axis=0)
    grad_resid_two = norm_back(upstream, normed_two, inverse_two, gain_two)
    grad_branch_two = grad_resid_two.astype(jnp.bfloat16)
    grad_reduce_bias = jnp.sum(grad_branch_two, axis=0, dtype=jnp.float32)
    grad_reduce = transpose_left(hidden_full, grad_branch_two)
    grad_hidden = transpose_right(grad_branch_two, reduce_full)
    grad_pre = (grad_hidden * gelu_slope(pre_full)).astype(jnp.bfloat16)
    grad_expand_bias = jnp.sum(grad_pre, axis=0, dtype=jnp.float32)
    grad_expand = transpose_left(middle_low, grad_pre)
    grad_middle = grad_resid_two + transpose_right(grad_pre, expand_full)
    grad_first_gain = jnp.sum(grad_middle * normed_one, axis=0)
    grad_first_shift = jnp.sum(grad_middle, axis=0)
    grad_resid_one = norm_back(grad_middle, normed_one, inverse_one, gain_one)
    grad_branch_one = grad_resid_one.astype(jnp.bfloat16)
    grad_output_bias = jnp.sum(grad_branch_one, axis=0, dtype=jnp.float32)
    grad_output = transpose_left(context_rows, grad_branch_one)
    grad_context = transpose_right(grad_branch_one, output_full).astype(jnp.bfloat16)
    grad_sorted = sort_heads(grad_context.reshape(seqs, cluster, width), query_table, heads)
    grad_received = lax.all_to_all(grad_sorted, "seq", split_axis=1, concat_axis=1, tiled=True)
    kept_scores = cluster_scores(forward_out[2], forward_out[3], heads)
    home = send_grads(
        cluster_backward(
            kept_scores,
            forward_out[1],
            forward_out[2],
            forward_out[3],
            forward_out[4],
            grad_received,
            heads,
        )
    )
    grad_queries = unsort_heads(home[0], query_table, heads).reshape(rows, width)
    grad_keys = unsort_heads(home[1], key_table, heads).reshape(rows, width)
    grad_values = unsort_heads(home[2], key_table, heads).reshape(rows, width)
    grad_mixed = jnp.concatenate([grad_queries, grad_keys, grad_values], axis=1)
    grad_query_bias = jnp.sum(grad_queries, axis=0, dtype=jnp.float32)
    grad_value_bias = jnp.sum(grad_values, axis=0, dtype=jnp.float32)
    grad_attend = transpose_left(flat, grad_mixed)
    token_grad = (
        (grad_resid_one + transpose_right(grad_mixed, attend_full))
        .astype(jnp.bfloat16)
        .reshape(seqs, cluster, width)
    )
    owned = (
        lax.psum_scatter(
            grad_attend.astype(jnp.bfloat16), "batch", scatter_dimension=0, tiled=True
        ).astype(jnp.float32),
        lax.psum_scatter(
            grad_query_bias.astype(jnp.bfloat16), "batch", scatter_dimension=0, tiled=True
        ).astype(jnp.float32),
        lax.psum_scatter(
            grad_value_bias.astype(jnp.bfloat16), "batch", scatter_dimension=0, tiled=True
        ).astype(jnp.float32),
        lax.psum_scatter(
            grad_output.astype(jnp.bfloat16), "batch", scatter_dimension=0, tiled=True
        ).astype(jnp.float32),
        lax.psum_scatter(
            grad_output_bias.astype(jnp.bfloat16), "batch", scatter_dimension=0, tiled=True
        ).astype(jnp.float32),
        lax.psum_scatter(
            grad_first_gain.astype(jnp.bfloat16), "batch", scatter_dimension=0, tiled=True
        ).astype(jnp.float32),
        lax.psum_scatter(
            grad_first_shift.astype(jnp.bfloat16), "batch", scatter_dimension=0, tiled=True
        ).astype(jnp.float32),
        lax.psum_scatter(
            grad_expand.astype(jnp.bfloat16), "batch", scatter_dimension=0, tiled=True
        ).astype(jnp.float32),
        lax.psum_scatter(
            grad_expand_bias.astype(jnp.bfloat16), "batch", scatter_dimension=0, tiled=True
        ).astype(jnp.float32),
        lax.psum_scatter(
            grad_reduce.astype(jnp.bfloat16), "batch", scatter_dimension=0, tiled=True
        ).astype(jnp.float32),
        lax.psum_scatter(
            grad_reduce_bias.astype(jnp.bfloat16), "batch", scatter_dimension=0, tiled=True
        ).astype(jnp.float32),
        lax.psum_scatter(
            grad_second_gain.astype(jnp.bfloat16), "batch", scatter_dimension=0, tiled=True
        ).astype(jnp.float32),
        lax.psum_scatter(
            grad_second_shift.astype(jnp.bfloat16), "batch", scatter_dimension=0, tiled=True
        ).astype(jnp.float32),
    )
    shared = (
        lax.psum(owned[0].astype(jnp.bfloat16), "seq").astype(jnp.float32),
        lax.psum(owned[1].astype(jnp.bfloat16), "seq").astype(jnp.float32),
        lax.psum(owned[2].astype(jnp.bfloat16), "seq").astype(jnp.float32),
        lax.psum(owned[3].astype(jnp.bfloat16), "seq").astype(jnp.float32),
        lax.psum(owned[4].astype(jnp.bfloat16), "seq").astype(jnp.float32),
        lax.psum(owned[5].astype(jnp.bfloat16), "seq").astype(jnp.float32),
        lax.psum(owned[6].astype(jnp.bfloat16), "seq").astype(jnp.float32),
        lax.psum(owned[7].astype(jnp.bfloat16), "seq").astype(jnp.float32),
        lax.psum(owned[8].astype(jnp.bfloat16), "seq").astype(jnp.float32),
        lax.psum(owned[9].astype(jnp.bfloat16), "seq").astype(jnp.float32),
        lax.psum(owned[10].astype(jnp.bfloat16), "seq").astype(jnp.float32),
        lax.psum(owned[11].astype(jnp.bfloat16), "seq").astype(jnp.float32),
        lax.psum(owned[12].astype(jnp.bfloat16), "seq").astype(jnp.float32),
    )
    return (
        layer_out,
        token_grad,
        shared[0],
        shared[1],
        shared[2],
        shared[3],
        shared[4],
        shared[5],
        shared[6],
        shared[7],
        shared[8],
        shared[9],
        shared[10],
        shared[11],
        shared[12],
    )


MESH = pl.DeviceIdType.MESH
f32 = jnp.float32
bf16 = jnp.bfloat16


class Place:
    def __init__(self, chips, depth):
        self.chips, self.depth = chips, depth
        self.z = lax.axis_index("batch")
        spot = lax.axis_index("seq")
        self.chip, self.core = lax.div(spot, 2), lax.rem(spot, 2)

    def chip_at(self, k):
        return lax.rem(self.chip + k + self.chips, self.chips)

    def z_at(self, k):
        return lax.rem(self.z + k + self.depth, self.depth)

    def plane(self, k):
        return (self.z, self.chip_at(k) * 2 + self.core)

    def tower(self, k):
        return (self.z_at(k), self.chip * 2 + self.core)

    def sibling(self):
        return (self.z, self.chip * 2 + 1 - self.core)

    def greet(self):
        bell = pltpu.get_barrier_semaphore()
        others = [self.plane(k) for k in range(1, self.chips)]
        others += [self.tower(k) for k in range(1, self.depth)]
        others.append(self.sibling())
        for other in others:
            pl.semaphore_signal(bell, inc=1, device_id=other, device_id_type=MESH)
        pl.semaphore_wait(bell, len(others))


def far_copy(src, dst, sems, at, device):
    return pltpu.make_async_remote_copy(
        src_ref=src,
        dst_ref=dst,
        send_sem=sems[0].at[at],
        recv_sem=sems[1].at[at],
        device_id=device,
        device_id_type=MESH,
    )


def one_hot(row, slots):
    return jnp.where(slots == row, 1.0, 0.0).astype(bf16)


def split_lanes(tile, low):
    zero = jnp.zeros_like(tile)
    return jnp.where(low, tile, zero), jnp.where(low, zero, tile)


def stack_lanes(tile, low):
    first, second = split_lanes(tile, low)
    return jnp.concatenate([first, second], axis=0)


def dot_rows(a, b):
    return jnp.dot(a, b, preferred_element_type=f32)


def dot_lanes(a, b):
    return lax.dot_general(a, b, (((1,), (1,)), ((), ())), preferred_element_type=f32)


def dot_first(a, b):
    return lax.dot_general(a, b, (((0,), (0,)), ((), ())), preferred_element_type=f32)


def multiple(value, by):
    return pl.multiple_of(value, by)


def attend_kernel(
    chips,
    depth,
    heads,
    tok_ref,
    pos_ref,
    aw_ref,
    vec_ref,
    ow_ref,
    ew_ref,
    rw_ref,
    x_out,
    ctx_out,
    q_out,
    k_out,
    v_out,
    p_out,
    pos_out,
    aw_out,
    vec_out,
    ow_out,
    ew_out,
    rw_out,
    xbuf,
    posbuf,
    wbuf,
    vbuf,
    bias,
    qkv,
    qs,
    ks,
    vs,
    ps,
    os,
    ctxb,
    tok_s,
    tok_r,
    tokc_s,
    tokc_r,
    pos_s,
    pos_r,
    posc_s,
    posc_r,
    aw_s,
    aw_r,
    awc_s,
    awc_r,
    vec_s,
    vec_r,
    wz_s,
    wz_r,
    wp_s,
    wp_r,
    wc_s,
    wc_r,
    ctx_s,
    ctx_r,
    loc,
    out_sem,
):
    me = Place(chips, depth)
    z, chip, core = me.z, me.chip, me.core
    per = tok_ref.shape[0] // chips
    half = aw_ref.shape[1] // 6
    rows_z = aw_ref.shape[0]
    pairs = heads // 4
    size = half // (2 * pairs)
    me.greet()

    def aw_copy(k, part):
        columns = pl.ds(multiple(part * 2 * half + core * half, 128), half)
        return far_copy(
            aw_ref.at[:, columns],
            wbuf.at[pl.ds(multiple(z * rows_z, 8), rows_z), pl.ds(part * half, half)],
            (aw_s, aw_r),
            (k - 1) * 3 + part,
            me.tower(k),
        )

    def mine(ref, target):
        return ref.at[pl.ds(target * per, per)]

    def tok_copy(k):
        return far_copy(
            mine(tok_ref, me.chip_at(k)), xbuf.at[core, chip], (tok_s, tok_r), k - 1, me.plane(k)
        )

    def pos_copy(k):
        return far_copy(
            mine(pos_ref, me.chip_at(k)), posbuf.at[core, chip], (pos_s, pos_r), k - 1, me.plane(k)
        )

    def vec_copy(k):
        return far_copy(vec_ref, vbuf.at[z], (vec_s, vec_r), k - 1, me.tower(k))

    sends = []
    for k in range(1, chips):
        sends.append(pos_copy(k))
        sends[-1].start()
    for k in range(1, depth):
        sends.append(vec_copy(k))
        sends[-1].start()
    for k in range(1, max(chips, depth)):
        if k < depth:
            for part in range(3):
                sends.append(aw_copy(k, part))
                sends[-1].start()
        if k < chips:
            sends.append(tok_copy(k))
            sends[-1].start()
    local = []

    def keep(src, dst):
        copy = pltpu.make_async_copy(src, dst, loc.at[len(local)])
        copy.start()
        local.append(copy)

    keep(mine(tok_ref, chip), xbuf.at[core, chip])
    keep(mine(pos_ref, chip), posbuf.at[core, chip])
    keep(vec_ref, vbuf.at[z])
    for part in range(3):
        keep(
            aw_ref.at[:, pl.ds(multiple(part * 2 * half + core * half, 128), half)],
            wbuf.at[pl.ds(multiple(z * rows_z, 8), rows_z), pl.ds(part * half, half)],
        )
    eighth = ow_ref.shape[0] // (2 * chips)
    wide = ew_ref.shape[1] // (2 * chips)
    tall = rw_ref.shape[0] // (2 * chips)

    def piece(ref, kind, at):
        if kind == 0:
            return ref.at[pl.ds(multiple(at * eighth, 8), eighth)]
        if kind == 1:
            return ref.at[:, pl.ds(multiple(at * wide, 128), wide)]
        return ref.at[pl.ds(multiple(at * tall, 8), tall)]

    shards = (ow_ref, ew_ref, rw_ref)
    fulls = (ow_out, ew_out, rw_out)
    mine_at = core * chips + chip

    def place(kind, zz, at):
        if kind == 0:
            return ow_out.at[zz, at]
        if kind == 1:
            return ew_out.at[zz, :, pl.ds(multiple(at * wide, 128), wide)]
        return rw_out.at[zz, at]

    def place_all(kind, at):
        if kind == 0:
            return ow_out.at[:, at]
        if kind == 1:
            return ew_out.at[:, :, pl.ds(multiple(at * wide, 128), wide)]
        return rw_out.at[:, at]

    for kind in range(3):
        keep(piece(shards[kind], kind, mine_at), place(kind, z, mine_at))

    def wz_copy(kind, k):
        return far_copy(
            piece(shards[kind], kind, mine_at),
            place(kind, z, mine_at),
            (wz_s, wz_r),
            kind * (depth - 1) + k - 1,
            me.tower(k),
        )

    def wp_copy(kind, k, origin):
        at = core * chips + origin
        return far_copy(
            place_all(kind, at),
            place_all(kind, at),
            (wp_s, wp_r),
            kind * (chips - 1) + k - 1,
            me.plane(k),
        )

    def wc_copy(kind, origin_k):
        at = core * chips + me.chip_at(origin_k)
        return far_copy(
            place_all(kind, at),
            place_all(kind, at),
            (wc_s, wc_r),
            kind * chips + origin_k,
            me.sibling(),
        )

    for copy in local[:2]:
        copy.wait()

    def tokc_copy(k):
        source = me.chip_at(-k)
        return far_copy(
            xbuf.at[core, source], xbuf.at[core, source], (tokc_s, tokc_r), k, me.sibling()
        )

    def posc_copy(k):
        source = me.chip_at(-k)
        return far_copy(
            posbuf.at[core, source], posbuf.at[core, source], (posc_s, posc_r), k, me.sibling()
        )

    for k in range(chips):
        if k:
            pos_copy(k).wait_recv()
            tok_copy(k).wait_recv()
        for copy in (posc_copy(k), tokc_copy(k)):
            copy.start()
            sends.append(copy)
    for copy in local[2:6]:
        copy.wait()
    for k in range(1, depth):
        vec_copy(k).wait_recv()
        for part in range(3):
            aw_copy(k, part).wait_recv()
    for k in range(chips):
        posc_copy(k).wait_recv()
        tokc_copy(k).wait_recv()
    for copy in local[6:]:
        copy.wait()
    for kind in range(3):
        for k in range(1, depth):
            sends.append(wz_copy(kind, k))
            sends[-1].start()

    outs = []

    def emit(src, dst):
        copy = pltpu.make_async_copy(src, dst, out_sem.at[len(outs)])
        copy.start()
        outs.append(copy)

    emit(xbuf, x_out)
    emit(posbuf, pos_out)
    emit(wbuf, aw_out.at[core])
    emit(vbuf, vec_out)
    awc = far_copy(wbuf, aw_out.at[core], (awc_s, awc_r), 0, me.sibling())
    awc.start()
    sends.append(awc)

    quarter = rows_z
    for zz in range(depth):
        begin = zz * quarter
        for row, at in ((0, 0), (1, 2)):
            for side in range(2):
                lo = max(begin, side * half)
                hi = min(begin + quarter, (side + 1) * half)
                if lo < hi:
                    bias[side, 0:1, at * half + lo - side * half : at * half + hi - side * half] = (
                        vbuf[zz, row : row + 1, lo - begin : hi - begin]
                    )
    bias[0, 0:1, half : 2 * half] = jnp.zeros((1, half), f32)
    bias[1, 0:1, half : 2 * half] = jnp.zeros((1, half), f32)
    added = bias[core, 0:1, :]

    cluster = tok_ref.shape[1]
    blocks = 2 * chips
    share = cluster // blocks
    width = tok_ref.shape[2]

    @pl.loop(0, blocks)
    def _(jj):
        x = xbuf[lax.div(jj, chips), lax.rem(jj, chips)].reshape(per * cluster, width)
        mixed = (dot_rows(x, wbuf[...]) + added).astype(bf16)
        for at in range(3 * pairs):
            qkv[at, jj] = mixed[:, at * 128 : (at + 1) * 128].reshape(per, cluster, 128)

    slots = lax.broadcasted_iota(jnp.int32, (cluster, cluster), 0)
    low = lax.broadcasted_iota(jnp.int32, (cluster, 128), 1) < size
    scale = size ** (-0.5)

    def tables(jj, i, pair, part):
        first = part * heads + core * (heads // 2) + 2 * pair
        rows = [
            one_hot(posbuf[jj // chips, jj % chips, i, pl.ds(first + h, 1), :], slots)
            for h in range(2)
        ]
        return rows

    def weights_step(stage):
        if stage == 0:
            for kind in range(3):
                for k in range(1, depth):
                    wz_copy(kind, k).wait_recv()
                for k in range(1, chips):
                    wp_copy(kind, k, chip).start()
                wc_copy(kind, 0).start()

    @pl.loop(0, per)
    def _(i):
        @pl.loop(0, pairs)
        def _(pair):
            at = i * pairs + pair
            for jj in range(blocks):
                tq = jnp.concatenate(tables(jj, i, pair, 0), axis=1)
                tk = jnp.concatenate(tables(jj, i, pair, 1), axis=1)
                q = stack_lanes(qkv[pair, jj, i], low)
                k = stack_lanes(qkv[pairs + pair, jj, i], low)
                v = stack_lanes(qkv[2 * pairs + pair, jj, i], low)
                span = slice(jj * share, (jj + 1) * share)
                sq = dot_rows(tq, q).astype(bf16)
                skv = dot_rows(tk, jnp.concatenate([k, v], axis=1)).astype(bf16)
                qs[at, :, span, :] = sq.reshape(blocks, share, 128)
                ks[at, :, span, :] = skv[:, :128].reshape(blocks, share, 128)
                vs[at, :, span, :] = skv[:, 128:].reshape(blocks, share, 128)
            for c in range(blocks):
                scores = dot_lanes(qs[at, c], stack_lanes(ks[at, c], low)) * scale
                halves = []
                for h in range(2):
                    s = scores[:, h * cluster : (h + 1) * cluster]
                    e = jnp.exp(s - jnp.max(s, axis=1, keepdims=True))
                    halves.append((e / jnp.sum(e, axis=1, keepdims=True)).astype(bf16))
                probs = jnp.concatenate(halves, axis=1)
                ps[at, c] = probs
                o = dot_rows(probs, stack_lanes(vs[at, c], low)).astype(bf16)
                os[c] = o
            for jj in range(blocks):
                tq = jnp.concatenate(tables(jj, i, pair, 0), axis=0)
                rows = os[:, jj * share : (jj + 1) * share, :].reshape(cluster, 128)
                back = dot_first(tq, stack_lanes(rows, low)).astype(bf16)
                ctxb[jj // chips, jj % chips, i, :, pl.ds(multiple(pair * 128, 128), 128)] = back

        @pl.when(i == 0)
        def _():
            weights_step(0)

    far = far_copy(
        ctxb.at[1 - core],
        ctx_out.at[:, :, :, pl.ds(multiple(core * half, 128), half)],
        (ctx_s, ctx_r),
        0,
        me.sibling(),
    )
    far.start()
    emit(ctxb.at[core], ctx_out.at[:, :, :, pl.ds(multiple(core * half, 128), half)])
    emit(qs, q_out)
    emit(ks, k_out)
    emit(vs, v_out)
    emit(ps, p_out)
    for kind in range(3):
        for k in range(1, chips):
            wp_copy(kind, k, me.chip_at(-k)).wait_recv()
            wc_copy(kind, chips - k).start()
    for kind in range(3):
        for k in range(chips):
            wc_copy(kind, k).wait()
        for k in range(1, chips):
            wp_copy(kind, k, chip).wait_send()
    far.wait()
    awc.wait_recv()
    for copy in sends:
        copy.wait_send()
    for copy in outs:
        copy.wait()


def attend(tokens, pos, attend_weight, vectors, output_weight, expand_weight, reduce_weight, chips, depth, heads):
    seqs, cluster, width = tokens.shape
    per, blocks, pairs = seqs // chips, 2 * chips, heads // 4
    half = width // 2
    rows_z = attend_weight.shape[0]
    wide = expand_weight.shape[1]
    items = per * pairs
    dma = pltpu.SemaphoreType.DMA
    anywhere = pl.BlockSpec(memory_space=pl.ANY)
    eighth = output_weight.shape[0] // blocks
    tall = reduce_weight.shape[0] // blocks
    shapes = [
        ((2, chips, per, cluster, width), bf16),
        ((chips, per, cluster, width), bf16),
        ((items, blocks, cluster, 128), bf16),
        ((items, blocks, cluster, 128), bf16),
        ((items, blocks, cluster, 128), bf16),
        ((items, blocks, cluster, 2 * cluster), bf16),
        ((2, chips, per, 2 * heads, cluster), jnp.int32),
        ((2, depth * rows_z, 3 * half), bf16),
        ((depth,) + vectors.shape, f32),
        ((depth, blocks, eighth, width), bf16),
        ((depth, rows_z, wide), bf16),
        ((depth, blocks, tall, width), bf16),
    ]
    t, c = depth - 1, chips - 1
    return pl.pallas_call(
        functools.partial(attend_kernel, chips, depth, heads),
        out_shape=[jax.ShapeDtypeStruct(*s) for s in shapes],
        in_specs=[anywhere] * 7,
        out_specs=[anywhere] * len(shapes),
        scratch_shapes=[
            pltpu.VMEM(shapes[0][0], bf16),
            pltpu.VMEM(shapes[6][0], jnp.int32),
            pltpu.VMEM(shapes[7][0][1:], bf16),
            pltpu.VMEM(shapes[8][0], f32),
            pltpu.VMEM((2, 8, 3 * half), f32),
            pltpu.VMEM((3 * pairs, blocks, per, cluster, 128), bf16),
            pltpu.VMEM(shapes[2][0], bf16),
            pltpu.VMEM(shapes[3][0], bf16),
            pltpu.VMEM(shapes[4][0], bf16),
            pltpu.VMEM(shapes[5][0], bf16),
            pltpu.VMEM((blocks, cluster, 128), bf16),
            pltpu.VMEM((2, chips, per, cluster, half), bf16),
            dma((c,)), dma((c,)), dma((chips,)), dma((chips,)),
            dma((c,)), dma((c,)), dma((chips,)), dma((chips,)),
            dma((3 * t,)), dma((3 * t,)), dma((1,)), dma((1,)),
            dma((t,)), dma((t,)),
            dma((3 * t,)), dma((3 * t,)),
            dma((3 * c,)), dma((3 * c,)),
            dma((3 * chips,)), dma((3 * chips,)),
            dma((1,)), dma((1,)),
            dma((9,)), dma((9,)),
        ],
        compiler_params=pltpu.CompilerParams(
            collective_id=1, has_side_effects=True, vmem_limit_bytes=60 * 2**20
        ),
        name="attend",
    )(tokens, pos, attend_weight, vectors, output_weight, expand_weight, reduce_weight)


def attend_back_kernel(
    chips,
    depth,
    heads,
    d_ref,
    q_ref,
    k_ref,
    v_ref,
    p_ref,
    pos_ref,
    x_ref,
    g_out,
    dw_out,
    db_out,
    dbuf,
    qs,
    ks,
    vs,
    ps,
    posbuf,
    xbuf,
    ds,
    gs,
    gbuf,
    dw,
    db,
    d_s,
    d_r,
    g_s,
    g_r,
    loc,
):
    me = Place(chips, depth)
    core = me.core
    per = d_ref.shape[1]
    cluster, width = d_ref.shape[2], d_ref.shape[3]
    half = width // 2
    pairs = heads // 4
    size = half // (2 * pairs)
    blocks = 2 * chips
    share = cluster // blocks
    me.greet()
    theirs = pl.ds(multiple((1 - core) * half, 128), half)
    far = far_copy(d_ref.at[:, :, :, theirs], dbuf.at[core], (d_s, d_r), 0, me.sibling())
    far.start()
    local = []

    def keep(src, dst):
        copy = pltpu.make_async_copy(src, dst, loc.at[len(local)])
        copy.start()
        local.append(copy)

    keep(d_ref.at[:, :, :, pl.ds(multiple(core * half, 128), half)], dbuf.at[core])
    keep(pos_ref, posbuf)
    keep(q_ref, qs)
    keep(k_ref, ks)
    keep(v_ref, vs)
    keep(p_ref, ps)
    keep(x_ref, xbuf)
    for copy in local[:6]:
        copy.wait()
    far.wait()
    slots = lax.broadcasted_iota(jnp.int32, (cluster, cluster), 0)
    low = lax.broadcasted_iota(jnp.int32, (cluster, 128), 1) < size
    scale = size ** (-0.5)
    db[...] = jnp.zeros_like(db)
    dw[...] = jnp.zeros_like(dw)

    def tables(jj, i, pair, part):
        first = part * heads + core * (heads // 2) + 2 * pair
        return [
            one_hot(posbuf[jj // chips, jj % chips, i, pl.ds(first + h, 1), :], slots)
            for h in range(2)
        ]

    for copy in local[6:]:
        copy.wait()

    @pl.loop(0, per)
    def _(i):
        @pl.loop(0, pairs)
        def _(pair):
            at = i * pairs + pair
            lanes = pl.ds(multiple(pair * 128, 128), 128)
            for jj in range(blocks):
                tq = jnp.concatenate(tables(jj, i, pair, 0), axis=1)
                rows = stack_lanes(dbuf[jj // chips, jj % chips, i, :, lanes], low)
                ds[:, jj * share : (jj + 1) * share, :] = (
                    dot_rows(tq, rows).astype(bf16).reshape(blocks, share, 128)
                )
            for c in range(blocks):
                d = ds[c]
                probs = ps[at, c]
                slope = dot_lanes(d, stack_lanes(vs[at, c], low))
                wide = probs.astype(f32)
                halves = []
                for h in range(2):
                    span = slice(h * cluster, (h + 1) * cluster)
                    inner = jnp.sum(wide[:, span] * slope[:, span], axis=1, keepdims=True)
                    halves.append((wide[:, span] * (slope[:, span] - inner)).astype(bf16))
                grads = jnp.concatenate(halves, axis=1)
                gq = dot_rows(grads, stack_lanes(ks[at, c], low)) * scale
                gk = dot_first(grads, qs[at, c]) * scale
                gv = dot_first(probs, d)
                gs[0, c] = gq.astype(bf16)
                gs[1, c] = jnp.where(low, gk[:cluster], gk[cluster:]).astype(bf16)
                gs[2, c] = jnp.where(low, gv[:cluster], gv[cluster:]).astype(bf16)
            for jj in range(blocks):
                for part in range(3):
                    if part < 2:
                        table = jnp.concatenate(tables(jj, i, pair, part), axis=0)
                    rows = gs[part, :, jj * share : (jj + 1) * share, :].reshape(cluster, 128)
                    back = dot_first(table, stack_lanes(rows, low))
                    to = pl.ds(multiple(part * half + pair * 128, 128), 128)
                    gbuf[jj // chips, jj % chips, i, :, to] = back.astype(bf16)

        for b in range(2):
            x = jnp.concatenate([xbuf[b, j, i] for j in range(chips)], axis=0)
            g = jnp.concatenate([gbuf[b, j, i] for j in range(chips)], axis=0)
            dw[...] += dot_first(x, g)
            db[0:1, :] += jnp.sum(g.astype(f32), axis=0, keepdims=True)

    give = far_copy(gbuf.at[1 - core], g_out.at[core], (g_s, g_r), 0, me.sibling())
    give.start()
    tail = []
    for n, (src, dst) in enumerate(
        ((gbuf.at[core], g_out.at[core]), (dw, dw_out), (db, db_out))
    ):
        tail.append(pltpu.make_async_copy(src, dst, loc.at[n]))
        tail[-1].start()
    for copy in tail:
        copy.wait()
    give.wait()


def attend_back(grad_context, q, k, v, p, pos, x, depth, heads):
    chips, per, cluster, width = grad_context.shape
    half, blocks, pairs = width // 2, 2 * chips, heads // 4
    dma = pltpu.SemaphoreType.DMA
    anywhere = pl.BlockSpec(memory_space=pl.ANY)
    shapes = [
        ((2, chips, per, cluster, 3 * half), bf16),
        ((width, 3 * half), f32),
        ((8, 3 * half), f32),
    ]
    return pl.pallas_call(
        functools.partial(attend_back_kernel, chips, depth, heads),
        out_shape=[jax.ShapeDtypeStruct(*s) for s in shapes],
        in_specs=[anywhere] * 7,
        out_specs=[anywhere] * 3,
        scratch_shapes=[
            pltpu.VMEM((2, chips, per, cluster, half), bf16),
            pltpu.VMEM(q.shape, bf16),
            pltpu.VMEM(q.shape, bf16),
            pltpu.VMEM(q.shape, bf16),
            pltpu.VMEM(p.shape, bf16),
            pltpu.VMEM(pos.shape, jnp.int32),
            pltpu.VMEM(x.shape, bf16),
            pltpu.VMEM((blocks, cluster, 128), bf16),
            pltpu.VMEM((3, blocks, cluster, 128), bf16),
            pltpu.VMEM(shapes[0][0], bf16),
            pltpu.VMEM(shapes[1][0], f32),
            pltpu.VMEM(shapes[2][0], f32),
            dma((1,)), dma((1,)), dma((1,)), dma((1,)),
            dma((7,)),
        ],
        compiler_params=pltpu.CompilerParams(
            collective_id=2, has_side_effects=True, vmem_limit_bytes=60 * 2**20
        ),
        name="attend_back",
    )(grad_context, q, k, v, p, pos, x)


def places(rank, cluster, share):
    seqs, rows, length = rank.shape
    clusters = cluster // share
    target = rank // cluster
    which = lax.broadcasted_iota(jnp.int32, (1, 1, clusters, 1), 2)
    inside = (target[:, :, None, :] == which).astype(bf16)
    first = lax.broadcasted_iota(jnp.int32, (length, length), 0)
    second = lax.broadcasted_iota(jnp.int32, (length, length), 1)
    before = (first < second).astype(bf16)
    count = lax.dot_general(
        inside.reshape(seqs * rows * clusters, length),
        before,
        (((1,), (0,)), ((), ())),
        preferred_element_type=f32,
    ).reshape(seqs, rows, clusters, length)
    spot = which.astype(f32) * share + count
    return jnp.sum(inside.astype(f32) * spot, axis=2).astype(jnp.int32)


def per_chip(
    tokens,
    attend_weight,
    query_bias,
    value_bias,
    output_weight,
    output_bias,
    first_gain,
    first_shift,
    expand_weight,
    expand_bias,
    reduce_weight,
    reduce_bias,
    second_gain,
    second_shift,
    query_rank,
    key_rank,
    cotangent,
):
    seqs, cluster, width = tokens.shape
    heads = query_rank.shape[1]
    owners = lax.axis_size("seq")
    depth = lax.axis_size("batch")
    chips = owners // 2
    per = seqs // chips
    rows = seqs * cluster
    half = width // 2
    share = cluster // owners
    core = lax.rem(lax.axis_index("seq"), 2)
    groups = [[2 * p + c for p in range(chips)] for c in range(2)]

    def swap(x):
        return lax.all_to_all(
            x, "seq", split_axis=0, concat_axis=0, tiled=True, axis_index_groups=groups
        )

    pos = places(jnp.concatenate([query_rank, key_rank], axis=1), cluster, share)
    quarter = width // depth
    small = jnp.concatenate(
        [
            v.astype(f32)
            for v in (
                query_bias,
                value_bias,
                output_bias,
                first_gain,
                first_shift,
                reduce_bias,
                second_gain,
                second_shift,
                expand_bias,
            )
        ]
    )
    count = small.shape[0] // quarter
    vectors = jnp.pad(small.reshape(count, quarter), ((0, 16 - count), (0, 256 - quarter)))
    (x_all, context, qs, ks, vs, ps, pos_all, attend_all, vec_all, out_all, exp_all, red_all) = attend(
        tokens, pos, attend_weight, vectors, output_weight, expand_weight, reduce_weight, chips, depth, heads
    )
    full = jnp.transpose(vec_all[:, :8, :quarter], (1, 0, 2)).reshape(8, width)
    bias_up = vec_all[:, 8:count, :quarter].reshape(-1)
    output_full = out_all.reshape(width, width)
    expand_full = exp_all.reshape(width, -1)
    reduce_full = red_all.reshape(-1, width)
    mine = lax.dynamic_index_in_dim(x_all, core, 0, keepdims=False).reshape(rows, width)
    context = context.reshape(rows, width)
    resid_one = mine.astype(f32) + jnp.dot(context, output_full, preferred_element_type=f32) + full[2]
    middle, normed_one, inverse_one = layer_norm(resid_one, full[3], full[4])
    middle_low = lax.optimization_barrier(middle.astype(bf16))
    pre = jnp.dot(middle_low, expand_full, preferred_element_type=f32) + bias_up
    hidden = jax.nn.gelu(pre, approximate=False).astype(bf16)
    hidden = lax.optimization_barrier(hidden)
    resid_two = middle + jnp.dot(hidden, reduce_full, preferred_element_type=f32) + full[5]
    final, normed_two, inverse_two = layer_norm(resid_two, full[6], full[7])
    layer_out = swap(final.astype(bf16).reshape(seqs, cluster, width))
    upstream = swap(cotangent).reshape(rows, width).astype(f32)
    grad_second_gain = jnp.sum(upstream * normed_two, axis=0)
    grad_second_shift = jnp.sum(upstream, axis=0)
    grad_resid_two = norm_back(upstream, normed_two, inverse_two, full[6])
    grad_branch_two = grad_resid_two.astype(bf16)
    grad_reduce_bias = jnp.sum(grad_branch_two, axis=0, dtype=f32)
    grad_reduce = transpose_left(hidden, grad_branch_two)
    grad_hidden = transpose_right(grad_branch_two, reduce_full)
    grad_pre = (grad_hidden * gelu_slope(pre)).astype(bf16)
    grad_pre = lax.optimization_barrier(grad_pre)
    grad_expand_bias = jnp.sum(grad_pre, axis=0, dtype=f32)
    grad_expand = transpose_left(middle_low, grad_pre)
    grad_middle = grad_resid_two + transpose_right(grad_pre, expand_full)
    grad_first_gain = jnp.sum(grad_middle * normed_one, axis=0)
    grad_first_shift = jnp.sum(grad_middle, axis=0)
    grad_resid_one = norm_back(grad_middle, normed_one, inverse_one, full[3])
    grad_branch_one = grad_resid_one.astype(bf16)
    grad_output_bias = jnp.sum(grad_branch_one, axis=0, dtype=f32)
    grad_output = transpose_left(context, grad_branch_one)
    grad_context = transpose_right(grad_branch_one, output_full).astype(bf16)
    grads, grad_attend_half, grad_bias_half = attend_back(
        grad_context.reshape(chips, per, cluster, width), qs, ks, vs, ps, pos_all, x_all, depth, heads
    )
    grads = grads.reshape(2, rows, 3 * half)
    token_grad = grad_resid_one
    for c in range(2):
        token_grad = token_grad + transpose_right(grads[c], attend_all[c])
    token_grad = swap(token_grad.astype(bf16).reshape(seqs, cluster, width))

    def spread(part):
        zero = jnp.zeros_like(part)
        pick = core == 0
        return jnp.where(pick, part, zero), jnp.where(pick, zero, part)

    columns = []
    for part in range(3):
        columns += spread(grad_attend_half[:, part * half : (part + 1) * half])
    grad_attend = jnp.concatenate(columns, axis=1)
    grad_query_bias = jnp.concatenate(spread(grad_bias_half[0, :half]))
    grad_value_bias = jnp.concatenate(spread(grad_bias_half[0, 2 * half :]))

    def owned(grad):
        part = lax.psum_scatter(grad.astype(bf16), "batch", scatter_dimension=0, tiled=True)
        return lax.psum(part, "seq").astype(f32)

    return (
        layer_out,
        token_grad,
        owned(grad_attend),
        owned(grad_query_bias),
        owned(grad_value_bias),
        owned(grad_output),
        owned(grad_output_bias),
        owned(grad_first_gain),
        owned(grad_first_shift),
        owned(grad_expand),
        owned(grad_expand_bias),
        owned(grad_reduce),
        owned(grad_reduce_bias),
        owned(grad_second_gain),
        owned(grad_second_shift),
    )


def layer(mesh):
    def run(*arrays):
        seqs, cluster, width = arrays[0].shape
        heads = arrays[14].shape[1]
        owners, depth = mesh.shape["seq"], mesh.shape["batch"]
        chips = owners // 2
        fits = (
            owners % 2 == 0
            and chips > 1
            and depth > 1
            and seqs % chips == 0
            and cluster == 128
            and heads % 4 == 0
            and width == heads * 64
            and cluster % (16 * owners) == 0
        )
        return (per_chip if fits else per_device)(*arrays)

    return run


def solution(mesh):
    in_specs = (
        P("batch", "seq", None),
        P("batch", None),
        P("batch"),
        P("batch"),
        P("batch", None),
        P("batch"),
        P("batch"),
        P("batch"),
        P("batch", None),
        P("batch"),
        P("batch", None),
        P("batch"),
        P("batch"),
        P("batch"),
        P("batch", None, "seq"),
        P("batch", None, "seq"),
        P("batch", "seq", None),
    )
    out_specs = (
        P("batch", "seq", None),
        P("batch", "seq", None),
        P("batch", None),
        P("batch"),
        P("batch"),
        P("batch", None),
        P("batch"),
        P("batch"),
        P("batch"),
        P("batch", None),
        P("batch"),
        P("batch", None),
        P("batch"),
        P("batch"),
        P("batch"),
    )
    return jax.shard_map(
        layer(mesh), mesh=mesh, in_specs=in_specs, out_specs=out_specs, check_vma=False
    )
```

```python
import functools
import math

import jax
import jax.numpy as jnp
from jax import lax
from jax.experimental import pallas as pl
from jax.experimental.pallas import tpu as pltpu
from jax.sharding import PartitionSpec as P

epsilon = 1e-05


def layer_norm(resid, gain, shift):
    center = jnp.mean(resid, axis=-1, keepdims=True)
    centered = resid - center
    spread = jnp.mean(centered * centered, axis=-1, keepdims=True)
    inverse = lax.rsqrt(spread + epsilon)
    normed = centered * inverse
    return (normed * gain + shift, normed, inverse)


def norm_back(upstream, normed, inverse, gain):
    scaled = upstream * gain
    first_mean = jnp.mean(scaled, axis=-1, keepdims=True)
    second_mean = jnp.mean(scaled * normed, axis=-1, keepdims=True)
    return inverse * (scaled - first_mean - normed * second_mean)


def gelu_slope(value):
    cumulative = 0.5 * (1.0 + lax.erf(value * 0.5**0.5))
    density = jnp.exp(-0.5 * value * value) * (2.0 * math.pi) ** (-0.5)
    return cumulative + value * density


def transpose_left(first, second):
    return lax.dot_general(
        first, second, (((0,), (0,)), ((), ())), preferred_element_type=jnp.float32
    )


def transpose_right(first, second):
    return lax.dot_general(
        first, second, (((1,), (1,)), ((), ())), preferred_element_type=jnp.float32
    )


def group_table(rank, cluster, owners):
    share = cluster // owners
    target = rank // cluster
    length = rank.shape[-1]
    places = lax.broadcasted_iota(jnp.int32, (length, length), 0)
    later = lax.broadcasted_iota(jnp.int32, (length, length), 1)
    before = (places < later)[None, None]
    same = target[..., :, None] == target[..., None, :]
    earlier = jnp.sum((same & before).astype(jnp.int32), axis=-2)
    position = target * share + earlier
    slots = lax.broadcasted_iota(jnp.int32, position.shape + (length,), 3)
    return (position[..., None] == slots).astype(jnp.bfloat16)


def sort_heads(rows, table, heads):
    seqs, length, width = rows.shape
    split = rows.reshape(seqs, length, heads, width // heads)
    moved = jnp.einsum("shtp,sthd->sphd", table, split, preferred_element_type=jnp.float32)
    return moved.astype(rows.dtype).reshape(seqs, length, width)


def unsort_heads(rows, table, heads):
    seqs, length, width = rows.shape
    split = rows.reshape(seqs, length, heads, width // heads)
    moved = jnp.einsum("shtp,sphd->sthd", table, split, preferred_element_type=jnp.float32)
    return moved.astype(rows.dtype).reshape(seqs, length, width)


def cluster_scores(queries, keys_rows, heads):
    items, length, width = queries.shape
    size = width // heads
    query_split = queries.reshape(items, length, heads, size)
    key_split = keys_rows.reshape(items, length, heads, size)
    scores = jnp.einsum(
        "sqhd,skhd->shqk", query_split, key_split, preferred_element_type=jnp.float32
    )
    return scores * size ** (-0.5)


def cluster_forward(queries, keys_rows, values_rows, heads):
    items, length, width = queries.shape
    scores = cluster_scores(queries, keys_rows, heads)
    top = jnp.max(scores, axis=-1, keepdims=True)
    weights = jnp.exp(scores - top)
    total = jnp.sum(weights, axis=-1, keepdims=True)
    probs = (weights / total).astype(jnp.bfloat16)
    value_split = values_rows.reshape(items, length, heads, width // heads)
    context = jnp.einsum("shqk,skhd->sqhd", probs, value_split, preferred_element_type=jnp.float32)
    return (
        context.reshape(items, length, width).astype(jnp.bfloat16),
        (top + jnp.log(total))[..., 0],
    )


def cluster_backward(scores, log_total, queries, keys_rows, values_rows, grad_context, heads):
    items, length, width = queries.shape
    size = width // heads
    query_split = queries.reshape(items, length, heads, size)
    key_split = keys_rows.reshape(items, length, heads, size)
    value_split = values_rows.reshape(items, length, heads, size)
    grad_split = grad_context.reshape(items, length, heads, size)
    probs = jnp.exp(scores - log_total[..., None])
    grad_probs = jnp.einsum(
        "sqhd,skhd->shqk", grad_split, value_split, preferred_element_type=jnp.float32
    )
    inner = jnp.sum(probs * grad_probs, axis=-1, keepdims=True)
    grad_scores = (probs * (grad_probs - inner)).astype(jnp.bfloat16)
    scale = size ** (-0.5)
    grad_query = (
        jnp.einsum("shqk,skhd->sqhd", grad_scores, key_split, preferred_element_type=jnp.float32)
        * scale
    )
    grad_key = (
        jnp.einsum("shqk,sqhd->skhd", grad_scores, query_split, preferred_element_type=jnp.float32)
        * scale
    )
    grad_value = jnp.einsum(
        "shqk,sqhd->skhd",
        probs.astype(jnp.bfloat16),
        grad_split,
        preferred_element_type=jnp.float32,
    )
    shape = (items, length, width)
    return (
        grad_query.reshape(shape).astype(jnp.bfloat16),
        grad_key.reshape(shape).astype(jnp.bfloat16),
        grad_value.reshape(shape).astype(jnp.bfloat16),
    )


def send_context(context):
    return lax.all_to_all(context, "seq", split_axis=1, concat_axis=1, tiled=True)


def send_grads(grads):
    return (
        lax.all_to_all(grads[0], "seq", split_axis=1, concat_axis=1, tiled=True),
        lax.all_to_all(grads[1], "seq", split_axis=1, concat_axis=1, tiled=True),
        lax.all_to_all(grads[2], "seq", split_axis=1, concat_axis=1, tiled=True),
    )


def make_step(left, pieces):
    total = jnp.dot(left, pieces[0], preferred_element_type=jnp.float32)
    stored = tuple(pieces[1:]) + ()
    placed = tuple((piece for piece in stored))
    return (total,) + placed


def make_hidden_step(before, pieces):
    section = before + pieces[1].astype(jnp.float32)
    activated = jax.nn.gelu(section, approximate=False).astype(jnp.bfloat16)
    total = jnp.dot(activated, pieces[0], preferred_element_type=jnp.float32)
    stored = ()
    return (total, section, activated) + stored


def per_device(
    tokens,
    attend_weight,
    query_bias,
    value_bias,
    output_weight,
    output_bias,
    first_gain,
    first_shift,
    expand_weight,
    expand_bias,
    reduce_weight,
    reduce_bias,
    second_gain,
    second_shift,
    query_rank,
    key_rank,
    cotangent,
):
    seqs, cluster, width = tokens.shape
    heads = query_rank.shape[1]
    rows = seqs * cluster
    owners = lax.axis_size("seq")
    flat = tokens.reshape(rows, width)
    attend_out = make_step(
        flat,
        (
            lax.all_gather(attend_weight, "batch", axis=0, tiled=True),
            lax.all_gather(query_bias, "batch", axis=0, tiled=True),
            lax.all_gather(value_bias, "batch", axis=0, tiled=True),
        ),
    )
    summed = attend_out[0]
    queries = (summed[:, :width] + attend_out[1].astype(jnp.float32)).astype(jnp.bfloat16)
    keys_rows = summed[:, width : 2 * width].astype(jnp.bfloat16)
    values_rows = (summed[:, 2 * width :] + attend_out[2].astype(jnp.float32)).astype(jnp.bfloat16)
    query_table = group_table(query_rank, cluster, owners)
    key_table = group_table(key_rank, cluster, owners)
    query_sorted = sort_heads(queries.reshape(seqs, cluster, width), query_table, heads)
    key_sorted = sort_heads(keys_rows.reshape(seqs, cluster, width), key_table, heads)
    value_sorted = sort_heads(values_rows.reshape(seqs, cluster, width), key_table, heads)
    received = (
        lax.all_to_all(query_sorted, "seq", split_axis=1, concat_axis=1, tiled=True),
        lax.all_to_all(key_sorted, "seq", split_axis=1, concat_axis=1, tiled=True),
        lax.all_to_all(value_sorted, "seq", split_axis=1, concat_axis=1, tiled=True),
    )
    context, log_total = cluster_forward(received[0], received[1], received[2], heads)
    forward_out = (send_context(context), log_total, received[0], received[1], received[2])
    context_rows = unsort_heads(forward_out[0], query_table, heads).reshape(rows, width)
    output_out = make_step(
        context_rows,
        (
            lax.all_gather(output_weight, "batch", axis=0, tiled=True),
            lax.all_gather(output_bias, "batch", axis=0, tiled=True),
            lax.all_gather(first_gain, "batch", axis=0, tiled=True),
            lax.all_gather(first_shift, "batch", axis=0, tiled=True),
        ),
    )
    resid_one = flat.astype(jnp.float32) + output_out[0] + output_out[1].astype(jnp.float32)
    gain_one = output_out[2].astype(jnp.float32)
    middle, normed_one, inverse_one = layer_norm(
        resid_one, gain_one, output_out[3].astype(jnp.float32)
    )
    middle_low = middle.astype(jnp.bfloat16)
    expand_out = make_step(
        middle_low,
        (
            lax.all_gather(expand_weight, "batch", axis=0, tiled=True),
            lax.all_gather(reduce_bias, "batch", axis=0, tiled=True),
            lax.all_gather(second_gain, "batch", axis=0, tiled=True),
            lax.all_gather(second_shift, "batch", axis=0, tiled=True),
        ),
    )
    hidden_out = make_hidden_step(
        expand_out[0],
        (
            lax.all_gather(reduce_weight, "batch", axis=0, tiled=True),
            lax.all_gather(expand_bias, "batch", axis=0, tiled=True),
        ),
    )
    pre_full, hidden_full = (hidden_out[1], hidden_out[2])
    resid_two = middle + hidden_out[0] + expand_out[1].astype(jnp.float32)
    gain_two = expand_out[2].astype(jnp.float32)
    final, normed_two, inverse_two = layer_norm(
        resid_two, gain_two, expand_out[3].astype(jnp.float32)
    )
    layer_out = final.astype(jnp.bfloat16).reshape(seqs, cluster, width)
    attend_full, output_full, expand_full, reduce_full = (
        lax.all_gather(attend_weight, "batch", axis=0, tiled=True),
        lax.all_gather(output_weight, "batch", axis=0, tiled=True),
        lax.all_gather(expand_weight, "batch", axis=0, tiled=True),
        lax.all_gather(reduce_weight, "batch", axis=0, tiled=True),
    )
    upstream = cotangent.reshape(rows, width).astype(jnp.float32)
    grad_second_gain = jnp.sum(upstream * normed_two, axis=0)
    grad_second_shift = jnp.sum(upstream, axis=0)
    grad_resid_two = norm_back(upstream, normed_two, inverse_two, gain_two)
    grad_branch_two = grad_resid_two.astype(jnp.bfloat16)
    grad_reduce_bias = jnp.sum(grad_branch_two, axis=0, dtype=jnp.float32)
    grad_reduce = transpose_left(hidden_full, grad_branch_two)
    grad_hidden = transpose_right(grad_branch_two, reduce_full)
    grad_pre = (grad_hidden * gelu_slope(pre_full)).astype(jnp.bfloat16)
    grad_expand_bias = jnp.sum(grad_pre, axis=0, dtype=jnp.float32)
    grad_expand = transpose_left(middle_low, grad_pre)
    grad_middle = grad_resid_two + transpose_right(grad_pre, expand_full)
    grad_first_gain = jnp.sum(grad_middle * normed_one, axis=0)
    grad_first_shift = jnp.sum(grad_middle, axis=0)
    grad_resid_one = norm_back(grad_middle, normed_one, inverse_one, gain_one)
    grad_branch_one = grad_resid_one.astype(jnp.bfloat16)
    grad_output_bias = jnp.sum(grad_branch_one, axis=0, dtype=jnp.float32)
    grad_output = transpose_left(context_rows, grad_branch_one)
    grad_context = transpose_right(grad_branch_one, output_full).astype(jnp.bfloat16)
    grad_sorted = sort_heads(grad_context.reshape(seqs, cluster, width), query_table, heads)
    grad_received = lax.all_to_all(grad_sorted, "seq", split_axis=1, concat_axis=1, tiled=True)
    kept_scores = cluster_scores(forward_out[2], forward_out[3], heads)
    home = send_grads(
        cluster_backward(
            kept_scores,
            forward_out[1],
            forward_out[2],
            forward_out[3],
            forward_out[4],
            grad_received,
            heads,
        )
    )
    grad_queries = unsort_heads(home[0], query_table, heads).reshape(rows, width)
    grad_keys = unsort_heads(home[1], key_table, heads).reshape(rows, width)
    grad_values = unsort_heads(home[2], key_table, heads).reshape(rows, width)
    grad_mixed = jnp.concatenate([grad_queries, grad_keys, grad_values], axis=1)
    grad_query_bias = jnp.sum(grad_queries, axis=0, dtype=jnp.float32)
    grad_value_bias = jnp.sum(grad_values, axis=0, dtype=jnp.float32)
    grad_attend = transpose_left(flat, grad_mixed)
    token_grad = (
        (grad_resid_one + transpose_right(grad_mixed, attend_full))
        .astype(jnp.bfloat16)
        .reshape(seqs, cluster, width)
    )
    owned = (
        lax.psum_scatter(
            grad_attend.astype(jnp.bfloat16), "batch", scatter_dimension=0, tiled=True
        ).astype(jnp.float32),
        lax.psum_scatter(
            grad_query_bias.astype(jnp.bfloat16), "batch", scatter_dimension=0, tiled=True
        ).astype(jnp.float32),
        lax.psum_scatter(
            grad_value_bias.astype(jnp.bfloat16), "batch", scatter_dimension=0, tiled=True
        ).astype(jnp.float32),
        lax.psum_scatter(
            grad_output.astype(jnp.bfloat16), "batch", scatter_dimension=0, tiled=True
        ).astype(jnp.float32),
        lax.psum_scatter(
            grad_output_bias.astype(jnp.bfloat16), "batch", scatter_dimension=0, tiled=True
        ).astype(jnp.float32),
        lax.psum_scatter(
            grad_first_gain.astype(jnp.bfloat16), "batch", scatter_dimension=0, tiled=True
        ).astype(jnp.float32),
        lax.psum_scatter(
            grad_first_shift.astype(jnp.bfloat16), "batch", scatter_dimension=0, tiled=True
        ).astype(jnp.float32),
        lax.psum_scatter(
            grad_expand.astype(jnp.bfloat16), "batch", scatter_dimension=0, tiled=True
        ).astype(jnp.float32),
        lax.psum_scatter(
            grad_expand_bias.astype(jnp.bfloat16), "batch", scatter_dimension=0, tiled=True
        ).astype(jnp.float32),
        lax.psum_scatter(
            grad_reduce.astype(jnp.bfloat16), "batch", scatter_dimension=0, tiled=True
        ).astype(jnp.float32),
        lax.psum_scatter(
            grad_reduce_bias.astype(jnp.bfloat16), "batch", scatter_dimension=0, tiled=True
        ).astype(jnp.float32),
        lax.psum_scatter(
            grad_second_gain.astype(jnp.bfloat16), "batch", scatter_dimension=0, tiled=True
        ).astype(jnp.float32),
        lax.psum_scatter(
            grad_second_shift.astype(jnp.bfloat16), "batch", scatter_dimension=0, tiled=True
        ).astype(jnp.float32),
    )
    shared = (
        lax.psum(owned[0].astype(jnp.bfloat16), "seq").astype(jnp.float32),
        lax.psum(owned[1].astype(jnp.bfloat16), "seq").astype(jnp.float32),
        lax.psum(owned[2].astype(jnp.bfloat16), "seq").astype(jnp.float32),
        lax.psum(owned[3].astype(jnp.bfloat16), "seq").astype(jnp.float32),
        lax.psum(owned[4].astype(jnp.bfloat16), "seq").astype(jnp.float32),
        lax.psum(owned[5].astype(jnp.bfloat16), "seq").astype(jnp.float32),
        lax.psum(owned[6].astype(jnp.bfloat16), "seq").astype(jnp.float32),
        lax.psum(owned[7].astype(jnp.bfloat16), "seq").astype(jnp.float32),
        lax.psum(owned[8].astype(jnp.bfloat16), "seq").astype(jnp.float32),
        lax.psum(owned[9].astype(jnp.bfloat16), "seq").astype(jnp.float32),
        lax.psum(owned[10].astype(jnp.bfloat16), "seq").astype(jnp.float32),
        lax.psum(owned[11].astype(jnp.bfloat16), "seq").astype(jnp.float32),
        lax.psum(owned[12].astype(jnp.bfloat16), "seq").astype(jnp.float32),
    )
    return (
        layer_out,
        token_grad,
        shared[0],
        shared[1],
        shared[2],
        shared[3],
        shared[4],
        shared[5],
        shared[6],
        shared[7],
        shared[8],
        shared[9],
        shared[10],
        shared[11],
        shared[12],
    )


MESH = pl.DeviceIdType.MESH
f32 = jnp.float32
bf16 = jnp.bfloat16


class Place:
    def __init__(self, chips, depth):
        self.chips, self.depth = chips, depth
        self.z = lax.axis_index("batch")
        spot = lax.axis_index("seq")
        self.chip, self.core = lax.div(spot, 2), lax.rem(spot, 2)

    def chip_at(self, k):
        return lax.rem(self.chip + k + self.chips, self.chips)

    def z_at(self, k):
        return lax.rem(self.z + k + self.depth, self.depth)

    def plane(self, k):
        return (self.z, self.chip_at(k) * 2 + self.core)

    def tower(self, k):
        return (self.z_at(k), self.chip * 2 + self.core)

    def sibling(self):
        return (self.z, self.chip * 2 + 1 - self.core)

    def greet(self):
        bell = pltpu.get_barrier_semaphore()
        others = [self.plane(k) for k in range(1, self.chips)]
        others += [self.tower(k) for k in range(1, self.depth)]
        others.append(self.sibling())
        for other in others:
            pl.semaphore_signal(bell, inc=1, device_id=other, device_id_type=MESH)
        pl.semaphore_wait(bell, len(others))


def far_copy(src, dst, sems, at, device):
    return pltpu.make_async_remote_copy(
        src_ref=src,
        dst_ref=dst,
        send_sem=sems[0].at[at],
        recv_sem=sems[1].at[at],
        device_id=device,
        device_id_type=MESH,
    )


def one_hot(row, slots):
    return jnp.where(slots == row, 1.0, 0.0).astype(bf16)


def split_lanes(tile, low):
    zero = jnp.zeros_like(tile)
    return jnp.where(low, tile, zero), jnp.where(low, zero, tile)


def stack_lanes(tile, low):
    first, second = split_lanes(tile, low)
    return jnp.concatenate([first, second], axis=0)


def dot_rows(a, b):
    return jnp.dot(a, b, preferred_element_type=f32)


def dot_lanes(a, b):
    return lax.dot_general(a, b, (((1,), (1,)), ((), ())), preferred_element_type=f32)


def dot_first(a, b):
    return lax.dot_general(a, b, (((0,), (0,)), ((), ())), preferred_element_type=f32)


def multiple(value, by):
    return pl.multiple_of(value, by)


def attend_kernel(
    chips,
    depth,
    heads,
    tok_ref,
    pos_ref,
    aw_ref,
    vec_ref,
    ow_ref,
    ew_ref,
    rw_ref,
    x_out,
    ctx_out,
    q_out,
    k_out,
    v_out,
    p_out,
    pos_out,
    aw_out,
    vec_out,
    ow_out,
    ew_out,
    rw_out,
    xbuf,
    posbuf,
    wbuf,
    vbuf,
    bias,
    qkv,
    qs,
    ks,
    vs,
    ps,
    os,
    ctxb,
    tok_s,
    tok_r,
    tokc_s,
    tokc_r,
    pos_s,
    pos_r,
    posc_s,
    posc_r,
    aw_s,
    aw_r,
    awc_s,
    awc_r,
    vec_s,
    vec_r,
    wz_s,
    wz_r,
    wp_s,
    wp_r,
    wc_s,
    wc_r,
    ctx_s,
    ctx_r,
    loc,
    out_sem,
):
    me = Place(chips, depth)
    z, chip, core = me.z, me.chip, me.core
    per = tok_ref.shape[0] // chips
    half = aw_ref.shape[1] // 6
    rows_z = aw_ref.shape[0]
    pairs = heads // 4
    size = half // (2 * pairs)
    me.greet()

    def aw_copy(k, part):
        columns = pl.ds(multiple(part * 2 * half + core * half, 128), half)
        return far_copy(
            aw_ref.at[:, columns],
            wbuf.at[pl.ds(multiple(z * rows_z, 8), rows_z), pl.ds(part * half, half)],
            (aw_s, aw_r),
            (k - 1) * 3 + part,
            me.tower(k),
        )

    def mine(ref, target):
        return ref.at[pl.ds(target * per, per)]

    def tok_copy(k):
        return far_copy(
            mine(tok_ref, me.chip_at(k)), xbuf.at[core, chip], (tok_s, tok_r), k - 1, me.plane(k)
        )

    def pos_copy(k):
        return far_copy(
            mine(pos_ref, me.chip_at(k)), posbuf.at[core, chip], (pos_s, pos_r), k - 1, me.plane(k)
        )

    def vec_copy(k):
        return far_copy(vec_ref, vbuf.at[z], (vec_s, vec_r), k - 1, me.tower(k))

    sends = []
    for k in range(1, chips):
        sends.append(pos_copy(k))
        sends[-1].start()
    for k in range(1, depth):
        sends.append(vec_copy(k))
        sends[-1].start()
    for k in range(1, max(chips, depth)):
        if k < depth:
            for part in range(3):
                sends.append(aw_copy(k, part))
                sends[-1].start()
        if k < chips:
            sends.append(tok_copy(k))
            sends[-1].start()
    local = []

    def keep(src, dst):
        copy = pltpu.make_async_copy(src, dst, loc.at[len(local)])
        copy.start()
        local.append(copy)

    keep(mine(tok_ref, chip), xbuf.at[core, chip])
    keep(mine(pos_ref, chip), posbuf.at[core, chip])
    keep(vec_ref, vbuf.at[z])
    for part in range(3):
        keep(
            aw_ref.at[:, pl.ds(multiple(part * 2 * half + core * half, 128), half)],
            wbuf.at[pl.ds(multiple(z * rows_z, 8), rows_z), pl.ds(part * half, half)],
        )
    eighth = ow_ref.shape[0] // (2 * chips)
    wide = ew_ref.shape[1] // (2 * chips)
    tall = rw_ref.shape[0] // (2 * chips)

    def piece(ref, kind, at):
        if kind == 0:
            return ref.at[pl.ds(multiple(at * eighth, 8), eighth)]
        if kind == 1:
            return ref.at[:, pl.ds(multiple(at * wide, 128), wide)]
        return ref.at[pl.ds(multiple(at * tall, 8), tall)]

    shards = (ow_ref, ew_ref, rw_ref)
    fulls = (ow_out, ew_out, rw_out)
    mine_at = core * chips + chip

    def place(kind, zz, at):
        if kind == 0:
            return ow_out.at[zz, at]
        if kind == 1:
            return ew_out.at[zz, :, pl.ds(multiple(at * wide, 128), wide)]
        return rw_out.at[zz, at]

    def place_all(kind, at):
        if kind == 0:
            return ow_out.at[:, at]
        if kind == 1:
            return ew_out.at[:, :, pl.ds(multiple(at * wide, 128), wide)]
        return rw_out.at[:, at]

    for kind in range(3):
        keep(piece(shards[kind], kind, mine_at), place(kind, z, mine_at))

    def wz_copy(kind, k):
        return far_copy(
            piece(shards[kind], kind, mine_at),
            place(kind, z, mine_at),
            (wz_s, wz_r),
            kind * (depth - 1) + k - 1,
            me.tower(k),
        )

    def wp_copy(kind, k, origin):
        at = core * chips + origin
        return far_copy(
            place_all(kind, at),
            place_all(kind, at),
            (wp_s, wp_r),
            kind * (chips - 1) + k - 1,
            me.plane(k),
        )

    def wc_copy(kind, origin_k):
        at = core * chips + me.chip_at(origin_k)
        return far_copy(
            place_all(kind, at),
            place_all(kind, at),
            (wc_s, wc_r),
            kind * chips + origin_k,
            me.sibling(),
        )

    for copy in local[:2]:
        copy.wait()

    def tokc_copy(k):
        source = me.chip_at(-k)
        return far_copy(
            xbuf.at[core, source], xbuf.at[core, source], (tokc_s, tokc_r), k, me.sibling()
        )

    def posc_copy(k):
        source = me.chip_at(-k)
        return far_copy(
            posbuf.at[core, source], posbuf.at[core, source], (posc_s, posc_r), k, me.sibling()
        )

    for k in range(chips):
        if k:
            pos_copy(k).wait_recv()
            tok_copy(k).wait_recv()
        for copy in (posc_copy(k), tokc_copy(k)):
            copy.start()
            sends.append(copy)
    for copy in local[2:6]:
        copy.wait()
    for k in range(1, depth):
        vec_copy(k).wait_recv()
        for part in range(3):
            aw_copy(k, part).wait_recv()
    for k in range(chips):
        posc_copy(k).wait_recv()
        tokc_copy(k).wait_recv()
    for copy in local[6:]:
        copy.wait()
    for kind in range(3):
        for k in range(1, depth):
            sends.append(wz_copy(kind, k))
            sends[-1].start()

    outs = []

    def emit(src, dst):
        copy = pltpu.make_async_copy(src, dst, out_sem.at[len(outs)])
        copy.start()
        outs.append(copy)

    emit(xbuf, x_out)
    emit(posbuf, pos_out)
    emit(wbuf, aw_out.at[core])
    emit(vbuf, vec_out)
    awc = far_copy(wbuf, aw_out.at[core], (awc_s, awc_r), 0, me.sibling())
    awc.start()
    sends.append(awc)

    quarter = rows_z
    for zz in range(depth):
        begin = zz * quarter
        for row, at in ((0, 0), (1, 2)):
            for side in range(2):
                lo = max(begin, side * half)
                hi = min(begin + quarter, (side + 1) * half)
                if lo < hi:
                    bias[side, 0:1, at * half + lo - side * half : at * half + hi - side * half] = (
                        vbuf[zz, row : row + 1, lo - begin : hi - begin]
                    )
    bias[0, 0:1, half : 2 * half] = jnp.zeros((1, half), f32)
    bias[1, 0:1, half : 2 * half] = jnp.zeros((1, half), f32)
    added = bias[core, 0:1, :]

    cluster = tok_ref.shape[1]
    blocks = 2 * chips
    share = cluster // blocks
    width = tok_ref.shape[2]

    @pl.loop(0, blocks)
    def _(jj):
        x = xbuf[lax.div(jj, chips), lax.rem(jj, chips)].reshape(per * cluster, width)
        mixed = (dot_rows(x, wbuf[...]) + added).astype(bf16)
        for at in range(3 * pairs):
            qkv[at, jj] = mixed[:, at * 128 : (at + 1) * 128].reshape(per, cluster, 128)

    slots = lax.broadcasted_iota(jnp.int32, (cluster, cluster), 0)
    low = lax.broadcasted_iota(jnp.int32, (cluster, 128), 1) < size
    scale = size ** (-0.5)

    def tables(jj, i, pair, part):
        first = part * heads + core * (heads // 2) + 2 * pair
        rows = [
            one_hot(posbuf[jj // chips, jj % chips, i, pl.ds(first + h, 1), :], slots)
            for h in range(2)
        ]
        return rows

    def weights_step(stage):
        if stage == 0:
            for kind in range(3):
                for k in range(1, depth):
                    wz_copy(kind, k).wait_recv()
                for k in range(1, chips):
                    wp_copy(kind, k, chip).start()
                wc_copy(kind, 0).start()

    @pl.loop(0, per)
    def _(i):
        @pl.loop(0, pairs)
        def _(pair):
            at = i * pairs + pair
            for jj in range(blocks):
                tq = jnp.concatenate(tables(jj, i, pair, 0), axis=1)
                tk = jnp.concatenate(tables(jj, i, pair, 1), axis=1)
                q = stack_lanes(qkv[pair, jj, i], low)
                k = stack_lanes(qkv[pairs + pair, jj, i], low)
                v = stack_lanes(qkv[2 * pairs + pair, jj, i], low)
                span = slice(jj * share, (jj + 1) * share)
                sq = dot_rows(tq, q).astype(bf16)
                skv = dot_rows(tk, jnp.concatenate([k, v], axis=1)).astype(bf16)
                qs[at, :, span, :] = sq.reshape(blocks, share, 128)
                ks[at, :, span, :] = skv[:, :128].reshape(blocks, share, 128)
                vs[at, :, span, :] = skv[:, 128:].reshape(blocks, share, 128)
            for c in range(blocks):
                scores = dot_lanes(qs[at, c], stack_lanes(ks[at, c], low)) * scale
                halves = []
                for h in range(2):
                    s = scores[:, h * cluster : (h + 1) * cluster]
                    e = jnp.exp(s - jnp.max(s, axis=1, keepdims=True))
                    halves.append((e / jnp.sum(e, axis=1, keepdims=True)).astype(bf16))
                probs = jnp.concatenate(halves, axis=1)
                ps[at, c] = probs
                o = dot_rows(probs, stack_lanes(vs[at, c], low)).astype(bf16)
                os[c] = o
            for jj in range(blocks):
                tq = jnp.concatenate(tables(jj, i, pair, 0), axis=0)
                rows = os[:, jj * share : (jj + 1) * share, :].reshape(cluster, 128)
                back = dot_first(tq, stack_lanes(rows, low)).astype(bf16)
                ctxb[jj // chips, jj % chips, i, :, pl.ds(multiple(pair * 128, 128), 128)] = back

        @pl.when(i == 0)
        def _():
            weights_step(0)

    far = far_copy(
        ctxb.at[1 - core],
        ctx_out.at[:, :, :, pl.ds(multiple(core * half, 128), half)],
        (ctx_s, ctx_r),
        0,
        me.sibling(),
    )
    far.start()
    emit(ctxb.at[core], ctx_out.at[:, :, :, pl.ds(multiple(core * half, 128), half)])
    emit(qs, q_out)
    emit(ks, k_out)
    emit(vs, v_out)
    emit(ps, p_out)
    for kind in range(3):
        for k in range(1, chips):
            wp_copy(kind, k, me.chip_at(-k)).wait_recv()
            wc_copy(kind, chips - k).start()
    for kind in range(3):
        for k in range(chips):
            wc_copy(kind, k).wait()
        for k in range(1, chips):
            wp_copy(kind, k, chip).wait_send()
    far.wait()
    awc.wait_recv()
    for copy in sends:
        copy.wait_send()
    for copy in outs:
        copy.wait()


def attend(tokens, pos, attend_weight, vectors, output_weight, expand_weight, reduce_weight, chips, depth, heads):
    seqs, cluster, width = tokens.shape
    per, blocks, pairs = seqs // chips, 2 * chips, heads // 4
    half = width // 2
    rows_z = attend_weight.shape[0]
    wide = expand_weight.shape[1]
    items = per * pairs
    dma = pltpu.SemaphoreType.DMA
    anywhere = pl.BlockSpec(memory_space=pl.ANY)
    eighth = output_weight.shape[0] // blocks
    tall = reduce_weight.shape[0] // blocks
    shapes = [
        ((2, chips, per, cluster, width), bf16),
        ((chips, per, cluster, width), bf16),
        ((items, blocks, cluster, 128), bf16),
        ((items, blocks, cluster, 128), bf16),
        ((items, blocks, cluster, 128), bf16),
        ((items, blocks, cluster, 2 * cluster), bf16),
        ((2, chips, per, 2 * heads, cluster), jnp.int32),
        ((2, depth * rows_z, 3 * half), bf16),
        ((depth,) + vectors.shape, f32),
        ((depth, blocks, eighth, width), bf16),
        ((depth, rows_z, wide), bf16),
        ((depth, blocks, tall, width), bf16),
    ]
    t, c = depth - 1, chips - 1
    return pl.pallas_call(
        functools.partial(attend_kernel, chips, depth, heads),
        out_shape=[jax.ShapeDtypeStruct(*s) for s in shapes],
        in_specs=[anywhere] * 7,
        out_specs=[anywhere] * len(shapes),
        scratch_shapes=[
            pltpu.VMEM(shapes[0][0], bf16),
            pltpu.VMEM(shapes[6][0], jnp.int32),
            pltpu.VMEM(shapes[7][0][1:], bf16),
            pltpu.VMEM(shapes[8][0], f32),
            pltpu.VMEM((2, 8, 3 * half), f32),
            pltpu.VMEM((3 * pairs, blocks, per, cluster, 128), bf16),
            pltpu.VMEM(shapes[2][0], bf16),
            pltpu.VMEM(shapes[3][0], bf16),
            pltpu.VMEM(shapes[4][0], bf16),
            pltpu.VMEM(shapes[5][0], bf16),
            pltpu.VMEM((blocks, cluster, 128), bf16),
            pltpu.VMEM((2, chips, per, cluster, half), bf16),
            dma((c,)), dma((c,)), dma((chips,)), dma((chips,)),
            dma((c,)), dma((c,)), dma((chips,)), dma((chips,)),
            dma((3 * t,)), dma((3 * t,)), dma((1,)), dma((1,)),
            dma((t,)), dma((t,)),
            dma((3 * t,)), dma((3 * t,)),
            dma((3 * c,)), dma((3 * c,)),
            dma((3 * chips,)), dma((3 * chips,)),
            dma((1,)), dma((1,)),
            dma((9,)), dma((9,)),
        ],
        compiler_params=pltpu.CompilerParams(
            collective_id=1, has_side_effects=True, vmem_limit_bytes=60 * 2**20
        ),
        name="attend",
    )(tokens, pos, attend_weight, vectors, output_weight, expand_weight, reduce_weight)


def add_into(target, at, parts):
    total = target[at].astype(f32)
    for part in parts:
        total = total + part.astype(f32)
    target[at] = total.astype(target.dtype)


class Reducer:
    def __init__(self, me, src_half, own, near, mid, last, done, sems, tower_first):
        self.me, self.src_half = me, src_half
        self.own, self.near, self.mid, self.last, self.done = own, near, mid, last, done
        (self.near_s, self.near_r, self.mid_s, self.mid_r, self.last_s, self.last_r) = sems[:6]
        (self.back_s, self.back_r, self.side_s, self.side_r) = sems[6:10]
        self.loc = sems[10]
        self.tower_first = tower_first
        self.depth, self.chips = own.shape[0], own.shape[1]

    def near_copy(self):
        me = self.me
        return far_copy(
            self.src_half(1 - me.core), self.near, (self.near_s, self.near_r), 0, me.sibling()
        )

    def own_copy(self):
        return pltpu.make_async_copy(self.src_half(self.me.core), self.own, self.loc.at[0])

    def begin(self):
        self.near_copy().start()
        self.own_copy().start()

    def fold_near(self):
        self.own_copy().wait()
        self.near_copy().wait()

        @pl.loop(0, self.depth)
        def _(a):
            for b in range(self.chips):
                add_into(self.own, (a, b), [self.near[a, b]])

    def mid_copy(self, k):
        me = self.me
        if self.tower_first:
            src, device = self.own.at[me.z_at(k)], me.tower(k)
        else:
            src, device = self.own.at[:, me.chip_at(k)], me.plane(k)
        return far_copy(src, self.mid.at[k - 1], (self.mid_s, self.mid_r), k - 1, device)

    def mid_range(self):
        return range(1, self.depth if self.tower_first else self.chips)

    def send_mid(self):
        for k in self.mid_range():
            self.mid_copy(k).start()

    def fold_mid(self):
        me = self.me
        for k in self.mid_range():
            self.mid_copy(k).wait()
        if self.tower_first:
            for b in range(self.chips):
                add_into(self.own, (me.z, b), [self.mid[k - 1, b] for k in self.mid_range()])
        else:
            for a in range(self.depth):
                add_into(self.own, (a, me.chip), [self.mid[k - 1, a] for k in self.mid_range()])

    def last_range(self):
        return range(1, self.chips if self.tower_first else self.depth)

    def last_copy(self, k):
        me = self.me
        if self.tower_first:
            src, device = self.own.at[me.z, me.chip_at(k)], me.plane(k)
        else:
            src, device = self.own.at[me.z_at(k), me.chip], me.tower(k)
        return far_copy(src, self.last.at[k - 1], (self.last_s, self.last_r), k - 1, device)

    def send_last(self):
        for k in self.last_range():
            self.last_copy(k).start()

    def fold_last(self):
        me = self.me
        for k in self.last_range():
            self.last_copy(k).wait()
        total = self.own[me.z, me.chip].astype(f32)
        for k in self.last_range():
            total = total + self.last[k - 1].astype(f32)
        self.done[me.core, me.chip] = total.astype(bf16)

    def back_copy(self, k):
        me = self.me
        spot = self.done.at[me.core, me.chip]
        return far_copy(spot, spot, (self.back_s, self.back_r), k - 1, me.plane(k))

    def send_back(self):
        for k in range(1, self.chips):
            self.back_copy(k).start()

    def side_copy(self):
        me = self.me
        spot = self.done.at[me.core]
        return far_copy(spot, spot, (self.side_s, self.side_r), 0, me.sibling())

    def send_side(self):
        for k in range(1, self.chips):
            self.back_copy(k).wait()
        self.side_copy().start()

    def finish(self):
        self.side_copy().wait()


def back_kernel(
    chips,
    depth,
    heads,
    d_ref,
    q_ref,
    k_ref,
    v_ref,
    p_ref,
    pos_ref,
    x_ref,
    aw_ref,
    res_ref,
    go_ref,
    ge_ref,
    gr_ref,
    gv_ref,
    token_out,
    aw_out,
    ow_out,
    ew_out,
    rw_out,
    vec_out,
    bias_out,
    dbuf,
    qs,
    ks,
    vs,
    ps,
    posbuf,
    xbuf,
    wbuf,
    rbuf,
    ds,
    gs,
    gbuf,
    gfar,
    tbuf,
    dw,
    dwb,
    amid,
    alast,
    adone,
    o_own,
    o_near,
    o_mid,
    o_last,
    o_done,
    e_own,
    e_near,
    e_mid,
    e_last,
    e_done,
    r_own,
    r_near,
    r_mid,
    r_last,
    r_done,
    a32,
    o32,
    e32,
    r32,
    vbuf,
    vgot,
    bbuf,
    bgot,
    d_s,
    d_r,
    g_s,
    g_r,
    t_s,
    t_r,
    load,
    out_sem,
    v_s,
    v_r,
    b_s,
    b_r,
    *sems,
):
    me = Place(chips, depth)
    core, chip = me.core, me.chip
    per = d_ref.shape[1]
    cluster, width = d_ref.shape[2], d_ref.shape[3]
    half = width // 2
    pairs = heads // 4
    size = half // (2 * pairs)
    blocks = 2 * chips
    share = cluster // blocks
    me.greet()
    groups = [sems[n * 11 : (n + 1) * 11] for n in range(4)]
    wide = ge_ref.shape[2] // (2 * chips)

    def out_half(c):
        return go_ref.at[:, pl.ds(c * chips, chips)]

    def reduce_half(c):
        return gr_ref.at[:, pl.ds(c * chips, chips)]

    def expand_half(c):
        return ge_ref.at[:, :, pl.ds(multiple(c * chips * wide, 128), chips * wide)]

    red = Reducer(me, reduce_half, r_own, r_near, r_mid, r_last, r_done, groups[0], True)
    exp = Expander(me, expand_half, e_own, e_near, e_mid, e_last, e_done, groups[1], False)
    out = Reducer(me, out_half, o_own, o_near, o_mid, o_last, o_done, groups[2], False)
    att = Reducer(me, None, dwb, None, amid, alast, adone, groups[3], False)

    theirs = pl.ds(multiple((1 - core) * half, 128), half)
    far = far_copy(d_ref.at[:, :, :, theirs], dbuf.at[core], (d_s, d_r), 0, me.sibling())
    far.start()
    first = [
        pltpu.make_async_copy(
            d_ref.at[:, :, :, pl.ds(multiple(core * half, 128), half)], dbuf.at[core], load.at[12]
        ),
        pltpu.make_async_copy(pos_ref, posbuf, load.at[13]),
        pltpu.make_async_copy(aw_ref, wbuf, load.at[14]),
        pltpu.make_async_copy(gv_ref, vbuf, load.at[15]),
    ]

    def loads(i, slot):
        span = pl.ds(i * pairs, pairs)
        pieces = (
            (q_ref.at[span], qs),
            (k_ref.at[span], ks),
            (v_ref.at[span], vs),
            (p_ref.at[span], ps),
        )
        return [
            pltpu.make_async_copy(src, dst.at[slot], load.at[slot * 4 + n])
            for n, (src, dst) in enumerate(pieces)
        ]

    def load_x(i):
        return pltpu.make_async_copy(x_ref.at[:, :, i], xbuf, load.at[8])

    def load_r(i):
        return pltpu.make_async_copy(res_ref.at[:, i], rbuf, load.at[9])

    for copy in first + loads(0, 0) + [load_x(0)]:
        copy.start()
    red.begin()
    exp.begin()
    out.begin()

    slots = lax.broadcasted_iota(jnp.int32, (cluster, cluster), 0)
    low = lax.broadcasted_iota(jnp.int32, (cluster, 128), 1) < size
    scale = size ** (-0.5)
    bbuf[...] = jnp.zeros_like(bbuf)
    for copy in first:
        copy.wait()
    far.wait()

    def tables(jj, i, pair, part):
        begin = part * heads + core * (heads // 2) + 2 * pair
        return [
            one_hot(posbuf[jj // chips, jj % chips, i, pl.ds(begin + h, 1), :], slots)
            for h in range(2)
        ]

    def clusters(i, slot, pair):
        lanes = pl.ds(multiple(pair * 128, 128), 128)
        for jj in range(blocks):
            tq = jnp.concatenate(tables(jj, i, pair, 0), axis=1)
            rows = stack_lanes(dbuf[jj // chips, jj % chips, i, :, lanes], low)
            ds[:, jj * share : (jj + 1) * share, :] = (
                dot_rows(tq, rows).astype(bf16).reshape(blocks, share, 128)
            )
        for c in range(blocks):
            d = ds[c]
            probs = ps[slot, pair, c]
            slope = dot_lanes(d, stack_lanes(vs[slot, pair, c], low))
            broad = probs.astype(f32)
            halves = []
            for h in range(2):
                span = slice(h * cluster, (h + 1) * cluster)
                inner = jnp.sum(broad[:, span] * slope[:, span], axis=1, keepdims=True)
                halves.append((broad[:, span] * (slope[:, span] - inner)).astype(bf16))
            grads = jnp.concatenate(halves, axis=1)
            gq = dot_rows(grads, stack_lanes(ks[slot, pair, c], low)) * scale
            gk = dot_first(grads, qs[slot, pair, c]) * scale
            gv = dot_first(probs, d)
            gs[0, c] = gq.astype(bf16)
            gs[1, c] = jnp.where(low, gk[:cluster], gk[cluster:]).astype(bf16)
            gs[2, c] = jnp.where(low, gv[:cluster], gv[cluster:]).astype(bf16)
        for jj in range(blocks):
            for part in range(3):
                if part < 2:
                    table = jnp.concatenate(tables(jj, i, pair, part), axis=0)
                rows = gs[part, :, jj * share : (jj + 1) * share, :].reshape(cluster, 128)
                back = dot_first(table, stack_lanes(rows, low))
                to = pl.ds(multiple(part * half + pair * 128, 128), 128)
                gbuf[slot, jj // chips, jj % chips, :, to] = back.astype(bf16)

    def give(slot):
        return far_copy(gbuf.at[slot, 1 - core], gfar.at[slot], (g_s, g_r), slot, me.sibling())

    def token_copy(i, slot, k):
        return far_copy(
            tbuf.at[slot, me.chip_at(k)],
            token_out.at[chip * per + i],
            (t_s, t_r),
            i * (chips - 1) + k - 1,
            me.plane(k),
        )

    def token_keep(i, slot):
        return pltpu.make_async_copy(
            tbuf.at[slot, chip], token_out.at[chip * per + i], out_sem.at[i]
        )

    def token_rows(i, slot):
        load_r(i).wait()
        give(slot).wait()
        for j in range(chips):
            near = dot_lanes(gbuf[slot, core, j], wbuf[core])
            distant = dot_lanes(gfar[slot, j], wbuf[1 - core])
            tbuf[slot, j] = (rbuf[j] + near + distant).astype(bf16)
        token_keep(i, slot).start()
        for k in range(1, chips):
            token_copy(i, slot, k).start()

    for i in range(per):
        slot = i % 2
        for copy in loads(i, slot):
            copy.wait()
        if i >= 1:
            token_rows(i - 1, 1 - slot)
        load_r(i).start()
        if i + 1 < per:
            for copy in loads(i + 1, 1 - slot):
                copy.start()

        @pl.loop(0, pairs)
        def _(pair):
            clusters(i, slot, pair)

            if i == 0:

                @pl.when(pair == 0)
                def _():
                    red.fold_near()
                    red.send_mid()
                    exp.fold_near()
                    exp.send_mid()
                    out.fold_near()
                    out.send_mid()

        if i >= 2:
            token_keep(i - 2, slot).wait()
            for k in range(1, chips):
                token_copy(i - 2, slot, k).wait()
        give(slot).start()
        load_x(i).wait()
        for b in range(2):
            x = jnp.concatenate([xbuf[b, j] for j in range(chips)], axis=0)
            g = jnp.concatenate([gbuf[slot, b, j] for j in range(chips)], axis=0)
            term = dot_first(x, g)
            if i == 0 and b == 0:
                dw[...] = term
            else:
                dw[...] += term
            bbuf[0:1, :] += jnp.sum(g.astype(f32), axis=0, keepdims=True)
        if i + 1 < per:
            load_x(i + 1).start()
        if i == per - 2:
            exp.fold_mid()
            exp.send_last()
            out.fold_mid()
            out.send_last()

    rows = dwb.shape[2]
    for a in range(depth):
        for b in range(chips):
            begin = (a * chips + b) * rows
            dwb[a, b] = dw[begin : begin + rows, :].astype(bf16)
    att.send_mid()
    token_rows(per - 1, (per - 1) % 2)
    exp.fold_last()
    exp.send_back()
    out.fold_last()
    out.send_back()
    red.fold_mid()
    red.send_last()
    for hop in range(3):
        for vec, got, s, r, skip in ((vbuf, vgot, v_s, v_r, -1), (bbuf, bgot, b_s, b_r, 0)):
            if hop == skip:
                continue
            if hop == 0:
                copies = [far_copy(vec, got.at[0], (s, r), 0, me.sibling())]
                begin = 0
            elif hop == 1:
                begin = 1
                copies = [
                    far_copy(vec, got.at[k], (s, r), k, me.plane(k)) for k in range(1, chips)
                ]
            else:
                begin = chips
                copies = [
                    far_copy(vec, got.at[chips + k - 1], (s, r), chips + k - 1, me.tower(k))
                    for k in range(1, depth)
                ]
            for copy in copies:
                copy.start()
            for copy in copies:
                copy.wait()
            total = vec[...]
            for n in range(len(copies)):
                total = total + got[begin + n]
            vec[...] = total
    att.fold_mid()
    att.send_last()
    last = [pltpu.make_async_copy(vbuf, vec_out, out_sem.at[per])]
    last[-1].start()
    share_bias = far_copy(bbuf, bias_out.at[core], (b_s, b_r), 0, me.sibling())
    share_bias.start()
    last.append(pltpu.make_async_copy(bbuf, bias_out.at[core], out_sem.at[per + 1]))
    last[-1].start()
    red.fold_last()
    red.send_back()
    exp.send_side()
    out.send_side()
    att.fold_last()
    att.send_back()
    red.send_side()
    exp.finish()
    tall = e_done.shape[2]
    for c in range(2):
        for p in range(chips):
            at = (c * chips + p) * wide
            e32[:, at : at + wide] = e_done[c, p].astype(f32)
    last.append(pltpu.make_async_copy(e32, ew_out, out_sem.at[per + 2]))
    last[-1].start()
    out.finish()
    o32[...] = o_done[...].astype(f32)
    last.append(pltpu.make_async_copy(o32, ow_out, out_sem.at[per + 3]))
    last[-1].start()
    red.finish()
    r32[...] = r_done[...].astype(f32)
    last.append(pltpu.make_async_copy(r32, rw_out, out_sem.at[per + 4]))
    last[-1].start()
    att.send_side()
    att.finish()
    for c in range(2):
        for p in range(chips):
            for part in range(3):
                to = (2 * part + c) * half
                a32[p * rows : (p + 1) * rows, to : to + half] = adone[
                    c, p, :, part * half : (part + 1) * half
                ].astype(f32)
    last.append(pltpu.make_async_copy(a32, aw_out, out_sem.at[per + 5]))
    last[-1].start()
    for i in range(max(per - 2, 0), per):
        token_keep(i, i % 2).wait()
        for k in range(1, chips):
            token_copy(i, i % 2, k).wait()
    share_bias.wait()
    for copy in last:
        copy.wait()


class Expander(Reducer):
    def __init__(self, me, src_half, own, near, mid, last, done, sems, tower_first):
        self.wide = done.shape[3]
        Reducer.__init__(self, me, src_half, own, near, mid, last, done, sems, tower_first)
        self.chips = done.shape[1]

    def lanes(self, chip):
        return pl.ds(multiple(chip * self.wide, 128), self.wide)

    def fold_near(self):
        self.own_copy().wait()
        self.near_copy().wait()

        @pl.loop(0, self.depth)
        def _(a):
            add_into(self.own, a, [self.near[a]])

    def mid_copy(self, k):
        me = self.me
        src = self.own.at[:, :, self.lanes(me.chip_at(k))]
        return far_copy(src, self.mid.at[k - 1], (self.mid_s, self.mid_r), k - 1, me.plane(k))

    def fold_mid(self):
        me = self.me
        for k in self.mid_range():
            self.mid_copy(k).wait()
        here = self.lanes(me.chip)
        for a in range(self.depth):
            total = self.own[a, :, here].astype(f32)
            for k in self.mid_range():
                total = total + self.mid[k - 1, a].astype(f32)
            self.own[a, :, here] = total.astype(bf16)

    def last_copy(self, k):
        me = self.me
        src = self.own.at[me.z_at(k), :, self.lanes(me.chip)]
        return far_copy(src, self.last.at[k - 1], (self.last_s, self.last_r), k - 1, me.tower(k))

    def fold_last(self):
        me = self.me
        for k in self.last_range():
            self.last_copy(k).wait()
        total = self.own[me.z, :, self.lanes(me.chip)].astype(f32)
        for k in self.last_range():
            total = total + self.last[k - 1].astype(f32)
        self.done[me.core, me.chip] = total.astype(bf16)


def back(
    grad_context, q, k, v, p, pos, x, attend_all, resid, g_out, g_exp, g_red, g_vec, depth, heads
):
    chips, per, cluster, width = grad_context.shape
    half, blocks, pairs = width // 2, 2 * chips, heads // 4
    dma = pltpu.SemaphoreType.DMA
    anywhere = pl.BlockSpec(memory_space=pl.ANY)
    quarter = width // depth
    hidden = g_exp.shape[-1]
    eighth, tall, wide = quarter // blocks, hidden // depth // blocks, hidden // blocks
    rows = quarter // chips
    c, t = chips - 1, depth - 1
    shapes = [
        ((chips * per, cluster, width), bf16),
        ((quarter, 3 * width), f32),
        ((2, chips, eighth, width), f32),
        ((quarter, hidden), f32),
        ((2, chips, tall, width), f32),
        (g_vec.shape, f32),
        ((2, 8, 3 * half), f32),
    ]
    vm = pltpu.VMEM
    one = dma((1,))
    reducer = [one, one, dma((c,)), dma((c,)), dma((t,)), dma((t,)), dma((c,)), dma((c,)), one, one, one]
    tower = [one, one, dma((t,)), dma((t,)), dma((c,)), dma((c,)), dma((c,)), dma((c,)), one, one, one]
    return pl.pallas_call(
        functools.partial(back_kernel, chips, depth, heads),
        out_shape=[jax.ShapeDtypeStruct(*s) for s in shapes],
        in_specs=[anywhere] * 13,
        out_specs=[anywhere] * len(shapes),
        scratch_shapes=[
            vm((2, chips, per, cluster, half), bf16),
            vm((2, pairs, blocks, cluster, 128), bf16),
            vm((2, pairs, blocks, cluster, 128), bf16),
            vm((2, pairs, blocks, cluster, 128), bf16),
            vm((2, pairs, blocks, cluster, 2 * cluster), bf16),
            vm(pos.shape, jnp.int32),
            vm((2, chips, cluster, width), bf16),
            vm(attend_all.shape, bf16),
            vm((chips, cluster, width), f32),
            vm((blocks, cluster, 128), bf16),
            vm((3, blocks, cluster, 128), bf16),
            vm((2, 2, chips, cluster, 3 * half), bf16),
            vm((2, chips, cluster, 3 * half), bf16),
            vm((2, chips, cluster, width), bf16),
            vm((width, 3 * half), f32),
            vm((depth, chips, rows, 3 * half), bf16),
            vm((c, depth, rows, 3 * half), bf16),
            vm((t, rows, 3 * half), bf16),
            vm((2, chips, rows, 3 * half), bf16),
            vm((depth, chips, eighth, width), bf16),
            vm((depth, chips, eighth, width), bf16),
            vm((c, depth, eighth, width), bf16),
            vm((t, eighth, width), bf16),
            vm((2, chips, eighth, width), bf16),
            vm((depth, quarter, chips * wide), bf16),
            vm((depth, quarter, chips * wide), bf16),
            vm((c, depth, quarter, wide), bf16),
            vm((t, quarter, wide), bf16),
            vm((2, chips, quarter, wide), bf16),
            vm((depth, chips, tall, width), bf16),
            vm((depth, chips, tall, width), bf16),
            vm((t, chips, tall, width), bf16),
            vm((c, tall, width), bf16),
            vm((2, chips, tall, width), bf16),
            vm(shapes[1][0], f32),
            vm(shapes[2][0], f32),
            vm(shapes[3][0], f32),
            vm(shapes[4][0], f32),
            vm(g_vec.shape, f32),
            vm((chips + t,) + g_vec.shape, f32),
            vm((8, 3 * half), f32),
            vm((chips + t, 8, 3 * half), f32),
            one, one, dma((2,)), dma((2,)),
            dma((per * c,)), dma((per * c,)),
            dma((16,)), dma((per + 6,)),
            dma((chips + t,)), dma((chips + t,)), dma((chips + t,)), dma((chips + t,)),
            *tower, *reducer, *reducer, *reducer,
        ],
        compiler_params=pltpu.CompilerParams(
            collective_id=2, has_side_effects=True, vmem_limit_bytes=63 * 2**20
        ),
        name="back",
    )(grad_context, q, k, v, p, pos, x, attend_all, resid, g_out, g_exp, g_red, g_vec)


def places(rank, cluster, share):
    seqs, rows, length = rank.shape
    clusters = cluster // share
    target = rank // cluster
    which = lax.broadcasted_iota(jnp.int32, (1, 1, clusters, 1), 2)
    inside = (target[:, :, None, :] == which).astype(bf16)
    first = lax.broadcasted_iota(jnp.int32, (length, length), 0)
    second = lax.broadcasted_iota(jnp.int32, (length, length), 1)
    before = (first < second).astype(bf16)
    count = lax.dot_general(
        inside.reshape(seqs * rows * clusters, length),
        before,
        (((1,), (0,)), ((), ())),
        preferred_element_type=f32,
    ).reshape(seqs, rows, clusters, length)
    spot = which.astype(f32) * share + count
    return jnp.sum(inside.astype(f32) * spot, axis=2).astype(jnp.int32)


def per_chip(
    tokens,
    attend_weight,
    query_bias,
    value_bias,
    output_weight,
    output_bias,
    first_gain,
    first_shift,
    expand_weight,
    expand_bias,
    reduce_weight,
    reduce_bias,
    second_gain,
    second_shift,
    query_rank,
    key_rank,
    cotangent,
):
    seqs, cluster, width = tokens.shape
    heads = query_rank.shape[1]
    owners = lax.axis_size("seq")
    depth = lax.axis_size("batch")
    chips = owners // 2
    per = seqs // chips
    rows = seqs * cluster
    half = width // 2
    share = cluster // owners
    core = lax.rem(lax.axis_index("seq"), 2)
    groups = [[2 * p + c for p in range(chips)] for c in range(2)]

    def swap(x):
        return lax.all_to_all(
            x, "seq", split_axis=0, concat_axis=0, tiled=True, axis_index_groups=groups
        )

    pos = places(jnp.concatenate([query_rank, key_rank], axis=1), cluster, share)
    quarter = width // depth
    small = jnp.concatenate(
        [
            v.astype(f32)
            for v in (
                query_bias,
                value_bias,
                output_bias,
                first_gain,
                first_shift,
                reduce_bias,
                second_gain,
                second_shift,
                expand_bias,
            )
        ]
    )
    count = small.shape[0] // quarter
    vectors = jnp.pad(small.reshape(count, quarter), ((0, 16 - count), (0, 256 - quarter)))
    (x_all, context, qs, ks, vs, ps, pos_all, attend_all, vec_all, out_all, exp_all, red_all) = attend(
        tokens, pos, attend_weight, vectors, output_weight, expand_weight, reduce_weight, chips, depth, heads
    )
    full = jnp.transpose(vec_all[:, :8, :quarter], (1, 0, 2)).reshape(8, width)
    bias_up = vec_all[:, 8:count, :quarter].reshape(-1)
    output_full = out_all.reshape(width, width)
    expand_full = exp_all.reshape(width, -1)
    reduce_full = red_all.reshape(-1, width)
    mine = lax.dynamic_index_in_dim(x_all, core, 0, keepdims=False).reshape(rows, width)
    context = context.reshape(rows, width)
    resid_one = mine.astype(f32) + jnp.dot(context, output_full, preferred_element_type=f32) + full[2]
    middle, normed_one, inverse_one = layer_norm(resid_one, full[3], full[4])
    middle_low = lax.optimization_barrier(middle.astype(bf16))
    pre = jnp.dot(middle_low, expand_full, preferred_element_type=f32) + bias_up
    hidden = jax.nn.gelu(pre, approximate=False).astype(bf16)
    hidden = lax.optimization_barrier(hidden)
    resid_two = middle + jnp.dot(hidden, reduce_full, preferred_element_type=f32) + full[5]
    final, normed_two, inverse_two = layer_norm(resid_two, full[6], full[7])
    layer_out = swap(final.astype(bf16).reshape(seqs, cluster, width))
    upstream = swap(cotangent).reshape(rows, width).astype(f32)
    grad_second_gain = jnp.sum(upstream * normed_two, axis=0)
    grad_second_shift = jnp.sum(upstream, axis=0)
    grad_resid_two = norm_back(upstream, normed_two, inverse_two, full[6])
    grad_branch_two = grad_resid_two.astype(bf16)
    grad_reduce_bias = jnp.sum(grad_branch_two, axis=0, dtype=f32)
    grad_reduce = transpose_left(hidden, grad_branch_two)
    grad_hidden = transpose_right(grad_branch_two, reduce_full)
    grad_pre = (grad_hidden * gelu_slope(pre)).astype(bf16)
    grad_pre = lax.optimization_barrier(grad_pre)
    grad_expand_bias = jnp.sum(grad_pre, axis=0, dtype=f32)
    grad_expand = transpose_left(middle_low, grad_pre)
    grad_middle = grad_resid_two + transpose_right(grad_pre, expand_full)
    grad_first_gain = jnp.sum(grad_middle * normed_one, axis=0)
    grad_first_shift = jnp.sum(grad_middle, axis=0)
    grad_resid_one = norm_back(grad_middle, normed_one, inverse_one, full[3])
    grad_branch_one = grad_resid_one.astype(bf16)
    grad_output_bias = jnp.sum(grad_branch_one, axis=0, dtype=f32)
    grad_output = transpose_left(context, grad_branch_one)
    grad_context = transpose_right(grad_branch_one, output_full).astype(bf16)
    vector_grads = jnp.concatenate(
        [
            grad_output_bias,
            grad_first_gain,
            grad_first_shift,
            grad_reduce_bias,
            grad_second_gain,
            grad_second_shift,
            grad_expand_bias,
        ]
    )
    lanes = -(-vector_grads.shape[0] // 1024) * 8
    vector_grads = jnp.pad(vector_grads, (0, lanes * 128 - vector_grads.shape[0])).reshape(lanes, 128)
    layer_out, grad_context = lax.optimization_barrier((layer_out, grad_context))
    token_grad, aw_grad, ow_grad, ew_grad, rw_grad, vec_sum, bias_sum = back(
        grad_context.reshape(chips, per, cluster, width),
        qs,
        ks,
        vs,
        ps,
        pos_all,
        x_all,
        attend_all,
        grad_resid_one.reshape(chips, per, cluster, width),
        grad_output.astype(bf16).reshape(depth, owners, -1, width),
        grad_expand.astype(bf16).reshape(depth, quarter, -1),
        grad_reduce.astype(bf16).reshape(depth, owners, -1, width),
        vector_grads,
        depth,
        heads,
    )
    z = lax.axis_index("batch")
    vec_sum = vec_sum.reshape(-1)
    six = lax.dynamic_slice_in_dim(vec_sum[: 6 * width].reshape(6, width), z * quarter, quarter, 1)
    up = vec_sum[6 * width :]
    tall = expand_bias.shape[0]
    up = lax.dynamic_slice_in_dim(up, z * tall, tall, 0)
    both = jnp.concatenate([bias_sum[0, 0], bias_sum[1, 0]]).reshape(2, 3, half)
    query_value = jnp.transpose(both, (1, 0, 2)).reshape(3, width)
    query_value = lax.dynamic_slice_in_dim(query_value, z * quarter, quarter, 1)
    return (
        layer_out,
        token_grad,
        aw_grad,
        query_value[0],
        query_value[2],
        ow_grad.reshape(quarter, width),
        six[0],
        six[1],
        six[2],
        ew_grad,
        up,
        rw_grad.reshape(-1, width),
        six[3],
        six[4],
        six[5],
    )


def layer(mesh):
    def run(*arrays):
        seqs, cluster, width = arrays[0].shape
        heads = arrays[14].shape[1]
        owners, depth = mesh.shape["seq"], mesh.shape["batch"]
        chips = owners // 2
        fits = (
            owners % 2 == 0
            and chips > 1
            and depth > 1
            and seqs % chips == 0
            and cluster == 128
            and heads % 4 == 0
            and width == heads * 64
            and cluster % (16 * owners) == 0
        )
        return (per_chip if fits else per_device)(*arrays)

    return run


def solution(mesh):
    in_specs = (
        P("batch", "seq", None),
        P("batch", None),
        P("batch"),
        P("batch"),
        P("batch", None),
        P("batch"),
        P("batch"),
        P("batch"),
        P("batch", None),
        P("batch"),
        P("batch", None),
        P("batch"),
        P("batch"),
        P("batch"),
        P("batch", None, "seq"),
        P("batch", None, "seq"),
        P("batch", "seq", None),
    )
    out_specs = (
        P("batch", "seq", None),
        P("batch", "seq", None),
        P("batch", None),
        P("batch"),
        P("batch"),
        P("batch", None),
        P("batch"),
        P("batch"),
        P("batch"),
        P("batch", None),
        P("batch"),
        P("batch", None),
        P("batch"),
        P("batch"),
        P("batch"),
    )
    return jax.shard_map(
        layer(mesh), mesh=mesh, in_specs=in_specs, out_specs=out_specs, check_vma=False
    )
```

```python
import functools
import math

import jax
import jax.numpy as jnp
from jax import lax
from jax.experimental import pallas as pl
from jax.experimental.pallas import tpu as pltpu
from jax.sharding import PartitionSpec as P

epsilon = 1e-05


def layer_norm(resid, gain, shift):
    center = jnp.mean(resid, axis=-1, keepdims=True)
    centered = resid - center
    spread = jnp.mean(centered * centered, axis=-1, keepdims=True)
    inverse = lax.rsqrt(spread + epsilon)
    normed = centered * inverse
    return (normed * gain + shift, normed, inverse)


def norm_back(upstream, normed, inverse, gain):
    scaled = upstream * gain
    first_mean = jnp.mean(scaled, axis=-1, keepdims=True)
    second_mean = jnp.mean(scaled * normed, axis=-1, keepdims=True)
    return inverse * (scaled - first_mean - normed * second_mean)


def gelu_slope(value):
    cumulative = 0.5 * (1.0 + lax.erf(value * 0.5**0.5))
    density = jnp.exp(-0.5 * value * value) * (2.0 * math.pi) ** (-0.5)
    return cumulative + value * density


def transpose_left(first, second):
    return lax.dot_general(
        first, second, (((0,), (0,)), ((), ())), preferred_element_type=jnp.float32
    )


def transpose_right(first, second):
    return lax.dot_general(
        first, second, (((1,), (1,)), ((), ())), preferred_element_type=jnp.float32
    )


def group_table(rank, cluster, owners):
    share = cluster // owners
    target = rank // cluster
    length = rank.shape[-1]
    places = lax.broadcasted_iota(jnp.int32, (length, length), 0)
    later = lax.broadcasted_iota(jnp.int32, (length, length), 1)
    before = (places < later)[None, None]
    same = target[..., :, None] == target[..., None, :]
    earlier = jnp.sum((same & before).astype(jnp.int32), axis=-2)
    position = target * share + earlier
    slots = lax.broadcasted_iota(jnp.int32, position.shape + (length,), 3)
    return (position[..., None] == slots).astype(jnp.bfloat16)


def sort_heads(rows, table, heads):
    seqs, length, width = rows.shape
    split = rows.reshape(seqs, length, heads, width // heads)
    moved = jnp.einsum("shtp,sthd->sphd", table, split, preferred_element_type=jnp.float32)
    return moved.astype(rows.dtype).reshape(seqs, length, width)


def unsort_heads(rows, table, heads):
    seqs, length, width = rows.shape
    split = rows.reshape(seqs, length, heads, width // heads)
    moved = jnp.einsum("shtp,sphd->sthd", table, split, preferred_element_type=jnp.float32)
    return moved.astype(rows.dtype).reshape(seqs, length, width)


def cluster_scores(queries, keys_rows, heads):
    items, length, width = queries.shape
    size = width // heads
    query_split = queries.reshape(items, length, heads, size)
    key_split = keys_rows.reshape(items, length, heads, size)
    scores = jnp.einsum(
        "sqhd,skhd->shqk", query_split, key_split, preferred_element_type=jnp.float32
    )
    return scores * size ** (-0.5)


def cluster_forward(queries, keys_rows, values_rows, heads):
    items, length, width = queries.shape
    scores = cluster_scores(queries, keys_rows, heads)
    top = jnp.max(scores, axis=-1, keepdims=True)
    weights = jnp.exp(scores - top)
    total = jnp.sum(weights, axis=-1, keepdims=True)
    probs = (weights / total).astype(jnp.bfloat16)
    value_split = values_rows.reshape(items, length, heads, width // heads)
    context = jnp.einsum("shqk,skhd->sqhd", probs, value_split, preferred_element_type=jnp.float32)
    return (
        context.reshape(items, length, width).astype(jnp.bfloat16),
        (top + jnp.log(total))[..., 0],
    )


def cluster_backward(scores, log_total, queries, keys_rows, values_rows, grad_context, heads):
    items, length, width = queries.shape
    size = width // heads
    query_split = queries.reshape(items, length, heads, size)
    key_split = keys_rows.reshape(items, length, heads, size)
    value_split = values_rows.reshape(items, length, heads, size)
    grad_split = grad_context.reshape(items, length, heads, size)
    probs = jnp.exp(scores - log_total[..., None])
    grad_probs = jnp.einsum(
        "sqhd,skhd->shqk", grad_split, value_split, preferred_element_type=jnp.float32
    )
    inner = jnp.sum(probs * grad_probs, axis=-1, keepdims=True)
    grad_scores = (probs * (grad_probs - inner)).astype(jnp.bfloat16)
    scale = size ** (-0.5)
    grad_query = (
        jnp.einsum("shqk,skhd->sqhd", grad_scores, key_split, preferred_element_type=jnp.float32)
        * scale
    )
    grad_key = (
        jnp.einsum("shqk,sqhd->skhd", grad_scores, query_split, preferred_element_type=jnp.float32)
        * scale
    )
    grad_value = jnp.einsum(
        "shqk,sqhd->skhd",
        probs.astype(jnp.bfloat16),
        grad_split,
        preferred_element_type=jnp.float32,
    )
    shape = (items, length, width)
    return (
        grad_query.reshape(shape).astype(jnp.bfloat16),
        grad_key.reshape(shape).astype(jnp.bfloat16),
        grad_value.reshape(shape).astype(jnp.bfloat16),
    )


def send_context(context):
    return lax.all_to_all(context, "seq", split_axis=1, concat_axis=1, tiled=True)


def send_grads(grads):
    return (
        lax.all_to_all(grads[0], "seq", split_axis=1, concat_axis=1, tiled=True),
        lax.all_to_all(grads[1], "seq", split_axis=1, concat_axis=1, tiled=True),
        lax.all_to_all(grads[2], "seq", split_axis=1, concat_axis=1, tiled=True),
    )


def make_step(left, pieces):
    total = jnp.dot(left, pieces[0], preferred_element_type=jnp.float32)
    stored = tuple(pieces[1:]) + ()
    placed = tuple((piece for piece in stored))
    return (total,) + placed


def make_hidden_step(before, pieces):
    section = before + pieces[1].astype(jnp.float32)
    activated = jax.nn.gelu(section, approximate=False).astype(jnp.bfloat16)
    total = jnp.dot(activated, pieces[0], preferred_element_type=jnp.float32)
    stored = ()
    return (total, section, activated) + stored


def per_device(
    tokens,
    attend_weight,
    query_bias,
    value_bias,
    output_weight,
    output_bias,
    first_gain,
    first_shift,
    expand_weight,
    expand_bias,
    reduce_weight,
    reduce_bias,
    second_gain,
    second_shift,
    query_rank,
    key_rank,
    cotangent,
):
    seqs, cluster, width = tokens.shape
    heads = query_rank.shape[1]
    rows = seqs * cluster
    owners = lax.axis_size("seq")
    flat = tokens.reshape(rows, width)
    attend_out = make_step(
        flat,
        (
            lax.all_gather(attend_weight, "batch", axis=0, tiled=True),
            lax.all_gather(query_bias, "batch", axis=0, tiled=True),
            lax.all_gather(value_bias, "batch", axis=0, tiled=True),
        ),
    )
    summed = attend_out[0]
    queries = (summed[:, :width] + attend_out[1].astype(jnp.float32)).astype(jnp.bfloat16)
    keys_rows = summed[:, width : 2 * width].astype(jnp.bfloat16)
    values_rows = (summed[:, 2 * width :] + attend_out[2].astype(jnp.float32)).astype(jnp.bfloat16)
    query_table = group_table(query_rank, cluster, owners)
    key_table = group_table(key_rank, cluster, owners)
    query_sorted = sort_heads(queries.reshape(seqs, cluster, width), query_table, heads)
    key_sorted = sort_heads(keys_rows.reshape(seqs, cluster, width), key_table, heads)
    value_sorted = sort_heads(values_rows.reshape(seqs, cluster, width), key_table, heads)
    received = (
        lax.all_to_all(query_sorted, "seq", split_axis=1, concat_axis=1, tiled=True),
        lax.all_to_all(key_sorted, "seq", split_axis=1, concat_axis=1, tiled=True),
        lax.all_to_all(value_sorted, "seq", split_axis=1, concat_axis=1, tiled=True),
    )
    context, log_total = cluster_forward(received[0], received[1], received[2], heads)
    forward_out = (send_context(context), log_total, received[0], received[1], received[2])
    context_rows = unsort_heads(forward_out[0], query_table, heads).reshape(rows, width)
    output_out = make_step(
        context_rows,
        (
            lax.all_gather(output_weight, "batch", axis=0, tiled=True),
            lax.all_gather(output_bias, "batch", axis=0, tiled=True),
            lax.all_gather(first_gain, "batch", axis=0, tiled=True),
            lax.all_gather(first_shift, "batch", axis=0, tiled=True),
        ),
    )
    resid_one = flat.astype(jnp.float32) + output_out[0] + output_out[1].astype(jnp.float32)
    gain_one = output_out[2].astype(jnp.float32)
    middle, normed_one, inverse_one = layer_norm(
        resid_one, gain_one, output_out[3].astype(jnp.float32)
    )
    middle_low = middle.astype(jnp.bfloat16)
    expand_out = make_step(
        middle_low,
        (
            lax.all_gather(expand_weight, "batch", axis=0, tiled=True),
            lax.all_gather(reduce_bias, "batch", axis=0, tiled=True),
            lax.all_gather(second_gain, "batch", axis=0, tiled=True),
            lax.all_gather(second_shift, "batch", axis=0, tiled=True),
        ),
    )
    hidden_out = make_hidden_step(
        expand_out[0],
        (
            lax.all_gather(reduce_weight, "batch", axis=0, tiled=True),
            lax.all_gather(expand_bias, "batch", axis=0, tiled=True),
        ),
    )
    pre_full, hidden_full = (hidden_out[1], hidden_out[2])
    resid_two = middle + hidden_out[0] + expand_out[1].astype(jnp.float32)
    gain_two = expand_out[2].astype(jnp.float32)
    final, normed_two, inverse_two = layer_norm(
        resid_two, gain_two, expand_out[3].astype(jnp.float32)
    )
    layer_out = final.astype(jnp.bfloat16).reshape(seqs, cluster, width)
    attend_full, output_full, expand_full, reduce_full = (
        lax.all_gather(attend_weight, "batch", axis=0, tiled=True),
        lax.all_gather(output_weight, "batch", axis=0, tiled=True),
        lax.all_gather(expand_weight, "batch", axis=0, tiled=True),
        lax.all_gather(reduce_weight, "batch", axis=0, tiled=True),
    )
    upstream = cotangent.reshape(rows, width).astype(jnp.float32)
    grad_second_gain = jnp.sum(upstream * normed_two, axis=0)
    grad_second_shift = jnp.sum(upstream, axis=0)
    grad_resid_two = norm_back(upstream, normed_two, inverse_two, gain_two)
    grad_branch_two = grad_resid_two.astype(jnp.bfloat16)
    grad_reduce_bias = jnp.sum(grad_branch_two, axis=0, dtype=jnp.float32)
    grad_reduce = transpose_left(hidden_full, grad_branch_two)
    grad_hidden = transpose_right(grad_branch_two, reduce_full)
    grad_pre = (grad_hidden * gelu_slope(pre_full)).astype(jnp.bfloat16)
    grad_expand_bias = jnp.sum(grad_pre, axis=0, dtype=jnp.float32)
    grad_expand = transpose_left(middle_low, grad_pre)
    grad_middle = grad_resid_two + transpose_right(grad_pre, expand_full)
    grad_first_gain = jnp.sum(grad_middle * normed_one, axis=0)
    grad_first_shift = jnp.sum(grad_middle, axis=0)
    grad_resid_one = norm_back(grad_middle, normed_one, inverse_one, gain_one)
    grad_branch_one = grad_resid_one.astype(jnp.bfloat16)
    grad_output_bias = jnp.sum(grad_branch_one, axis=0, dtype=jnp.float32)
    grad_output = transpose_left(context_rows, grad_branch_one)
    grad_context = transpose_right(grad_branch_one, output_full).astype(jnp.bfloat16)
    grad_sorted = sort_heads(grad_context.reshape(seqs, cluster, width), query_table, heads)
    grad_received = lax.all_to_all(grad_sorted, "seq", split_axis=1, concat_axis=1, tiled=True)
    kept_scores = cluster_scores(forward_out[2], forward_out[3], heads)
    home = send_grads(
        cluster_backward(
            kept_scores,
            forward_out[1],
            forward_out[2],
            forward_out[3],
            forward_out[4],
            grad_received,
            heads,
        )
    )
    grad_queries = unsort_heads(home[0], query_table, heads).reshape(rows, width)
    grad_keys = unsort_heads(home[1], key_table, heads).reshape(rows, width)
    grad_values = unsort_heads(home[2], key_table, heads).reshape(rows, width)
    grad_mixed = jnp.concatenate([grad_queries, grad_keys, grad_values], axis=1)
    grad_query_bias = jnp.sum(grad_queries, axis=0, dtype=jnp.float32)
    grad_value_bias = jnp.sum(grad_values, axis=0, dtype=jnp.float32)
    grad_attend = transpose_left(flat, grad_mixed)
    token_grad = (
        (grad_resid_one + transpose_right(grad_mixed, attend_full))
        .astype(jnp.bfloat16)
        .reshape(seqs, cluster, width)
    )
    owned = (
        lax.psum_scatter(
            grad_attend.astype(jnp.bfloat16), "batch", scatter_dimension=0, tiled=True
        ).astype(jnp.float32),
        lax.psum_scatter(
            grad_query_bias.astype(jnp.bfloat16), "batch", scatter_dimension=0, tiled=True
        ).astype(jnp.float32),
        lax.psum_scatter(
            grad_value_bias.astype(jnp.bfloat16), "batch", scatter_dimension=0, tiled=True
        ).astype(jnp.float32),
        lax.psum_scatter(
            grad_output.astype(jnp.bfloat16), "batch", scatter_dimension=0, tiled=True
        ).astype(jnp.float32),
        lax.psum_scatter(
            grad_output_bias.astype(jnp.bfloat16), "batch", scatter_dimension=0, tiled=True
        ).astype(jnp.float32),
        lax.psum_scatter(
            grad_first_gain.astype(jnp.bfloat16), "batch", scatter_dimension=0, tiled=True
        ).astype(jnp.float32),
        lax.psum_scatter(
            grad_first_shift.astype(jnp.bfloat16), "batch", scatter_dimension=0, tiled=True
        ).astype(jnp.float32),
        lax.psum_scatter(
            grad_expand.astype(jnp.bfloat16), "batch", scatter_dimension=0, tiled=True
        ).astype(jnp.float32),
        lax.psum_scatter(
            grad_expand_bias.astype(jnp.bfloat16), "batch", scatter_dimension=0, tiled=True
        ).astype(jnp.float32),
        lax.psum_scatter(
            grad_reduce.astype(jnp.bfloat16), "batch", scatter_dimension=0, tiled=True
        ).astype(jnp.float32),
        lax.psum_scatter(
            grad_reduce_bias.astype(jnp.bfloat16), "batch", scatter_dimension=0, tiled=True
        ).astype(jnp.float32),
        lax.psum_scatter(
            grad_second_gain.astype(jnp.bfloat16), "batch", scatter_dimension=0, tiled=True
        ).astype(jnp.float32),
        lax.psum_scatter(
            grad_second_shift.astype(jnp.bfloat16), "batch", scatter_dimension=0, tiled=True
        ).astype(jnp.float32),
    )
    shared = (
        lax.psum(owned[0].astype(jnp.bfloat16), "seq").astype(jnp.float32),
        lax.psum(owned[1].astype(jnp.bfloat16), "seq").astype(jnp.float32),
        lax.psum(owned[2].astype(jnp.bfloat16), "seq").astype(jnp.float32),
        lax.psum(owned[3].astype(jnp.bfloat16), "seq").astype(jnp.float32),
        lax.psum(owned[4].astype(jnp.bfloat16), "seq").astype(jnp.float32),
        lax.psum(owned[5].astype(jnp.bfloat16), "seq").astype(jnp.float32),
        lax.psum(owned[6].astype(jnp.bfloat16), "seq").astype(jnp.float32),
        lax.psum(owned[7].astype(jnp.bfloat16), "seq").astype(jnp.float32),
        lax.psum(owned[8].astype(jnp.bfloat16), "seq").astype(jnp.float32),
        lax.psum(owned[9].astype(jnp.bfloat16), "seq").astype(jnp.float32),
        lax.psum(owned[10].astype(jnp.bfloat16), "seq").astype(jnp.float32),
        lax.psum(owned[11].astype(jnp.bfloat16), "seq").astype(jnp.float32),
        lax.psum(owned[12].astype(jnp.bfloat16), "seq").astype(jnp.float32),
    )
    return (
        layer_out,
        token_grad,
        shared[0],
        shared[1],
        shared[2],
        shared[3],
        shared[4],
        shared[5],
        shared[6],
        shared[7],
        shared[8],
        shared[9],
        shared[10],
        shared[11],
        shared[12],
    )


MESH = pl.DeviceIdType.MESH
f32 = jnp.float32
bf16 = jnp.bfloat16


class Place:
    def __init__(self, chips, depth):
        self.chips, self.depth = chips, depth
        self.z = lax.axis_index("batch")
        spot = lax.axis_index("seq")
        self.chip, self.core = lax.div(spot, 2), lax.rem(spot, 2)

    def chip_at(self, k):
        return lax.rem(self.chip + k + self.chips, self.chips)

    def z_at(self, k):
        return lax.rem(self.z + k + self.depth, self.depth)

    def plane(self, k):
        return (self.z, self.chip_at(k) * 2 + self.core)

    def tower(self, k):
        return (self.z_at(k), self.chip * 2 + self.core)

    def sibling(self):
        return (self.z, self.chip * 2 + 1 - self.core)

    def greet(self):
        bell = pltpu.get_barrier_semaphore()
        others = [self.plane(k) for k in range(1, self.chips)]
        others += [self.tower(k) for k in range(1, self.depth)]
        others.append(self.sibling())
        for other in others:
            pl.semaphore_signal(bell, inc=1, device_id=other, device_id_type=MESH)
        pl.semaphore_wait(bell, len(others))


def far_copy(src, dst, sems, at, device):
    return pltpu.make_async_remote_copy(
        src_ref=src,
        dst_ref=dst,
        send_sem=sems[0].at[at],
        recv_sem=sems[1].at[at],
        device_id=device,
        device_id_type=MESH,
    )


def one_hot(row, slots):
    return jnp.where(slots == row, 1.0, 0.0).astype(bf16)


def split_lanes(tile, low):
    zero = jnp.zeros_like(tile)
    return jnp.where(low, tile, zero), jnp.where(low, zero, tile)


def stack_lanes(tile, low):
    first, second = split_lanes(tile, low)
    return jnp.concatenate([first, second], axis=0)


def dot_rows(a, b):
    return jnp.dot(a, b, preferred_element_type=f32)


def dot_lanes(a, b):
    return lax.dot_general(a, b, (((1,), (1,)), ((), ())), preferred_element_type=f32)


def dot_first(a, b):
    return lax.dot_general(a, b, (((0,), (0,)), ((), ())), preferred_element_type=f32)


def multiple(value, by):
    return pl.multiple_of(value, by)


def forward_kernel(
    chips,
    depth,
    heads,
    tok_ref,
    pos_ref,
    aw_ref,
    vec_ref,
    ow_ref,
    ew_ref,
    rw_ref,
    cot_ref,
    x_out,
    ctx_out,
    q_out,
    k_out,
    v_out,
    p_out,
    pos_out,
    aw_out,
    vec_out,
    ow_out,
    ew_out,
    rw_out,
    n1_out,
    inv_out,
    ml_out,
    hid_out,
    slope_out,
    lo_out,
    gr_out,
    gb_out,
    sum_out,
    xbuf,
    posbuf,
    wbuf,
    vbuf,
    bias,
    ctxb,
    ctxt,
    owbuf,
    ewbuf,
    rwbuf,
    cbuf,
    n1buf,
    invbuf,
    mlbuf,
    vecs,
    upb,
    sums,
    tok_s,
    tok_r,
    tokc_s,
    tokc_r,
    pos_s,
    pos_r,
    posc_s,
    posc_r,
    aw_s,
    aw_r,
    awc_s,
    awc_r,
    vec_s,
    vec_r,
    wz_s,
    wz_r,
    wp_s,
    wp_r,
    wc_s,
    wc_r,
    ctx_s,
    ctx_r,
    cot_s,
    cot_r,
    oc_s,
    oc_r,
    loc,
    out_sem,
    slope_sem,
    att_sem,
):
    me = Place(chips, depth)
    z, chip, core = me.z, me.chip, me.core
    per = tok_ref.shape[0] // chips
    half = aw_ref.shape[1] // 6
    rows_z = aw_ref.shape[0]
    pairs = heads // 4
    size = half // (2 * pairs)
    me.greet()

    def aw_copy(k, part):
        columns = pl.ds(multiple(part * 2 * half + core * half, 128), half)
        return far_copy(
            aw_ref.at[:, columns],
            wbuf.at[pl.ds(multiple(z * rows_z, 8), rows_z), pl.ds(part * half, half)],
            (aw_s, aw_r),
            (k - 1) * 3 + part,
            me.tower(k),
        )

    def mine(ref, target):
        return ref.at[pl.ds(target * per, per)]

    def tok_copy(k):
        return far_copy(
            mine(tok_ref, me.chip_at(k)), xbuf.at[core, chip], (tok_s, tok_r), k - 1, me.plane(k)
        )

    def pos_copy(k):
        return far_copy(
            mine(pos_ref, me.chip_at(k)), posbuf.at[core, chip], (pos_s, pos_r), k - 1, me.plane(k)
        )

    def vec_copy(k):
        return far_copy(vec_ref, vbuf.at[z], (vec_s, vec_r), k - 1, me.tower(k))

    sends = []
    for k in range(1, chips):
        sends.append(pos_copy(k))
        sends[-1].start()
    for k in range(1, depth):
        sends.append(vec_copy(k))
        sends[-1].start()
    for k in range(1, max(chips, depth)):
        if k < depth:
            for part in range(3):
                sends.append(aw_copy(k, part))
                sends[-1].start()
        if k < chips:
            sends.append(tok_copy(k))
            sends[-1].start()
    local = []

    def keep(src, dst):
        copy = pltpu.make_async_copy(src, dst, loc.at[len(local)])
        copy.start()
        local.append(copy)

    keep(mine(tok_ref, chip), xbuf.at[core, chip])
    keep(mine(pos_ref, chip), posbuf.at[core, chip])
    keep(vec_ref, vbuf.at[z])
    for part in range(3):
        keep(
            aw_ref.at[:, pl.ds(multiple(part * 2 * half + core * half, 128), half)],
            wbuf.at[pl.ds(multiple(z * rows_z, 8), rows_z), pl.ds(part * half, half)],
        )
    wide = ew_ref.shape[1] // (2 * chips)
    tall = rw_ref.shape[0] // (2 * chips)
    mid_rows = rows_z // 2
    mine_at = core * chips + chip

    def piece(kind):
        if kind == 0:
            return ow_ref.at[pl.ds(multiple(core * mid_rows, 8), mid_rows)]
        if kind == 1:
            return ew_ref.at[:, pl.ds(multiple(mine_at * wide, 128), wide)]
        return rw_ref.at[pl.ds(multiple(mine_at * tall, 8), tall)]

    def place(kind, zz):
        if kind == 0:
            return owbuf.at[zz, core]
        if kind == 1:
            return ewbuf.at[zz, :, pl.ds(multiple(mine_at * wide, 128), wide)]
        return rwbuf.at[zz, mine_at]

    def place_all(kind, at):
        if kind == 1:
            return ewbuf.at[:, :, pl.ds(multiple(at * wide, 128), wide)]
        return rwbuf.at[:, at]

    for kind in range(3):
        keep(piece(kind), place(kind, z))

    def wz_copy(kind, k):
        return far_copy(
            piece(kind),
            place(kind, z),
            (wz_s, wz_r),
            kind * (depth - 1) + k - 1,
            me.tower(k),
        )

    def wp_copy(kind, k, origin):
        at = core * chips + origin
        return far_copy(
            place_all(kind, at),
            place_all(kind, at),
            (wp_s, wp_r),
            (kind - 1) * (chips - 1) + k - 1,
            me.plane(k),
        )

    def wc_copy(kind, origin_k):
        at = core * chips + me.chip_at(origin_k)
        return far_copy(
            place_all(kind, at),
            place_all(kind, at),
            (wc_s, wc_r),
            (kind - 1) * chips + origin_k,
            me.sibling(),
        )

    def oc_copy():
        spot = owbuf.at[:, core]
        return far_copy(spot, spot, (oc_s, oc_r), 0, me.sibling())

    def cot_copy(k):
        return far_copy(
            mine(cot_ref, me.chip_at(k)), cbuf.at[chip], (cot_s, cot_r), k - 1, me.plane(k)
        )

    keep(mine(cot_ref, chip), cbuf.at[chip])

    for copy in local[:2]:
        copy.wait()

    def tokc_copy(k):
        source = me.chip_at(-k)
        return far_copy(
            xbuf.at[core, source], xbuf.at[core, source], (tokc_s, tokc_r), k, me.sibling()
        )

    def posc_copy(k):
        source = me.chip_at(-k)
        return far_copy(
            posbuf.at[core, source], posbuf.at[core, source], (posc_s, posc_r), k, me.sibling()
        )

    for k in range(chips):
        if k:
            pos_copy(k).wait_recv()
            tok_copy(k).wait_recv()
        for copy in (posc_copy(k), tokc_copy(k)):
            copy.start()
            sends.append(copy)
    for k in range(1, chips):
        cot_copy(k).start()
        sends.append(cot_copy(k))
    for copy in local[2:6]:
        copy.wait()
    for k in range(1, depth):
        vec_copy(k).wait_recv()
        for part in range(3):
            aw_copy(k, part).wait_recv()
    for k in range(1, depth):
        wz_copy(1, k).start()
        for kind in range(3):
            sends.append(wz_copy(kind, k))
    for k in range(chips):
        posc_copy(k).wait_recv()
        tokc_copy(k).wait_recv()
    for copy in local[6:]:
        copy.wait()

    outs = []

    def emit(src, dst):
        copy = pltpu.make_async_copy(src, dst, out_sem.at[len(outs)])
        copy.start()
        outs.append(copy)

    emit(xbuf, x_out)
    emit(posbuf, pos_out)
    emit(wbuf, aw_out.at[core])
    emit(vbuf, vec_out)
    awc = far_copy(wbuf, aw_out.at[core], (awc_s, awc_r), 0, me.sibling())
    awc.start()
    sends.append(awc)

    quarter = rows_z
    for zz in range(depth):
        begin = zz * quarter
        for row, at in ((0, 0), (1, 2)):
            for side in range(2):
                lo = max(begin, side * half)
                hi = min(begin + quarter, (side + 1) * half)
                if lo < hi:
                    bias[side, 0:1, at * half + lo - side * half : at * half + hi - side * half] = (
                        vbuf[zz, row : row + 1, lo - begin : hi - begin]
                    )
    bias[0, 0:1, half : 2 * half] = jnp.zeros((1, half), f32)
    bias[1, 0:1, half : 2 * half] = jnp.zeros((1, half), f32)
    added = bias[core, 0:1, :]
    for zz in range(depth):
        for row in range(8):
            vecs[row : row + 1, zz * quarter : (zz + 1) * quarter] = vbuf[
                zz, row : row + 1, :quarter
            ]
        steps = upb.shape[1] // (depth * quarter)
        for row in range(steps):
            to = (zz * steps + row) * quarter
            upb[0:1, to : to + quarter] = vbuf[zz, 8 + row : 9 + row, :quarter]

    cluster = tok_ref.shape[1]
    blocks = 2 * chips
    share = cluster // blocks
    width = tok_ref.shape[2]

    slots = lax.broadcasted_iota(jnp.int32, (cluster, cluster), 0)
    low = lax.broadcasted_iota(jnp.int32, (cluster, 128), 1) < size
    scale = size ** (-0.5)

    def tables(jj, i, pair, part):
        first = part * heads + core * (heads // 2) + 2 * pair
        rows = [
            one_hot(posbuf[jj // chips, jj % chips, i, pl.ds(first + h, 1), :], slots)
            for h in range(2)
        ]
        return rows

    def plane_stage(kind):
        for k in range(1, depth):
            wz_copy(kind, k).wait_recv()
        for k in range(1, chips):
            wp_copy(kind, k, chip).start()
        wc_copy(kind, 0).start()

    def hook(i, pair):
        @pl.when((i == 0) & (pair == 0))
        def _():
            plane_stage(1)
            for k in range(1, depth):
                wz_copy(2, k).start()
            for k in range(1, depth):
                wz_copy(0, k).start()

        @pl.when((i == min(1, per - 1)) & (pair == pairs - 1))
        def _():
            plane_stage(2)
            for k in range(1, depth):
                wz_copy(0, k).wait_recv()
            oc_copy().start()

    def attention(qkv, qs, ks, vs, ps, os):
        @pl.loop(0, blocks)
        def _(jj):
            x = xbuf[lax.div(jj, chips), lax.rem(jj, chips)].reshape(per * cluster, width)
            mixed = (dot_rows(x, wbuf[...]) + added).astype(bf16)
            for at in range(3 * pairs):
                qkv[at, jj] = mixed[:, at * 128 : (at + 1) * 128].reshape(per, cluster, 128)

        @pl.loop(0, per)
        def _(i):
            @pl.loop(0, pairs)
            def _(pair):
                at = i * pairs + pair
                for jj in range(blocks):
                    tq = jnp.concatenate(tables(jj, i, pair, 0), axis=1)
                    tk = jnp.concatenate(tables(jj, i, pair, 1), axis=1)
                    q = stack_lanes(qkv[pair, jj, i], low)
                    k = stack_lanes(qkv[pairs + pair, jj, i], low)
                    v = stack_lanes(qkv[2 * pairs + pair, jj, i], low)
                    span = slice(jj * share, (jj + 1) * share)
                    sq = dot_rows(tq, q).astype(bf16)
                    skv = dot_rows(tk, jnp.concatenate([k, v], axis=1)).astype(bf16)
                    qs[at, :, span, :] = sq.reshape(blocks, share, 128)
                    ks[at, :, span, :] = skv[:, :128].reshape(blocks, share, 128)
                    vs[at, :, span, :] = skv[:, 128:].reshape(blocks, share, 128)
                for c in range(blocks):
                    scores = dot_lanes(qs[at, c], stack_lanes(ks[at, c], low)) * scale
                    halves = []
                    for h in range(2):
                        s = scores[:, h * cluster : (h + 1) * cluster]
                        e = jnp.exp(s - jnp.max(s, axis=1, keepdims=True))
                        halves.append((e / jnp.sum(e, axis=1, keepdims=True)).astype(bf16))
                    probs = jnp.concatenate(halves, axis=1)
                    ps[at, c] = probs
                    o = dot_rows(probs, stack_lanes(vs[at, c], low)).astype(bf16)
                    os[c] = o
                for jj in range(blocks):
                    tq = jnp.concatenate(tables(jj, i, pair, 0), axis=0)
                    rows = os[:, jj * share : (jj + 1) * share, :].reshape(cluster, 128)
                    back = dot_first(tq, stack_lanes(rows, low)).astype(bf16)
                    ctxb[jj // chips, jj % chips, i, :, pl.ds(multiple(pair * 128, 128), 128)] = back
                hook(i, pair)

        pieces = ((qs, q_out), (ks, k_out), (vs, v_out), (ps, p_out))
        copies = [
            pltpu.make_async_copy(src, dst, att_sem.at[n]) for n, (src, dst) in enumerate(pieces)
        ]
        far, own = ctx_copies()
        for copy in copies + [far, own]:
            copy.start()
        for copy in copies + [far, own]:
            copy.wait()

    def ctx_copies():
        lanes = pl.ds(multiple(core * half, 128), half)
        far = far_copy(
            ctxb.at[1 - core], ctxt.at[:, :, :, lanes], (ctx_s, ctx_r), 0, me.sibling()
        )
        own = pltpu.make_async_copy(ctxb.at[core], ctxt.at[:, :, :, lanes], att_sem.at[4])
        return far, own

    group = (per * pairs, blocks, cluster, 128)
    pl.run_scoped(
        attention,
        pltpu.VMEM((3 * pairs, blocks, per, cluster, 128), bf16),
        pltpu.VMEM(group, bf16),
        pltpu.VMEM(group, bf16),
        pltpu.VMEM(group, bf16),
        pltpu.VMEM((per * pairs, blocks, cluster, 2 * cluster), bf16),
        pltpu.VMEM((blocks, cluster, 128), bf16),
    )

    def from_plane(kind):
        for k in range(1, chips):
            wp_copy(kind, k, me.chip_at(-k)).wait_recv()
            wc_copy(kind, chips - k).start()

    def from_sibling(kind):
        for k in range(chips):
            wc_copy(kind, k).wait()
        for k in range(1, chips):
            wp_copy(kind, k, chip).wait_send()

    oc_copy().wait()
    from_plane(1)
    from_sibling(1)
    emit(ctxt, ctx_out)
    emit(owbuf, ow_out)
    emit(ewbuf, ew_out)
    tile = per * cluster
    hidden = upb.shape[1]
    eps = epsilon

    def moments(rows):
        center = jnp.mean(rows, axis=1, keepdims=True)
        centered = rows - center
        spread = jnp.mean(centered * centered, axis=1, keepdims=True)
        inverse = lax.rsqrt(spread + eps)
        return centered * inverse, inverse

    def slope_out_copy(j, slot):
        return pltpu.make_async_copy(sbuf.at[slot], slope_out.at[j], slope_sem.at[slot])

    def vec(row):
        return vecs[row : row + 1, :]

    def feed(hbuf, sbuf):
        def slope_copy(j, slot):
            return pltpu.make_async_copy(sbuf.at[slot], slope_out.at[j], slope_sem.at[slot])

        @pl.loop(0, chips)
        def _(j):
            slot = lax.rem(j, 2)

            @pl.when(j >= 2)
            def _():
                slope_copy(j - 2, slot).wait()

            rows = ctxt[j].reshape(tile, width)
            branch = dot_rows(rows, owbuf[...].reshape(width, width))
            resid = xbuf[core, j].reshape(tile, width).astype(f32) + branch + vec(2)
            normed, inverse = moments(resid)
            n1buf[j] = normed
            invbuf[j] = jnp.broadcast_to(inverse, (tile, 128))
            mlbuf[j] = (normed * vec(3) + vec(4)).astype(bf16)

            @pl.loop(0, hidden // 384)
            def _(n):
                lanes = pl.ds(multiple(n * 384, 128), 384)
                weight = ewbuf[:, :, lanes].reshape(width, 384)
                pre = dot_rows(mlbuf[j], weight) + upb[0:1, lanes]
                cumulative = 0.5 * (1.0 + lax.erf(pre * 0.5**0.5))
                density = jnp.exp(-0.5 * pre * pre) * (2.0 * math.pi) ** (-0.5)
                hbuf[j, :, lanes] = (pre * cumulative).astype(bf16)
                sbuf[slot, :, lanes] = (cumulative + pre * density).astype(bf16)

            slope_copy(j, slot).start()

        emit(n1buf, n1_out)
        emit(invbuf, inv_out)
        emit(mlbuf, ml_out)
        emit(hbuf, hid_out)
        from_plane(2)
        from_sibling(2)
        emit(rwbuf, rw_out)
        for copy in sends:
            copy.wait_send()
        for k in range(1, chips):
            cot_copy(k).wait_recv()
        for j in range(max(chips - 2, 0), chips):
            slope_copy(j, j % 2).wait()
        for copy in outs:
            copy.wait()
        sums[...] = jnp.zeros_like(sums)

        @pl.loop(0, chips)
        def _(j):
            branch = vec(5)
            for zz in range(depth):
                span = hidden // depth
                branch = branch + dot_rows(
                    hbuf[j, :, zz * span : (zz + 1) * span], rwbuf[zz].reshape(span, width)
                )
            middle = n1buf[j] * vec(3) + vec(4)
            normed, inverse = moments(middle + branch)
            upstream = cbuf[j].reshape(tile, width).astype(f32)
            cbuf[j] = (normed * vec(6) + vec(7)).astype(bf16).reshape(per, cluster, width)
            sums[0:1, :] += jnp.sum(upstream * normed, axis=0, keepdims=True)
            sums[1:2, :] += jnp.sum(upstream, axis=0, keepdims=True)
            scaled = upstream * vec(6)
            first = jnp.mean(scaled, axis=1, keepdims=True)
            second = jnp.mean(scaled * normed, axis=1, keepdims=True)
            grad = inverse * (scaled - first - normed * second)
            n1buf[j] = grad
            low_grad = grad.astype(bf16)
            sums[2:3, :] += jnp.sum(low_grad.astype(f32), axis=0, keepdims=True)
            ctxt[j] = low_grad.reshape(per, cluster, width)

        done = len(outs)
        emit(cbuf, lo_out)
        emit(n1buf, gr_out)
        emit(ctxt, gb_out)
        emit(sums, sum_out)
        awc.wait_recv()
        for copy in outs[done:]:
            copy.wait()

    pl.run_scoped(
        feed,
        pltpu.VMEM((chips, tile, hidden), bf16),
        pltpu.VMEM((2, tile, hidden), bf16),
    )


def forward(
    tokens,
    pos,
    attend_weight,
    vectors,
    output_weight,
    expand_weight,
    reduce_weight,
    cotangent,
    chips,
    depth,
    heads,
):
    seqs, cluster, width = tokens.shape
    per, blocks, pairs = seqs // chips, 2 * chips, heads // 4
    half = width // 2
    rows_z = attend_weight.shape[0]
    hidden = expand_weight.shape[1]
    items = per * pairs
    tile = per * cluster
    dma = pltpu.SemaphoreType.DMA
    anywhere = pl.BlockSpec(memory_space=pl.ANY)
    tall = reduce_weight.shape[0] // blocks
    shapes = [
        ((2, chips, per, cluster, width), bf16),
        ((chips, per, cluster, width), bf16),
        ((items, blocks, cluster, 128), bf16),
        ((items, blocks, cluster, 128), bf16),
        ((items, blocks, cluster, 128), bf16),
        ((items, blocks, cluster, 2 * cluster), bf16),
        ((2, chips, per, 2 * heads, cluster), jnp.int32),
        ((2, depth * rows_z, 3 * half), bf16),
        ((depth,) + vectors.shape, f32),
        ((depth, 2, rows_z // 2, width), bf16),
        ((depth, rows_z, hidden), bf16),
        ((depth, blocks, tall, width), bf16),
        ((chips, tile, width), f32),
        ((chips, tile, 128), f32),
        ((chips, tile, width), bf16),
        ((chips, tile, hidden), bf16),
        ((chips, tile, hidden), bf16),
        ((chips, per, cluster, width), bf16),
        ((chips, tile, width), f32),
        ((chips, per, cluster, width), bf16),
        ((8, width), f32),
    ]
    t, c = depth - 1, chips - 1
    vm = pltpu.VMEM
    return pl.pallas_call(
        functools.partial(forward_kernel, chips, depth, heads),
        out_shape=[jax.ShapeDtypeStruct(*s) for s in shapes],
        in_specs=[anywhere] * 8,
        out_specs=[anywhere] * len(shapes),
        scratch_shapes=[
            vm(shapes[0][0], bf16),
            vm(shapes[6][0], jnp.int32),
            vm(shapes[7][0][1:], bf16),
            vm(shapes[8][0], f32),
            vm((2, 8, 3 * half), f32),
            vm((2, chips, per, cluster, half), bf16),
            vm(shapes[1][0], bf16),
            vm(shapes[9][0], bf16),
            vm(shapes[10][0], bf16),
            vm(shapes[11][0], bf16),
            vm(shapes[17][0], bf16),
            vm(shapes[12][0], f32),
            vm(shapes[13][0], f32),
            vm(shapes[14][0], bf16),
            vm((8, width), f32),
            vm((8, hidden), f32),
            vm((8, width), f32),
            dma((c,)), dma((c,)), dma((chips,)), dma((chips,)),
            dma((c,)), dma((c,)), dma((chips,)), dma((chips,)),
            dma((3 * t,)), dma((3 * t,)), dma((1,)), dma((1,)),
            dma((t,)), dma((t,)),
            dma((3 * t,)), dma((3 * t,)),
            dma((2 * c,)), dma((2 * c,)),
            dma((2 * chips,)), dma((2 * chips,)),
            dma((1,)), dma((1,)),
            dma((c,)), dma((c,)),
            dma((1,)), dma((1,)),
            dma((12,)), dma((24,)), dma((2,)), dma((5,)),
        ],
        compiler_params=pltpu.CompilerParams(
            collective_id=1, has_side_effects=True, vmem_limit_bytes=63 * 2**20
        ),
        name="forward",
    )(
        tokens,
        pos,
        attend_weight,
        vectors,
        output_weight,
        expand_weight,
        reduce_weight,
        cotangent,
    )


def add_into(target, at, parts):
    total = target[at].astype(f32)
    for part in parts:
        total = total + part.astype(f32)
    target[at] = total.astype(target.dtype)


class Reducer:
    def __init__(self, me, src_half, own, near, mid, last, done, sems, tower_first):
        self.me, self.src_half = me, src_half
        self.own, self.near, self.mid, self.last, self.done = own, near, mid, last, done
        (self.near_s, self.near_r, self.mid_s, self.mid_r, self.last_s, self.last_r) = sems[:6]
        (self.back_s, self.back_r, self.side_s, self.side_r) = sems[6:10]
        self.loc = sems[10]
        self.tower_first = tower_first
        self.depth, self.chips = own.shape[0], own.shape[1]

    def near_copy(self):
        me = self.me
        return far_copy(
            self.src_half(1 - me.core), self.near, (self.near_s, self.near_r), 0, me.sibling()
        )

    def own_copy(self):
        return pltpu.make_async_copy(self.src_half(self.me.core), self.own, self.loc.at[0])

    def begin(self):
        self.near_copy().start()
        self.own_copy().start()

    def fold_near(self):
        self.own_copy().wait()
        self.near_copy().wait()

        @pl.loop(0, self.depth)
        def _(a):
            for b in range(self.chips):
                add_into(self.own, (a, b), [self.near[a, b]])

    def mid_copy(self, k):
        me = self.me
        if self.tower_first:
            src, device = self.own.at[me.z_at(k)], me.tower(k)
        else:
            src, device = self.own.at[:, me.chip_at(k)], me.plane(k)
        return far_copy(src, self.mid.at[k - 1], (self.mid_s, self.mid_r), k - 1, device)

    def mid_range(self):
        return range(1, self.depth if self.tower_first else self.chips)

    def send_mid(self):
        for k in self.mid_range():
            self.mid_copy(k).start()

    def fold_mid(self):
        me = self.me
        for k in self.mid_range():
            self.mid_copy(k).wait()
        if self.tower_first:
            for b in range(self.chips):
                add_into(self.own, (me.z, b), [self.mid[k - 1, b] for k in self.mid_range()])
        else:
            for a in range(self.depth):
                add_into(self.own, (a, me.chip), [self.mid[k - 1, a] for k in self.mid_range()])

    def last_range(self):
        return range(1, self.chips if self.tower_first else self.depth)

    def last_copy(self, k):
        me = self.me
        if self.tower_first:
            src, device = self.own.at[me.z, me.chip_at(k)], me.plane(k)
        else:
            src, device = self.own.at[me.z_at(k), me.chip], me.tower(k)
        return far_copy(src, self.last.at[k - 1], (self.last_s, self.last_r), k - 1, device)

    def send_last(self):
        for k in self.last_range():
            self.last_copy(k).start()

    def fold_last(self):
        me = self.me
        for k in self.last_range():
            self.last_copy(k).wait()
        total = self.own[me.z, me.chip].astype(f32)
        for k in self.last_range():
            total = total + self.last[k - 1].astype(f32)
        self.done[me.core, me.chip] = total.astype(bf16)

    def back_copy(self, k):
        me = self.me
        spot = self.done.at[me.core, me.chip]
        return far_copy(spot, spot, (self.back_s, self.back_r), k - 1, me.plane(k))

    def send_back(self):
        for k in range(1, self.chips):
            self.back_copy(k).start()

    def side_copy(self):
        me = self.me
        spot = self.done.at[me.core]
        return far_copy(spot, spot, (self.side_s, self.side_r), 0, me.sibling())

    def send_side(self):
        for k in range(1, self.chips):
            self.back_copy(k).wait()
        self.side_copy().start()

    def finish(self):
        self.side_copy().wait()


def back_kernel(
    chips,
    depth,
    heads,
    d_ref,
    q_ref,
    k_ref,
    v_ref,
    p_ref,
    pos_ref,
    x_ref,
    aw_ref,
    res_ref,
    go_ref,
    ge_ref,
    gr_ref,
    gv_ref,
    token_out,
    aw_out,
    ow_out,
    ew_out,
    rw_out,
    vec_out,
    bias_out,
    dbuf,
    qs,
    ks,
    vs,
    ps,
    posbuf,
    xbuf,
    wbuf,
    rbuf,
    ds,
    gs,
    gbuf,
    gfar,
    tbuf,
    dw,
    dwb,
    amid,
    alast,
    adone,
    o_own,
    o_near,
    o_mid,
    o_last,
    o_done,
    e_own,
    e_near,
    e_mid,
    e_last,
    e_done,
    r_own,
    r_near,
    r_mid,
    r_last,
    r_done,
    a32,
    o32,
    e32,
    r32,
    vbuf,
    vgot,
    bbuf,
    bgot,
    d_s,
    d_r,
    g_s,
    g_r,
    t_s,
    t_r,
    load,
    out_sem,
    v_s,
    v_r,
    b_s,
    b_r,
    *sems,
):
    me = Place(chips, depth)
    core, chip = me.core, me.chip
    per = d_ref.shape[1]
    cluster, width = d_ref.shape[2], d_ref.shape[3]
    half = width // 2
    pairs = heads // 4
    size = half // (2 * pairs)
    blocks = 2 * chips
    share = cluster // blocks
    me.greet()
    groups = [sems[n * 11 : (n + 1) * 11] for n in range(4)]
    wide = ge_ref.shape[2] // (2 * chips)

    def out_half(c):
        return go_ref.at[:, pl.ds(c * chips, chips)]

    def reduce_half(c):
        return gr_ref.at[:, pl.ds(c * chips, chips)]

    def expand_half(c):
        return ge_ref.at[:, :, pl.ds(multiple(c * chips * wide, 128), chips * wide)]

    red = Reducer(me, reduce_half, r_own, r_near, r_mid, r_last, r_done, groups[0], True)
    exp = Expander(me, expand_half, e_own, e_near, e_mid, e_last, e_done, groups[1], False)
    out = Reducer(me, out_half, o_own, o_near, o_mid, o_last, o_done, groups[2], False)
    att = Reducer(me, None, dwb, None, amid, alast, adone, groups[3], False)

    theirs = pl.ds(multiple((1 - core) * half, 128), half)
    far = far_copy(d_ref.at[:, :, :, theirs], dbuf.at[core], (d_s, d_r), 0, me.sibling())
    far.start()
    first = [
        pltpu.make_async_copy(
            d_ref.at[:, :, :, pl.ds(multiple(core * half, 128), half)], dbuf.at[core], load.at[12]
        ),
        pltpu.make_async_copy(pos_ref, posbuf, load.at[13]),
        pltpu.make_async_copy(aw_ref, wbuf, load.at[14]),
        pltpu.make_async_copy(gv_ref, vbuf, load.at[15]),
    ]

    def loads(i, slot):
        span = pl.ds(i * pairs, pairs)
        pieces = (
            (q_ref.at[span], qs),
            (k_ref.at[span], ks),
            (v_ref.at[span], vs),
            (p_ref.at[span], ps),
        )
        return [
            pltpu.make_async_copy(src, dst.at[slot], load.at[slot * 4 + n])
            for n, (src, dst) in enumerate(pieces)
        ]

    def load_x(i):
        return pltpu.make_async_copy(x_ref.at[:, :, i], xbuf, load.at[8])

    def load_r(i):
        return pltpu.make_async_copy(res_ref.at[:, i], rbuf, load.at[9])

    for copy in first + loads(0, 0) + [load_x(0)]:
        copy.start()
    red.begin()
    exp.begin()
    out.begin()

    slots = lax.broadcasted_iota(jnp.int32, (cluster, cluster), 0)
    low = lax.broadcasted_iota(jnp.int32, (cluster, 128), 1) < size
    scale = size ** (-0.5)
    bbuf[...] = jnp.zeros_like(bbuf)
    for copy in first:
        copy.wait()
    far.wait()

    def tables(jj, i, pair, part):
        begin = part * heads + core * (heads // 2) + 2 * pair
        return [
            one_hot(posbuf[jj // chips, jj % chips, i, pl.ds(begin + h, 1), :], slots)
            for h in range(2)
        ]

    def clusters(i, slot, pair):
        lanes = pl.ds(multiple(pair * 128, 128), 128)
        for jj in range(blocks):
            tq = jnp.concatenate(tables(jj, i, pair, 0), axis=1)
            rows = stack_lanes(dbuf[jj // chips, jj % chips, i, :, lanes], low)
            ds[:, jj * share : (jj + 1) * share, :] = (
                dot_rows(tq, rows).astype(bf16).reshape(blocks, share, 128)
            )
        for c in range(blocks):
            d = ds[c]
            probs = ps[slot, pair, c]
            slope = dot_lanes(d, stack_lanes(vs[slot, pair, c], low))
            broad = probs.astype(f32)
            halves = []
            for h in range(2):
                span = slice(h * cluster, (h + 1) * cluster)
                inner = jnp.sum(broad[:, span] * slope[:, span], axis=1, keepdims=True)
                halves.append((broad[:, span] * (slope[:, span] - inner)).astype(bf16))
            grads = jnp.concatenate(halves, axis=1)
            gq = dot_rows(grads, stack_lanes(ks[slot, pair, c], low)) * scale
            gk = dot_first(grads, qs[slot, pair, c]) * scale
            gv = dot_first(probs, d)
            gs[0, c] = gq.astype(bf16)
            gs[1, c] = jnp.where(low, gk[:cluster], gk[cluster:]).astype(bf16)
            gs[2, c] = jnp.where(low, gv[:cluster], gv[cluster:]).astype(bf16)
        for jj in range(blocks):
            for part in range(3):
                if part < 2:
                    table = jnp.concatenate(tables(jj, i, pair, part), axis=0)
                rows = gs[part, :, jj * share : (jj + 1) * share, :].reshape(cluster, 128)
                back = dot_first(table, stack_lanes(rows, low))
                to = pl.ds(multiple(part * half + pair * 128, 128), 128)
                gbuf[slot, jj // chips, jj % chips, :, to] = back.astype(bf16)

    def give(slot):
        return far_copy(gbuf.at[slot, 1 - core], gfar.at[slot], (g_s, g_r), slot, me.sibling())

    def token_copy(i, slot, k):
        return far_copy(
            tbuf.at[slot, me.chip_at(k)],
            token_out.at[chip * per + i],
            (t_s, t_r),
            i * (chips - 1) + k - 1,
            me.plane(k),
        )

    def token_keep(i, slot):
        return pltpu.make_async_copy(
            tbuf.at[slot, chip], token_out.at[chip * per + i], out_sem.at[i]
        )

    def token_rows(i, slot):
        load_r(i).wait()
        give(slot).wait()
        for j in range(chips):
            near = dot_lanes(gbuf[slot, core, j], wbuf[core])
            distant = dot_lanes(gfar[slot, j], wbuf[1 - core])
            tbuf[slot, j] = (rbuf[j] + near + distant).astype(bf16)
        token_keep(i, slot).start()
        for k in range(1, chips):
            token_copy(i, slot, k).start()

    for i in range(per):
        slot = i % 2
        for copy in loads(i, slot):
            copy.wait()
        if i >= 1:
            token_rows(i - 1, 1 - slot)
        load_r(i).start()
        if i + 1 < per:
            for copy in loads(i + 1, 1 - slot):
                copy.start()

        @pl.loop(0, pairs)
        def _(pair):
            clusters(i, slot, pair)

            if i == 0:

                @pl.when(pair == 0)
                def _():
                    red.fold_near()
                    red.send_mid()
                    exp.fold_near()
                    exp.send_mid()
                    out.fold_near()
                    out.send_mid()

        if i >= 2:
            token_keep(i - 2, slot).wait()
            for k in range(1, chips):
                token_copy(i - 2, slot, k).wait()
        give(slot).start()
        load_x(i).wait()
        for b in range(2):
            x = jnp.concatenate([xbuf[b, j] for j in range(chips)], axis=0)
            g = jnp.concatenate([gbuf[slot, b, j] for j in range(chips)], axis=0)
            term = dot_first(x, g)
            if i == 0 and b == 0:
                dw[...] = term
            else:
                dw[...] += term
            bbuf[0:1, :] += jnp.sum(g.astype(f32), axis=0, keepdims=True)
        if i + 1 < per:
            load_x(i + 1).start()
        if i == per - 2:
            exp.fold_mid()
            exp.send_last()
            out.fold_mid()
            out.send_last()

    rows = dwb.shape[2]
    for a in range(depth):
        for b in range(chips):
            begin = (a * chips + b) * rows
            dwb[a, b] = dw[begin : begin + rows, :].astype(bf16)
    att.send_mid()
    token_rows(per - 1, (per - 1) % 2)
    exp.fold_last()
    exp.send_back()
    out.fold_last()
    out.send_back()
    red.fold_mid()
    red.send_last()
    for hop in range(3):
        for vec, got, s, r, skip in ((vbuf, vgot, v_s, v_r, -1), (bbuf, bgot, b_s, b_r, 0)):
            if hop == skip:
                continue
            if hop == 0:
                copies = [far_copy(vec, got.at[0], (s, r), 0, me.sibling())]
                begin = 0
            elif hop == 1:
                begin = 1
                copies = [
                    far_copy(vec, got.at[k], (s, r), k, me.plane(k)) for k in range(1, chips)
                ]
            else:
                begin = chips
                copies = [
                    far_copy(vec, got.at[chips + k - 1], (s, r), chips + k - 1, me.tower(k))
                    for k in range(1, depth)
                ]
            for copy in copies:
                copy.start()
            for copy in copies:
                copy.wait()
            total = vec[...]
            for n in range(len(copies)):
                total = total + got[begin + n]
            vec[...] = total
    att.fold_mid()
    att.send_last()
    last = [pltpu.make_async_copy(vbuf, vec_out, out_sem.at[per])]
    last[-1].start()
    share_bias = far_copy(bbuf, bias_out.at[core], (b_s, b_r), 0, me.sibling())
    share_bias.start()
    last.append(pltpu.make_async_copy(bbuf, bias_out.at[core], out_sem.at[per + 1]))
    last[-1].start()
    red.fold_last()
    red.send_back()
    exp.send_side()
    out.send_side()
    att.fold_last()
    att.send_back()
    red.send_side()
    exp.finish()
    tall = e_done.shape[2]
    for c in range(2):
        for p in range(chips):
            at = (c * chips + p) * wide
            e32[:, at : at + wide] = e_done[c, p].astype(f32)
    last.append(pltpu.make_async_copy(e32, ew_out, out_sem.at[per + 2]))
    last[-1].start()
    out.finish()
    o32[...] = o_done[...].astype(f32)
    last.append(pltpu.make_async_copy(o32, ow_out, out_sem.at[per + 3]))
    last[-1].start()
    red.finish()
    r32[...] = r_done[...].astype(f32)
    last.append(pltpu.make_async_copy(r32, rw_out, out_sem.at[per + 4]))
    last[-1].start()
    att.send_side()
    att.finish()
    for c in range(2):
        for p in range(chips):
            for part in range(3):
                to = (2 * part + c) * half
                a32[p * rows : (p + 1) * rows, to : to + half] = adone[
                    c, p, :, part * half : (part + 1) * half
                ].astype(f32)
    last.append(pltpu.make_async_copy(a32, aw_out, out_sem.at[per + 5]))
    last[-1].start()
    for i in range(max(per - 2, 0), per):
        token_keep(i, i % 2).wait()
        for k in range(1, chips):
            token_copy(i, i % 2, k).wait()
    share_bias.wait()
    for copy in last:
        copy.wait()


class Expander(Reducer):
    def __init__(self, me, src_half, own, near, mid, last, done, sems, tower_first):
        self.wide = done.shape[3]
        Reducer.__init__(self, me, src_half, own, near, mid, last, done, sems, tower_first)
        self.chips = done.shape[1]

    def lanes(self, chip):
        return pl.ds(multiple(chip * self.wide, 128), self.wide)

    def fold_near(self):
        self.own_copy().wait()
        self.near_copy().wait()

        @pl.loop(0, self.depth)
        def _(a):
            add_into(self.own, a, [self.near[a]])

    def mid_copy(self, k):
        me = self.me
        src = self.own.at[:, :, self.lanes(me.chip_at(k))]
        return far_copy(src, self.mid.at[k - 1], (self.mid_s, self.mid_r), k - 1, me.plane(k))

    def fold_mid(self):
        me = self.me
        for k in self.mid_range():
            self.mid_copy(k).wait()
        here = self.lanes(me.chip)
        for a in range(self.depth):
            total = self.own[a, :, here].astype(f32)
            for k in self.mid_range():
                total = total + self.mid[k - 1, a].astype(f32)
            self.own[a, :, here] = total.astype(bf16)

    def last_copy(self, k):
        me = self.me
        src = self.own.at[me.z_at(k), :, self.lanes(me.chip)]
        return far_copy(src, self.last.at[k - 1], (self.last_s, self.last_r), k - 1, me.tower(k))

    def fold_last(self):
        me = self.me
        for k in self.last_range():
            self.last_copy(k).wait()
        total = self.own[me.z, :, self.lanes(me.chip)].astype(f32)
        for k in self.last_range():
            total = total + self.last[k - 1].astype(f32)
        self.done[me.core, me.chip] = total.astype(bf16)


def back(
    grad_context, q, k, v, p, pos, x, attend_all, resid, g_out, g_exp, g_red, g_vec, depth, heads
):
    chips, per, cluster, width = grad_context.shape
    half, blocks, pairs = width // 2, 2 * chips, heads // 4
    dma = pltpu.SemaphoreType.DMA
    anywhere = pl.BlockSpec(memory_space=pl.ANY)
    quarter = width // depth
    hidden = g_exp.shape[-1]
    eighth, tall, wide = quarter // blocks, hidden // depth // blocks, hidden // blocks
    rows = quarter // chips
    c, t = chips - 1, depth - 1
    shapes = [
        ((chips * per, cluster, width), bf16),
        ((quarter, 3 * width), f32),
        ((2, chips, eighth, width), f32),
        ((quarter, hidden), f32),
        ((2, chips, tall, width), f32),
        (g_vec.shape, f32),
        ((2, 8, 3 * half), f32),
    ]
    vm = pltpu.VMEM
    one = dma((1,))
    reducer = [one, one, dma((c,)), dma((c,)), dma((t,)), dma((t,)), dma((c,)), dma((c,)), one, one, one]
    tower = [one, one, dma((t,)), dma((t,)), dma((c,)), dma((c,)), dma((c,)), dma((c,)), one, one, one]
    return pl.pallas_call(
        functools.partial(back_kernel, chips, depth, heads),
        out_shape=[jax.ShapeDtypeStruct(*s) for s in shapes],
        in_specs=[anywhere] * 13,
        out_specs=[anywhere] * len(shapes),
        scratch_shapes=[
            vm((2, chips, per, cluster, half), bf16),
            vm((2, pairs, blocks, cluster, 128), bf16),
            vm((2, pairs, blocks, cluster, 128), bf16),
            vm((2, pairs, blocks, cluster, 128), bf16),
            vm((2, pairs, blocks, cluster, 2 * cluster), bf16),
            vm(pos.shape, jnp.int32),
            vm((2, chips, cluster, width), bf16),
            vm(attend_all.shape, bf16),
            vm((chips, cluster, width), f32),
            vm((blocks, cluster, 128), bf16),
            vm((3, blocks, cluster, 128), bf16),
            vm((2, 2, chips, cluster, 3 * half), bf16),
            vm((2, chips, cluster, 3 * half), bf16),
            vm((2, chips, cluster, width), bf16),
            vm((width, 3 * half), f32),
            vm((depth, chips, rows, 3 * half), bf16),
            vm((c, depth, rows, 3 * half), bf16),
            vm((t, rows, 3 * half), bf16),
            vm((2, chips, rows, 3 * half), bf16),
            vm((depth, chips, eighth, width), bf16),
            vm((depth, chips, eighth, width), bf16),
            vm((c, depth, eighth, width), bf16),
            vm((t, eighth, width), bf16),
            vm((2, chips, eighth, width), bf16),
            vm((depth, quarter, chips * wide), bf16),
            vm((depth, quarter, chips * wide), bf16),
            vm((c, depth, quarter, wide), bf16),
            vm((t, quarter, wide), bf16),
            vm((2, chips, quarter, wide), bf16),
            vm((depth, chips, tall, width), bf16),
            vm((depth, chips, tall, width), bf16),
            vm((t, chips, tall, width), bf16),
            vm((c, tall, width), bf16),
            vm((2, chips, tall, width), bf16),
            vm(shapes[1][0], f32),
            vm(shapes[2][0], f32),
            vm(shapes[3][0], f32),
            vm(shapes[4][0], f32),
            vm(g_vec.shape, f32),
            vm((chips + t,) + g_vec.shape, f32),
            vm((8, 3 * half), f32),
            vm((chips + t, 8, 3 * half), f32),
            one, one, dma((2,)), dma((2,)),
            dma((per * c,)), dma((per * c,)),
            dma((16,)), dma((per + 6,)),
            dma((chips + t,)), dma((chips + t,)), dma((chips + t,)), dma((chips + t,)),
            *tower, *reducer, *reducer, *reducer,
        ],
        compiler_params=pltpu.CompilerParams(
            collective_id=2, has_side_effects=True, vmem_limit_bytes=63 * 2**20
        ),
        name="back",
    )(grad_context, q, k, v, p, pos, x, attend_all, resid, g_out, g_exp, g_red, g_vec)


def places(rank, cluster, share):
    seqs, rows, length = rank.shape
    clusters = cluster // share
    target = rank // cluster
    which = lax.broadcasted_iota(jnp.int32, (1, 1, clusters, 1), 2)
    inside = (target[:, :, None, :] == which).astype(bf16)
    first = lax.broadcasted_iota(jnp.int32, (length, length), 0)
    second = lax.broadcasted_iota(jnp.int32, (length, length), 1)
    before = (first < second).astype(bf16)
    count = lax.dot_general(
        inside.reshape(seqs * rows * clusters, length),
        before,
        (((1,), (0,)), ((), ())),
        preferred_element_type=f32,
    ).reshape(seqs, rows, clusters, length)
    spot = which.astype(f32) * share + count
    return jnp.sum(inside.astype(f32) * spot, axis=2).astype(jnp.int32)


def per_chip(
    tokens,
    attend_weight,
    query_bias,
    value_bias,
    output_weight,
    output_bias,
    first_gain,
    first_shift,
    expand_weight,
    expand_bias,
    reduce_weight,
    reduce_bias,
    second_gain,
    second_shift,
    query_rank,
    key_rank,
    cotangent,
):
    seqs, cluster, width = tokens.shape
    heads = query_rank.shape[1]
    owners = lax.axis_size("seq")
    depth = lax.axis_size("batch")
    chips = owners // 2
    per = seqs // chips
    rows = seqs * cluster
    half = width // 2
    share = cluster // owners
    core = lax.rem(lax.axis_index("seq"), 2)
    groups = [[2 * p + c for p in range(chips)] for c in range(2)]

    def swap(x):
        return lax.all_to_all(
            x, "seq", split_axis=0, concat_axis=0, tiled=True, axis_index_groups=groups
        )

    pos = places(jnp.concatenate([query_rank, key_rank], axis=1), cluster, share)
    quarter = width // depth
    small = jnp.concatenate(
        [
            v.astype(f32)
            for v in (
                query_bias,
                value_bias,
                output_bias,
                first_gain,
                first_shift,
                reduce_bias,
                second_gain,
                second_shift,
                expand_bias,
            )
        ]
    )
    count = small.shape[0] // quarter
    vectors = jnp.pad(small.reshape(count, quarter), ((0, 16 - count), (0, 256 - quarter)))
    (
        x_all,
        context,
        qs,
        ks,
        vs,
        ps,
        pos_all,
        attend_all,
        vec_all,
        out_all,
        exp_all,
        red_all,
        normed_one,
        inverse_one,
        middle_low,
        hidden,
        slope,
        layer_out,
        grad_resid_two,
        grad_branch_two,
        late_sums,
    ) = forward(
        tokens,
        pos,
        attend_weight,
        vectors,
        output_weight,
        expand_weight,
        reduce_weight,
        cotangent,
        chips,
        depth,
        heads,
    )
    full = jnp.transpose(vec_all[:, :8, :quarter], (1, 0, 2)).reshape(8, width)
    output_full = out_all.reshape(width, width)
    expand_full = exp_all.reshape(width, -1)
    reduce_full = red_all.reshape(-1, width)
    context = context.reshape(rows, width)
    normed_one = normed_one.reshape(rows, width)
    inverse_one = inverse_one.reshape(rows, 128)[:, :1]
    middle_low = middle_low.reshape(rows, width)
    hidden = hidden.reshape(rows, -1)
    slope = slope.reshape(rows, -1)
    grad_resid_two = grad_resid_two.reshape(rows, width)
    grad_branch_two = grad_branch_two.reshape(rows, width)
    layer_out = swap(layer_out.reshape(seqs, cluster, width))
    grad_second_gain, grad_second_shift, grad_reduce_bias = late_sums[0], late_sums[1], late_sums[2]
    grad_reduce = transpose_left(hidden, grad_branch_two)
    grad_hidden = transpose_right(grad_branch_two, reduce_full)
    grad_pre = (grad_hidden * slope.astype(f32)).astype(bf16)
    grad_pre = lax.optimization_barrier(grad_pre)
    grad_expand_bias = jnp.sum(grad_pre, axis=0, dtype=f32)
    grad_expand = transpose_left(middle_low, grad_pre)
    grad_middle = grad_resid_two + transpose_right(grad_pre, expand_full)
    grad_first_gain = jnp.sum(grad_middle * normed_one, axis=0)
    grad_first_shift = jnp.sum(grad_middle, axis=0)
    grad_resid_one = norm_back(grad_middle, normed_one, inverse_one, full[3])
    grad_branch_one = grad_resid_one.astype(bf16)
    grad_output_bias = jnp.sum(grad_branch_one, axis=0, dtype=f32)
    grad_output = transpose_left(context, grad_branch_one)
    grad_context = transpose_right(grad_branch_one, output_full).astype(bf16)
    vector_grads = jnp.concatenate(
        [
            grad_output_bias,
            grad_first_gain,
            grad_first_shift,
            grad_reduce_bias,
            grad_second_gain,
            grad_second_shift,
            grad_expand_bias,
        ]
    )
    lanes = -(-vector_grads.shape[0] // 1024) * 8
    vector_grads = jnp.pad(vector_grads, (0, lanes * 128 - vector_grads.shape[0])).reshape(lanes, 128)
    layer_out, grad_context = lax.optimization_barrier((layer_out, grad_context))
    token_grad, aw_grad, ow_grad, ew_grad, rw_grad, vec_sum, bias_sum = back(
        grad_context.reshape(chips, per, cluster, width),
        qs,
        ks,
        vs,
        ps,
        pos_all,
        x_all,
        attend_all,
        grad_resid_one.reshape(chips, per, cluster, width),
        grad_output.astype(bf16).reshape(depth, owners, -1, width),
        grad_expand.astype(bf16).reshape(depth, quarter, -1),
        grad_reduce.astype(bf16).reshape(depth, owners, -1, width),
        vector_grads,
        depth,
        heads,
    )
    z = lax.axis_index("batch")
    vec_sum = vec_sum.reshape(-1)
    six = lax.dynamic_slice_in_dim(vec_sum[: 6 * width].reshape(6, width), z * quarter, quarter, 1)
    up = vec_sum[6 * width :]
    tall = expand_bias.shape[0]
    up = lax.dynamic_slice_in_dim(up, z * tall, tall, 0)
    both = jnp.concatenate([bias_sum[0, 0], bias_sum[1, 0]]).reshape(2, 3, half)
    query_value = jnp.transpose(both, (1, 0, 2)).reshape(3, width)
    query_value = lax.dynamic_slice_in_dim(query_value, z * quarter, quarter, 1)
    return (
        layer_out,
        token_grad,
        aw_grad,
        query_value[0],
        query_value[2],
        ow_grad.reshape(quarter, width),
        six[0],
        six[1],
        six[2],
        ew_grad,
        up,
        rw_grad.reshape(-1, width),
        six[3],
        six[4],
        six[5],
    )


def layer(mesh):
    def run(*arrays):
        seqs, cluster, width = arrays[0].shape
        heads = arrays[14].shape[1]
        owners, depth = mesh.shape["seq"], mesh.shape["batch"]
        chips = owners // 2
        fits = (
            owners % 2 == 0
            and chips > 1
            and depth > 1
            and seqs % chips == 0
            and cluster == 128
            and heads % 4 == 0
            and width == heads * 64
            and cluster % (16 * owners) == 0
        )
        return (per_chip if fits else per_device)(*arrays)

    return run


def solution(mesh):
    in_specs = (
        P("batch", "seq", None),
        P("batch", None),
        P("batch"),
        P("batch"),
        P("batch", None),
        P("batch"),
        P("batch"),
        P("batch"),
        P("batch", None),
        P("batch"),
        P("batch", None),
        P("batch"),
        P("batch"),
        P("batch"),
        P("batch", None, "seq"),
        P("batch", None, "seq"),
        P("batch", "seq", None),
    )
    out_specs = (
        P("batch", "seq", None),
        P("batch", "seq", None),
        P("batch", None),
        P("batch"),
        P("batch"),
        P("batch", None),
        P("batch"),
        P("batch"),
        P("batch"),
        P("batch", None),
        P("batch"),
        P("batch", None),
        P("batch"),
        P("batch"),
        P("batch"),
    )
    return jax.shard_map(
        layer(mesh), mesh=mesh, in_specs=in_specs, out_specs=out_specs, check_vma=False
    )
```

```python
import functools
import math

import jax
import jax.numpy as jnp
from jax import lax
from jax.experimental import pallas as pl
from jax.experimental.pallas import tpu as pltpu
from jax.sharding import PartitionSpec as P

epsilon = 1e-05


def layer_norm(resid, gain, shift):
    center = jnp.mean(resid, axis=-1, keepdims=True)
    centered = resid - center
    spread = jnp.mean(centered * centered, axis=-1, keepdims=True)
    inverse = lax.rsqrt(spread + epsilon)
    normed = centered * inverse
    return (normed * gain + shift, normed, inverse)


def norm_back(upstream, normed, inverse, gain):
    scaled = upstream * gain
    first_mean = jnp.mean(scaled, axis=-1, keepdims=True)
    second_mean = jnp.mean(scaled * normed, axis=-1, keepdims=True)
    return inverse * (scaled - first_mean - normed * second_mean)


def gelu_slope(value):
    cumulative = 0.5 * (1.0 + lax.erf(value * 0.5**0.5))
    density = jnp.exp(-0.5 * value * value) * (2.0 * math.pi) ** (-0.5)
    return cumulative + value * density


def transpose_left(first, second):
    return lax.dot_general(
        first, second, (((0,), (0,)), ((), ())), preferred_element_type=jnp.float32
    )


def transpose_right(first, second):
    return lax.dot_general(
        first, second, (((1,), (1,)), ((), ())), preferred_element_type=jnp.float32
    )


def group_table(rank, cluster, owners):
    share = cluster // owners
    target = rank // cluster
    length = rank.shape[-1]
    places = lax.broadcasted_iota(jnp.int32, (length, length), 0)
    later = lax.broadcasted_iota(jnp.int32, (length, length), 1)
    before = (places < later)[None, None]
    same = target[..., :, None] == target[..., None, :]
    earlier = jnp.sum((same & before).astype(jnp.int32), axis=-2)
    position = target * share + earlier
    slots = lax.broadcasted_iota(jnp.int32, position.shape + (length,), 3)
    return (position[..., None] == slots).astype(jnp.bfloat16)


def sort_heads(rows, table, heads):
    seqs, length, width = rows.shape
    split = rows.reshape(seqs, length, heads, width // heads)
    moved = jnp.einsum("shtp,sthd->sphd", table, split, preferred_element_type=jnp.float32)
    return moved.astype(rows.dtype).reshape(seqs, length, width)


def unsort_heads(rows, table, heads):
    seqs, length, width = rows.shape
    split = rows.reshape(seqs, length, heads, width // heads)
    moved = jnp.einsum("shtp,sphd->sthd", table, split, preferred_element_type=jnp.float32)
    return moved.astype(rows.dtype).reshape(seqs, length, width)


def cluster_scores(queries, keys_rows, heads):
    items, length, width = queries.shape
    size = width // heads
    query_split = queries.reshape(items, length, heads, size)
    key_split = keys_rows.reshape(items, length, heads, size)
    scores = jnp.einsum(
        "sqhd,skhd->shqk", query_split, key_split, preferred_element_type=jnp.float32
    )
    return scores * size ** (-0.5)


def cluster_forward(queries, keys_rows, values_rows, heads):
    items, length, width = queries.shape
    scores = cluster_scores(queries, keys_rows, heads)
    top = jnp.max(scores, axis=-1, keepdims=True)
    weights = jnp.exp(scores - top)
    total = jnp.sum(weights, axis=-1, keepdims=True)
    probs = (weights / total).astype(jnp.bfloat16)
    value_split = values_rows.reshape(items, length, heads, width // heads)
    context = jnp.einsum("shqk,skhd->sqhd", probs, value_split, preferred_element_type=jnp.float32)
    return (
        context.reshape(items, length, width).astype(jnp.bfloat16),
        (top + jnp.log(total))[..., 0],
    )


def cluster_backward(scores, log_total, queries, keys_rows, values_rows, grad_context, heads):
    items, length, width = queries.shape
    size = width // heads
    query_split = queries.reshape(items, length, heads, size)
    key_split = keys_rows.reshape(items, length, heads, size)
    value_split = values_rows.reshape(items, length, heads, size)
    grad_split = grad_context.reshape(items, length, heads, size)
    probs = jnp.exp(scores - log_total[..., None])
    grad_probs = jnp.einsum(
        "sqhd,skhd->shqk", grad_split, value_split, preferred_element_type=jnp.float32
    )
    inner = jnp.sum(probs * grad_probs, axis=-1, keepdims=True)
    grad_scores = (probs * (grad_probs - inner)).astype(jnp.bfloat16)
    scale = size ** (-0.5)
    grad_query = (
        jnp.einsum("shqk,skhd->sqhd", grad_scores, key_split, preferred_element_type=jnp.float32)
        * scale
    )
    grad_key = (
        jnp.einsum("shqk,sqhd->skhd", grad_scores, query_split, preferred_element_type=jnp.float32)
        * scale
    )
    grad_value = jnp.einsum(
        "shqk,sqhd->skhd",
        probs.astype(jnp.bfloat16),
        grad_split,
        preferred_element_type=jnp.float32,
    )
    shape = (items, length, width)
    return (
        grad_query.reshape(shape).astype(jnp.bfloat16),
        grad_key.reshape(shape).astype(jnp.bfloat16),
        grad_value.reshape(shape).astype(jnp.bfloat16),
    )


def send_context(context):
    return lax.all_to_all(context, "seq", split_axis=1, concat_axis=1, tiled=True)


def send_grads(grads):
    return (
        lax.all_to_all(grads[0], "seq", split_axis=1, concat_axis=1, tiled=True),
        lax.all_to_all(grads[1], "seq", split_axis=1, concat_axis=1, tiled=True),
        lax.all_to_all(grads[2], "seq", split_axis=1, concat_axis=1, tiled=True),
    )


def make_step(left, pieces):
    total = jnp.dot(left, pieces[0], preferred_element_type=jnp.float32)
    stored = tuple(pieces[1:]) + ()
    placed = tuple((piece for piece in stored))
    return (total,) + placed


def make_hidden_step(before, pieces):
    section = before + pieces[1].astype(jnp.float32)
    activated = jax.nn.gelu(section, approximate=False).astype(jnp.bfloat16)
    total = jnp.dot(activated, pieces[0], preferred_element_type=jnp.float32)
    stored = ()
    return (total, section, activated) + stored


def per_device(
    tokens,
    attend_weight,
    query_bias,
    value_bias,
    output_weight,
    output_bias,
    first_gain,
    first_shift,
    expand_weight,
    expand_bias,
    reduce_weight,
    reduce_bias,
    second_gain,
    second_shift,
    query_rank,
    key_rank,
    cotangent,
):
    seqs, cluster, width = tokens.shape
    heads = query_rank.shape[1]
    rows = seqs * cluster
    owners = lax.axis_size("seq")
    flat = tokens.reshape(rows, width)
    attend_out = make_step(
        flat,
        (
            lax.all_gather(attend_weight, "batch", axis=0, tiled=True),
            lax.all_gather(query_bias, "batch", axis=0, tiled=True),
            lax.all_gather(value_bias, "batch", axis=0, tiled=True),
        ),
    )
    summed = attend_out[0]
    queries = (summed[:, :width] + attend_out[1].astype(jnp.float32)).astype(jnp.bfloat16)
    keys_rows = summed[:, width : 2 * width].astype(jnp.bfloat16)
    values_rows = (summed[:, 2 * width :] + attend_out[2].astype(jnp.float32)).astype(jnp.bfloat16)
    query_table = group_table(query_rank, cluster, owners)
    key_table = group_table(key_rank, cluster, owners)
    query_sorted = sort_heads(queries.reshape(seqs, cluster, width), query_table, heads)
    key_sorted = sort_heads(keys_rows.reshape(seqs, cluster, width), key_table, heads)
    value_sorted = sort_heads(values_rows.reshape(seqs, cluster, width), key_table, heads)
    received = (
        lax.all_to_all(query_sorted, "seq", split_axis=1, concat_axis=1, tiled=True),
        lax.all_to_all(key_sorted, "seq", split_axis=1, concat_axis=1, tiled=True),
        lax.all_to_all(value_sorted, "seq", split_axis=1, concat_axis=1, tiled=True),
    )
    context, log_total = cluster_forward(received[0], received[1], received[2], heads)
    forward_out = (send_context(context), log_total, received[0], received[1], received[2])
    context_rows = unsort_heads(forward_out[0], query_table, heads).reshape(rows, width)
    output_out = make_step(
        context_rows,
        (
            lax.all_gather(output_weight, "batch", axis=0, tiled=True),
            lax.all_gather(output_bias, "batch", axis=0, tiled=True),
            lax.all_gather(first_gain, "batch", axis=0, tiled=True),
            lax.all_gather(first_shift, "batch", axis=0, tiled=True),
        ),
    )
    resid_one = flat.astype(jnp.float32) + output_out[0] + output_out[1].astype(jnp.float32)
    gain_one = output_out[2].astype(jnp.float32)
    middle, normed_one, inverse_one = layer_norm(
        resid_one, gain_one, output_out[3].astype(jnp.float32)
    )
    middle_low = middle.astype(jnp.bfloat16)
    expand_out = make_step(
        middle_low,
        (
            lax.all_gather(expand_weight, "batch", axis=0, tiled=True),
            lax.all_gather(reduce_bias, "batch", axis=0, tiled=True),
            lax.all_gather(second_gain, "batch", axis=0, tiled=True),
            lax.all_gather(second_shift, "batch", axis=0, tiled=True),
        ),
    )
    hidden_out = make_hidden_step(
        expand_out[0],
        (
            lax.all_gather(reduce_weight, "batch", axis=0, tiled=True),
            lax.all_gather(expand_bias, "batch", axis=0, tiled=True),
        ),
    )
    pre_full, hidden_full = (hidden_out[1], hidden_out[2])
    resid_two = middle + hidden_out[0] + expand_out[1].astype(jnp.float32)
    gain_two = expand_out[2].astype(jnp.float32)
    final, normed_two, inverse_two = layer_norm(
        resid_two, gain_two, expand_out[3].astype(jnp.float32)
    )
    layer_out = final.astype(jnp.bfloat16).reshape(seqs, cluster, width)
    attend_full, output_full, expand_full, reduce_full = (
        lax.all_gather(attend_weight, "batch", axis=0, tiled=True),
        lax.all_gather(output_weight, "batch", axis=0, tiled=True),
        lax.all_gather(expand_weight, "batch", axis=0, tiled=True),
        lax.all_gather(reduce_weight, "batch", axis=0, tiled=True),
    )
    upstream = cotangent.reshape(rows, width).astype(jnp.float32)
    grad_second_gain = jnp.sum(upstream * normed_two, axis=0)
    grad_second_shift = jnp.sum(upstream, axis=0)
    grad_resid_two = norm_back(upstream, normed_two, inverse_two, gain_two)
    grad_branch_two = grad_resid_two.astype(jnp.bfloat16)
    grad_reduce_bias = jnp.sum(grad_branch_two, axis=0, dtype=jnp.float32)
    grad_reduce = transpose_left(hidden_full, grad_branch_two)
    grad_hidden = transpose_right(grad_branch_two, reduce_full)
    grad_pre = (grad_hidden * gelu_slope(pre_full)).astype(jnp.bfloat16)
    grad_expand_bias = jnp.sum(grad_pre, axis=0, dtype=jnp.float32)
    grad_expand = transpose_left(middle_low, grad_pre)
    grad_middle = grad_resid_two + transpose_right(grad_pre, expand_full)
    grad_first_gain = jnp.sum(grad_middle * normed_one, axis=0)
    grad_first_shift = jnp.sum(grad_middle, axis=0)
    grad_resid_one = norm_back(grad_middle, normed_one, inverse_one, gain_one)
    grad_branch_one = grad_resid_one.astype(jnp.bfloat16)
    grad_output_bias = jnp.sum(grad_branch_one, axis=0, dtype=jnp.float32)
    grad_output = transpose_left(context_rows, grad_branch_one)
    grad_context = transpose_right(grad_branch_one, output_full).astype(jnp.bfloat16)
    grad_sorted = sort_heads(grad_context.reshape(seqs, cluster, width), query_table, heads)
    grad_received = lax.all_to_all(grad_sorted, "seq", split_axis=1, concat_axis=1, tiled=True)
    kept_scores = cluster_scores(forward_out[2], forward_out[3], heads)
    home = send_grads(
        cluster_backward(
            kept_scores,
            forward_out[1],
            forward_out[2],
            forward_out[3],
            forward_out[4],
            grad_received,
            heads,
        )
    )
    grad_queries = unsort_heads(home[0], query_table, heads).reshape(rows, width)
    grad_keys = unsort_heads(home[1], key_table, heads).reshape(rows, width)
    grad_values = unsort_heads(home[2], key_table, heads).reshape(rows, width)
    grad_mixed = jnp.concatenate([grad_queries, grad_keys, grad_values], axis=1)
    grad_query_bias = jnp.sum(grad_queries, axis=0, dtype=jnp.float32)
    grad_value_bias = jnp.sum(grad_values, axis=0, dtype=jnp.float32)
    grad_attend = transpose_left(flat, grad_mixed)
    token_grad = (
        (grad_resid_one + transpose_right(grad_mixed, attend_full))
        .astype(jnp.bfloat16)
        .reshape(seqs, cluster, width)
    )
    owned = (
        lax.psum_scatter(
            grad_attend.astype(jnp.bfloat16), "batch", scatter_dimension=0, tiled=True
        ).astype(jnp.float32),
        lax.psum_scatter(
            grad_query_bias.astype(jnp.bfloat16), "batch", scatter_dimension=0, tiled=True
        ).astype(jnp.float32),
        lax.psum_scatter(
            grad_value_bias.astype(jnp.bfloat16), "batch", scatter_dimension=0, tiled=True
        ).astype(jnp.float32),
        lax.psum_scatter(
            grad_output.astype(jnp.bfloat16), "batch", scatter_dimension=0, tiled=True
        ).astype(jnp.float32),
        lax.psum_scatter(
            grad_output_bias.astype(jnp.bfloat16), "batch", scatter_dimension=0, tiled=True
        ).astype(jnp.float32),
        lax.psum_scatter(
            grad_first_gain.astype(jnp.bfloat16), "batch", scatter_dimension=0, tiled=True
        ).astype(jnp.float32),
        lax.psum_scatter(
            grad_first_shift.astype(jnp.bfloat16), "batch", scatter_dimension=0, tiled=True
        ).astype(jnp.float32),
        lax.psum_scatter(
            grad_expand.astype(jnp.bfloat16), "batch", scatter_dimension=0, tiled=True
        ).astype(jnp.float32),
        lax.psum_scatter(
            grad_expand_bias.astype(jnp.bfloat16), "batch", scatter_dimension=0, tiled=True
        ).astype(jnp.float32),
        lax.psum_scatter(
            grad_reduce.astype(jnp.bfloat16), "batch", scatter_dimension=0, tiled=True
        ).astype(jnp.float32),
        lax.psum_scatter(
            grad_reduce_bias.astype(jnp.bfloat16), "batch", scatter_dimension=0, tiled=True
        ).astype(jnp.float32),
        lax.psum_scatter(
            grad_second_gain.astype(jnp.bfloat16), "batch", scatter_dimension=0, tiled=True
        ).astype(jnp.float32),
        lax.psum_scatter(
            grad_second_shift.astype(jnp.bfloat16), "batch", scatter_dimension=0, tiled=True
        ).astype(jnp.float32),
    )
    shared = (
        lax.psum(owned[0].astype(jnp.bfloat16), "seq").astype(jnp.float32),
        lax.psum(owned[1].astype(jnp.bfloat16), "seq").astype(jnp.float32),
        lax.psum(owned[2].astype(jnp.bfloat16), "seq").astype(jnp.float32),
        lax.psum(owned[3].astype(jnp.bfloat16), "seq").astype(jnp.float32),
        lax.psum(owned[4].astype(jnp.bfloat16), "seq").astype(jnp.float32),
        lax.psum(owned[5].astype(jnp.bfloat16), "seq").astype(jnp.float32),
        lax.psum(owned[6].astype(jnp.bfloat16), "seq").astype(jnp.float32),
        lax.psum(owned[7].astype(jnp.bfloat16), "seq").astype(jnp.float32),
        lax.psum(owned[8].astype(jnp.bfloat16), "seq").astype(jnp.float32),
        lax.psum(owned[9].astype(jnp.bfloat16), "seq").astype(jnp.float32),
        lax.psum(owned[10].astype(jnp.bfloat16), "seq").astype(jnp.float32),
        lax.psum(owned[11].astype(jnp.bfloat16), "seq").astype(jnp.float32),
        lax.psum(owned[12].astype(jnp.bfloat16), "seq").astype(jnp.float32),
    )
    return (
        layer_out,
        token_grad,
        shared[0],
        shared[1],
        shared[2],
        shared[3],
        shared[4],
        shared[5],
        shared[6],
        shared[7],
        shared[8],
        shared[9],
        shared[10],
        shared[11],
        shared[12],
    )


MESH = pl.DeviceIdType.MESH
f32 = jnp.float32
bf16 = jnp.bfloat16


class Place:
    def __init__(self, chips, depth):
        self.chips, self.depth = chips, depth
        self.z = lax.axis_index("batch")
        spot = lax.axis_index("seq")
        self.chip, self.core = lax.div(spot, 2), lax.rem(spot, 2)

    def chip_at(self, k):
        return lax.rem(self.chip + k + self.chips, self.chips)

    def z_at(self, k):
        return lax.rem(self.z + k + self.depth, self.depth)

    def plane(self, k):
        return (self.z, self.chip_at(k) * 2 + self.core)

    def tower(self, k):
        return (self.z_at(k), self.chip * 2 + self.core)

    def sibling(self):
        return (self.z, self.chip * 2 + 1 - self.core)

    def greet(self):
        bell = pltpu.get_barrier_semaphore()
        others = [self.plane(k) for k in range(1, self.chips)]
        others += [self.tower(k) for k in range(1, self.depth)]
        others.append(self.sibling())
        for other in others:
            pl.semaphore_signal(bell, inc=1, device_id=other, device_id_type=MESH)
        pl.semaphore_wait(bell, len(others))


def far_copy(src, dst, sems, at, device):
    return pltpu.make_async_remote_copy(
        src_ref=src,
        dst_ref=dst,
        send_sem=sems[0].at[at],
        recv_sem=sems[1].at[at],
        device_id=device,
        device_id_type=MESH,
    )


def one_hot(row, slots):
    return jnp.where(slots == row, 1.0, 0.0).astype(bf16)


def split_lanes(tile, low):
    zero = jnp.zeros_like(tile)
    return jnp.where(low, tile, zero), jnp.where(low, zero, tile)


def stack_lanes(tile, low):
    first, second = split_lanes(tile, low)
    return jnp.concatenate([first, second], axis=0)


def dot_rows(a, b):
    return jnp.dot(a, b, preferred_element_type=f32)


def dot_lanes(a, b):
    return lax.dot_general(a, b, (((1,), (1,)), ((), ())), preferred_element_type=f32)


def dot_first(a, b):
    return lax.dot_general(a, b, (((0,), (0,)), ((), ())), preferred_element_type=f32)


def multiple(value, by):
    return pl.multiple_of(value, by)


def forward_kernel(
    chips,
    depth,
    heads,
    tok_ref,
    pos_ref,
    aw_ref,
    vec_ref,
    ow_ref,
    ew_ref,
    rw_ref,
    cot_ref,
    x_out,
    ctx_out,
    q_out,
    k_out,
    v_out,
    p_out,
    pos_out,
    aw_out,
    vec_out,
    ow_out,
    ew_out,
    rw_out,
    n1_out,
    inv_out,
    ml_out,
    hid_out,
    slope_out,
    lo_out,
    gr_out,
    gb_out,
    sum_out,
    xbuf,
    posbuf,
    wbuf,
    vbuf,
    bias,
    ctxb,
    ctxt,
    owbuf,
    ewbuf,
    rwbuf,
    cbuf,
    n1buf,
    invbuf,
    mlbuf,
    vecs,
    upb,
    sums,
    tok_s,
    tok_r,
    tokc_s,
    tokc_r,
    pos_s,
    pos_r,
    posc_s,
    posc_r,
    aw_s,
    aw_r,
    awc_s,
    awc_r,
    vec_s,
    vec_r,
    wz_s,
    wz_r,
    wp_s,
    wp_r,
    wc_s,
    wc_r,
    ctx_s,
    ctx_r,
    cot_s,
    cot_r,
    oc_s,
    oc_r,
    loc,
    out_sem,
    slope_sem,
    att_sem,
):
    me = Place(chips, depth)
    z, chip, core = me.z, me.chip, me.core
    per = tok_ref.shape[0] // chips
    half = aw_ref.shape[1] // 6
    rows_z = aw_ref.shape[0]
    pairs = heads // 4
    size = half // (2 * pairs)
    me.greet()

    def aw_copy(k, part):
        columns = pl.ds(multiple(part * 2 * half + core * half, 128), half)
        return far_copy(
            aw_ref.at[:, columns],
            wbuf.at[pl.ds(multiple(z * rows_z, 8), rows_z), pl.ds(part * half, half)],
            (aw_s, aw_r),
            (k - 1) * 3 + part,
            me.tower(k),
        )

    def mine(ref, target):
        return ref.at[pl.ds(target * per, per)]

    def tok_copy(k):
        return far_copy(
            mine(tok_ref, me.chip_at(k)), xbuf.at[core, chip], (tok_s, tok_r), k - 1, me.plane(k)
        )

    def pos_copy(k):
        return far_copy(
            mine(pos_ref, me.chip_at(k)), posbuf.at[core, chip], (pos_s, pos_r), k - 1, me.plane(k)
        )

    def vec_copy(k):
        return far_copy(vec_ref, vbuf.at[z], (vec_s, vec_r), k - 1, me.tower(k))

    sends = []
    for k in range(1, chips):
        sends.append(pos_copy(k))
        sends[-1].start()
    for k in range(1, depth):
        sends.append(vec_copy(k))
        sends[-1].start()
    for k in range(1, max(chips, depth)):
        if k < depth:
            for part in range(3):
                sends.append(aw_copy(k, part))
                sends[-1].start()
        if k < chips:
            sends.append(tok_copy(k))
            sends[-1].start()
    local = []

    def keep(src, dst):
        copy = pltpu.make_async_copy(src, dst, loc.at[len(local)])
        copy.start()
        local.append(copy)

    keep(mine(tok_ref, chip), xbuf.at[core, chip])
    keep(mine(pos_ref, chip), posbuf.at[core, chip])
    keep(vec_ref, vbuf.at[z])
    for part in range(3):
        keep(
            aw_ref.at[:, pl.ds(multiple(part * 2 * half + core * half, 128), half)],
            wbuf.at[pl.ds(multiple(z * rows_z, 8), rows_z), pl.ds(part * half, half)],
        )
    wide = ew_ref.shape[1] // (2 * chips)
    tall = rw_ref.shape[0] // (2 * chips)
    mid_rows = rows_z // 2
    mine_at = core * chips + chip

    def piece(kind):
        if kind == 0:
            return ow_ref.at[pl.ds(multiple(core * mid_rows, 8), mid_rows)]
        if kind == 1:
            return ew_ref.at[:, pl.ds(multiple(mine_at * wide, 128), wide)]
        return rw_ref.at[pl.ds(multiple(mine_at * tall, 8), tall)]

    def place(kind, zz):
        if kind == 0:
            return owbuf.at[zz, core]
        if kind == 1:
            return ewbuf.at[zz, :, pl.ds(multiple(mine_at * wide, 128), wide)]
        return rwbuf.at[zz, mine_at]

    def place_all(kind, at):
        if kind == 1:
            return ewbuf.at[:, :, pl.ds(multiple(at * wide, 128), wide)]
        return rwbuf.at[:, at]

    for kind in range(3):
        keep(piece(kind), place(kind, z))

    def wz_copy(kind, k):
        return far_copy(
            piece(kind),
            place(kind, z),
            (wz_s, wz_r),
            kind * (depth - 1) + k - 1,
            me.tower(k),
        )

    def wp_copy(kind, k, origin):
        at = core * chips + origin
        return far_copy(
            place_all(kind, at),
            place_all(kind, at),
            (wp_s, wp_r),
            (kind - 1) * (chips - 1) + k - 1,
            me.plane(k),
        )

    def wc_copy(kind, origin_k):
        at = core * chips + me.chip_at(origin_k)
        return far_copy(
            place_all(kind, at),
            place_all(kind, at),
            (wc_s, wc_r),
            (kind - 1) * chips + origin_k,
            me.sibling(),
        )

    def oc_copy():
        spot = owbuf.at[:, core]
        return far_copy(spot, spot, (oc_s, oc_r), 0, me.sibling())

    def cot_copy(k):
        return far_copy(
            mine(cot_ref, me.chip_at(k)), cbuf.at[chip], (cot_s, cot_r), k - 1, me.plane(k)
        )

    keep(mine(cot_ref, chip), cbuf.at[chip])

    for copy in local[:2]:
        copy.wait()

    def tokc_copy(k):
        source = me.chip_at(-k)
        return far_copy(
            xbuf.at[core, source], xbuf.at[core, source], (tokc_s, tokc_r), k, me.sibling()
        )

    def posc_copy(k):
        source = me.chip_at(-k)
        return far_copy(
            posbuf.at[core, source], posbuf.at[core, source], (posc_s, posc_r), k, me.sibling()
        )

    for k in range(chips):
        if k:
            pos_copy(k).wait_recv()
            tok_copy(k).wait_recv()
        for copy in (posc_copy(k), tokc_copy(k)):
            copy.start()
            sends.append(copy)
    for k in range(1, chips):
        cot_copy(k).start()
        sends.append(cot_copy(k))
    for copy in local[2:6]:
        copy.wait()
    for k in range(1, depth):
        vec_copy(k).wait_recv()
        for part in range(3):
            aw_copy(k, part).wait_recv()
    for k in range(1, depth):
        wz_copy(1, k).start()
        for kind in range(3):
            sends.append(wz_copy(kind, k))
    for k in range(chips):
        posc_copy(k).wait_recv()
        tokc_copy(k).wait_recv()
    for copy in local[6:]:
        copy.wait()

    outs = []

    def emit(src, dst):
        copy = pltpu.make_async_copy(src, dst, out_sem.at[len(outs)])
        copy.start()
        outs.append(copy)

    emit(xbuf, x_out)
    emit(posbuf, pos_out)
    emit(wbuf, aw_out.at[core])
    awc = far_copy(wbuf, aw_out.at[core], (awc_s, awc_r), 0, me.sibling())
    awc.start()
    sends.append(awc)

    quarter = rows_z
    for zz in range(depth):
        begin = zz * quarter
        for row, at in ((0, 0), (1, 2)):
            for side in range(2):
                lo = max(begin, side * half)
                hi = min(begin + quarter, (side + 1) * half)
                if lo < hi:
                    bias[side, 0:1, at * half + lo - side * half : at * half + hi - side * half] = (
                        vbuf[zz, row : row + 1, lo - begin : hi - begin]
                    )
    bias[0, 0:1, half : 2 * half] = jnp.zeros((1, half), f32)
    bias[1, 0:1, half : 2 * half] = jnp.zeros((1, half), f32)
    added = bias[core, 0:1, :]
    for zz in range(depth):
        for row in range(8):
            vecs[row : row + 1, zz * quarter : (zz + 1) * quarter] = vbuf[
                zz, row : row + 1, :quarter
            ]
        steps = upb.shape[1] // (depth * quarter)
        for row in range(steps):
            to = (zz * steps + row) * quarter
            upb[0:1, to : to + quarter] = vbuf[zz, 8 + row : 9 + row, :quarter]

    cluster = tok_ref.shape[1]
    blocks = 2 * chips
    share = cluster // blocks
    width = tok_ref.shape[2]

    slots = lax.broadcasted_iota(jnp.int32, (cluster, cluster), 0)
    low = lax.broadcasted_iota(jnp.int32, (cluster, 128), 1) < size
    scale = size ** (-0.5)

    def tables(jj, i, pair, part):
        first = part * heads + core * (heads // 2) + 2 * pair
        rows = [
            one_hot(posbuf[jj // chips, jj % chips, i, pl.ds(first + h, 1), :], slots)
            for h in range(2)
        ]
        return rows

    def plane_stage(kind):
        for k in range(1, depth):
            wz_copy(kind, k).wait_recv()
        for k in range(1, chips):
            wp_copy(kind, k, chip).start()
        wc_copy(kind, 0).start()

    def hook(i, pair):
        @pl.when((i == 0) & (pair == 0))
        def _():
            plane_stage(1)
            for k in range(1, depth):
                wz_copy(2, k).start()
            for k in range(1, depth):
                wz_copy(0, k).start()

        @pl.when((i == min(1, per - 1)) & (pair == pairs - 1))
        def _():
            plane_stage(2)
            for k in range(1, depth):
                wz_copy(0, k).wait_recv()
            oc_copy().start()

    def attention(qkv, qs, ks, vs, ps, os):
        @pl.loop(0, blocks)
        def _(jj):
            x = xbuf[lax.div(jj, chips), lax.rem(jj, chips)].reshape(per * cluster, width)
            mixed = (dot_rows(x, wbuf[...]) + added).astype(bf16)
            for at in range(3 * pairs):
                qkv[at, jj] = mixed[:, at * 128 : (at + 1) * 128].reshape(per, cluster, 128)

        @pl.loop(0, per)
        def _(i):
            @pl.loop(0, pairs)
            def _(pair):
                at = i * pairs + pair
                for jj in range(blocks):
                    tq = jnp.concatenate(tables(jj, i, pair, 0), axis=1)
                    tk = jnp.concatenate(tables(jj, i, pair, 1), axis=1)
                    q = stack_lanes(qkv[pair, jj, i], low)
                    k = stack_lanes(qkv[pairs + pair, jj, i], low)
                    v = stack_lanes(qkv[2 * pairs + pair, jj, i], low)
                    span = slice(jj * share, (jj + 1) * share)
                    sq = dot_rows(tq, q).astype(bf16)
                    skv = dot_rows(tk, jnp.concatenate([k, v], axis=1)).astype(bf16)
                    qs[at, :, span, :] = sq.reshape(blocks, share, 128)
                    ks[at, :, span, :] = skv[:, :128].reshape(blocks, share, 128)
                    vs[at, :, span, :] = skv[:, 128:].reshape(blocks, share, 128)
                for c in range(blocks):
                    scores = dot_lanes(qs[at, c], stack_lanes(ks[at, c], low)) * scale
                    halves = []
                    for h in range(2):
                        s = scores[:, h * cluster : (h + 1) * cluster]
                        e = jnp.exp(s - jnp.max(s, axis=1, keepdims=True))
                        halves.append((e / jnp.sum(e, axis=1, keepdims=True)).astype(bf16))
                    probs = jnp.concatenate(halves, axis=1)
                    ps[at, c] = probs
                    o = dot_rows(probs, stack_lanes(vs[at, c], low)).astype(bf16)
                    os[c] = o
                for jj in range(blocks):
                    tq = jnp.concatenate(tables(jj, i, pair, 0), axis=0)
                    rows = os[:, jj * share : (jj + 1) * share, :].reshape(cluster, 128)
                    back = dot_first(tq, stack_lanes(rows, low)).astype(bf16)
                    ctxb[jj // chips, jj % chips, i, :, pl.ds(multiple(pair * 128, 128), 128)] = back
                hook(i, pair)

        pieces = ((qs, q_out), (ks, k_out), (vs, v_out), (ps, p_out))
        copies = [
            pltpu.make_async_copy(src, dst, att_sem.at[n]) for n, (src, dst) in enumerate(pieces)
        ]
        far, own = ctx_copies()
        for copy in copies + [far, own]:
            copy.start()
        for copy in copies + [far, own]:
            copy.wait()

    def ctx_copies():
        lanes = pl.ds(multiple(core * half, 128), half)
        far = far_copy(
            ctxb.at[1 - core], ctxt.at[:, :, :, lanes], (ctx_s, ctx_r), 0, me.sibling()
        )
        own = pltpu.make_async_copy(ctxb.at[core], ctxt.at[:, :, :, lanes], att_sem.at[4])
        return far, own

    group = (per * pairs, blocks, cluster, 128)
    pl.run_scoped(
        attention,
        pltpu.VMEM((3 * pairs, blocks, per, cluster, 128), bf16),
        pltpu.VMEM(group, bf16),
        pltpu.VMEM(group, bf16),
        pltpu.VMEM(group, bf16),
        pltpu.VMEM((per * pairs, blocks, cluster, 2 * cluster), bf16),
        pltpu.VMEM((blocks, cluster, 128), bf16),
    )

    def from_plane(kind):
        for k in range(1, chips):
            wp_copy(kind, k, me.chip_at(-k)).wait_recv()
            wc_copy(kind, chips - k).start()

    def from_sibling(kind):
        for k in range(chips):
            wc_copy(kind, k).wait()
        for k in range(1, chips):
            wp_copy(kind, k, chip).wait_send()

    oc_copy().wait()
    from_plane(1)
    from_sibling(1)
    emit(ctxt, ctx_out)
    emit(owbuf, ow_out)
    emit(ewbuf, ew_out)
    tile = per * cluster
    hidden = upb.shape[1]
    eps = epsilon

    def moments(rows):
        center = jnp.mean(rows, axis=1, keepdims=True)
        centered = rows - center
        spread = jnp.mean(centered * centered, axis=1, keepdims=True)
        inverse = lax.rsqrt(spread + eps)
        return centered * inverse, inverse

    def slope_out_copy(j, slot):
        return pltpu.make_async_copy(sbuf.at[slot], slope_out.at[j], slope_sem.at[slot])

    def vec(row):
        return vecs[row : row + 1, :]

    def feed(hbuf, sbuf):
        def slope_copy(j, slot):
            return pltpu.make_async_copy(sbuf.at[slot], slope_out.at[j], slope_sem.at[slot])

        @pl.loop(0, chips)
        def _(j):
            slot = lax.rem(j, 2)

            @pl.when(j >= 2)
            def _():
                slope_copy(j - 2, slot).wait()

            rows = ctxt[j].reshape(tile, width)
            branch = dot_rows(rows, owbuf[...].reshape(width, width))
            resid = xbuf[core, j].reshape(tile, width).astype(f32) + branch + vec(2)
            normed, inverse = moments(resid)
            n1buf[j] = normed
            invbuf[j] = jnp.broadcast_to(inverse, (tile, 128))
            mlbuf[j] = (normed * vec(3) + vec(4)).astype(bf16)

            @pl.loop(0, hidden // 384)
            def _(n):
                lanes = pl.ds(multiple(n * 384, 128), 384)
                weight = ewbuf[:, :, lanes].reshape(width, 384)
                pre = dot_rows(mlbuf[j], weight) + upb[0:1, lanes]
                cumulative = 0.5 * (1.0 + lax.erf(pre * 0.5**0.5))
                density = jnp.exp(-0.5 * pre * pre) * (2.0 * math.pi) ** (-0.5)
                hbuf[j, :, lanes] = (pre * cumulative).astype(bf16)
                sbuf[slot, :, lanes] = (cumulative + pre * density).astype(bf16)

            slope_copy(j, slot).start()

        emit(vecs, vec_out)
        emit(n1buf, n1_out)
        emit(invbuf, inv_out)
        emit(mlbuf, ml_out)
        emit(hbuf, hid_out)
        from_plane(2)
        from_sibling(2)
        emit(rwbuf, rw_out)
        for copy in sends:
            copy.wait_send()
        for k in range(1, chips):
            cot_copy(k).wait_recv()
        for j in range(max(chips - 2, 0), chips):
            slope_copy(j, j % 2).wait()
        for copy in outs:
            copy.wait()
        sums[...] = jnp.zeros_like(sums)

        @pl.loop(0, chips)
        def _(j):
            branch = vec(5)
            for zz in range(depth):
                span = hidden // depth
                branch = branch + dot_rows(
                    hbuf[j, :, zz * span : (zz + 1) * span], rwbuf[zz].reshape(span, width)
                )
            middle = n1buf[j] * vec(3) + vec(4)
            normed, inverse = moments(middle + branch)
            upstream = cbuf[j].reshape(tile, width).astype(f32)
            cbuf[j] = (normed * vec(6) + vec(7)).astype(bf16).reshape(per, cluster, width)
            sums[0:1, :] += jnp.sum(upstream * normed, axis=0, keepdims=True)
            sums[1:2, :] += jnp.sum(upstream, axis=0, keepdims=True)
            scaled = upstream * vec(6)
            first = jnp.mean(scaled, axis=1, keepdims=True)
            second = jnp.mean(scaled * normed, axis=1, keepdims=True)
            grad = inverse * (scaled - first - normed * second)
            n1buf[j] = grad
            low_grad = grad.astype(bf16)
            sums[2:3, :] += jnp.sum(low_grad.astype(f32), axis=0, keepdims=True)
            ctxt[j] = low_grad.reshape(per, cluster, width)

        done = len(outs)
        emit(cbuf, lo_out)
        emit(n1buf, gr_out)
        emit(ctxt, gb_out)
        emit(sums, sum_out)
        awc.wait_recv()
        for copy in outs[done:]:
            copy.wait()

    pl.run_scoped(
        feed,
        pltpu.VMEM((chips, tile, hidden), bf16),
        pltpu.VMEM((2, tile, hidden), bf16),
    )


def forward(
    tokens,
    pos,
    attend_weight,
    vectors,
    output_weight,
    expand_weight,
    reduce_weight,
    cotangent,
    chips,
    depth,
    heads,
):
    seqs, cluster, width = tokens.shape
    per, blocks, pairs = seqs // chips, 2 * chips, heads // 4
    half = width // 2
    rows_z = attend_weight.shape[0]
    hidden = expand_weight.shape[1]
    items = per * pairs
    tile = per * cluster
    dma = pltpu.SemaphoreType.DMA
    anywhere = pl.BlockSpec(memory_space=pl.ANY)
    tall = reduce_weight.shape[0] // blocks
    shapes = [
        ((2, chips, per, cluster, width), bf16),
        ((chips, per, cluster, width), bf16),
        ((items, blocks, cluster, 128), bf16),
        ((items, blocks, cluster, 128), bf16),
        ((items, blocks, cluster, 128), bf16),
        ((items, blocks, cluster, 2 * cluster), bf16),
        ((2, chips, per, 2 * heads, cluster), jnp.int32),
        ((2, depth * rows_z, 3 * half), bf16),
        ((8, width), f32),
        ((depth, 2, rows_z // 2, width), bf16),
        ((depth, rows_z, hidden), bf16),
        ((depth, blocks, tall, width), bf16),
        ((chips, tile, width), f32),
        ((chips, tile, 128), f32),
        ((chips, tile, width), bf16),
        ((chips, tile, hidden), bf16),
        ((chips, tile, hidden), bf16),
        ((chips, per, cluster, width), bf16),
        ((chips, tile, width), f32),
        ((chips, per, cluster, width), bf16),
        ((8, width), f32),
    ]
    t, c = depth - 1, chips - 1
    vm = pltpu.VMEM
    return pl.pallas_call(
        functools.partial(forward_kernel, chips, depth, heads),
        out_shape=[jax.ShapeDtypeStruct(*s) for s in shapes],
        in_specs=[anywhere] * 8,
        out_specs=[anywhere] * len(shapes),
        scratch_shapes=[
            vm(shapes[0][0], bf16),
            vm(shapes[6][0], jnp.int32),
            vm(shapes[7][0][1:], bf16),
            vm((depth,) + vectors.shape, f32),
            vm((2, 8, 3 * half), f32),
            vm((2, chips, per, cluster, half), bf16),
            vm(shapes[1][0], bf16),
            vm(shapes[9][0], bf16),
            vm(shapes[10][0], bf16),
            vm(shapes[11][0], bf16),
            vm(shapes[17][0], bf16),
            vm(shapes[12][0], f32),
            vm(shapes[13][0], f32),
            vm(shapes[14][0], bf16),
            vm((8, width), f32),
            vm((8, hidden), f32),
            vm((8, width), f32),
            dma((c,)), dma((c,)), dma((chips,)), dma((chips,)),
            dma((c,)), dma((c,)), dma((chips,)), dma((chips,)),
            dma((3 * t,)), dma((3 * t,)), dma((1,)), dma((1,)),
            dma((t,)), dma((t,)),
            dma((3 * t,)), dma((3 * t,)),
            dma((2 * c,)), dma((2 * c,)),
            dma((2 * chips,)), dma((2 * chips,)),
            dma((1,)), dma((1,)),
            dma((c,)), dma((c,)),
            dma((1,)), dma((1,)),
            dma((12,)), dma((24,)), dma((2,)), dma((5,)),
        ],
        compiler_params=pltpu.CompilerParams(
            collective_id=1, has_side_effects=True, vmem_limit_bytes=63 * 2**20
        ),
        name="forward",
    )(
        tokens,
        pos,
        attend_weight,
        vectors,
        output_weight,
        expand_weight,
        reduce_weight,
        cotangent,
    )


def add_into(target, at, parts):
    total = target[at].astype(f32)
    for part in parts:
        total = total + part.astype(f32)
    target[at] = total.astype(target.dtype)


class Reducer:
    def __init__(self, me, own, other, near, mid, last, done, sems, tower_first):
        self.me, self.own, self.other = me, own, other
        self.near, self.mid, self.last, self.done = near, mid, last, done
        (self.near_s, self.near_r, self.mid_s, self.mid_r, self.last_s, self.last_r) = sems[:6]
        (self.back_s, self.back_r, self.side_s, self.side_r) = sems[6:10]
        self.tower_first = tower_first
        self.sizes = (mid.shape[0] + 1, last.shape[0] + 1)

    def spot(self, axis, k):
        me = self.me
        if self.tower_first == (axis == 0):
            return me.z_at(k), me.tower(k)
        return me.chip_at(k), me.plane(k)

    def near_copy(self, a):
        return far_copy(
            self.other.at[a], self.near.at[a], (self.near_s, self.near_r), a, self.me.sibling()
        )

    def fold_near(self, a):
        self.near_copy(a).wait_recv()
        for b in range(self.sizes[1]):
            add_into(self.own, (a, b), [self.near[a, b]])

    def mid_copy(self, k):
        where, device = self.spot(0, k)
        return far_copy(
            self.own.at[where], self.mid.at[k - 1], (self.mid_s, self.mid_r), k - 1, device
        )

    def send_mid(self):
        for k in range(1, self.sizes[0]):
            self.mid_copy(k).start()

    def fold_mid(self):
        for k in range(1, self.sizes[0]):
            self.mid_copy(k).wait()
        here = self.spot(0, 0)[0]
        for b in range(self.sizes[1]):
            add_into(self.own, (here, b), [self.mid[k - 1, b] for k in range(1, self.sizes[0])])

    def last_copy(self, k):
        here = self.spot(0, 0)[0]
        where, device = self.spot(1, k)
        return far_copy(
            self.own.at[here, where],
            self.last.at[k - 1],
            (self.last_s, self.last_r),
            k - 1,
            device,
        )

    def send_last(self):
        for k in range(1, self.sizes[1]):
            self.last_copy(k).start()

    def fold_last(self):
        me = self.me
        for k in range(1, self.sizes[1]):
            self.last_copy(k).wait()
        total = self.own[self.spot(0, 0)[0], self.spot(1, 0)[0]].astype(f32)
        for k in range(1, self.sizes[1]):
            total = total + self.last[k - 1].astype(f32)
        self.done[me.core, me.chip] = total.astype(bf16)

    def back_copy(self, k):
        me = self.me
        spot = self.done.at[me.core, me.chip]
        return far_copy(spot, spot, (self.back_s, self.back_r), k - 1, me.plane(k))

    def send_back(self):
        for k in range(1, self.done.shape[1]):
            self.back_copy(k).start()

    def side_copy(self):
        spot = self.done.at[self.me.core]
        return far_copy(spot, spot, (self.side_s, self.side_r), 0, self.me.sibling())

    def send_side(self):
        for k in range(1, self.done.shape[1]):
            self.back_copy(k).wait()
        self.side_copy().start()

    def finish(self):
        self.side_copy().wait()


class Sum:
    def __init__(self, me, vec, got, s, r):
        self.me, self.vec, self.got, self.s, self.r = me, vec, got, s, r

    def copies(self, hop):
        me = self.me
        if hop == 0:
            spots = [(0, me.sibling())]
        elif hop == 1:
            spots = [(k, me.plane(k)) for k in range(1, me.chips)]
        else:
            spots = [(me.chips + k - 1, me.tower(k)) for k in range(1, me.depth)]
        return [far_copy(self.vec, self.got.at[n], (self.s, self.r), n, d) for n, d in spots], spots

    def send(self, hop):
        for copy in self.copies(hop)[0]:
            copy.start()

    def fold(self, hop):
        copies, spots = self.copies(hop)
        for copy in copies:
            copy.wait()
        total = self.vec[...]
        for n, _ in spots:
            total = total + self.got[n]
        self.vec[...] = total


def back_kernel(
    chips,
    depth,
    heads,
    q_ref,
    k_ref,
    v_ref,
    p_ref,
    pos_ref,
    x_ref,
    aw_ref,
    ow_ref,
    ew_ref,
    rw_ref,
    vec_ref,
    ctx_ref,
    n1_ref,
    inv_ref,
    ml_ref,
    hid_ref,
    slope_ref,
    lo_ref,
    gr_ref,
    gb_ref,
    late_ref,
    token_out,
    layer_out,
    aw_out,
    ow_out,
    ew_out,
    rw_out,
    vec_out,
    bias_out,
    dbuf,
    posbuf,
    acc,
    gfar,
    a_mid,
    a_last,
    a_done,
    o_all,
    o_near,
    o_mid,
    o_last,
    o_done,
    e_all,
    e_near,
    e_mid,
    e_last,
    e_done,
    r_all,
    r_near,
    r_mid,
    r_last,
    r_done,
    vbuf,
    vgot,
    bbuf,
    bgot,
    vecs,
    d_s,
    d_r,
    g_s,
    g_r,
    t_s,
    t_r,
    lo_s,
    lo_r,
    load,
    out_sem,
    v_s,
    v_r,
    b_s,
    b_r,
    *sems,
):
    me = Place(chips, depth)
    z, core, chip = me.z, me.core, me.chip
    per, cluster, width = lo_ref.shape[1:]
    half = width // 2
    pairs = heads // 4
    size = half // (2 * pairs)
    blocks = 2 * chips
    share = cluster // blocks
    tile = per * cluster
    hidden = hid_ref.shape[2]
    wide = hidden // blocks
    tall = wide // chips
    quarter = width // depth
    eighth = quarter // blocks
    rows = chips * tile
    me.greet()
    groups = [sems[n * 10 : (n + 1) * 10] for n in range(4)]
    red = Reducer(
        me, r_all.at[core], r_all.at[1 - core], r_near, r_mid, r_last, r_done, groups[0], True
    )
    exp = Reducer(
        me, e_all.at[core], e_all.at[1 - core], e_near, e_mid, e_last, e_done, groups[1], False
    )
    out = Reducer(
        me, o_all.at[core], o_all.at[1 - core], o_near, o_mid, o_last, o_done, groups[2], False
    )
    sums = Sum(me, vbuf, vgot, v_s, v_r)
    biases = Sum(me, bbuf, bgot, b_s, b_r)

    def fetch(src, dst, at):
        return pltpu.make_async_copy(src, dst, load.at[at])

    def lo_copy(k):
        return far_copy(
            lo_ref.at[me.chip_at(k)],
            layer_out.at[pl.ds(chip * per, per)],
            (lo_s, lo_r),
            k - 1,
            me.plane(k),
        )

    lo_keep = pltpu.make_async_copy(
        lo_ref.at[chip], layer_out.at[pl.ds(chip * per, per)], out_sem.at[0]
    )

    def feed_back(gb, ml, hid, slope, rwc, ewc, gpb, n1, inv, ctx, ow, dsnd):
        def order(n):
            return lax.rem(n + 2 * z + chip, blocks)

        def chunk(n, slot):
            at = order(n)
            lanes = pl.ds(multiple(at * wide, 128), wide)
            first = lax.rem(at, 2) * chips
            return [
                fetch(hid_ref.at[:, :, lanes], hid.at[slot], slot * 4),
                fetch(slope_ref.at[:, :, lanes], slope.at[slot], slot * 4 + 1),
                fetch(rw_ref.at[lax.div(at, 2), pl.ds(first, chips)], rwc.at[slot], slot * 4 + 2),
                fetch(ew_ref.at[:, :, lanes], ewc.at[slot], slot * 4 + 3),
            ]

        begin = [
            fetch(gb_ref, gb, 8),
            fetch(ml_ref, ml, 9),
            fetch(gr_ref, acc, 10),
        ]
        later = [
            fetch(vec_ref, vecs, 11),
            fetch(late_ref, vbuf.at[pl.ds(0, 8)], 12),
            fetch(ctx_ref, ctx, 13),
            fetch(ow_ref, ow, 14),
            fetch(inv_ref, inv, 15),
            fetch(pos_ref, posbuf, 18),
        ]
        for copy in chunk(0, 0) + begin + later:
            copy.start()
        for k in range(1, chips):
            lo_copy(k).start()
        lo_keep.start()
        vbuf[8:, :] = jnp.zeros((blocks, width), f32)
        for copy in begin:
            copy.wait()
        later[1].wait()

        def fold(n):
            at = order(n)
            a = lax.div(at, 2)

            @pl.when(lax.rem(at, 2) == core)
            def _():
                red.fold_near(a)
                k = lax.rem(a - z + depth, depth)

                @pl.when(k != 0)
                def _():
                    red.mid_copy(k).start()

            b = lax.rem(at, chips)

            @pl.when(lax.div(at, chips) == core)
            def _():
                exp.fold_near(b)
                k = lax.rem(b - chip + chips, chips)

                @pl.when(k != 0)
                def _():
                    exp.mid_copy(k).start()

        @pl.loop(0, blocks)
        def _(n):
            slot = lax.rem(n, 2)
            at = order(n)
            for copy in chunk(n, slot):
                copy.wait()

            @pl.when(n + 1 < blocks)
            def _():
                for copy in chunk(n + 1, 1 - slot):
                    copy.start()

            up = rwc[slot].reshape(wide, width)
            down = ewc[slot].reshape(width, wide)
            total = jnp.zeros((1, wide), f32)
            for j in range(chips):
                grad = dot_lanes(gb[j].reshape(tile, width), up)
                low = (grad * slope[slot, j].astype(f32)).astype(bf16)
                gpb[j] = low
                acc[j] += dot_lanes(low, down)
                total = total + jnp.sum(low.astype(f32), axis=0, keepdims=True)
            vbuf[pl.ds(8 + at, 1), :wide] = total
            term = dot_first(hid[slot].reshape(rows, wide), gb[...].reshape(rows, width))
            r_all[lax.rem(at, 2), lax.div(at, 2)] = term.astype(bf16).reshape(chips, tall, width)
            term = dot_first(ml[...].reshape(rows, width), gpb[...].reshape(rows, wide))
            e_all[lax.div(at, chips), lax.rem(at, chips)] = term.astype(bf16).reshape(
                depth, quarter, wide
            )

            @pl.when(lax.rem(at, 2) != core)
            def _():
                red.near_copy(lax.div(at, 2)).start()

            @pl.when(lax.div(at, chips) != core)
            def _():
                exp.near_copy(lax.rem(at, chips)).start()

            @pl.when(n > 0)
            def _():
                fold(n - 1)

        def n1_copy(j):
            return fetch(n1_ref.at[j], n1.at[j % 2], 16 + j % 2)

        def d_copy(j):
            return far_copy(dsnd.at[j], dbuf.at[core, j], (d_s, d_r), j, me.sibling())

        n1_copy(0).start()
        fold(blocks - 1)
        for copy in later[:1] + later[2:]:
            copy.wait()
        gain = vecs[3:4, :]
        for row in range(3, 8):
            vbuf[row : row + 1, :] = jnp.zeros((1, width), f32)
        for j in range(chips):
            n1_copy(j).wait()
            if j + 1 < chips:
                n1_copy(j + 1).start()
            grad = acc[j]
            normed = n1[j % 2]
            vbuf[3:4, :] += jnp.sum(grad * normed, axis=0, keepdims=True)
            vbuf[4:5, :] += jnp.sum(grad, axis=0, keepdims=True)
            scaled = grad * gain
            first = jnp.mean(scaled, axis=1, keepdims=True)
            second = jnp.mean(scaled * normed, axis=1, keepdims=True)
            grad = inv[j][:, :1] * (scaled - first - normed * second)
            acc[j] = grad
            low = grad.astype(bf16)
            gb[j] = low.reshape(per, cluster, width)
            vbuf[5:6, :] += jnp.sum(low.astype(f32), axis=0, keepdims=True)
            back = dot_lanes(low, ow[...].reshape(width, width)).astype(bf16)

            for c in range(2):
                piece = back[:, c * half : (c + 1) * half]

                @pl.when(core == c)
                def _():
                    dbuf[c, j] = piece.reshape(per, cluster, half)

                @pl.when(core != c)
                def _():
                    dsnd[j] = piece.reshape(per, cluster, half)

            d_copy(j).start()
        sums.send(0)
        term = dot_first(ctx[...].reshape(rows, width), gb[...].reshape(rows, width))
        for zz in range(depth):
            for c in range(2):
                for p in range(chips):
                    begin_at = zz * quarter + (c * chips + p) * eighth
                    o_all[c, p, zz] = term[begin_at : begin_at + eighth, :].astype(bf16)
        for p in range(chips):
            out.near_copy(p).start()
        for j in range(chips):
            d_copy(j).wait()
        for a in range(depth):
            red.near_copy(a).wait_send()
        for b in range(chips):
            exp.near_copy(b).wait_send()

    shape = (chips, per, cluster, width)
    vm = pltpu.VMEM
    pl.run_scoped(
        feed_back,
        vm(shape, bf16),
        vm((chips, tile, width), bf16),
        vm((2, chips, tile, wide), bf16),
        vm((2, chips, tile, wide), bf16),
        vm((2, chips, tall, width), bf16),
        vm((2, depth, quarter, wide), bf16),
        vm((chips, tile, wide), bf16),
        vm((2, tile, width), f32),
        vm((chips, tile, 128), f32),
        vm(shape, bf16),
        vm((depth, 2, quarter // 2, width), bf16),
        vm((chips, per, cluster, half), bf16),
    )

    def attend_back(qs, ks, vs, ps, xbuf, wbuf, ds, gs, gbuf, tbuf, dw, dwb):
        att = Reducer(me, dwb, None, None, a_mid, a_last, a_done, groups[3], False)

        def loads(i, slot):
            span = pl.ds(i * pairs, pairs)
            pieces = (
                (q_ref.at[span], qs),
                (k_ref.at[span], ks),
                (v_ref.at[span], vs),
                (p_ref.at[span], ps),
            )
            return [fetch(src, dst.at[slot], slot * 4 + n) for n, (src, dst) in enumerate(pieces)]

        def load_x(i):
            return fetch(x_ref.at[:, :, i], xbuf, 8)

        load_w = fetch(aw_ref, wbuf, 9)
        for copy in loads(0, 0) + [load_x(0), load_w]:
            copy.start()
        bbuf[...] = jnp.zeros_like(bbuf)
        slots = lax.broadcasted_iota(jnp.int32, (cluster, cluster), 0)
        low = lax.broadcasted_iota(jnp.int32, (cluster, 128), 1) < size
        scale = size ** (-0.5)

        def tables(jj, i, pair, part):
            begin = part * heads + core * (heads // 2) + 2 * pair
            return [
                one_hot(posbuf[jj // chips, jj % chips, i, pl.ds(begin + h, 1), :], slots)
                for h in range(2)
            ]

        def clusters(i, slot, pair):
            lanes = pl.ds(multiple(pair * 128, 128), 128)
            for jj in range(blocks):
                tq = jnp.concatenate(tables(jj, i, pair, 0), axis=1)
                rows = stack_lanes(dbuf[jj // chips, jj % chips, i, :, lanes], low)
                ds[:, jj * share : (jj + 1) * share, :] = (
                    dot_rows(tq, rows).astype(bf16).reshape(blocks, share, 128)
                )
            for c in range(blocks):
                d = ds[c]
                probs = ps[slot, pair, c]
                slope = dot_lanes(d, stack_lanes(vs[slot, pair, c], low))
                broad = probs.astype(f32)
                halves = []
                for h in range(2):
                    span = slice(h * cluster, (h + 1) * cluster)
                    inner = jnp.sum(broad[:, span] * slope[:, span], axis=1, keepdims=True)
                    halves.append((broad[:, span] * (slope[:, span] - inner)).astype(bf16))
                grads = jnp.concatenate(halves, axis=1)
                gq = dot_rows(grads, stack_lanes(ks[slot, pair, c], low)) * scale
                gk = dot_first(grads, qs[slot, pair, c]) * scale
                gv = dot_first(probs, d)
                gs[0, c] = gq.astype(bf16)
                gs[1, c] = jnp.where(low, gk[:cluster], gk[cluster:]).astype(bf16)
                gs[2, c] = jnp.where(low, gv[:cluster], gv[cluster:]).astype(bf16)
            for jj in range(blocks):
                for part in range(3):
                    if part < 2:
                        table = jnp.concatenate(tables(jj, i, pair, part), axis=0)
                    rows = gs[part, :, jj * share : (jj + 1) * share, :].reshape(cluster, 128)
                    back = dot_first(table, stack_lanes(rows, low))
                    to = pl.ds(multiple(part * half + pair * 128, 128), 128)
                    gbuf[slot, jj // chips, jj % chips, :, to] = back.astype(bf16)

        def give(slot):
            return far_copy(gbuf.at[slot, 1 - core], gfar.at[slot], (g_s, g_r), slot, me.sibling())

        def token_copy(i, slot, k):
            return far_copy(
                tbuf.at[slot, me.chip_at(k)],
                token_out.at[chip * per + i],
                (t_s, t_r),
                i * (chips - 1) + k - 1,
                me.plane(k),
            )

        def token_keep(i, slot):
            return pltpu.make_async_copy(
                tbuf.at[slot, chip], token_out.at[chip * per + i], out_sem.at[1 + i]
            )

        def token_rows(i, slot):
            give(slot).wait()
            for j in range(chips):
                near = dot_lanes(gbuf[slot, core, j], wbuf[core])
                distant = dot_lanes(gfar[slot, j], wbuf[1 - core])
                resid = acc[j, i * cluster : (i + 1) * cluster, :]
                tbuf[slot, j] = (resid + near + distant).astype(bf16)
            token_keep(i, slot).start()
            for k in range(1, chips):
                token_copy(i, slot, k).start()

        ready = []

        def emit(src, dst):
            copy = pltpu.make_async_copy(src, dst, out_sem.at[1 + per + len(ready)])
            copy.start()
            ready.append(copy)

        def step_out_near():
            for p in range(chips):
                out.fold_near(p)
            out.send_mid()
            for p in range(chips):
                out.near_copy(p).wait_send()
            sums.fold(0)
            sums.send(1)

        def step_exp_mid():
            exp.fold_mid()
            exp.send_last()

        def step_red_mid():
            red.fold_mid()
            red.send_last()
            sums.fold(1)
            sums.send(2)

        def step_exp_last():
            exp.fold_last()
            exp.send_back()
            out.fold_mid()
            out.send_last()

        def step_red_last():
            red.fold_last()
            red.send_back()
            sums.fold(2)

        def step_out_last():
            out.fold_last()
            out.send_back()
            exp.send_side()

        def step_sides():
            red.send_side()
            out.send_side()

        hooks = {}
        steps = [
            step_out_near,
            step_exp_mid,
            step_red_mid,
            step_exp_last,
            step_red_last,
            step_out_last,
            step_sides,
        ]
        for n, step in enumerate(steps):
            hooks.setdefault(min(n, per * pairs - 1), []).append(step)

        for i in range(per):
            slot = i % 2
            for copy in loads(i, slot):
                copy.wait()
            if i == 0:
                load_w.wait()
            if i >= 1:
                token_rows(i - 1, 1 - slot)
            if i + 1 < per:
                for copy in loads(i + 1, 1 - slot):
                    copy.start()

            @pl.loop(0, pairs)
            def _(pair):
                clusters(i, slot, pair)
                for n in range(pairs):
                    if hooks.get(i * pairs + n):

                        @pl.when(pair == n)
                        def _():
                            for step in hooks[i * pairs + n]:
                                step()

            if i >= 2:
                token_keep(i - 2, slot).wait()
                for k in range(1, chips):
                    token_copy(i - 2, slot, k).wait()
            give(slot).start()
            load_x(i).wait()
            for b in range(2):
                x = jnp.concatenate([xbuf[b, j] for j in range(chips)], axis=0)
                g = jnp.concatenate([gbuf[slot, b, j] for j in range(chips)], axis=0)
                term = dot_first(x, g)
                if i == 0 and b == 0:
                    dw[...] = term
                else:
                    dw[...] += term
                bbuf[0:1, :] += jnp.sum(g.astype(f32), axis=0, keepdims=True)
            if i + 1 < per:
                load_x(i + 1).start()

        depth_rows = quarter // chips
        for a in range(depth):
            for b in range(chips):
                begin = (a * chips + b) * depth_rows
                dwb[b, a] = dw[begin : begin + depth_rows, :].astype(bf16)
        att.send_mid()
        biases.send(1)
        token_rows(per - 1, (per - 1) % 2)
        emit(vbuf, vec_out)
        exp.finish()
        for c in range(2):
            for p in range(chips):
                emit(e_done.at[c, p], ew_out.at[:, pl.ds((c * chips + p) * wide, wide)])
        red.finish()
        emit(r_done, rw_out)
        out.finish()
        emit(o_done, ow_out)
        biases.fold(1)
        biases.send(2)
        att.fold_mid()
        att.send_last()
        biases.fold(2)
        share_bias = far_copy(bbuf, bias_out.at[core], (b_s, b_r), 0, me.sibling())
        share_bias.start()
        emit(bbuf, bias_out.at[core])
        att.fold_last()
        att.send_back()
        att.send_side()
        att.finish()
        for c in range(2):
            for part in range(3):
                emit(
                    a_done.at[c, :, :, pl.ds(part * half, half)],
                    aw_out.at[:, :, pl.ds((2 * part + c) * half, half)],
                )
        for i in range(max(per - 2, 0), per):
            token_keep(i, i % 2).wait()
            for k in range(1, chips):
                token_copy(i, i % 2, k).wait()
        share_bias.wait()
        for copy in ready:
            copy.wait()
        lo_keep.wait()
        for k in range(1, chips):
            lo_copy(k).wait()

    group = (2, pairs, blocks, cluster)
    pl.run_scoped(
        attend_back,
        vm(group + (128,), bf16),
        vm(group + (128,), bf16),
        vm(group + (128,), bf16),
        vm(group + (2 * cluster,), bf16),
        vm((2, chips, cluster, width), bf16),
        vm(aw_ref.shape, bf16),
        vm((blocks, cluster, 128), bf16),
        vm((3, blocks, cluster, 128), bf16),
        vm((2, 2, chips, cluster, 3 * half), bf16),
        vm((2, chips, cluster, width), bf16),
        vm((width, 3 * half), f32),
        vm((chips, depth, quarter // chips, 3 * half), bf16),
    )


def back(arrays, depth, heads):
    chips, per, cluster, width = arrays[17].shape
    half, blocks = width // 2, 2 * chips
    dma = pltpu.SemaphoreType.DMA
    anywhere = pl.BlockSpec(memory_space=pl.ANY)
    quarter = width // depth
    hidden = arrays[15].shape[2]
    eighth, tall, wide = quarter // blocks, hidden // depth // blocks, hidden // blocks
    rows = quarter // chips
    c, t = chips - 1, depth - 1
    shapes = [
        ((chips * per, cluster, width), bf16),
        ((chips * per, cluster, width), bf16),
        ((chips, rows, 3 * width), bf16),
        ((2, chips, eighth, width), bf16),
        ((quarter, hidden), bf16),
        ((2, chips, tall, width), bf16),
        ((8 + blocks, width), f32),
        ((2, 8, 3 * half), f32),
    ]
    vm = pltpu.VMEM

    def reducing(near, first, second):
        return [
            dma((near,)), dma((near,)),
            dma((first,)), dma((first,)),
            dma((second,)), dma((second,)),
            dma((c,)), dma((c,)),
            dma((1,)), dma((1,)),
        ]

    return pl.pallas_call(
        functools.partial(back_kernel, chips, depth, heads),
        out_shape=[jax.ShapeDtypeStruct(*s) for s in shapes],
        in_specs=[anywhere] * len(arrays),
        out_specs=[anywhere] * len(shapes),
        scratch_shapes=[
            vm((2, chips, per, cluster, half), bf16),
            vm(arrays[4].shape, jnp.int32),
            vm((chips, per * cluster, width), f32),
            vm((2, chips, cluster, 3 * half), bf16),
            vm((c, depth, rows, 3 * half), bf16),
            vm((t, rows, 3 * half), bf16),
            vm((2, chips, rows, 3 * half), bf16),
            vm((2, chips, depth, eighth, width), bf16),
            vm((chips, depth, eighth, width), bf16),
            vm((c, depth, eighth, width), bf16),
            vm((t, eighth, width), bf16),
            vm((2, chips, eighth, width), bf16),
            vm((2, chips, depth, quarter, wide), bf16),
            vm((chips, depth, quarter, wide), bf16),
            vm((c, depth, quarter, wide), bf16),
            vm((t, quarter, wide), bf16),
            vm((2, chips, quarter, wide), bf16),
            vm((2, depth, chips, tall, width), bf16),
            vm((depth, chips, tall, width), bf16),
            vm((t, chips, tall, width), bf16),
            vm((c, tall, width), bf16),
            vm((2, chips, tall, width), bf16),
            vm((8 + blocks, width), f32),
            vm((chips + t, 8 + blocks, width), f32),
            vm((8, 3 * half), f32),
            vm((chips + t, 8, 3 * half), f32),
            vm((8, width), f32),
            dma((chips,)), dma((chips,)), dma((2,)), dma((2,)),
            dma((per * c,)), dma((per * c,)),
            dma((c,)), dma((c,)),
            dma((19,)), dma((1 + per + 12 + blocks,)),
            dma((chips + t,)), dma((chips + t,)), dma((chips + t,)), dma((chips + t,)),
            *reducing(depth, t, c),
            *reducing(chips, c, t),
            *reducing(chips, c, t),
            *reducing(1, c, t),
        ],
        compiler_params=pltpu.CompilerParams(
            collective_id=2, has_side_effects=True, vmem_limit_bytes=63 * 2**20
        ),
        name="back",
    )(*arrays)


def places(rank, cluster, share):
    seqs, rows, length = rank.shape
    clusters = cluster // share
    target = rank // cluster
    which = lax.broadcasted_iota(jnp.int32, (1, 1, clusters, 1), 2)
    inside = (target[:, :, None, :] == which).astype(bf16)
    first = lax.broadcasted_iota(jnp.int32, (length, length), 0)
    second = lax.broadcasted_iota(jnp.int32, (length, length), 1)
    before = (first < second).astype(bf16)
    count = lax.dot_general(
        inside.reshape(seqs * rows * clusters, length),
        before,
        (((1,), (0,)), ((), ())),
        preferred_element_type=f32,
    ).reshape(seqs, rows, clusters, length)
    spot = which.astype(f32) * share + count
    return jnp.sum(inside.astype(f32) * spot, axis=2).astype(jnp.int32)


def per_chip(
    tokens,
    attend_weight,
    query_bias,
    value_bias,
    output_weight,
    output_bias,
    first_gain,
    first_shift,
    expand_weight,
    expand_bias,
    reduce_weight,
    reduce_bias,
    second_gain,
    second_shift,
    query_rank,
    key_rank,
    cotangent,
):
    seqs, cluster, width = tokens.shape
    heads = query_rank.shape[1]
    owners = lax.axis_size("seq")
    depth = lax.axis_size("batch")
    chips = owners // 2
    half = width // 2
    share = cluster // owners
    pos = places(jnp.concatenate([query_rank, key_rank], axis=1), cluster, share)
    quarter = width // depth
    small = jnp.concatenate(
        [
            v.astype(f32)
            for v in (
                query_bias,
                value_bias,
                output_bias,
                first_gain,
                first_shift,
                reduce_bias,
                second_gain,
                second_shift,
                expand_bias,
            )
        ]
    )
    count = small.shape[0] // quarter
    vectors = jnp.pad(small.reshape(count, quarter), ((0, 16 - count), (0, 256 - quarter)))
    (
        x_all,
        context,
        qs,
        ks,
        vs,
        ps,
        pos_all,
        attend_all,
        vecs,
        out_all,
        exp_all,
        red_all,
        normed_one,
        inverse_one,
        middle_low,
        hidden,
        slope,
        layer_out,
        grad_resid_two,
        grad_branch_two,
        late_sums,
    ) = forward(
        tokens,
        pos,
        attend_weight,
        vectors,
        output_weight,
        expand_weight,
        reduce_weight,
        cotangent,
        chips,
        depth,
        heads,
    )
    token_grad, layer_out, aw_grad, ow_grad, ew_grad, rw_grad, vec_sum, bias_sum = back(
        (
            qs,
            ks,
            vs,
            ps,
            pos_all,
            x_all,
            attend_all,
            out_all,
            exp_all,
            red_all,
            vecs,
            context,
            normed_one,
            inverse_one,
            middle_low,
            hidden,
            slope,
            layer_out,
            grad_resid_two,
            grad_branch_two,
            late_sums,
        ),
        depth,
        heads,
    )
    z = lax.axis_index("batch")
    six = lax.dynamic_slice_in_dim(vec_sum[:6], z * quarter, quarter, 1)
    wide = expand_weight.shape[1] // owners
    up = lax.dynamic_slice_in_dim(vec_sum[8:, :wide], z * 2, owners // depth, 0).reshape(-1)
    both = jnp.concatenate([bias_sum[0, 0], bias_sum[1, 0]]).reshape(2, 3, half)
    query_value = jnp.transpose(both, (1, 0, 2)).reshape(3, width)
    query_value = lax.dynamic_slice_in_dim(query_value, z * quarter, quarter, 1)
    return (
        layer_out,
        token_grad,
        aw_grad.reshape(quarter, 3 * width).astype(f32),
        query_value[0],
        query_value[2],
        ow_grad.reshape(quarter, width).astype(f32),
        six[5],
        six[3],
        six[4],
        ew_grad.astype(f32),
        up,
        rw_grad.reshape(-1, width).astype(f32),
        six[2],
        six[0],
        six[1],
    )


def layer(mesh):
    def run(*arrays):
        seqs, cluster, width = arrays[0].shape
        heads = arrays[14].shape[1]
        owners, depth = mesh.shape["seq"], mesh.shape["batch"]
        chips = owners // 2
        fits = (
            owners % 2 == 0
            and chips > 1
            and depth == chips
            and seqs % chips == 0
            and cluster == 128
            and heads % 4 == 0
            and width == heads * 64
            and cluster % (16 * owners) == 0
        )
        return (per_chip if fits else per_device)(*arrays)

    return run


def solution(mesh):
    in_specs = (
        P("batch", "seq", None),
        P("batch", None),
        P("batch"),
        P("batch"),
        P("batch", None),
        P("batch"),
        P("batch"),
        P("batch"),
        P("batch", None),
        P("batch"),
        P("batch", None),
        P("batch"),
        P("batch"),
        P("batch"),
        P("batch", None, "seq"),
        P("batch", None, "seq"),
        P("batch", "seq", None),
    )
    out_specs = (
        P("batch", "seq", None),
        P("batch", "seq", None),
        P("batch", None),
        P("batch"),
        P("batch"),
        P("batch", None),
        P("batch"),
        P("batch"),
        P("batch"),
        P("batch", None),
        P("batch"),
        P("batch", None),
        P("batch"),
        P("batch"),
        P("batch"),
    )
    return jax.shard_map(
        layer(mesh), mesh=mesh, in_specs=in_specs, out_specs=out_specs, check_vma=False
    )
```

```python
import functools
import math

import jax
import jax.numpy as jnp
from jax import lax
from jax.experimental import pallas as pl
from jax.experimental.pallas import tpu as pltpu
from jax.sharding import PartitionSpec as P

epsilon = 1e-05


def layer_norm(resid, gain, shift):
    center = jnp.mean(resid, axis=-1, keepdims=True)
    centered = resid - center
    spread = jnp.mean(centered * centered, axis=-1, keepdims=True)
    inverse = lax.rsqrt(spread + epsilon)
    normed = centered * inverse
    return (normed * gain + shift, normed, inverse)


def norm_back(upstream, normed, inverse, gain):
    scaled = upstream * gain
    first_mean = jnp.mean(scaled, axis=-1, keepdims=True)
    second_mean = jnp.mean(scaled * normed, axis=-1, keepdims=True)
    return inverse * (scaled - first_mean - normed * second_mean)


def gelu_slope(value):
    cumulative = 0.5 * (1.0 + lax.erf(value * 0.5**0.5))
    density = jnp.exp(-0.5 * value * value) * (2.0 * math.pi) ** (-0.5)
    return cumulative + value * density


def transpose_left(first, second):
    return lax.dot_general(
        first, second, (((0,), (0,)), ((), ())), preferred_element_type=jnp.float32
    )


def transpose_right(first, second):
    return lax.dot_general(
        first, second, (((1,), (1,)), ((), ())), preferred_element_type=jnp.float32
    )


def group_table(rank, cluster, owners):
    share = cluster // owners
    target = rank // cluster
    length = rank.shape[-1]
    places = lax.broadcasted_iota(jnp.int32, (length, length), 0)
    later = lax.broadcasted_iota(jnp.int32, (length, length), 1)
    before = (places < later)[None, None]
    same = target[..., :, None] == target[..., None, :]
    earlier = jnp.sum((same & before).astype(jnp.int32), axis=-2)
    position = target * share + earlier
    slots = lax.broadcasted_iota(jnp.int32, position.shape + (length,), 3)
    return (position[..., None] == slots).astype(jnp.bfloat16)


def sort_heads(rows, table, heads):
    seqs, length, width = rows.shape
    split = rows.reshape(seqs, length, heads, width // heads)
    moved = jnp.einsum("shtp,sthd->sphd", table, split, preferred_element_type=jnp.float32)
    return moved.astype(rows.dtype).reshape(seqs, length, width)


def unsort_heads(rows, table, heads):
    seqs, length, width = rows.shape
    split = rows.reshape(seqs, length, heads, width // heads)
    moved = jnp.einsum("shtp,sphd->sthd", table, split, preferred_element_type=jnp.float32)
    return moved.astype(rows.dtype).reshape(seqs, length, width)


def cluster_scores(queries, keys_rows, heads):
    items, length, width = queries.shape
    size = width // heads
    query_split = queries.reshape(items, length, heads, size)
    key_split = keys_rows.reshape(items, length, heads, size)
    scores = jnp.einsum(
        "sqhd,skhd->shqk", query_split, key_split, preferred_element_type=jnp.float32
    )
    return scores * size ** (-0.5)


def cluster_forward(queries, keys_rows, values_rows, heads):
    items, length, width = queries.shape
    scores = cluster_scores(queries, keys_rows, heads)
    top = jnp.max(scores, axis=-1, keepdims=True)
    weights = jnp.exp(scores - top)
    total = jnp.sum(weights, axis=-1, keepdims=True)
    probs = (weights / total).astype(jnp.bfloat16)
    value_split = values_rows.reshape(items, length, heads, width // heads)
    context = jnp.einsum("shqk,skhd->sqhd", probs, value_split, preferred_element_type=jnp.float32)
    return (
        context.reshape(items, length, width).astype(jnp.bfloat16),
        (top + jnp.log(total))[..., 0],
    )


def cluster_backward(scores, log_total, queries, keys_rows, values_rows, grad_context, heads):
    items, length, width = queries.shape
    size = width // heads
    query_split = queries.reshape(items, length, heads, size)
    key_split = keys_rows.reshape(items, length, heads, size)
    value_split = values_rows.reshape(items, length, heads, size)
    grad_split = grad_context.reshape(items, length, heads, size)
    probs = jnp.exp(scores - log_total[..., None])
    grad_probs = jnp.einsum(
        "sqhd,skhd->shqk", grad_split, value_split, preferred_element_type=jnp.float32
    )
    inner = jnp.sum(probs * grad_probs, axis=-1, keepdims=True)
    grad_scores = (probs * (grad_probs - inner)).astype(jnp.bfloat16)
    scale = size ** (-0.5)
    grad_query = (
        jnp.einsum("shqk,skhd->sqhd", grad_scores, key_split, preferred_element_type=jnp.float32)
        * scale
    )
    grad_key = (
        jnp.einsum("shqk,sqhd->skhd", grad_scores, query_split, preferred_element_type=jnp.float32)
        * scale
    )
    grad_value = jnp.einsum(
        "shqk,sqhd->skhd",
        probs.astype(jnp.bfloat16),
        grad_split,
        preferred_element_type=jnp.float32,
    )
    shape = (items, length, width)
    return (
        grad_query.reshape(shape).astype(jnp.bfloat16),
        grad_key.reshape(shape).astype(jnp.bfloat16),
        grad_value.reshape(shape).astype(jnp.bfloat16),
    )


def send_context(context):
    return lax.all_to_all(context, "seq", split_axis=1, concat_axis=1, tiled=True)


def send_grads(grads):
    return (
        lax.all_to_all(grads[0], "seq", split_axis=1, concat_axis=1, tiled=True),
        lax.all_to_all(grads[1], "seq", split_axis=1, concat_axis=1, tiled=True),
        lax.all_to_all(grads[2], "seq", split_axis=1, concat_axis=1, tiled=True),
    )


def make_step(left, pieces):
    total = jnp.dot(left, pieces[0], preferred_element_type=jnp.float32)
    stored = tuple(pieces[1:]) + ()
    placed = tuple((piece for piece in stored))
    return (total,) + placed


def make_hidden_step(before, pieces):
    section = before + pieces[1].astype(jnp.float32)
    activated = jax.nn.gelu(section, approximate=False).astype(jnp.bfloat16)
    total = jnp.dot(activated, pieces[0], preferred_element_type=jnp.float32)
    stored = ()
    return (total, section, activated) + stored


def per_device(
    tokens,
    attend_weight,
    query_bias,
    value_bias,
    output_weight,
    output_bias,
    first_gain,
    first_shift,
    expand_weight,
    expand_bias,
    reduce_weight,
    reduce_bias,
    second_gain,
    second_shift,
    query_rank,
    key_rank,
    cotangent,
):
    seqs, cluster, width = tokens.shape
    heads = query_rank.shape[1]
    rows = seqs * cluster
    owners = lax.axis_size("seq")
    flat = tokens.reshape(rows, width)
    attend_out = make_step(
        flat,
        (
            lax.all_gather(attend_weight, "batch", axis=0, tiled=True),
            lax.all_gather(query_bias, "batch", axis=0, tiled=True),
            lax.all_gather(value_bias, "batch", axis=0, tiled=True),
        ),
    )
    summed = attend_out[0]
    queries = (summed[:, :width] + attend_out[1].astype(jnp.float32)).astype(jnp.bfloat16)
    keys_rows = summed[:, width : 2 * width].astype(jnp.bfloat16)
    values_rows = (summed[:, 2 * width :] + attend_out[2].astype(jnp.float32)).astype(jnp.bfloat16)
    query_table = group_table(query_rank, cluster, owners)
    key_table = group_table(key_rank, cluster, owners)
    query_sorted = sort_heads(queries.reshape(seqs, cluster, width), query_table, heads)
    key_sorted = sort_heads(keys_rows.reshape(seqs, cluster, width), key_table, heads)
    value_sorted = sort_heads(values_rows.reshape(seqs, cluster, width), key_table, heads)
    received = (
        lax.all_to_all(query_sorted, "seq", split_axis=1, concat_axis=1, tiled=True),
        lax.all_to_all(key_sorted, "seq", split_axis=1, concat_axis=1, tiled=True),
        lax.all_to_all(value_sorted, "seq", split_axis=1, concat_axis=1, tiled=True),
    )
    context, log_total = cluster_forward(received[0], received[1], received[2], heads)
    forward_out = (send_context(context), log_total, received[0], received[1], received[2])
    context_rows = unsort_heads(forward_out[0], query_table, heads).reshape(rows, width)
    output_out = make_step(
        context_rows,
        (
            lax.all_gather(output_weight, "batch", axis=0, tiled=True),
            lax.all_gather(output_bias, "batch", axis=0, tiled=True),
            lax.all_gather(first_gain, "batch", axis=0, tiled=True),
            lax.all_gather(first_shift, "batch", axis=0, tiled=True),
        ),
    )
    resid_one = flat.astype(jnp.float32) + output_out[0] + output_out[1].astype(jnp.float32)
    gain_one = output_out[2].astype(jnp.float32)
    middle, normed_one, inverse_one = layer_norm(
        resid_one, gain_one, output_out[3].astype(jnp.float32)
    )
    middle_low = middle.astype(jnp.bfloat16)
    expand_out = make_step(
        middle_low,
        (
            lax.all_gather(expand_weight, "batch", axis=0, tiled=True),
            lax.all_gather(reduce_bias, "batch", axis=0, tiled=True),
            lax.all_gather(second_gain, "batch", axis=0, tiled=True),
            lax.all_gather(second_shift, "batch", axis=0, tiled=True),
        ),
    )
    hidden_out = make_hidden_step(
        expand_out[0],
        (
            lax.all_gather(reduce_weight, "batch", axis=0, tiled=True),
            lax.all_gather(expand_bias, "batch", axis=0, tiled=True),
        ),
    )
    pre_full, hidden_full = (hidden_out[1], hidden_out[2])
    resid_two = middle + hidden_out[0] + expand_out[1].astype(jnp.float32)
    gain_two = expand_out[2].astype(jnp.float32)
    final, normed_two, inverse_two = layer_norm(
        resid_two, gain_two, expand_out[3].astype(jnp.float32)
    )
    layer_out = final.astype(jnp.bfloat16).reshape(seqs, cluster, width)
    attend_full, output_full, expand_full, reduce_full = (
        lax.all_gather(attend_weight, "batch", axis=0, tiled=True),
        lax.all_gather(output_weight, "batch", axis=0, tiled=True),
        lax.all_gather(expand_weight, "batch", axis=0, tiled=True),
        lax.all_gather(reduce_weight, "batch", axis=0, tiled=True),
    )
    upstream = cotangent.reshape(rows, width).astype(jnp.float32)
    grad_second_gain = jnp.sum(upstream * normed_two, axis=0)
    grad_second_shift = jnp.sum(upstream, axis=0)
    grad_resid_two = norm_back(upstream, normed_two, inverse_two, gain_two)
    grad_branch_two = grad_resid_two.astype(jnp.bfloat16)
    grad_reduce_bias = jnp.sum(grad_branch_two, axis=0, dtype=jnp.float32)
    grad_reduce = transpose_left(hidden_full, grad_branch_two)
    grad_hidden = transpose_right(grad_branch_two, reduce_full)
    grad_pre = (grad_hidden * gelu_slope(pre_full)).astype(jnp.bfloat16)
    grad_expand_bias = jnp.sum(grad_pre, axis=0, dtype=jnp.float32)
    grad_expand = transpose_left(middle_low, grad_pre)
    grad_middle = grad_resid_two + transpose_right(grad_pre, expand_full)
    grad_first_gain = jnp.sum(grad_middle * normed_one, axis=0)
    grad_first_shift = jnp.sum(grad_middle, axis=0)
    grad_resid_one = norm_back(grad_middle, normed_one, inverse_one, gain_one)
    grad_branch_one = grad_resid_one.astype(jnp.bfloat16)
    grad_output_bias = jnp.sum(grad_branch_one, axis=0, dtype=jnp.float32)
    grad_output = transpose_left(context_rows, grad_branch_one)
    grad_context = transpose_right(grad_branch_one, output_full).astype(jnp.bfloat16)
    grad_sorted = sort_heads(grad_context.reshape(seqs, cluster, width), query_table, heads)
    grad_received = lax.all_to_all(grad_sorted, "seq", split_axis=1, concat_axis=1, tiled=True)
    kept_scores = cluster_scores(forward_out[2], forward_out[3], heads)
    home = send_grads(
        cluster_backward(
            kept_scores,
            forward_out[1],
            forward_out[2],
            forward_out[3],
            forward_out[4],
            grad_received,
            heads,
        )
    )
    grad_queries = unsort_heads(home[0], query_table, heads).reshape(rows, width)
    grad_keys = unsort_heads(home[1], key_table, heads).reshape(rows, width)
    grad_values = unsort_heads(home[2], key_table, heads).reshape(rows, width)
    grad_mixed = jnp.concatenate([grad_queries, grad_keys, grad_values], axis=1)
    grad_query_bias = jnp.sum(grad_queries, axis=0, dtype=jnp.float32)
    grad_value_bias = jnp.sum(grad_values, axis=0, dtype=jnp.float32)
    grad_attend = transpose_left(flat, grad_mixed)
    token_grad = (
        (grad_resid_one + transpose_right(grad_mixed, attend_full))
        .astype(jnp.bfloat16)
        .reshape(seqs, cluster, width)
    )
    owned = (
        lax.psum_scatter(
            grad_attend.astype(jnp.bfloat16), "batch", scatter_dimension=0, tiled=True
        ).astype(jnp.float32),
        lax.psum_scatter(
            grad_query_bias.astype(jnp.bfloat16), "batch", scatter_dimension=0, tiled=True
        ).astype(jnp.float32),
        lax.psum_scatter(
            grad_value_bias.astype(jnp.bfloat16), "batch", scatter_dimension=0, tiled=True
        ).astype(jnp.float32),
        lax.psum_scatter(
            grad_output.astype(jnp.bfloat16), "batch", scatter_dimension=0, tiled=True
        ).astype(jnp.float32),
        lax.psum_scatter(
            grad_output_bias.astype(jnp.bfloat16), "batch", scatter_dimension=0, tiled=True
        ).astype(jnp.float32),
        lax.psum_scatter(
            grad_first_gain.astype(jnp.bfloat16), "batch", scatter_dimension=0, tiled=True
        ).astype(jnp.float32),
        lax.psum_scatter(
            grad_first_shift.astype(jnp.bfloat16), "batch", scatter_dimension=0, tiled=True
        ).astype(jnp.float32),
        lax.psum_scatter(
            grad_expand.astype(jnp.bfloat16), "batch", scatter_dimension=0, tiled=True
        ).astype(jnp.float32),
        lax.psum_scatter(
            grad_expand_bias.astype(jnp.bfloat16), "batch", scatter_dimension=0, tiled=True
        ).astype(jnp.float32),
        lax.psum_scatter(
            grad_reduce.astype(jnp.bfloat16), "batch", scatter_dimension=0, tiled=True
        ).astype(jnp.float32),
        lax.psum_scatter(
            grad_reduce_bias.astype(jnp.bfloat16), "batch", scatter_dimension=0, tiled=True
        ).astype(jnp.float32),
        lax.psum_scatter(
            grad_second_gain.astype(jnp.bfloat16), "batch", scatter_dimension=0, tiled=True
        ).astype(jnp.float32),
        lax.psum_scatter(
            grad_second_shift.astype(jnp.bfloat16), "batch", scatter_dimension=0, tiled=True
        ).astype(jnp.float32),
    )
    shared = (
        lax.psum(owned[0].astype(jnp.bfloat16), "seq").astype(jnp.float32),
        lax.psum(owned[1].astype(jnp.bfloat16), "seq").astype(jnp.float32),
        lax.psum(owned[2].astype(jnp.bfloat16), "seq").astype(jnp.float32),
        lax.psum(owned[3].astype(jnp.bfloat16), "seq").astype(jnp.float32),
        lax.psum(owned[4].astype(jnp.bfloat16), "seq").astype(jnp.float32),
        lax.psum(owned[5].astype(jnp.bfloat16), "seq").astype(jnp.float32),
        lax.psum(owned[6].astype(jnp.bfloat16), "seq").astype(jnp.float32),
        lax.psum(owned[7].astype(jnp.bfloat16), "seq").astype(jnp.float32),
        lax.psum(owned[8].astype(jnp.bfloat16), "seq").astype(jnp.float32),
        lax.psum(owned[9].astype(jnp.bfloat16), "seq").astype(jnp.float32),
        lax.psum(owned[10].astype(jnp.bfloat16), "seq").astype(jnp.float32),
        lax.psum(owned[11].astype(jnp.bfloat16), "seq").astype(jnp.float32),
        lax.psum(owned[12].astype(jnp.bfloat16), "seq").astype(jnp.float32),
    )
    return (
        layer_out,
        token_grad,
        shared[0],
        shared[1],
        shared[2],
        shared[3],
        shared[4],
        shared[5],
        shared[6],
        shared[7],
        shared[8],
        shared[9],
        shared[10],
        shared[11],
        shared[12],
    )


MESH = pl.DeviceIdType.MESH
f32 = jnp.float32
bf16 = jnp.bfloat16


class Place:
    def __init__(self, chips, depth):
        self.chips, self.depth = chips, depth
        self.z = lax.axis_index("batch")
        spot = lax.axis_index("seq")
        self.chip, self.core = lax.div(spot, 2), lax.rem(spot, 2)

    def chip_at(self, k):
        return lax.rem(self.chip + k + self.chips, self.chips)

    def z_at(self, k):
        return lax.rem(self.z + k + self.depth, self.depth)

    def plane(self, k):
        return (self.z, self.chip_at(k) * 2 + self.core)

    def tower(self, k):
        return (self.z_at(k), self.chip * 2 + self.core)

    def sibling(self):
        return (self.z, self.chip * 2 + 1 - self.core)

    def greet(self):
        bell = pltpu.get_barrier_semaphore()
        others = [self.plane(k) for k in range(1, self.chips)]
        others += [self.tower(k) for k in range(1, self.depth)]
        others.append(self.sibling())
        for other in others:
            pl.semaphore_signal(bell, inc=1, device_id=other, device_id_type=MESH)
        pl.semaphore_wait(bell, len(others))


def far_copy(src, dst, sems, at, device):
    return pltpu.make_async_remote_copy(
        src_ref=src,
        dst_ref=dst,
        send_sem=sems[0].at[at],
        recv_sem=sems[1].at[at],
        device_id=device,
        device_id_type=MESH,
    )


def one_hot(row, slots):
    return jnp.where(slots == row, 1.0, 0.0).astype(bf16)


def split_lanes(tile, low):
    zero = jnp.zeros_like(tile)
    return jnp.where(low, tile, zero), jnp.where(low, zero, tile)


def stack_lanes(tile, low):
    first, second = split_lanes(tile, low)
    return jnp.concatenate([first, second], axis=0)


def dot_rows(a, b):
    return jnp.dot(a, b, preferred_element_type=f32)


def dot_lanes(a, b):
    return lax.dot_general(a, b, (((1,), (1,)), ((), ())), preferred_element_type=f32)


def dot_first(a, b):
    return lax.dot_general(a, b, (((0,), (0,)), ((), ())), preferred_element_type=f32)


def multiple(value, by):
    return pl.multiple_of(value, by)


def forward_kernel(
    chips,
    depth,
    heads,
    tok_ref,
    pos_ref,
    aw_ref,
    vec_ref,
    ow_ref,
    ew_ref,
    rw_ref,
    cot_ref,
    x_out,
    ctx_out,
    q_out,
    k_out,
    v_out,
    p_out,
    pos_out,
    aw_out,
    vec_out,
    ow_out,
    ew_out,
    rw_out,
    n1_out,
    inv_out,
    ml_out,
    hid_out,
    slope_out,
    lo_out,
    gr_out,
    gb_out,
    sum_out,
    xbuf,
    posbuf,
    wbuf,
    vbuf,
    bias,
    ctxb,
    ctxt,
    owbuf,
    ewbuf,
    rwbuf,
    cbuf,
    n1buf,
    invbuf,
    mlbuf,
    vecs,
    upb,
    sums,
    tok_s,
    tok_r,
    tokc_s,
    tokc_r,
    pos_s,
    pos_r,
    posc_s,
    posc_r,
    up_s,
    up_r,
    dn_s,
    dn_r,
    awc_s,
    awc_r,
    vec_s,
    vec_r,
    wz_s,
    wz_r,
    wp_s,
    wp_r,
    wd_s,
    wd_r,
    wc_s,
    wc_r,
    ctx_s,
    ctx_r,
    cot_s,
    cot_r,
    oc_s,
    oc_r,
    loc,
    out_sem,
    slope_sem,
    att_sem,
):
    me = Place(chips, depth)
    z, chip, core = me.z, me.chip, me.core
    per = tok_ref.shape[0] // chips
    half = aw_ref.shape[1] // 6
    rows_z = aw_ref.shape[0]
    pairs = heads // 4
    size = half // (2 * pairs)
    me.greet()

    def aw_block(zz):
        return wbuf.at[pl.ds(multiple(zz * rows_z, 8), rows_z)]

    def up_copy(h):
        return far_copy(
            aw_block(z - h), aw_block(z - h), (up_s, up_r), h, (z + 1, chip * 2 + core)
        )

    def down_copy(h):
        return far_copy(
            aw_block(z + h), aw_block(z + h), (dn_s, dn_r), h, (z - 1, chip * 2 + core)
        )

    def up_got(h):
        return far_copy(
            aw_block(z - 1 - h), aw_block(z - 1 - h), (up_s, up_r), h, me.sibling()
        )

    def down_got(h):
        return far_copy(
            aw_block(z + 1 + h), aw_block(z + 1 + h), (dn_s, dn_r), h, me.sibling()
        )

    def pass_on():
        @pl.when(z < depth - 1)
        def _():
            up_copy(0).start()

        @pl.when(z > 0)
        def _():
            down_copy(0).start()

    def pass_rest():
        for h in range(depth - 1):

            @pl.when(z > h)
            def _():
                up_got(h).wait_recv()
                if h + 1 < depth - 1:

                    @pl.when(z < depth - 1)
                    def _():
                        up_copy(h + 1).start()

            @pl.when(z + 1 + h < depth)
            def _():
                down_got(h).wait_recv()
                if h + 1 < depth - 1:

                    @pl.when(z > 0)
                    def _():
                        down_copy(h + 1).start()

    def pass_end():
        for h in range(depth - 1):

            @pl.when((z >= h) & (z < depth - 1))
            def _():
                up_copy(h).wait_send()

            @pl.when((z + h < depth) & (z > 0))
            def _():
                down_copy(h).wait_send()

    def mine(ref, target):
        return ref.at[pl.ds(target * per, per)]

    def tok_copy(k):
        return far_copy(
            mine(tok_ref, me.chip_at(k)), xbuf.at[core, chip], (tok_s, tok_r), k - 1, me.plane(k)
        )

    def pos_copy(k):
        return far_copy(
            mine(pos_ref, me.chip_at(k)), posbuf.at[core, chip], (pos_s, pos_r), k - 1, me.plane(k)
        )

    def vec_copy(k):
        return far_copy(vec_ref, vbuf.at[z], (vec_s, vec_r), k - 1, me.tower(k))

    sends = []
    for k in range(1, chips):
        sends.append(pos_copy(k))
        sends[-1].start()
    for k in range(1, depth):
        sends.append(vec_copy(k))
        sends[-1].start()
    for k in range(1, chips):
        sends.append(tok_copy(k))
        sends[-1].start()
    local = []

    def keep(src, dst):
        copy = pltpu.make_async_copy(src, dst, loc.at[len(local)])
        copy.start()
        local.append(copy)

    for part in range(3):
        keep(
            aw_ref.at[:, pl.ds(multiple(part * 2 * half + core * half, 128), half)],
            wbuf.at[pl.ds(multiple(z * rows_z, 8), rows_z), pl.ds(part * half, half)],
        )
    keep(mine(tok_ref, chip), xbuf.at[core, chip])
    keep(mine(pos_ref, chip), posbuf.at[core, chip])
    keep(vec_ref, vbuf.at[z])
    for copy in local[:3]:
        copy.wait()
    pass_on()
    wide = ew_ref.shape[1] // (2 * chips)
    tall = rw_ref.shape[0] // (2 * chips)
    mid_rows = rows_z // 2
    mine_at = core * chips + chip

    def piece(kind):
        if kind == 0:
            return ow_ref.at[pl.ds(multiple(core * mid_rows, 8), mid_rows)]
        if kind == 1:
            return ew_ref.at[:, pl.ds(multiple(mine_at * wide, 128), wide)]
        return rw_ref.at[pl.ds(multiple(mine_at * tall, 8), tall)]

    def place(kind, zz):
        if kind == 0:
            return owbuf.at[zz, core]
        if kind == 1:
            return ewbuf.at[zz, :, pl.ds(multiple(mine_at * wide, 128), wide)]
        return rwbuf.at[zz, mine_at]

    def place_all(kind, at):
        if kind == 1:
            return ewbuf.at[:, :, pl.ds(multiple(at * wide, 128), wide)]
        return rwbuf.at[:, at]

    for kind in range(3):
        keep(piece(kind), place(kind, z))

    def wz_copy(kind, k):
        return far_copy(
            piece(kind),
            place(kind, z),
            (wz_s, wz_r),
            kind * (depth - 1) + k - 1,
            me.tower(k),
        )

    beside = (chip + 1 - 2 * lax.rem(chip, 2), lax.rem(chip + 2, chips))
    across = chips - 1 - chip

    def part_of(kind, origin, side):
        at = core * chips + origin
        span = pl.ds(side * (depth // 2), depth // 2)
        if kind == 1:
            return ewbuf.at[span, :, pl.ds(multiple(at * wide, 128), wide)]
        return rwbuf.at[span, at]

    def wp_copy(kind, d):
        spot = place_all(kind, mine_at)
        return far_copy(
            spot, spot, (wp_s, wp_r), (kind - 1) * 2 + d, (z, beside[d] * 2 + core)
        )

    def wd_copy(kind, d):
        spot = part_of(kind, beside[d], d)
        return far_copy(
            spot, spot, (wd_s, wd_r), (kind - 1) * 2 + d, (z, beside[1 - d] * 2 + core)
        )

    def wc_copy(kind, n):
        at = core * chips + (chip, beside[0], beside[1], across)[n]
        return far_copy(
            place_all(kind, at),
            place_all(kind, at),
            (wc_s, wc_r),
            (kind - 1) * chips + n,
            me.sibling(),
        )

    def oc_copy():
        spot = owbuf.at[:, core]
        return far_copy(spot, spot, (oc_s, oc_r), 0, me.sibling())

    def cot_copy(k):
        return far_copy(
            mine(cot_ref, me.chip_at(k)), cbuf.at[chip], (cot_s, cot_r), k - 1, me.plane(k)
        )

    keep(mine(cot_ref, chip), cbuf.at[chip])

    for copy in local[3:5]:
        copy.wait()

    def tokc_copy(k):
        source = me.chip_at(-k)
        return far_copy(
            xbuf.at[core, source], xbuf.at[core, source], (tokc_s, tokc_r), k, me.sibling()
        )

    def posc_copy(k):
        source = me.chip_at(-k)
        return far_copy(
            posbuf.at[core, source], posbuf.at[core, source], (posc_s, posc_r), k, me.sibling()
        )

    for k in range(chips):
        if k:
            pos_copy(k).wait_recv()
            tok_copy(k).wait_recv()
        for copy in (posc_copy(k), tokc_copy(k)):
            copy.start()
            sends.append(copy)
    for k in range(1, chips):
        cot_copy(k).start()
        sends.append(cot_copy(k))
    pass_rest()
    for k in range(1, depth):
        wz_copy(1, k).start()
        for kind in range(3):
            sends.append(wz_copy(kind, k))
    for k in range(1, depth):
        vec_copy(k).wait_recv()
    for k in range(chips):
        posc_copy(k).wait_recv()
        tokc_copy(k).wait_recv()
    for copy in local[5:]:
        copy.wait()

    outs = []

    def emit(src, dst):
        copy = pltpu.make_async_copy(src, dst, out_sem.at[len(outs)])
        copy.start()
        outs.append(copy)

    emit(xbuf, x_out)
    emit(posbuf, pos_out)
    emit(wbuf, aw_out.at[core])
    awc = far_copy(wbuf, aw_out.at[core], (awc_s, awc_r), 0, me.sibling())
    awc.start()
    sends.append(awc)

    quarter = rows_z
    for zz in range(depth):
        begin = zz * quarter
        for row, at in ((0, 0), (1, 2)):
            for side in range(2):
                lo = max(begin, side * half)
                hi = min(begin + quarter, (side + 1) * half)
                if lo < hi:
                    bias[side, 0:1, at * half + lo - side * half : at * half + hi - side * half] = (
                        vbuf[zz, row : row + 1, lo - begin : hi - begin]
                    )
    bias[0, 0:1, half : 2 * half] = jnp.zeros((1, half), f32)
    bias[1, 0:1, half : 2 * half] = jnp.zeros((1, half), f32)
    added = bias[core, 0:1, :]
    for zz in range(depth):
        for row in range(8):
            vecs[row : row + 1, zz * quarter : (zz + 1) * quarter] = vbuf[
                zz, row : row + 1, :quarter
            ]
        steps = upb.shape[1] // (depth * quarter)
        for row in range(steps):
            to = (zz * steps + row) * quarter
            upb[0:1, to : to + quarter] = vbuf[zz, 8 + row : 9 + row, :quarter]

    cluster = tok_ref.shape[1]
    blocks = 2 * chips
    share = cluster // blocks
    width = tok_ref.shape[2]

    slots = lax.broadcasted_iota(jnp.int32, (cluster, cluster), 0)
    low = lax.broadcasted_iota(jnp.int32, (cluster, 128), 1) < size
    scale = size ** (-0.5)

    def tables(jj, i, pair, part):
        first = part * heads + core * (heads // 2) + 2 * pair
        rows = [
            one_hot(posbuf[jj // chips, jj % chips, i, pl.ds(first + h, 1), :], slots)
            for h in range(2)
        ]
        return rows

    def tower_wait(kind):
        for k in range(1, depth):
            wz_copy(kind, k).wait_recv()

    def plane_first(kind):
        for d in range(2):
            wp_copy(kind, d).start()
        wc_copy(kind, 0).start()

    def plane_second(kind):
        for d in range(2):
            wp_copy(kind, d).wait_recv()
            wd_copy(kind, d).start()
            wc_copy(kind, 1 + d).start()

    def plane_last(kind):
        for d in range(2):
            wd_copy(kind, d).wait_recv()
        wc_copy(kind, 3).start()
        for n in range(chips):
            wc_copy(kind, n).wait()
        for d in range(2):
            wp_copy(kind, d).wait_send()
            wd_copy(kind, d).wait_send()

    def hook(i, pair):
        step = i * pairs + pair
        last = per * pairs - 1

        @pl.when(step == min(1, last))
        def _():
            tower_wait(1)
            plane_first(1)
            for k in range(1, depth):
                wz_copy(2, k).start()

        @pl.when(step == min(5, last))
        def _():
            tower_wait(2)
            for k in range(1, depth):
                wz_copy(0, k).start()

        @pl.when(step == min(7, last))
        def _():
            plane_second(1)
            plane_first(2)

    def attention(qkv, qs, ks, vs, ps, os):
        @pl.loop(0, blocks)
        def _(jj):
            x = xbuf[lax.div(jj, chips), lax.rem(jj, chips)].reshape(per * cluster, width)
            mixed = (dot_rows(x, wbuf[...]) + added).astype(bf16)
            for at in range(3 * pairs):
                qkv[at, jj] = mixed[:, at * 128 : (at + 1) * 128].reshape(per, cluster, 128)

        @pl.loop(0, per)
        def _(i):
            @pl.loop(0, pairs)
            def _(pair):
                at = i * pairs + pair
                for jj in range(blocks):
                    tq = jnp.concatenate(tables(jj, i, pair, 0), axis=1)
                    tk = jnp.concatenate(tables(jj, i, pair, 1), axis=1)
                    q = stack_lanes(qkv[pair, jj, i], low)
                    k = stack_lanes(qkv[pairs + pair, jj, i], low)
                    v = stack_lanes(qkv[2 * pairs + pair, jj, i], low)
                    span = slice(jj * share, (jj + 1) * share)
                    sq = dot_rows(tq, q).astype(bf16)
                    skv = dot_rows(tk, jnp.concatenate([k, v], axis=1)).astype(bf16)
                    qs[at, :, span, :] = sq.reshape(blocks, share, 128)
                    ks[at, :, span, :] = skv[:, :128].reshape(blocks, share, 128)
                    vs[at, :, span, :] = skv[:, 128:].reshape(blocks, share, 128)
                for c in range(blocks):
                    scores = dot_lanes(qs[at, c], stack_lanes(ks[at, c], low)) * scale
                    halves = []
                    for h in range(2):
                        s = scores[:, h * cluster : (h + 1) * cluster]
                        e = jnp.exp(s - jnp.max(s, axis=1, keepdims=True))
                        halves.append((e / jnp.sum(e, axis=1, keepdims=True)).astype(bf16))
                    probs = jnp.concatenate(halves, axis=1)
                    ps[at, c] = probs
                    o = dot_rows(probs, stack_lanes(vs[at, c], low)).astype(bf16)
                    os[c] = o
                for jj in range(blocks):
                    tq = jnp.concatenate(tables(jj, i, pair, 0), axis=0)
                    rows = os[:, jj * share : (jj + 1) * share, :].reshape(cluster, 128)
                    back = dot_first(tq, stack_lanes(rows, low)).astype(bf16)
                    ctxb[jj // chips, jj % chips, i, :, pl.ds(multiple(pair * 128, 128), 128)] = back
                hook(i, pair)

        pieces = ((qs, q_out), (ks, k_out), (vs, v_out), (ps, p_out))
        copies = [
            pltpu.make_async_copy(src, dst, att_sem.at[n]) for n, (src, dst) in enumerate(pieces)
        ]
        far, own = ctx_copies()
        for copy in copies + [far, own]:
            copy.start()
        for copy in copies + [far, own]:
            copy.wait()

    def ctx_copies():
        lanes = pl.ds(multiple(core * half, 128), half)
        far = far_copy(
            ctxb.at[1 - core], ctxt.at[:, :, :, lanes], (ctx_s, ctx_r), 0, me.sibling()
        )
        own = pltpu.make_async_copy(ctxb.at[core], ctxt.at[:, :, :, lanes], att_sem.at[4])
        return far, own

    group = (per * pairs, blocks, cluster, 128)
    pl.run_scoped(
        attention,
        pltpu.VMEM((3 * pairs, blocks, per, cluster, 128), bf16),
        pltpu.VMEM(group, bf16),
        pltpu.VMEM(group, bf16),
        pltpu.VMEM(group, bf16),
        pltpu.VMEM((per * pairs, blocks, cluster, 2 * cluster), bf16),
        pltpu.VMEM((blocks, cluster, 128), bf16),
    )

    tower_wait(0)
    oc_copy().start()
    oc_copy().wait()
    emit(ctxt, ctx_out)
    context_out = outs[-1]
    emit(owbuf, ow_out)
    tile = per * cluster
    hidden = upb.shape[1]
    eps = epsilon

    def moments(rows):
        center = jnp.mean(rows, axis=1, keepdims=True)
        centered = rows - center
        spread = jnp.mean(centered * centered, axis=1, keepdims=True)
        inverse = lax.rsqrt(spread + eps)
        return centered * inverse, inverse

    def slope_out_copy(j, slot):
        return pltpu.make_async_copy(sbuf.at[slot], slope_out.at[j], slope_sem.at[slot])

    def vec(row):
        return vecs[row : row + 1, :]

    def feed(hbuf, sbuf):
        step = sbuf.shape[3]

        def slope_copy(n):
            return pltpu.make_async_copy(
                sbuf.at[n % 2],
                slope_out.at[:, :, pl.ds(n * step, step)],
                slope_sem.at[n % 2],
            )

        @pl.loop(0, chips)
        def _(j):
            rows = ctxt[j].reshape(tile, width)
            branch = dot_rows(rows, owbuf[...].reshape(width, width))
            resid = xbuf[core, j].reshape(tile, width).astype(f32) + branch + vec(2)
            normed, inverse = moments(resid)
            n1buf[j] = normed
            invbuf[j] = jnp.broadcast_to(inverse, (tile, 128))
            mlbuf[j] = (normed * vec(3) + vec(4)).astype(bf16).reshape(per, cluster, width)

        plane_last(1)
        emit(ewbuf, ew_out)
        for n in range(hidden // step):
            lanes = slice(n * step, (n + 1) * step)
            if n >= 2:
                slope_copy(n - 2).wait()
            for j in range(chips):
                weight = ewbuf[:, :, lanes].reshape(width, step)
                pre = dot_rows(mlbuf[j].reshape(tile, width), weight) + upb[0:1, lanes]
                cumulative = 0.5 * (1.0 + lax.erf(pre * 0.5**0.5))
                density = jnp.exp(-0.5 * pre * pre) * (2.0 * math.pi) ** (-0.5)
                hbuf[j, :, lanes] = (pre * cumulative).astype(bf16)
                sbuf[n % 2, j] = (cumulative + pre * density).astype(bf16)
            slope_copy(n).start()
            if n == 1:
                plane_second(2)

        emit(vecs, vec_out)
        held = len(outs)
        emit(n1buf, n1_out)
        emit(invbuf, inv_out)
        emit(mlbuf, ml_out)
        emit(hbuf, hid_out)
        plane_last(2)
        pass_end()
        emit(rwbuf, rw_out)
        for k in range(1, chips):
            cot_copy(k).wait_recv()
        sums[...] = jnp.zeros_like(sums)
        waited = (context_out, outs[held])
        for copy in waited:
            copy.wait()

        @pl.loop(0, chips)
        def _(j):
            branch = vec(5)
            for zz in range(depth):
                span = hidden // depth
                branch = branch + dot_rows(
                    hbuf[j, :, zz * span : (zz + 1) * span], rwbuf[zz].reshape(span, width)
                )
            middle = n1buf[j] * vec(3) + vec(4)
            normed, inverse = moments(middle + branch)
            upstream = cbuf[j].reshape(tile, width).astype(f32)
            cbuf[j] = (normed * vec(6) + vec(7)).astype(bf16).reshape(per, cluster, width)
            sums[0:1, :] += jnp.sum(upstream * normed, axis=0, keepdims=True)
            sums[1:2, :] += jnp.sum(upstream, axis=0, keepdims=True)
            scaled = upstream * vec(6)
            first = jnp.mean(scaled, axis=1, keepdims=True)
            second = jnp.mean(scaled * normed, axis=1, keepdims=True)
            grad = inverse * (scaled - first - normed * second)
            n1buf[j] = grad
            low_grad = grad.astype(bf16)
            sums[2:3, :] += jnp.sum(low_grad.astype(f32), axis=0, keepdims=True)
            ctxt[j] = low_grad.reshape(per, cluster, width)

        emit(cbuf, lo_out)
        emit(n1buf, gr_out)
        emit(ctxt, gb_out)
        emit(sums, sum_out)
        for copy in sends:
            copy.wait_send()
        awc.wait_recv()
        for n in range(max(hidden // step - 2, 0), hidden // step):
            slope_copy(n).wait()
        for copy in outs:
            if not any(copy is other for other in waited):
                copy.wait()

    pl.run_scoped(
        feed,
        pltpu.VMEM((chips, tile, hidden), bf16),
        pltpu.VMEM((2, chips, tile, hidden // depth), bf16),
    )


def forward(
    tokens,
    pos,
    attend_weight,
    vectors,
    output_weight,
    expand_weight,
    reduce_weight,
    cotangent,
    chips,
    depth,
    heads,
):
    seqs, cluster, width = tokens.shape
    per, blocks, pairs = seqs // chips, 2 * chips, heads // 4
    half = width // 2
    rows_z = attend_weight.shape[0]
    hidden = expand_weight.shape[1]
    items = per * pairs
    tile = per * cluster
    dma = pltpu.SemaphoreType.DMA
    anywhere = pl.BlockSpec(memory_space=pl.ANY)
    tall = reduce_weight.shape[0] // blocks
    shapes = [
        ((2, chips, per, cluster, width), bf16),
        ((chips, per, cluster, width), bf16),
        ((items, blocks, cluster, 128), bf16),
        ((items, blocks, cluster, 128), bf16),
        ((items, blocks, cluster, 128), bf16),
        ((items, blocks, cluster, 2 * cluster), bf16),
        ((2, chips, per, 2 * heads, cluster), jnp.int32),
        ((2, depth * rows_z, 3 * half), bf16),
        ((8, width), f32),
        ((depth, 2, rows_z // 2, width), bf16),
        ((depth, rows_z, hidden), bf16),
        ((depth, blocks, tall, width), bf16),
        ((chips, tile, width), f32),
        ((chips, tile, 128), f32),
        ((chips, per, cluster, width), bf16),
        ((chips, tile, hidden), bf16),
        ((chips, tile, hidden), bf16),
        ((chips, per, cluster, width), bf16),
        ((chips, tile, width), f32),
        ((chips, per, cluster, width), bf16),
        ((8, width), f32),
    ]
    t, c = depth - 1, chips - 1
    vm = pltpu.VMEM
    return pl.pallas_call(
        functools.partial(forward_kernel, chips, depth, heads),
        out_shape=[jax.ShapeDtypeStruct(*s) for s in shapes],
        in_specs=[anywhere] * 8,
        out_specs=[anywhere] * len(shapes),
        scratch_shapes=[
            vm(shapes[0][0], bf16),
            vm(shapes[6][0], jnp.int32),
            vm(shapes[7][0][1:], bf16),
            vm((depth,) + vectors.shape, f32),
            vm((2, 8, 3 * half), f32),
            vm((2, chips, per, cluster, half), bf16),
            vm(shapes[1][0], bf16),
            vm(shapes[9][0], bf16),
            vm(shapes[10][0], bf16),
            vm(shapes[11][0], bf16),
            vm(shapes[17][0], bf16),
            vm(shapes[12][0], f32),
            vm(shapes[13][0], f32),
            vm(shapes[14][0], bf16),
            vm((8, width), f32),
            vm((8, hidden), f32),
            vm((8, width), f32),
            dma((c,)), dma((c,)), dma((chips,)), dma((chips,)),
            dma((c,)), dma((c,)), dma((chips,)), dma((chips,)),
            dma((t,)), dma((t,)), dma((t,)), dma((t,)), dma((1,)), dma((1,)),
            dma((t,)), dma((t,)),
            dma((3 * t,)), dma((3 * t,)),
            dma((4,)), dma((4,)), dma((4,)), dma((4,)),
            dma((2 * chips,)), dma((2 * chips,)),
            dma((1,)), dma((1,)),
            dma((c,)), dma((c,)),
            dma((1,)), dma((1,)),
            dma((12,)), dma((24,)), dma((2,)), dma((5,)),
        ],
        compiler_params=pltpu.CompilerParams(
            collective_id=1, has_side_effects=True, vmem_limit_bytes=63 * 2**20
        ),
        name="forward",
    )(
        tokens,
        pos,
        attend_weight,
        vectors,
        output_weight,
        expand_weight,
        reduce_weight,
        cotangent,
    )


def add_into(target, at, parts):
    total = target[at].astype(f32)
    for part in parts:
        total = total + part.astype(f32)
    target[at] = total.astype(target.dtype)


class Reducer:
    def __init__(self, me, own, other, near, mid, last, done, sems, tower_first):
        self.me, self.own, self.other = me, own, other
        self.near, self.mid, self.last, self.done = near, mid, last, done
        (self.near_s, self.near_r, self.mid_s, self.mid_r, self.last_s, self.last_r) = sems[:6]
        (self.back_s, self.back_r, self.side_s, self.side_r) = sems[6:10]
        self.tower_first = tower_first
        self.sizes = (mid.shape[0] + 1, last.shape[0] + 1)

    def spot(self, axis, k):
        me = self.me
        if self.tower_first == (axis == 0):
            return me.z_at(k), me.tower(k)
        return me.chip_at(k), me.plane(k)

    def near_copy(self, a):
        return far_copy(
            self.other.at[a], self.near.at[a], (self.near_s, self.near_r), a, self.me.sibling()
        )

    def fold_near(self, a):
        self.near_copy(a).wait_recv()
        for b in range(self.sizes[1]):
            add_into(self.own, (a, b), [self.near[a, b]])

    def mid_copy(self, k):
        where, device = self.spot(0, k)
        return far_copy(
            self.own.at[where], self.mid.at[k - 1], (self.mid_s, self.mid_r), k - 1, device
        )

    def send_mid(self):
        for k in range(1, self.sizes[0]):
            self.mid_copy(k).start()

    def fold_mid(self):
        for k in range(1, self.sizes[0]):
            self.mid_copy(k).wait()
        here = self.spot(0, 0)[0]
        for b in range(self.sizes[1]):
            add_into(self.own, (here, b), [self.mid[k - 1, b] for k in range(1, self.sizes[0])])

    def last_copy(self, k):
        here = self.spot(0, 0)[0]
        where, device = self.spot(1, k)
        return far_copy(
            self.own.at[here, where],
            self.last.at[k - 1],
            (self.last_s, self.last_r),
            k - 1,
            device,
        )

    def send_last(self):
        for k in range(1, self.sizes[1]):
            self.last_copy(k).start()

    def fold_last(self):
        me = self.me
        for k in range(1, self.sizes[1]):
            self.last_copy(k).wait()
        total = self.own[self.spot(0, 0)[0], self.spot(1, 0)[0]].astype(f32)
        for k in range(1, self.sizes[1]):
            total = total + self.last[k - 1].astype(f32)
        self.done[me.core, me.chip] = total.astype(bf16)

    def back_copy(self, k):
        me = self.me
        spot = self.done.at[me.core, me.chip]
        return far_copy(spot, spot, (self.back_s, self.back_r), k - 1, me.plane(k))

    def send_back(self):
        for k in range(1, self.done.shape[1]):
            self.back_copy(k).start()

    def side_copy(self):
        spot = self.done.at[self.me.core]
        return far_copy(spot, spot, (self.side_s, self.side_r), 0, self.me.sibling())

    def send_side(self):
        for k in range(1, self.done.shape[1]):
            self.back_copy(k).wait()
        self.side_copy().start()

    def finish(self):
        self.side_copy().wait()


class Sum:
    def __init__(self, me, vec, got, s, r):
        self.me, self.vec, self.got, self.s, self.r = me, vec, got, s, r

    def copies(self, hop):
        me = self.me
        if hop == 0:
            spots = [(0, me.sibling())]
        elif hop == 1:
            spots = [(k, me.plane(k)) for k in range(1, me.chips)]
        else:
            spots = [(me.chips + k - 1, me.tower(k)) for k in range(1, me.depth)]
        return [far_copy(self.vec, self.got.at[n], (self.s, self.r), n, d) for n, d in spots], spots

    def send(self, hop):
        for copy in self.copies(hop)[0]:
            copy.start()

    def fold(self, hop):
        copies, spots = self.copies(hop)
        for copy in copies:
            copy.wait()
        total = self.vec[...]
        for n, _ in spots:
            total = total + self.got[n]
        self.vec[...] = total


def back_kernel(
    chips,
    depth,
    heads,
    q_ref,
    k_ref,
    v_ref,
    p_ref,
    pos_ref,
    x_ref,
    aw_ref,
    ow_ref,
    ew_ref,
    rw_ref,
    vec_ref,
    ctx_ref,
    n1_ref,
    inv_ref,
    ml_ref,
    hid_ref,
    slope_ref,
    lo_ref,
    gr_ref,
    gb_ref,
    late_ref,
    token_out,
    layer_out,
    aw_out,
    ow_out,
    ew_out,
    rw_out,
    vec_out,
    bias_out,
    dbuf,
    posbuf,
    acc,
    gfar,
    a_mid,
    a_last,
    a_done,
    c_mid,
    c_last,
    c_done,
    o_all,
    o_near,
    o_mid,
    o_last,
    o_done,
    e_all,
    e_near,
    e_mid,
    e_last,
    e_done,
    r_all,
    r_near,
    r_mid,
    r_last,
    r_done,
    vbuf,
    vgot,
    bbuf,
    bgot,
    vecs,
    d_s,
    d_r,
    g_s,
    g_r,
    t_s,
    t_r,
    lo_s,
    lo_r,
    load,
    out_sem,
    v_s,
    v_r,
    b_s,
    b_r,
    *sems,
):
    me = Place(chips, depth)
    z, core, chip = me.z, me.core, me.chip
    per, cluster, width = lo_ref.shape[1:]
    half = width // 2
    pairs = heads // 4
    size = half // (2 * pairs)
    blocks = 2 * chips
    share = cluster // blocks
    tile = per * cluster
    hidden = hid_ref.shape[2]
    wide = hidden // blocks
    strip = width // chips
    quarter = width // depth
    eighth = quarter // blocks
    rows = chips * tile
    me.greet()
    groups = [sems[n * 10 : (n + 1) * 10] for n in range(5)]
    red = Reducer(
        me, r_all.at[core], r_all.at[1 - core], r_near, r_mid, r_last, r_done, groups[0], True
    )
    exp = Reducer(
        me, e_all.at[core], e_all.at[1 - core], e_near, e_mid, e_last, e_done, groups[1], False
    )
    out = Reducer(
        me, o_all.at[core], o_all.at[1 - core], o_near, o_mid, o_last, o_done, groups[2], False
    )
    sums = Sum(me, vbuf, vgot, v_s, v_r)
    biases = Sum(me, bbuf, bgot, b_s, b_r)

    def fetch(src, dst, at):
        return pltpu.make_async_copy(src, dst, load.at[at])

    def lo_copy(k):
        return far_copy(
            lo_ref.at[me.chip_at(k)],
            layer_out.at[pl.ds(chip * per, per)],
            (lo_s, lo_r),
            k - 1,
            me.plane(k),
        )

    lo_keep = pltpu.make_async_copy(
        lo_ref.at[chip], layer_out.at[pl.ds(chip * per, per)], out_sem.at[0]
    )

    block = 2 * wide
    counts = blocks // 2

    def order(n):
        return lax.rem(n + z + chip, counts)

    def fold(n):
        at = order(n)
        red.fold_near(at)
        k = lax.rem(at - z + depth, depth)

        @pl.when(k != 0)
        def _():
            red.mid_copy(k).start()

        @pl.when(lax.div(at, 2) == core)
        def _():
            for side in range(2):
                b = lax.rem(at, 2) * 2 + side
                exp.fold_near(b)
                k = lax.rem(b - chip + chips, chips)

                @pl.when(k != 0)
                def _():
                    exp.mid_copy(k).start()

    def chunks(gb, gbt, mlt, hid, slope, rwc, ewc, gpb):
        def chunk(n, slot):
            at = order(n)
            lanes = pl.ds(multiple(at * block, 128), block)
            return [
                fetch(hid_ref.at[:, :, lanes], hid.at[slot], slot * 4),
                fetch(slope_ref.at[:, :, lanes], slope.at[slot], slot * 4 + 1),
                fetch(rw_ref.at[at], rwc.at[slot], slot * 4 + 2),
                fetch(ew_ref.at[:, :, lanes], ewc.at[slot], slot * 4 + 3),
            ]

        begin = [
            fetch(gb_ref, gb, 8),
            fetch(ml_ref, gpb, 9),
            fetch(gr_ref, acc, 10),
        ]
        later = [
            fetch(vec_ref, vecs, 11),
            fetch(late_ref, vbuf.at[pl.ds(0, 8)], 12),
            fetch(pos_ref, posbuf, 18),
        ]
        for copy in begin + chunk(0, 0) + later:
            copy.start()
        for k in range(1, chips):
            lo_copy(k).start()
        lo_keep.start()
        vbuf[8:, :] = jnp.zeros((blocks, width), f32)
        for copy in begin:
            copy.wait()
        for j in range(chips):
            span = slice(j * tile, (j + 1) * tile)
            mlt[:, span] = jnp.transpose(gpb[j].reshape(tile, width))
            gbt[:, span] = jnp.transpose(gb[j].reshape(tile, width))
        for copy in later:
            copy.wait()

        @pl.loop(0, counts)
        def _(n):
            slot = lax.rem(n, 2)
            at = order(n)
            for copy in chunk(n, slot):
                copy.wait()

            @pl.when(n + 1 < counts)
            def _():
                for copy in chunk(n + 1, 1 - slot):
                    copy.start()

            up = rwc[slot].reshape(block, width)
            down = ewc[slot].reshape(width, block)
            total = jnp.zeros((1, block), f32)
            for j in range(chips):
                grad = dot_lanes(gb[j].reshape(tile, width), up)
                low = (grad * slope[slot, j].astype(f32)).astype(bf16)
                gpb[j] = low.reshape(per, cluster, block)
                acc[j] += dot_lanes(low, down)
                total = total + jnp.sum(low.astype(f32), axis=0, keepdims=True)
            vbuf[pl.ds(8 + at, 1), :block] = total
            term = dot_rows(gbt[...], hid[slot].reshape(rows, block)).astype(bf16)
            for side in range(2):
                r_all[side, at] = term[:, side * wide : (side + 1) * wide].reshape(
                    chips, strip, wide
                )
            red.near_copy(at).start()
            term = dot_rows(mlt[...], gpb[...].reshape(rows, block)).astype(bf16)
            for side in range(2):
                e_all[lax.div(at, 2), lax.rem(at, 2) * 2 + side] = term[
                    :, side * wide : (side + 1) * wide
                ].reshape(depth, quarter, wide)

            @pl.when(lax.div(at, 2) != core)
            def _():
                for side in range(2):
                    exp.near_copy(lax.rem(at, 2) * 2 + side).start()

            @pl.when(n > 0)
            def _():
                fold(n - 1)

    def first_norm(gb, n1, inv, ctx, ow, dsnd):
        later = [
            fetch(ctx_ref, ctx, 13),
            fetch(ow_ref, ow, 14),
            fetch(inv_ref, inv, 15),
        ]
        def n1_copy(j):
            return fetch(n1_ref.at[j], n1.at[j % 2], 16 + j % 2)

        def d_copy(j):
            return far_copy(dsnd.at[j], dbuf.at[core, j], (d_s, d_r), j, me.sibling())

        n1_copy(0).start()
        for copy in later:
            copy.start()
        fold(counts - 1)
        for copy in later:
            copy.wait()
        gain = vecs[3:4, :]
        for row in range(3, 8):
            vbuf[row : row + 1, :] = jnp.zeros((1, width), f32)
        for j in range(chips):
            n1_copy(j).wait()
            if j + 1 < chips:
                n1_copy(j + 1).start()
            grad = acc[j]
            normed = n1[j % 2]
            vbuf[3:4, :] += jnp.sum(grad * normed, axis=0, keepdims=True)
            vbuf[4:5, :] += jnp.sum(grad, axis=0, keepdims=True)
            scaled = grad * gain
            first = jnp.mean(scaled, axis=1, keepdims=True)
            second = jnp.mean(scaled * normed, axis=1, keepdims=True)
            grad = inv[j][:, :1] * (scaled - first - normed * second)
            acc[j] = grad
            low = grad.astype(bf16)
            gb[j] = low.reshape(per, cluster, width)
            vbuf[5:6, :] += jnp.sum(low.astype(f32), axis=0, keepdims=True)
            back = dot_lanes(low, ow[...].reshape(width, width)).astype(bf16)

            for c in range(2):
                piece = back[:, c * half : (c + 1) * half]

                @pl.when(core == c)
                def _():
                    dbuf[c, j] = piece.reshape(per, cluster, half)

                @pl.when(core != c)
                def _():
                    dsnd[j] = piece.reshape(per, cluster, half)

            d_copy(j).start()
        sums.send(0)
        term = dot_first(ctx[...].reshape(rows, width), gb[...].reshape(rows, width))
        for zz in range(depth):
            for c in range(2):
                for p in range(chips):
                    begin_at = zz * quarter + (c * chips + p) * eighth
                    o_all[c, p, zz] = term[begin_at : begin_at + eighth, :].astype(bf16)
        for p in range(chips):
            out.near_copy(p).start()
        for j in range(chips):
            d_copy(j).wait()
        for a in range(depth):
            red.near_copy(a).wait_send()
        for b in range(chips):
            exp.near_copy(b).wait_send()

    shape = (chips, per, cluster, width)
    vm = pltpu.VMEM

    def feed_back(gb):
        pl.run_scoped(
            functools.partial(chunks, gb),
            vm((width, rows), bf16),
            vm((width, rows), bf16),
            vm((2, chips, tile, block), bf16),
            vm((2, chips, tile, block), bf16),
            vm((2, blocks, block // blocks, width), bf16),
            vm((2, depth, quarter, block), bf16),
            vm(shape[:3] + (block,), bf16),
        )
        pl.run_scoped(
            functools.partial(first_norm, gb),
            vm((2, tile, width), f32),
            vm((chips, tile, 128), f32),
            vm(shape, bf16),
            vm((depth, 2, quarter // 2, width), bf16),
            vm((chips, per, cluster, half), bf16),
        )

    pl.run_scoped(feed_back, vm(shape, bf16))

    def attend_back(qs, ks, vs, ps, xbuf, wbuf, ds, gs, gbuf, tbuf, dw, dwa, dwc):
        att = Reducer(me, dwa, None, None, a_mid, a_last, a_done, groups[3], False)
        rest = Reducer(me, dwc, None, None, c_mid, c_last, c_done, groups[4], True)
        cut = dwa.shape[3]

        def loads(i, slot):
            span = pl.ds(i * pairs, pairs)
            pieces = (
                (q_ref.at[span], qs),
                (k_ref.at[span], ks),
                (v_ref.at[span], vs),
                (p_ref.at[span], ps),
            )
            return [fetch(src, dst.at[slot], slot * 4 + n) for n, (src, dst) in enumerate(pieces)]

        def load_x(i):
            return fetch(x_ref.at[:, :, i], xbuf, 8)

        load_w = fetch(aw_ref, wbuf, 9)
        for copy in loads(0, 0) + [load_x(0), load_w]:
            copy.start()
        bbuf[...] = jnp.zeros_like(bbuf)
        slots = lax.broadcasted_iota(jnp.int32, (cluster, cluster), 0)
        low = lax.broadcasted_iota(jnp.int32, (cluster, 128), 1) < size
        scale = size ** (-0.5)

        def tables(jj, i, pair, part):
            begin = part * heads + core * (heads // 2) + 2 * pair
            return [
                one_hot(posbuf[jj // chips, jj % chips, i, pl.ds(begin + h, 1), :], slots)
                for h in range(2)
            ]

        def clusters(i, slot, pair):
            lanes = pl.ds(multiple(pair * 128, 128), 128)
            for jj in range(blocks):
                tq = jnp.concatenate(tables(jj, i, pair, 0), axis=1)
                rows = stack_lanes(dbuf[jj // chips, jj % chips, i, :, lanes], low)
                ds[:, jj * share : (jj + 1) * share, :] = (
                    dot_rows(tq, rows).astype(bf16).reshape(blocks, share, 128)
                )
            for c in range(blocks):
                d = ds[c]
                probs = ps[slot, pair, c]
                slope = dot_lanes(d, stack_lanes(vs[slot, pair, c], low))
                broad = probs.astype(f32)
                halves = []
                for h in range(2):
                    span = slice(h * cluster, (h + 1) * cluster)
                    inner = jnp.sum(broad[:, span] * slope[:, span], axis=1, keepdims=True)
                    halves.append((broad[:, span] * (slope[:, span] - inner)).astype(bf16))
                grads = jnp.concatenate(halves, axis=1)
                gq = dot_rows(grads, stack_lanes(ks[slot, pair, c], low)) * scale
                gk = dot_first(grads, qs[slot, pair, c]) * scale
                gv = dot_first(probs, d)
                gs[0, c] = gq.astype(bf16)
                gs[1, c] = jnp.where(low, gk[:cluster], gk[cluster:]).astype(bf16)
                gs[2, c] = jnp.where(low, gv[:cluster], gv[cluster:]).astype(bf16)
            for jj in range(blocks):
                for part in range(3):
                    if part < 2:
                        table = jnp.concatenate(tables(jj, i, pair, part), axis=0)
                    rows = gs[part, :, jj * share : (jj + 1) * share, :].reshape(cluster, 128)
                    back = dot_first(table, stack_lanes(rows, low))
                    to = pl.ds(multiple(part * half + pair * 128, 128), 128)
                    gbuf[slot, jj // chips, jj % chips, :, to] = back.astype(bf16)

        def give(slot):
            return far_copy(gbuf.at[slot, 1 - core], gfar.at[slot], (g_s, g_r), slot, me.sibling())

        def token_copy(i, slot, k):
            return far_copy(
                tbuf.at[slot, me.chip_at(k)],
                token_out.at[chip * per + i],
                (t_s, t_r),
                i * (chips - 1) + k - 1,
                me.plane(k),
            )

        def token_keep(i, slot):
            return pltpu.make_async_copy(
                tbuf.at[slot, chip], token_out.at[chip * per + i], out_sem.at[1 + i]
            )

        def token_rows(i, slot):
            give(slot).wait()
            for j in range(chips):
                near = dot_lanes(gbuf[slot, core, j], wbuf[core])
                distant = dot_lanes(gfar[slot, j], wbuf[1 - core])
                resid = acc[j, i * cluster : (i + 1) * cluster, :]
                tbuf[slot, j] = (resid + near + distant).astype(bf16)
            token_keep(i, slot).start()
            for k in range(1, chips):
                token_copy(i, slot, k).start()

        ready = []

        def emit(src, dst):
            copy = pltpu.make_async_copy(src, dst, out_sem.at[1 + per + len(ready)])
            copy.start()
            ready.append(copy)

        def step_out_near():
            for p in range(chips):
                out.fold_near(p)
            out.send_mid()
            for p in range(chips):
                out.near_copy(p).wait_send()
            sums.fold(0)
            sums.send(1)

        def step_exp_mid():
            exp.fold_mid()
            exp.send_last()

        def step_red_mid():
            red.fold_mid()
            red.send_last()
            sums.fold(1)
            sums.send(2)

        def step_exp_last():
            exp.fold_last()
            exp.send_back()
            out.fold_mid()
            out.send_last()

        def step_red_last():
            red.fold_last()
            red.send_back()
            sums.fold(2)

        def step_out_last():
            out.fold_last()
            out.send_back()
            exp.send_side()

        def step_sides():
            red.send_side()
            out.send_side()

        hooks = {}
        steps = [
            step_out_near,
            step_exp_mid,
            step_red_mid,
            step_exp_last,
            step_red_last,
            step_out_last,
            step_sides,
        ]
        for n, step in enumerate(steps):
            hooks.setdefault(min(n, per * pairs - 1), []).append(step)

        for i in range(per):
            slot = i % 2
            for copy in loads(i, slot):
                copy.wait()
            if i == 0:
                load_w.wait()
            if i >= 1:
                token_rows(i - 1, 1 - slot)
            if i + 1 < per:
                for copy in loads(i + 1, 1 - slot):
                    copy.start()

            @pl.loop(0, pairs)
            def _(pair):
                clusters(i, slot, pair)
                for n in range(pairs):
                    if hooks.get(i * pairs + n):

                        @pl.when(pair == n)
                        def _():
                            for step in hooks[i * pairs + n]:
                                step()

            if i >= 2:
                token_keep(i - 2, slot).wait()
                for k in range(1, chips):
                    token_copy(i - 2, slot, k).wait()
            give(slot).start()
            load_x(i).wait()
            for b in range(2):
                x = jnp.concatenate([xbuf[b, j] for j in range(chips)], axis=0)
                g = jnp.concatenate([gbuf[slot, b, j] for j in range(chips)], axis=0)
                term = dot_first(x, g)
                if i == 0 and b == 0:
                    dw[...] = term
                else:
                    dw[...] += term
                bbuf[0:1, :] += jnp.sum(g.astype(f32), axis=0, keepdims=True)
            if i + 1 < per:
                load_x(i + 1).start()

        depth_rows = quarter // chips
        for a in range(depth):
            for b in range(chips):
                begin = (a * chips + b) * depth_rows
                dwa[b, a] = dw[begin : begin + depth_rows, :cut].astype(bf16)
                dwc[a, b] = dw[begin : begin + depth_rows, cut:].astype(bf16)
        att.send_mid()
        rest.send_mid()
        biases.send(1)
        token_rows(per - 1, (per - 1) % 2)
        emit(vbuf, vec_out)
        exp.finish()
        for c in range(2):
            for p in range(chips):
                emit(e_done.at[c, p], ew_out.at[:, pl.ds((c * chips + p) * wide, wide)])
        red.finish()
        for c in range(2):
            emit(r_done.at[c], rw_out.at[:, :, pl.ds(c * wide, wide)])
        out.finish()
        emit(o_done, ow_out)
        biases.fold(1)
        biases.send(2)
        att.fold_mid()
        att.send_last()
        rest.fold_mid()
        rest.send_last()
        biases.fold(2)
        share_bias = far_copy(bbuf, bias_out.at[core], (b_s, b_r), 0, me.sibling())
        share_bias.start()
        emit(bbuf, bias_out.at[core])
        att.fold_last()
        att.send_back()
        rest.fold_last()
        rest.send_back()
        att.send_side()
        rest.send_side()
        for reducer, done, begin in ((att, a_done, 0), (rest, c_done, cut)):
            reducer.finish()
            end = begin + done.shape[3]
            for part in range(3):
                lo, hi = max(begin, part * half), min(end, (part + 1) * half)
                for c in range(2):
                    if lo < hi:
                        emit(
                            done.at[c, :, :, pl.ds(lo - begin, hi - lo)],
                            aw_out.at[:, :, pl.ds((part + c) * half + lo, hi - lo)],
                        )
        for i in range(max(per - 2, 0), per):
            token_keep(i, i % 2).wait()
            for k in range(1, chips):
                token_copy(i, i % 2, k).wait()
        share_bias.wait()
        for copy in ready:
            copy.wait()
        lo_keep.wait()
        for k in range(1, chips):
            lo_copy(k).wait()

    group = (2, pairs, blocks, cluster)
    pl.run_scoped(
        attend_back,
        vm(group + (128,), bf16),
        vm(group + (128,), bf16),
        vm(group + (128,), bf16),
        vm(group + (2 * cluster,), bf16),
        vm((2, chips, cluster, width), bf16),
        vm(aw_ref.shape, bf16),
        vm((blocks, cluster, 128), bf16),
        vm((3, blocks, cluster, 128), bf16),
        vm((2, 2, chips, cluster, 3 * half), bf16),
        vm((2, chips, cluster, width), bf16),
        vm((width, 3 * half), f32),
        vm((chips, depth, quarter // chips, a_mid.shape[3]), bf16),
        vm((depth, chips, quarter // chips, c_mid.shape[3]), bf16),
    )


def back(arrays, depth, heads):
    chips, per, cluster, width = arrays[17].shape
    half, blocks = width // 2, 2 * chips
    dma = pltpu.SemaphoreType.DMA
    anywhere = pl.BlockSpec(memory_space=pl.ANY)
    quarter = width // depth
    hidden = arrays[15].shape[2]
    eighth, strip, wide = quarter // blocks, width // chips, hidden // blocks
    rows = quarter // chips
    c, t = chips - 1, depth - 1
    cut = 3 * half // 128 * 5 // 9 * 128
    shapes = [
        ((chips * per, cluster, width), bf16),
        ((chips * per, cluster, width), bf16),
        ((chips, rows, 3 * width), bf16),
        ((2, chips, eighth, width), bf16),
        ((quarter, hidden), bf16),
        ((chips, strip, 2 * wide), bf16),
        ((8 + blocks, width), f32),
        ((2, 8, 3 * half), f32),
    ]
    vm = pltpu.VMEM

    def reducing(near, first, second):
        return [
            dma((near,)), dma((near,)),
            dma((first,)), dma((first,)),
            dma((second,)), dma((second,)),
            dma((c,)), dma((c,)),
            dma((1,)), dma((1,)),
        ]

    return pl.pallas_call(
        functools.partial(back_kernel, chips, depth, heads),
        out_shape=[jax.ShapeDtypeStruct(*s) for s in shapes],
        in_specs=[anywhere] * len(arrays),
        out_specs=[anywhere] * len(shapes),
        scratch_shapes=[
            vm((2, chips, per, cluster, half), bf16),
            vm(arrays[4].shape, jnp.int32),
            vm((chips, per * cluster, width), f32),
            vm((2, chips, cluster, 3 * half), bf16),
            vm((c, depth, rows, cut), bf16),
            vm((t, rows, cut), bf16),
            vm((2, chips, rows, cut), bf16),
            vm((t, chips, rows, 3 * half - cut), bf16),
            vm((c, rows, 3 * half - cut), bf16),
            vm((2, chips, rows, 3 * half - cut), bf16),
            vm((2, chips, depth, eighth, width), bf16),
            vm((chips, depth, eighth, width), bf16),
            vm((c, depth, eighth, width), bf16),
            vm((t, eighth, width), bf16),
            vm((2, chips, eighth, width), bf16),
            vm((2, chips, depth, quarter, wide), bf16),
            vm((chips, depth, quarter, wide), bf16),
            vm((c, depth, quarter, wide), bf16),
            vm((t, quarter, wide), bf16),
            vm((2, chips, quarter, wide), bf16),
            vm((2, depth, chips, strip, wide), bf16),
            vm((depth, chips, strip, wide), bf16),
            vm((t, chips, strip, wide), bf16),
            vm((c, strip, wide), bf16),
            vm((2, chips, strip, wide), bf16),
            vm((8 + blocks, width), f32),
            vm((chips + t, 8 + blocks, width), f32),
            vm((8, 3 * half), f32),
            vm((chips + t, 8, 3 * half), f32),
            vm((8, width), f32),
            dma((chips,)), dma((chips,)), dma((2,)), dma((2,)),
            dma((per * c,)), dma((per * c,)),
            dma((c,)), dma((c,)),
            dma((19,)), dma((1 + per + 16 + blocks,)),
            dma((chips + t,)), dma((chips + t,)), dma((chips + t,)), dma((chips + t,)),
            *reducing(depth, t, c),
            *reducing(chips, c, t),
            *reducing(chips, c, t),
            *reducing(1, c, t),
            *reducing(1, t, c),
        ],
        compiler_params=pltpu.CompilerParams(
            collective_id=2, has_side_effects=True, vmem_limit_bytes=63 * 2**20
        ),
        name="back",
    )(*arrays)


def places(rank, cluster, share):
    seqs, rows, length = rank.shape
    clusters = cluster // share
    target = rank // cluster
    which = lax.broadcasted_iota(jnp.int32, (1, 1, clusters, 1), 2)
    inside = (target[:, :, None, :] == which).astype(bf16)
    first = lax.broadcasted_iota(jnp.int32, (length, length), 0)
    second = lax.broadcasted_iota(jnp.int32, (length, length), 1)
    before = (first < second).astype(bf16)
    count = lax.dot_general(
        inside.reshape(seqs * rows * clusters, length),
        before,
        (((1,), (0,)), ((), ())),
        preferred_element_type=f32,
    ).reshape(seqs, rows, clusters, length)
    spot = which.astype(f32) * share + count
    return jnp.sum(inside.astype(f32) * spot, axis=2).astype(jnp.int32)


def per_chip(
    tokens,
    attend_weight,
    query_bias,
    value_bias,
    output_weight,
    output_bias,
    first_gain,
    first_shift,
    expand_weight,
    expand_bias,
    reduce_weight,
    reduce_bias,
    second_gain,
    second_shift,
    query_rank,
    key_rank,
    cotangent,
):
    seqs, cluster, width = tokens.shape
    heads = query_rank.shape[1]
    owners = lax.axis_size("seq")
    depth = lax.axis_size("batch")
    chips = owners // 2
    half = width // 2
    share = cluster // owners
    pos = places(jnp.concatenate([query_rank, key_rank], axis=1), cluster, share)
    quarter = width // depth
    lines = [
        query_bias,
        value_bias,
        output_bias,
        first_gain,
        first_shift,
        reduce_bias,
        second_gain,
        second_shift,
    ]
    lines += [
        expand_bias[at : at + quarter] for at in range(0, expand_bias.shape[0], quarter)
    ]
    vectors = jnp.zeros((16 * 256,), f32)
    for row, v in enumerate(lines):
        vectors += jnp.pad(v.astype(f32), (row * 256, (16 - row) * 256 - quarter))
    vectors = vectors.reshape(16, 256)
    (
        x_all,
        context,
        qs,
        ks,
        vs,
        ps,
        pos_all,
        attend_all,
        vecs,
        out_all,
        exp_all,
        red_all,
        normed_one,
        inverse_one,
        middle_low,
        hidden,
        slope,
        layer_out,
        grad_resid_two,
        grad_branch_two,
        late_sums,
    ) = forward(
        tokens,
        pos,
        attend_weight,
        vectors,
        output_weight,
        expand_weight,
        reduce_weight,
        cotangent,
        chips,
        depth,
        heads,
    )
    token_grad, layer_out, aw_grad, ow_grad, ew_grad, rw_grad, vec_sum, bias_sum = back(
        (
            qs,
            ks,
            vs,
            ps,
            pos_all,
            x_all,
            attend_all,
            out_all,
            exp_all,
            red_all,
            vecs,
            context,
            normed_one,
            inverse_one,
            middle_low,
            hidden,
            slope,
            layer_out,
            grad_resid_two,
            grad_branch_two,
            late_sums,
        ),
        depth,
        heads,
    )
    z = lax.axis_index("batch")
    six = lax.dynamic_slice_in_dim(vec_sum[:6], z * quarter, quarter, 1)
    up = lax.dynamic_index_in_dim(vec_sum[8:], z, 0, keepdims=False)
    both = jnp.concatenate([bias_sum[0, 0], bias_sum[1, 0]]).reshape(2, 3, half)
    query_value = jnp.transpose(both, (1, 0, 2)).reshape(3, width)
    query_value = lax.dynamic_slice_in_dim(query_value, z * quarter, quarter, 1)
    return (
        layer_out,
        token_grad,
        aw_grad.reshape(quarter, 3 * width).astype(f32),
        query_value[0],
        query_value[2],
        ow_grad.reshape(quarter, width).astype(f32),
        six[5],
        six[3],
        six[4],
        ew_grad.astype(f32),
        up,
        jnp.transpose(rw_grad.reshape(width, -1)).astype(f32),
        six[2],
        six[0],
        six[1],
    )


def layer(mesh):
    def run(*arrays):
        seqs, cluster, width = arrays[0].shape
        heads = arrays[14].shape[1]
        owners, depth = mesh.shape["seq"], mesh.shape["batch"]
        chips = owners // 2
        fits = (
            owners % 2 == 0
            and chips > 1
            and depth == chips == 4
            and seqs % chips == 0
            and cluster == 128
            and heads % 4 == 0
            and width == heads * 64
            and cluster == 16 * owners
            and arrays[8].shape[1] == 4 * width
        )
        return (per_chip if fits else per_device)(*arrays)

    return run


def solution(mesh):
    in_specs = (
        P("batch", "seq", None),
        P("batch", None),
        P("batch"),
        P("batch"),
        P("batch", None),
        P("batch"),
        P("batch"),
        P("batch"),
        P("batch", None),
        P("batch"),
        P("batch", None),
        P("batch"),
        P("batch"),
        P("batch"),
        P("batch", None, "seq"),
        P("batch", None, "seq"),
        P("batch", "seq", None),
    )
    out_specs = (
        P("batch", "seq", None),
        P("batch", "seq", None),
        P("batch", None),
        P("batch"),
        P("batch"),
        P("batch", None),
        P("batch"),
        P("batch"),
        P("batch"),
        P("batch", None),
        P("batch"),
        P("batch", None),
        P("batch"),
        P("batch"),
        P("batch"),
    )
    return jax.shard_map(
        layer(mesh), mesh=mesh, in_specs=in_specs, out_specs=out_specs, check_vma=False
    )
```

```python
import functools
import math

import jax
import jax.numpy as jnp
from jax import lax
from jax.experimental import pallas as pl
from jax.experimental.pallas import tpu as pltpu
from jax.sharding import PartitionSpec as P

epsilon = 1e-05


def layer_norm(resid, gain, shift):
    center = jnp.mean(resid, axis=-1, keepdims=True)
    centered = resid - center
    spread = jnp.mean(centered * centered, axis=-1, keepdims=True)
    inverse = lax.rsqrt(spread + epsilon)
    normed = centered * inverse
    return (normed * gain + shift, normed, inverse)


def norm_back(upstream, normed, inverse, gain):
    scaled = upstream * gain
    first_mean = jnp.mean(scaled, axis=-1, keepdims=True)
    second_mean = jnp.mean(scaled * normed, axis=-1, keepdims=True)
    return inverse * (scaled - first_mean - normed * second_mean)


def gelu_slope(value):
    cumulative = 0.5 * (1.0 + lax.erf(value * 0.5**0.5))
    density = jnp.exp(-0.5 * value * value) * (2.0 * math.pi) ** (-0.5)
    return cumulative + value * density


def transpose_left(first, second):
    return lax.dot_general(
        first, second, (((0,), (0,)), ((), ())), preferred_element_type=jnp.float32
    )


def transpose_right(first, second):
    return lax.dot_general(
        first, second, (((1,), (1,)), ((), ())), preferred_element_type=jnp.float32
    )


def group_table(rank, cluster, owners):
    share = cluster // owners
    target = rank // cluster
    length = rank.shape[-1]
    places = lax.broadcasted_iota(jnp.int32, (length, length), 0)
    later = lax.broadcasted_iota(jnp.int32, (length, length), 1)
    before = (places < later)[None, None]
    same = target[..., :, None] == target[..., None, :]
    earlier = jnp.sum((same & before).astype(jnp.int32), axis=-2)
    position = target * share + earlier
    slots = lax.broadcasted_iota(jnp.int32, position.shape + (length,), 3)
    return (position[..., None] == slots).astype(jnp.bfloat16)


def sort_heads(rows, table, heads):
    seqs, length, width = rows.shape
    split = rows.reshape(seqs, length, heads, width // heads)
    moved = jnp.einsum("shtp,sthd->sphd", table, split, preferred_element_type=jnp.float32)
    return moved.astype(rows.dtype).reshape(seqs, length, width)


def unsort_heads(rows, table, heads):
    seqs, length, width = rows.shape
    split = rows.reshape(seqs, length, heads, width // heads)
    moved = jnp.einsum("shtp,sphd->sthd", table, split, preferred_element_type=jnp.float32)
    return moved.astype(rows.dtype).reshape(seqs, length, width)


def cluster_scores(queries, keys_rows, heads):
    items, length, width = queries.shape
    size = width // heads
    query_split = queries.reshape(items, length, heads, size)
    key_split = keys_rows.reshape(items, length, heads, size)
    scores = jnp.einsum(
        "sqhd,skhd->shqk", query_split, key_split, preferred_element_type=jnp.float32
    )
    return scores * size ** (-0.5)


def cluster_forward(queries, keys_rows, values_rows, heads):
    items, length, width = queries.shape
    scores = cluster_scores(queries, keys_rows, heads)
    top = jnp.max(scores, axis=-1, keepdims=True)
    weights = jnp.exp(scores - top)
    total = jnp.sum(weights, axis=-1, keepdims=True)
    probs = (weights / total).astype(jnp.bfloat16)
    value_split = values_rows.reshape(items, length, heads, width // heads)
    context = jnp.einsum("shqk,skhd->sqhd", probs, value_split, preferred_element_type=jnp.float32)
    return (
        context.reshape(items, length, width).astype(jnp.bfloat16),
        (top + jnp.log(total))[..., 0],
    )


def cluster_backward(scores, log_total, queries, keys_rows, values_rows, grad_context, heads):
    items, length, width = queries.shape
    size = width // heads
    query_split = queries.reshape(items, length, heads, size)
    key_split = keys_rows.reshape(items, length, heads, size)
    value_split = values_rows.reshape(items, length, heads, size)
    grad_split = grad_context.reshape(items, length, heads, size)
    probs = jnp.exp(scores - log_total[..., None])
    grad_probs = jnp.einsum(
        "sqhd,skhd->shqk", grad_split, value_split, preferred_element_type=jnp.float32
    )
    inner = jnp.sum(probs * grad_probs, axis=-1, keepdims=True)
    grad_scores = (probs * (grad_probs - inner)).astype(jnp.bfloat16)
    scale = size ** (-0.5)
    grad_query = (
        jnp.einsum("shqk,skhd->sqhd", grad_scores, key_split, preferred_element_type=jnp.float32)
        * scale
    )
    grad_key = (
        jnp.einsum("shqk,sqhd->skhd", grad_scores, query_split, preferred_element_type=jnp.float32)
        * scale
    )
    grad_value = jnp.einsum(
        "shqk,sqhd->skhd",
        probs.astype(jnp.bfloat16),
        grad_split,
        preferred_element_type=jnp.float32,
    )
    shape = (items, length, width)
    return (
        grad_query.reshape(shape).astype(jnp.bfloat16),
        grad_key.reshape(shape).astype(jnp.bfloat16),
        grad_value.reshape(shape).astype(jnp.bfloat16),
    )


def send_context(context):
    return lax.all_to_all(context, "seq", split_axis=1, concat_axis=1, tiled=True)


def send_grads(grads):
    return (
        lax.all_to_all(grads[0], "seq", split_axis=1, concat_axis=1, tiled=True),
        lax.all_to_all(grads[1], "seq", split_axis=1, concat_axis=1, tiled=True),
        lax.all_to_all(grads[2], "seq", split_axis=1, concat_axis=1, tiled=True),
    )


def make_step(left, pieces):
    total = jnp.dot(left, pieces[0], preferred_element_type=jnp.float32)
    stored = tuple(pieces[1:]) + ()
    placed = tuple((piece for piece in stored))
    return (total,) + placed


def make_hidden_step(before, pieces):
    section = before + pieces[1].astype(jnp.float32)
    activated = jax.nn.gelu(section, approximate=False).astype(jnp.bfloat16)
    total = jnp.dot(activated, pieces[0], preferred_element_type=jnp.float32)
    stored = ()
    return (total, section, activated) + stored


def per_device(
    tokens,
    attend_weight,
    query_bias,
    value_bias,
    output_weight,
    output_bias,
    first_gain,
    first_shift,
    expand_weight,
    expand_bias,
    reduce_weight,
    reduce_bias,
    second_gain,
    second_shift,
    query_rank,
    key_rank,
    cotangent,
):
    seqs, cluster, width = tokens.shape
    heads = query_rank.shape[1]
    rows = seqs * cluster
    owners = lax.axis_size("seq")
    flat = tokens.reshape(rows, width)
    attend_out = make_step(
        flat,
        (
            lax.all_gather(attend_weight, "batch", axis=0, tiled=True),
            lax.all_gather(query_bias, "batch", axis=0, tiled=True),
            lax.all_gather(value_bias, "batch", axis=0, tiled=True),
        ),
    )
    summed = attend_out[0]
    queries = (summed[:, :width] + attend_out[1].astype(jnp.float32)).astype(jnp.bfloat16)
    keys_rows = summed[:, width : 2 * width].astype(jnp.bfloat16)
    values_rows = (summed[:, 2 * width :] + attend_out[2].astype(jnp.float32)).astype(jnp.bfloat16)
    query_table = group_table(query_rank, cluster, owners)
    key_table = group_table(key_rank, cluster, owners)
    query_sorted = sort_heads(queries.reshape(seqs, cluster, width), query_table, heads)
    key_sorted = sort_heads(keys_rows.reshape(seqs, cluster, width), key_table, heads)
    value_sorted = sort_heads(values_rows.reshape(seqs, cluster, width), key_table, heads)
    received = (
        lax.all_to_all(query_sorted, "seq", split_axis=1, concat_axis=1, tiled=True),
        lax.all_to_all(key_sorted, "seq", split_axis=1, concat_axis=1, tiled=True),
        lax.all_to_all(value_sorted, "seq", split_axis=1, concat_axis=1, tiled=True),
    )
    context, log_total = cluster_forward(received[0], received[1], received[2], heads)
    forward_out = (send_context(context), log_total, received[0], received[1], received[2])
    context_rows = unsort_heads(forward_out[0], query_table, heads).reshape(rows, width)
    output_out = make_step(
        context_rows,
        (
            lax.all_gather(output_weight, "batch", axis=0, tiled=True),
            lax.all_gather(output_bias, "batch", axis=0, tiled=True),
            lax.all_gather(first_gain, "batch", axis=0, tiled=True),
            lax.all_gather(first_shift, "batch", axis=0, tiled=True),
        ),
    )
    resid_one = flat.astype(jnp.float32) + output_out[0] + output_out[1].astype(jnp.float32)
    gain_one = output_out[2].astype(jnp.float32)
    middle, normed_one, inverse_one = layer_norm(
        resid_one, gain_one, output_out[3].astype(jnp.float32)
    )
    middle_low = middle.astype(jnp.bfloat16)
    expand_out = make_step(
        middle_low,
        (
            lax.all_gather(expand_weight, "batch", axis=0, tiled=True),
            lax.all_gather(reduce_bias, "batch", axis=0, tiled=True),
            lax.all_gather(second_gain, "batch", axis=0, tiled=True),
            lax.all_gather(second_shift, "batch", axis=0, tiled=True),
        ),
    )
    hidden_out = make_hidden_step(
        expand_out[0],
        (
            lax.all_gather(reduce_weight, "batch", axis=0, tiled=True),
            lax.all_gather(expand_bias, "batch", axis=0, tiled=True),
        ),
    )
    pre_full, hidden_full = (hidden_out[1], hidden_out[2])
    resid_two = middle + hidden_out[0] + expand_out[1].astype(jnp.float32)
    gain_two = expand_out[2].astype(jnp.float32)
    final, normed_two, inverse_two = layer_norm(
        resid_two, gain_two, expand_out[3].astype(jnp.float32)
    )
    layer_out = final.astype(jnp.bfloat16).reshape(seqs, cluster, width)
    attend_full, output_full, expand_full, reduce_full = (
        lax.all_gather(attend_weight, "batch", axis=0, tiled=True),
        lax.all_gather(output_weight, "batch", axis=0, tiled=True),
        lax.all_gather(expand_weight, "batch", axis=0, tiled=True),
        lax.all_gather(reduce_weight, "batch", axis=0, tiled=True),
    )
    upstream = cotangent.reshape(rows, width).astype(jnp.float32)
    grad_second_gain = jnp.sum(upstream * normed_two, axis=0)
    grad_second_shift = jnp.sum(upstream, axis=0)
    grad_resid_two = norm_back(upstream, normed_two, inverse_two, gain_two)
    grad_branch_two = grad_resid_two.astype(jnp.bfloat16)
    grad_reduce_bias = jnp.sum(grad_branch_two, axis=0, dtype=jnp.float32)
    grad_reduce = transpose_left(hidden_full, grad_branch_two)
    grad_hidden = transpose_right(grad_branch_two, reduce_full)
    grad_pre = (grad_hidden * gelu_slope(pre_full)).astype(jnp.bfloat16)
    grad_expand_bias = jnp.sum(grad_pre, axis=0, dtype=jnp.float32)
    grad_expand = transpose_left(middle_low, grad_pre)
    grad_middle = grad_resid_two + transpose_right(grad_pre, expand_full)
    grad_first_gain = jnp.sum(grad_middle * normed_one, axis=0)
    grad_first_shift = jnp.sum(grad_middle, axis=0)
    grad_resid_one = norm_back(grad_middle, normed_one, inverse_one, gain_one)
    grad_branch_one = grad_resid_one.astype(jnp.bfloat16)
    grad_output_bias = jnp.sum(grad_branch_one, axis=0, dtype=jnp.float32)
    grad_output = transpose_left(context_rows, grad_branch_one)
    grad_context = transpose_right(grad_branch_one, output_full).astype(jnp.bfloat16)
    grad_sorted = sort_heads(grad_context.reshape(seqs, cluster, width), query_table, heads)
    grad_received = lax.all_to_all(grad_sorted, "seq", split_axis=1, concat_axis=1, tiled=True)
    kept_scores = cluster_scores(forward_out[2], forward_out[3], heads)
    home = send_grads(
        cluster_backward(
            kept_scores,
            forward_out[1],
            forward_out[2],
            forward_out[3],
            forward_out[4],
            grad_received,
            heads,
        )
    )
    grad_queries = unsort_heads(home[0], query_table, heads).reshape(rows, width)
    grad_keys = unsort_heads(home[1], key_table, heads).reshape(rows, width)
    grad_values = unsort_heads(home[2], key_table, heads).reshape(rows, width)
    grad_mixed = jnp.concatenate([grad_queries, grad_keys, grad_values], axis=1)
    grad_query_bias = jnp.sum(grad_queries, axis=0, dtype=jnp.float32)
    grad_value_bias = jnp.sum(grad_values, axis=0, dtype=jnp.float32)
    grad_attend = transpose_left(flat, grad_mixed)
    token_grad = (
        (grad_resid_one + transpose_right(grad_mixed, attend_full))
        .astype(jnp.bfloat16)
        .reshape(seqs, cluster, width)
    )
    owned = (
        lax.psum_scatter(
            grad_attend.astype(jnp.bfloat16), "batch", scatter_dimension=0, tiled=True
        ).astype(jnp.float32),
        lax.psum_scatter(
            grad_query_bias.astype(jnp.bfloat16), "batch", scatter_dimension=0, tiled=True
        ).astype(jnp.float32),
        lax.psum_scatter(
            grad_value_bias.astype(jnp.bfloat16), "batch", scatter_dimension=0, tiled=True
        ).astype(jnp.float32),
        lax.psum_scatter(
            grad_output.astype(jnp.bfloat16), "batch", scatter_dimension=0, tiled=True
        ).astype(jnp.float32),
        lax.psum_scatter(
            grad_output_bias.astype(jnp.bfloat16), "batch", scatter_dimension=0, tiled=True
        ).astype(jnp.float32),
        lax.psum_scatter(
            grad_first_gain.astype(jnp.bfloat16), "batch", scatter_dimension=0, tiled=True
        ).astype(jnp.float32),
        lax.psum_scatter(
            grad_first_shift.astype(jnp.bfloat16), "batch", scatter_dimension=0, tiled=True
        ).astype(jnp.float32),
        lax.psum_scatter(
            grad_expand.astype(jnp.bfloat16), "batch", scatter_dimension=0, tiled=True
        ).astype(jnp.float32),
        lax.psum_scatter(
            grad_expand_bias.astype(jnp.bfloat16), "batch", scatter_dimension=0, tiled=True
        ).astype(jnp.float32),
        lax.psum_scatter(
            grad_reduce.astype(jnp.bfloat16), "batch", scatter_dimension=0, tiled=True
        ).astype(jnp.float32),
        lax.psum_scatter(
            grad_reduce_bias.astype(jnp.bfloat16), "batch", scatter_dimension=0, tiled=True
        ).astype(jnp.float32),
        lax.psum_scatter(
            grad_second_gain.astype(jnp.bfloat16), "batch", scatter_dimension=0, tiled=True
        ).astype(jnp.float32),
        lax.psum_scatter(
            grad_second_shift.astype(jnp.bfloat16), "batch", scatter_dimension=0, tiled=True
        ).astype(jnp.float32),
    )
    shared = (
        lax.psum(owned[0].astype(jnp.bfloat16), "seq").astype(jnp.float32),
        lax.psum(owned[1].astype(jnp.bfloat16), "seq").astype(jnp.float32),
        lax.psum(owned[2].astype(jnp.bfloat16), "seq").astype(jnp.float32),
        lax.psum(owned[3].astype(jnp.bfloat16), "seq").astype(jnp.float32),
        lax.psum(owned[4].astype(jnp.bfloat16), "seq").astype(jnp.float32),
        lax.psum(owned[5].astype(jnp.bfloat16), "seq").astype(jnp.float32),
        lax.psum(owned[6].astype(jnp.bfloat16), "seq").astype(jnp.float32),
        lax.psum(owned[7].astype(jnp.bfloat16), "seq").astype(jnp.float32),
        lax.psum(owned[8].astype(jnp.bfloat16), "seq").astype(jnp.float32),
        lax.psum(owned[9].astype(jnp.bfloat16), "seq").astype(jnp.float32),
        lax.psum(owned[10].astype(jnp.bfloat16), "seq").astype(jnp.float32),
        lax.psum(owned[11].astype(jnp.bfloat16), "seq").astype(jnp.float32),
        lax.psum(owned[12].astype(jnp.bfloat16), "seq").astype(jnp.float32),
    )
    return (
        layer_out,
        token_grad,
        shared[0],
        shared[1],
        shared[2],
        shared[3],
        shared[4],
        shared[5],
        shared[6],
        shared[7],
        shared[8],
        shared[9],
        shared[10],
        shared[11],
        shared[12],
    )


MESH = pl.DeviceIdType.MESH
f32 = jnp.float32
bf16 = jnp.bfloat16


class Place:
    def __init__(self, chips, depth):
        self.chips, self.depth = chips, depth
        self.z = lax.axis_index("batch")
        spot = lax.axis_index("seq")
        self.chip, self.core = lax.div(spot, 2), lax.rem(spot, 2)

    def chip_at(self, k):
        return lax.rem(self.chip + k + self.chips, self.chips)

    def z_at(self, k):
        return lax.rem(self.z + k + self.depth, self.depth)

    def plane(self, k):
        return (self.z, self.chip_at(k) * 2 + self.core)

    def tower(self, k):
        return (self.z_at(k), self.chip * 2 + self.core)

    def sibling(self):
        return (self.z, self.chip * 2 + 1 - self.core)

    def greet(self):
        bell = pltpu.get_barrier_semaphore()
        others = [self.plane(k) for k in range(1, self.chips)]
        others += [self.tower(k) for k in range(1, self.depth)]
        others.append(self.sibling())
        for other in others:
            pl.semaphore_signal(bell, inc=1, device_id=other, device_id_type=MESH)
        pl.semaphore_wait(bell, len(others))


def far_copy(src, dst, sems, at, device):
    return pltpu.make_async_remote_copy(
        src_ref=src,
        dst_ref=dst,
        send_sem=sems[0].at[at],
        recv_sem=sems[1].at[at],
        device_id=device,
        device_id_type=MESH,
    )


def one_hot(row, slots):
    return jnp.where(slots == row, 1.0, 0.0).astype(bf16)


def split_lanes(tile, low):
    zero = jnp.zeros_like(tile)
    return jnp.where(low, tile, zero), jnp.where(low, zero, tile)


def stack_lanes(tile, low):
    first, second = split_lanes(tile, low)
    return jnp.concatenate([first, second], axis=0)


def dot_rows(a, b):
    return jnp.dot(a, b, preferred_element_type=f32)


def dot_lanes(a, b):
    return lax.dot_general(a, b, (((1,), (1,)), ((), ())), preferred_element_type=f32)


def dot_first(a, b):
    return lax.dot_general(a, b, (((0,), (0,)), ((), ())), preferred_element_type=f32)


def multiple(value, by):
    return pl.multiple_of(value, by)


def forward_kernel(
    chips,
    depth,
    heads,
    tok_ref,
    pos_ref,
    aw_ref,
    vec_ref,
    ow_ref,
    ew_ref,
    rw_ref,
    cot_ref,
    x_out,
    ctx_out,
    q_out,
    k_out,
    v_out,
    p_out,
    pos_out,
    aw_out,
    vec_out,
    ow_out,
    ew_out,
    rw_out,
    n1_out,
    inv_out,
    ml_out,
    hid_out,
    slope_out,
    lo_out,
    gr_out,
    gb_out,
    sum_out,
    xbuf,
    posbuf,
    wbuf,
    vbuf,
    bias,
    ctxb,
    ctxt,
    owbuf,
    ewbuf,
    rwbuf,
    cbuf,
    n1buf,
    invbuf,
    mlbuf,
    vecs,
    upb,
    sums,
    tok_s,
    tok_r,
    tokc_s,
    tokc_r,
    pos_s,
    pos_r,
    posc_s,
    posc_r,
    up_s,
    up_r,
    dn_s,
    dn_r,
    awc_s,
    awc_r,
    vec_s,
    vec_r,
    wz_s,
    wz_r,
    wp_s,
    wp_r,
    wd_s,
    wd_r,
    wc_s,
    wc_r,
    ctx_s,
    ctx_r,
    cot_s,
    cot_r,
    oc_s,
    oc_r,
    loc,
    out_sem,
    slope_sem,
    att_sem,
    late_sem,
):
    me = Place(chips, depth)
    z, chip, core = me.z, me.chip, me.core
    per = tok_ref.shape[0] // chips
    half = aw_ref.shape[1] // 6
    rows_z = aw_ref.shape[0]
    pairs = heads // 4
    size = half // (2 * pairs)
    me.greet()

    def aw_block(zz):
        return wbuf.at[pl.ds(multiple(zz * rows_z, 8), rows_z)]

    def up_copy(h):
        return far_copy(
            aw_block(z - h), aw_block(z - h), (up_s, up_r), h, (z + 1, chip * 2 + core)
        )

    def down_copy(h):
        return far_copy(
            aw_block(z + h), aw_block(z + h), (dn_s, dn_r), h, (z - 1, chip * 2 + core)
        )

    def up_got(h):
        return far_copy(
            aw_block(z - 1 - h), aw_block(z - 1 - h), (up_s, up_r), h, me.sibling()
        )

    def down_got(h):
        return far_copy(
            aw_block(z + 1 + h), aw_block(z + 1 + h), (dn_s, dn_r), h, me.sibling()
        )

    def pass_on():
        @pl.when(z < depth - 1)
        def _():
            up_copy(0).start()

        @pl.when(z > 0)
        def _():
            down_copy(0).start()

    def pass_rest(hops):
        for h in hops:

            @pl.when(z > h)
            def _():
                up_got(h).wait_recv()
                if h + 1 < depth - 1:

                    @pl.when(z < depth - 1)
                    def _():
                        up_copy(h + 1).start()

            @pl.when(z + 1 + h < depth)
            def _():
                down_got(h).wait_recv()
                if h + 1 < depth - 1:

                    @pl.when(z > 0)
                    def _():
                        down_copy(h + 1).start()

    def pass_end():
        for h in range(depth - 1):

            @pl.when((z >= h) & (z < depth - 1))
            def _():
                up_copy(h).wait_send()

            @pl.when((z + h < depth) & (z > 0))
            def _():
                down_copy(h).wait_send()

    def mine(ref, target):
        return ref.at[pl.ds(target * per, per)]

    def tok_copy(k):
        return far_copy(
            mine(tok_ref, me.chip_at(k)), xbuf.at[core, chip], (tok_s, tok_r), k - 1, me.plane(k)
        )

    def pos_copy(k):
        return far_copy(
            mine(pos_ref, me.chip_at(k)), posbuf.at[core, chip], (pos_s, pos_r), k - 1, me.plane(k)
        )

    def vec_copy(k):
        return far_copy(vec_ref, vbuf.at[z], (vec_s, vec_r), k - 1, me.tower(k))

    sends = []
    for k in range(1, chips):
        sends.append(pos_copy(k))
        sends[-1].start()
    for k in range(1, depth):
        sends.append(vec_copy(k))
        sends[-1].start()
    for k in range(1, chips):
        sends.append(tok_copy(k))
        sends[-1].start()
    local = []

    def keep(src, dst):
        copy = pltpu.make_async_copy(src, dst, loc.at[len(local)])
        copy.start()
        local.append(copy)

    for part in range(3):
        keep(
            aw_ref.at[:, pl.ds(multiple(part * 2 * half + core * half, 128), half)],
            wbuf.at[pl.ds(multiple(z * rows_z, 8), rows_z), pl.ds(part * half, half)],
        )
    keep(mine(tok_ref, chip), xbuf.at[core, chip])
    keep(mine(pos_ref, chip), posbuf.at[core, chip])
    keep(vec_ref, vbuf.at[z])
    for copy in local[:3]:
        copy.wait()
    pass_on()
    wide = ew_ref.shape[1] // (2 * chips)
    tall = rw_ref.shape[0] // (2 * chips)
    mid_rows = rows_z // 2
    mine_at = core * chips + chip

    def piece(kind):
        if kind == 0:
            return ow_ref.at[pl.ds(multiple(core * mid_rows, 8), mid_rows)]
        if kind == 1:
            return ew_ref.at[:, pl.ds(multiple(mine_at * wide, 128), wide)]
        return rw_ref.at[pl.ds(multiple(mine_at * tall, 8), tall)]

    def place(kind, zz):
        if kind == 0:
            return owbuf.at[zz, core]
        if kind == 1:
            return ewbuf.at[zz, :, pl.ds(multiple(mine_at * wide, 128), wide)]
        return rwbuf.at[zz, mine_at]

    def place_all(kind, at):
        if kind == 1:
            return ewbuf.at[:, :, pl.ds(multiple(at * wide, 128), wide)]
        return rwbuf.at[:, at]

    for kind in range(3):
        keep(piece(kind), place(kind, z))

    def wz_copy(kind, k):
        return far_copy(
            piece(kind),
            place(kind, z),
            (wz_s, wz_r),
            kind * (depth - 1) + k - 1,
            me.tower(k),
        )

    beside = (chip + 1 - 2 * lax.rem(chip, 2), lax.rem(chip + 2, chips))
    across = chips - 1 - chip

    def part_of(kind, origin, side):
        at = core * chips + origin
        span = pl.ds(side * (depth // 2), depth // 2)
        if kind == 1:
            return ewbuf.at[span, :, pl.ds(multiple(at * wide, 128), wide)]
        return rwbuf.at[span, at]

    def wp_copy(kind, d):
        spot = place_all(kind, mine_at)
        return far_copy(
            spot, spot, (wp_s, wp_r), (kind - 1) * 2 + d, (z, beside[d] * 2 + core)
        )

    def wd_copy(kind, d):
        spot = part_of(kind, beside[d], d)
        return far_copy(
            spot, spot, (wd_s, wd_r), (kind - 1) * 2 + d, (z, beside[1 - d] * 2 + core)
        )

    def wc_copy(kind, n):
        at = core * chips + (chip, beside[0], beside[1], across)[n]
        return far_copy(
            place_all(kind, at),
            place_all(kind, at),
            (wc_s, wc_r),
            (kind - 1) * chips + n,
            me.sibling(),
        )

    def tower_wait(kind):
        for k in range(1, depth):
            wz_copy(kind, k).wait_recv()

    def plane_first(kind):
        for d in range(2):
            wp_copy(kind, d).start()
        wc_copy(kind, 0).start()

    def plane_second(kind):
        for d in range(2):
            wp_copy(kind, d).wait_recv()
            wd_copy(kind, d).start()
            wc_copy(kind, 1 + d).start()

    def plane_last(kind):
        for d in range(2):
            wd_copy(kind, d).wait_recv()
        wc_copy(kind, 3).start()
        for n in range(chips):
            wc_copy(kind, n).wait()
        for d in range(2):
            wp_copy(kind, d).wait_send()
            wd_copy(kind, d).wait_send()

    def oc_copy():
        spot = owbuf.at[:, core]
        return far_copy(spot, spot, (oc_s, oc_r), 0, me.sibling())

    def cot_copy(n):
        target = (beside[0], beside[1], across)[n]
        return far_copy(
            mine(cot_ref, target),
            cbuf.at[chip],
            (cot_s, cot_r),
            n,
            (z, target * 2 + core),
        )

    keep(mine(cot_ref, chip), cbuf.at[chip])

    for copy in local[3:5]:
        copy.wait()

    def tokc_copy(k):
        source = me.chip_at(-k)
        return far_copy(
            xbuf.at[core, source], xbuf.at[core, source], (tokc_s, tokc_r), k, me.sibling()
        )

    def posc_copy(k):
        source = me.chip_at(-k)
        return far_copy(
            posbuf.at[core, source], posbuf.at[core, source], (posc_s, posc_r), k, me.sibling()
        )

    for k in range(1, depth):
        wz_copy(1, k).start()
        for kind in range(3):
            sends.append(wz_copy(kind, k))
    pass_rest(range(depth - 2))
    for k in range(chips):
        if k:
            pos_copy(k).wait_recv()
            tok_copy(k).wait_recv()
        for copy in (posc_copy(k), tokc_copy(k)):
            copy.start()
            sends.append(copy)
    for copy in local[5:]:
        copy.wait()
    tower_wait(1)
    plane_first(1)
    pass_rest(range(depth - 2, depth - 1))
    for k in range(1, depth):
        wz_copy(2, k).start()
    plane_second(1)
    for n in range(2):
        cot_copy(n).start()
    for k in range(1, depth):
        vec_copy(k).wait_recv()
    for k in range(chips):
        posc_copy(k).wait_recv()
        tokc_copy(k).wait_recv()

    outs = []

    def emit(src, dst):
        copy = pltpu.make_async_copy(src, dst, out_sem.at[len(outs)])
        copy.start()
        outs.append(copy)

    emit(xbuf, x_out)
    emit(posbuf, pos_out)
    emit(wbuf, aw_out.at[core])
    awc = far_copy(wbuf, aw_out.at[core], (awc_s, awc_r), 0, me.sibling())
    awc.start()
    sends.append(awc)

    quarter = rows_z
    for zz in range(depth):
        begin = zz * quarter
        for row, at in ((0, 0), (1, 2)):
            for side in range(2):
                lo = max(begin, side * half)
                hi = min(begin + quarter, (side + 1) * half)
                if lo < hi:
                    bias[side, 0:1, at * half + lo - side * half : at * half + hi - side * half] = (
                        vbuf[zz, row : row + 1, lo - begin : hi - begin]
                    )
    bias[0, 0:1, half : 2 * half] = jnp.zeros((1, half), f32)
    bias[1, 0:1, half : 2 * half] = jnp.zeros((1, half), f32)
    added = bias[core, 0:1, :]
    for zz in range(depth):
        for row in range(8):
            vecs[row : row + 1, zz * quarter : (zz + 1) * quarter] = vbuf[
                zz, row : row + 1, :quarter
            ]
        steps = upb.shape[1] // (depth * quarter)
        for row in range(steps):
            to = (zz * steps + row) * quarter
            upb[0:1, to : to + quarter] = vbuf[zz, 8 + row : 9 + row, :quarter]

    cluster = tok_ref.shape[1]
    blocks = 2 * chips
    share = cluster // blocks
    width = tok_ref.shape[2]

    slots = lax.broadcasted_iota(jnp.int32, (cluster, cluster), 0)
    low = lax.broadcasted_iota(jnp.int32, (cluster, 128), 1) < size
    scale = size ** (-0.5)

    def tables(jj, i, pair, part):
        first = part * heads + core * (heads // 2) + 2 * pair
        rows = [
            one_hot(posbuf[jj // chips, jj % chips, i, pl.ds(first + h, 1), :], slots)
            for h in range(2)
        ]
        return rows

    def hook(i, pair):
        step = i * pairs + pair
        last = per * pairs - 1

        @pl.when(step == min(2, last))
        def _():
            tower_wait(2)
            plane_first(2)
            for k in range(1, depth):
                wz_copy(0, k).start()

        @pl.when(step == last)
        def _():
            plane_second(2)
            cot_copy(2).start()

    def attention(qkv, qs, ks, vs, ps, os):
        def group_copies(i):
            span = pl.ds(i * pairs, pairs)
            pieces = ((qs, q_out), (ks, k_out), (vs, v_out), (ps, p_out))
            return [
                pltpu.make_async_copy(src.at[span], dst.at[span], att_sem.at[5 + 4 * i + n])
                for n, (src, dst) in enumerate(pieces)
            ]

        @pl.loop(0, blocks)
        def _(jj):
            x = xbuf[lax.div(jj, chips), lax.rem(jj, chips)].reshape(per * cluster, width)
            mixed = (dot_rows(x, wbuf[...]) + added).astype(bf16)
            for at in range(3 * pairs):
                qkv[at, jj] = mixed[:, at * 128 : (at + 1) * 128].reshape(per, cluster, 128)

        @pl.loop(0, per)
        def _(i):
            @pl.loop(0, pairs)
            def _(pair):
                at = i * pairs + pair
                for jj in range(blocks):
                    tq = jnp.concatenate(tables(jj, i, pair, 0), axis=1)
                    tk = jnp.concatenate(tables(jj, i, pair, 1), axis=1)
                    q = stack_lanes(qkv[pair, jj, i], low)
                    k = stack_lanes(qkv[pairs + pair, jj, i], low)
                    v = stack_lanes(qkv[2 * pairs + pair, jj, i], low)
                    span = slice(jj * share, (jj + 1) * share)
                    sq = dot_rows(tq, q).astype(bf16)
                    skv = dot_rows(tk, jnp.concatenate([k, v], axis=1)).astype(bf16)
                    qs[at, :, span, :] = sq.reshape(blocks, share, 128)
                    ks[at, :, span, :] = skv[:, :128].reshape(blocks, share, 128)
                    vs[at, :, span, :] = skv[:, 128:].reshape(blocks, share, 128)
                for c in range(blocks):
                    scores = dot_lanes(qs[at, c], stack_lanes(ks[at, c], low)) * scale
                    halves = []
                    for h in range(2):
                        s = scores[:, h * cluster : (h + 1) * cluster]
                        e = jnp.exp(s - jnp.max(s, axis=1, keepdims=True))
                        halves.append((e / jnp.sum(e, axis=1, keepdims=True)).astype(bf16))
                    probs = jnp.concatenate(halves, axis=1)
                    ps[at, c] = probs
                    o = dot_rows(probs, stack_lanes(vs[at, c], low)).astype(bf16)
                    os[c] = o
                for jj in range(blocks):
                    tq = jnp.concatenate(tables(jj, i, pair, 0), axis=0)
                    rows = os[:, jj * share : (jj + 1) * share, :].reshape(cluster, 128)
                    back = dot_first(tq, stack_lanes(rows, low)).astype(bf16)
                    ctxb[jj // chips, jj % chips, i, :, pl.ds(multiple(pair * 128, 128), 128)] = back
                hook(i, pair)

                @pl.when(pair == pairs - 1)
                def _():
                    for copy in group_copies(i):
                        copy.start()


        far, own = ctx_copies()
        for copy in (far, own):
            copy.start()
        for copy in (far, own):
            copy.wait()
        for i in range(per):
            for copy in group_copies(i):
                copy.wait()

    def ctx_copies():
        lanes = pl.ds(multiple(core * half, 128), half)
        far = far_copy(
            ctxb.at[1 - core], ctxt.at[:, :, :, lanes], (ctx_s, ctx_r), 0, me.sibling()
        )
        own = pltpu.make_async_copy(ctxb.at[core], ctxt.at[:, :, :, lanes], att_sem.at[4])
        return far, own

    group = (per * pairs, blocks, cluster, 128)
    pl.run_scoped(
        attention,
        pltpu.VMEM((3 * pairs, blocks, per, cluster, 128), bf16),
        pltpu.VMEM(group, bf16),
        pltpu.VMEM(group, bf16),
        pltpu.VMEM(group, bf16),
        pltpu.VMEM((per * pairs, blocks, cluster, 2 * cluster), bf16),
        pltpu.VMEM((blocks, cluster, 128), bf16),
    )

    tower_wait(0)
    oc_copy().start()
    oc_copy().wait()
    emit(ctxt, ctx_out)
    context_out = outs[-1]
    emit(owbuf, ow_out)
    tile = per * cluster
    hidden = upb.shape[1]
    eps = epsilon

    def moments(rows):
        center = jnp.mean(rows, axis=1, keepdims=True)
        centered = rows - center
        spread = jnp.mean(centered * centered, axis=1, keepdims=True)
        inverse = lax.rsqrt(spread + eps)
        return centered * inverse, inverse

    def slope_out_copy(j, slot):
        return pltpu.make_async_copy(sbuf.at[slot], slope_out.at[j], slope_sem.at[slot])

    def vec(row):
        return vecs[row : row + 1, :]

    def feed(hbuf, sbuf):
        step = sbuf.shape[3]

        def late_copies(j):
            pieces = ((cbuf, lo_out), (n1buf, gr_out), (ctxt, gb_out))
            return [
                pltpu.make_async_copy(src.at[j], dst.at[j], late_sem.at[3 * j + n])
                for n, (src, dst) in enumerate(pieces)
            ]

        def slope_copy(n):
            return pltpu.make_async_copy(
                sbuf.at[n % 2],
                slope_out.at[:, :, pl.ds(n * step, step)],
                slope_sem.at[n % 2],
            )

        @pl.loop(0, chips)
        def _(j):
            rows = ctxt[j].reshape(tile, width)
            branch = dot_rows(rows, owbuf[...].reshape(width, width))
            resid = xbuf[core, j].reshape(tile, width).astype(f32) + branch + vec(2)
            normed, inverse = moments(resid)
            n1buf[j] = normed
            invbuf[j] = jnp.broadcast_to(inverse, (tile, 128))
            mlbuf[j] = (normed * vec(3) + vec(4)).astype(bf16).reshape(per, cluster, width)

        plane_last(1)
        emit(ewbuf, ew_out)
        for n in range(hidden // step):
            lanes = slice(n * step, (n + 1) * step)
            if n >= 2:
                slope_copy(n - 2).wait()
            for j in range(chips):
                weight = ewbuf[:, :, lanes].reshape(width, step)
                pre = dot_rows(mlbuf[j].reshape(tile, width), weight) + upb[0:1, lanes]
                cumulative = 0.5 * (1.0 + lax.erf(pre * 0.5**0.5))
                density = jnp.exp(-0.5 * pre * pre) * (2.0 * math.pi) ** (-0.5)
                hbuf[j, :, lanes] = (pre * cumulative).astype(bf16)
                sbuf[n % 2, j] = (cumulative + pre * density).astype(bf16)
            slope_copy(n).start()

        emit(vecs, vec_out)
        held = len(outs)
        emit(n1buf, n1_out)
        emit(invbuf, inv_out)
        emit(mlbuf, ml_out)
        emit(hbuf, hid_out)
        plane_last(2)
        pass_end()
        emit(rwbuf, rw_out)
        for n in range(3):
            cot_copy(n).wait()
        sums[...] = jnp.zeros_like(sums)
        waited = (context_out, outs[held])
        for copy in waited:
            copy.wait()

        @pl.loop(0, chips)
        def _(j):
            branch = vec(5)
            for zz in range(depth):
                span = hidden // depth
                branch = branch + dot_rows(
                    hbuf[j, :, zz * span : (zz + 1) * span], rwbuf[zz].reshape(span, width)
                )
            middle = n1buf[j] * vec(3) + vec(4)
            normed, inverse = moments(middle + branch)
            upstream = cbuf[j].reshape(tile, width).astype(f32)
            cbuf[j] = (normed * vec(6) + vec(7)).astype(bf16).reshape(per, cluster, width)
            sums[0:1, :] += jnp.sum(upstream * normed, axis=0, keepdims=True)
            sums[1:2, :] += jnp.sum(upstream, axis=0, keepdims=True)
            scaled = upstream * vec(6)
            first = jnp.mean(scaled, axis=1, keepdims=True)
            second = jnp.mean(scaled * normed, axis=1, keepdims=True)
            grad = inverse * (scaled - first - normed * second)
            n1buf[j] = grad
            low_grad = grad.astype(bf16)
            sums[2:3, :] += jnp.sum(low_grad.astype(f32), axis=0, keepdims=True)
            ctxt[j] = low_grad.reshape(per, cluster, width)
            for copy in late_copies(j):
                copy.start()

        emit(sums, sum_out)
        for j in range(chips):
            for copy in late_copies(j):
                copy.wait()
        for copy in sends:
            copy.wait_send()
        awc.wait_recv()
        for n in range(max(hidden // step - 2, 0), hidden // step):
            slope_copy(n).wait()
        for copy in outs:
            if not any(copy is other for other in waited):
                copy.wait()

    pl.run_scoped(
        feed,
        pltpu.VMEM((chips, tile, hidden), bf16),
        pltpu.VMEM((2, chips, tile, hidden // depth), bf16),
    )


def forward(
    tokens,
    pos,
    attend_weight,
    vectors,
    output_weight,
    expand_weight,
    reduce_weight,
    cotangent,
    chips,
    depth,
    heads,
):
    seqs, cluster, width = tokens.shape
    per, blocks, pairs = seqs // chips, 2 * chips, heads // 4
    half = width // 2
    rows_z = attend_weight.shape[0]
    hidden = expand_weight.shape[1]
    items = per * pairs
    tile = per * cluster
    dma = pltpu.SemaphoreType.DMA
    anywhere = pl.BlockSpec(memory_space=pl.ANY)
    tall = reduce_weight.shape[0] // blocks
    shapes = [
        ((2, chips, per, cluster, width), bf16),
        ((chips, per, cluster, width), bf16),
        ((items, blocks, cluster, 128), bf16),
        ((items, blocks, cluster, 128), bf16),
        ((items, blocks, cluster, 128), bf16),
        ((items, blocks, cluster, 2 * cluster), bf16),
        ((2, chips, per, 2 * heads, cluster), jnp.int32),
        ((2, depth * rows_z, 3 * half), bf16),
        ((8, width), f32),
        ((depth, 2, rows_z // 2, width), bf16),
        ((depth, rows_z, hidden), bf16),
        ((depth, blocks, tall, width), bf16),
        ((chips, tile, width), f32),
        ((chips, tile, 128), f32),
        ((chips, per, cluster, width), bf16),
        ((chips, tile, hidden), bf16),
        ((chips, tile, hidden), bf16),
        ((chips, per, cluster, width), bf16),
        ((chips, tile, width), f32),
        ((chips, per, cluster, width), bf16),
        ((8, width), f32),
    ]
    t, c = depth - 1, chips - 1
    vm = pltpu.VMEM
    return pl.pallas_call(
        functools.partial(forward_kernel, chips, depth, heads),
        out_shape=[jax.ShapeDtypeStruct(*s) for s in shapes],
        in_specs=[anywhere] * 8,
        out_specs=[anywhere] * len(shapes),
        scratch_shapes=[
            vm(shapes[0][0], bf16),
            vm(shapes[6][0], jnp.int32),
            vm(shapes[7][0][1:], bf16),
            vm((depth,) + vectors.shape, f32),
            vm((2, 8, 3 * half), f32),
            vm((2, chips, per, cluster, half), bf16),
            vm(shapes[1][0], bf16),
            vm(shapes[9][0], bf16),
            vm(shapes[10][0], bf16),
            vm(shapes[11][0], bf16),
            vm(shapes[17][0], bf16),
            vm(shapes[12][0], f32),
            vm(shapes[13][0], f32),
            vm(shapes[14][0], bf16),
            vm((8, width), f32),
            vm((8, hidden), f32),
            vm((8, width), f32),
            dma((c,)), dma((c,)), dma((chips,)), dma((chips,)),
            dma((c,)), dma((c,)), dma((chips,)), dma((chips,)),
            dma((t,)), dma((t,)), dma((t,)), dma((t,)), dma((1,)), dma((1,)),
            dma((t,)), dma((t,)),
            dma((3 * t,)), dma((3 * t,)),
            dma((4,)), dma((4,)), dma((4,)), dma((4,)),
            dma((2 * chips,)), dma((2 * chips,)),
            dma((1,)), dma((1,)),
            dma((c,)), dma((c,)),
            dma((1,)), dma((1,)),
            dma((12,)), dma((24,)), dma((2,)), dma((5 + 4 * per,)), dma((3 * chips,)),
        ],
        compiler_params=pltpu.CompilerParams(
            collective_id=1, has_side_effects=True, vmem_limit_bytes=63 * 2**20
        ),
        name="forward",
    )(
        tokens,
        pos,
        attend_weight,
        vectors,
        output_weight,
        expand_weight,
        reduce_weight,
        cotangent,
    )


def add_into(target, at, parts):
    total = target[at].astype(f32)
    for part in parts:
        total = total + part.astype(f32)
    target[at] = total.astype(target.dtype)


class Reducer:
    def __init__(self, me, own, other, near, mid, last, done, sems, tower_first):
        self.me, self.own, self.other = me, own, other
        self.near, self.mid, self.last, self.done = near, mid, last, done
        (self.near_s, self.near_r, self.mid_s, self.mid_r, self.last_s, self.last_r) = sems[:6]
        (self.back_s, self.back_r, self.side_s, self.side_r) = sems[6:10]
        self.tower_first = tower_first
        self.sizes = (mid.shape[0] + 1, last.shape[0] + 1)

    def spot(self, axis, k):
        me = self.me
        if self.tower_first == (axis == 0):
            return me.z_at(k), me.tower(k)
        return me.chip_at(k), me.plane(k)

    def near_copy(self, a):
        return far_copy(
            self.other.at[a], self.near.at[a], (self.near_s, self.near_r), a, self.me.sibling()
        )

    def fold_near(self, a):
        self.near_copy(a).wait_recv()
        for b in range(self.sizes[1]):
            add_into(self.own, (a, b), [self.near[a, b]])

    def mid_copy(self, k):
        where, device = self.spot(0, k)
        return far_copy(
            self.own.at[where], self.mid.at[k - 1], (self.mid_s, self.mid_r), k - 1, device
        )

    def send_mid(self):
        for k in range(1, self.sizes[0]):
            self.mid_copy(k).start()

    def fold_mid(self):
        for k in range(1, self.sizes[0]):
            self.mid_copy(k).wait()
        here = self.spot(0, 0)[0]
        for b in range(self.sizes[1]):
            add_into(self.own, (here, b), [self.mid[k - 1, b] for k in range(1, self.sizes[0])])

    def last_copy(self, k):
        here = self.spot(0, 0)[0]
        where, device = self.spot(1, k)
        return far_copy(
            self.own.at[here, where],
            self.last.at[k - 1],
            (self.last_s, self.last_r),
            k - 1,
            device,
        )

    def send_last(self):
        for k in range(1, self.sizes[1]):
            self.last_copy(k).start()

    def fold_last(self):
        me = self.me
        for k in range(1, self.sizes[1]):
            self.last_copy(k).wait()
        total = self.own[self.spot(0, 0)[0], self.spot(1, 0)[0]].astype(f32)
        for k in range(1, self.sizes[1]):
            total = total + self.last[k - 1].astype(f32)
        self.done[me.core, me.chip] = total.astype(bf16)

    def back_copy(self, k):
        me = self.me
        spot = self.done.at[me.core, me.chip]
        return far_copy(spot, spot, (self.back_s, self.back_r), k - 1, me.plane(k))

    def send_back(self):
        for k in range(1, self.done.shape[1]):
            self.back_copy(k).start()

    def side_copy(self):
        spot = self.done.at[self.me.core]
        return far_copy(spot, spot, (self.side_s, self.side_r), 0, self.me.sibling())

    def send_side(self):
        for k in range(1, self.done.shape[1]):
            self.back_copy(k).wait()
        self.side_copy().start()

    def finish(self):
        self.side_copy().wait()


class Sum:
    def __init__(self, me, vec, got, s, r):
        self.me, self.vec, self.got, self.s, self.r = me, vec, got, s, r

    def copies(self, hop):
        me = self.me
        if hop == 0:
            spots = [(0, me.sibling())]
        elif hop == 1:
            spots = [(k, me.plane(k)) for k in range(1, me.chips)]
        else:
            spots = [(me.chips + k - 1, me.tower(k)) for k in range(1, me.depth)]
        return [far_copy(self.vec, self.got.at[n], (self.s, self.r), n, d) for n, d in spots], spots

    def send(self, hop):
        for copy in self.copies(hop)[0]:
            copy.start()

    def fold(self, hop):
        copies, spots = self.copies(hop)
        for copy in copies:
            copy.wait()
        total = self.vec[...]
        for n, _ in spots:
            total = total + self.got[n]
        self.vec[...] = total


def back_kernel(
    chips,
    depth,
    heads,
    q_ref,
    k_ref,
    v_ref,
    p_ref,
    pos_ref,
    x_ref,
    aw_ref,
    ow_ref,
    ew_ref,
    rw_ref,
    vec_ref,
    ctx_ref,
    n1_ref,
    inv_ref,
    ml_ref,
    hid_ref,
    slope_ref,
    lo_ref,
    gr_ref,
    gb_ref,
    late_ref,
    token_out,
    layer_out,
    aw_out,
    ow_out,
    ew_out,
    rw_out,
    vec_out,
    bias_out,
    dbuf,
    posbuf,
    acc,
    gfar,
    p_mid,
    p_last,
    p_done,
    o_all,
    o_near,
    o_mid,
    o_last,
    o_done,
    e_all,
    e_near,
    e_mid,
    e_last,
    e_done,
    r_all,
    r_near,
    r_mid,
    r_last,
    r_done,
    vbuf,
    vgot,
    bbuf,
    bgot,
    vecs,
    d_s,
    d_r,
    g_s,
    g_r,
    t_s,
    t_r,
    lo_s,
    lo_r,
    load,
    out_sem,
    v_s,
    v_r,
    b_s,
    b_r,
    *sems,
):
    me = Place(chips, depth)
    z, core, chip = me.z, me.core, me.chip
    per, cluster, width = lo_ref.shape[1:]
    half = width // 2
    pairs = heads // 4
    size = half // (2 * pairs)
    blocks = 2 * chips
    share = cluster // blocks
    tile = per * cluster
    hidden = hid_ref.shape[2]
    wide = hidden // blocks
    strip = width // chips
    quarter = width // depth
    eighth = quarter // blocks
    rows = chips * tile
    me.greet()
    groups = [sems[n * 10 : (n + 1) * 10] for n in range(3 + heads // 4)]
    red = Reducer(
        me, r_all.at[core], r_all.at[1 - core], r_near, r_mid, r_last, r_done, groups[0], True
    )
    exp = Reducer(
        me, e_all.at[core], e_all.at[1 - core], e_near, e_mid, e_last, e_done, groups[1], False
    )
    out = Reducer(
        me, o_all.at[core], o_all.at[1 - core], o_near, o_mid, o_last, o_done, groups[2], False
    )
    sums = Sum(me, vbuf, vgot, v_s, v_r)
    biases = Sum(me, bbuf, bgot, b_s, b_r)

    def fetch(src, dst, at):
        return pltpu.make_async_copy(src, dst, load.at[at])

    def lo_copy(k):
        return far_copy(
            lo_ref.at[me.chip_at(k)],
            layer_out.at[pl.ds(chip * per, per)],
            (lo_s, lo_r),
            k - 1,
            me.plane(k),
        )

    lo_keep = pltpu.make_async_copy(
        lo_ref.at[chip], layer_out.at[pl.ds(chip * per, per)], out_sem.at[0]
    )

    block = 2 * wide
    counts = blocks // 2

    def order(n):
        return lax.rem(n + z + chip, counts)

    def fold(n):
        at = order(n)
        red.fold_near(at)
        k = lax.rem(at - z + depth, depth)

        @pl.when(k != 0)
        def _():
            red.mid_copy(k).start()

        @pl.when(lax.div(at, 2) == core)
        def _():
            for side in range(2):
                b = lax.rem(at, 2) * 2 + side
                exp.fold_near(b)
                k = lax.rem(b - chip + chips, chips)

                @pl.when(k != 0)
                def _():
                    exp.mid_copy(k).start()

    def chunks(gb, gbt, mlt, hid, slope, rwc, ewc, gpb):
        def chunk(n, slot):
            at = order(n)
            lanes = pl.ds(multiple(at * block, 128), block)
            return [
                fetch(hid_ref.at[:, :, lanes], hid.at[slot], slot * 4),
                fetch(slope_ref.at[:, :, lanes], slope.at[slot], slot * 4 + 1),
                fetch(rw_ref.at[at], rwc.at[slot], slot * 4 + 2),
                fetch(ew_ref.at[:, :, lanes], ewc.at[slot], slot * 4 + 3),
            ]

        begin = [
            fetch(gb_ref, gb, 8),
            fetch(ml_ref, gpb, 9),
            fetch(gr_ref, acc, 10),
        ]
        later = [
            fetch(vec_ref, vecs, 11),
            fetch(late_ref, vbuf.at[pl.ds(0, 8)], 12),
            fetch(pos_ref, posbuf, 18),
        ]
        for copy in begin + chunk(0, 0) + later:
            copy.start()
        for k in range(1, chips):
            lo_copy(k).start()
        lo_keep.start()
        vbuf[8:, :] = jnp.zeros((blocks, width), f32)
        for copy in begin:
            copy.wait()
        for j in range(chips):
            span = slice(j * tile, (j + 1) * tile)
            mlt[:, span] = jnp.transpose(gpb[j].reshape(tile, width))
            gbt[:, span] = jnp.transpose(gb[j].reshape(tile, width))
        for copy in later:
            copy.wait()

        @pl.loop(0, counts)
        def _(n):
            slot = lax.rem(n, 2)
            at = order(n)
            for copy in chunk(n, slot):
                copy.wait()

            @pl.when(n + 1 < counts)
            def _():
                for copy in chunk(n + 1, 1 - slot):
                    copy.start()

            up = rwc[slot].reshape(block, width)
            down = ewc[slot].reshape(width, block)
            total = jnp.zeros((1, block), f32)
            for j in range(chips):
                grad = dot_lanes(gb[j].reshape(tile, width), up)
                low = (grad * slope[slot, j].astype(f32)).astype(bf16)
                gpb[j] = low.reshape(per, cluster, block)
                acc[j] += dot_lanes(low, down)
                total = total + jnp.sum(low.astype(f32), axis=0, keepdims=True)
            vbuf[pl.ds(8 + at, 1), :block] = total
            term = dot_rows(gbt[...], hid[slot].reshape(rows, block)).astype(bf16)
            for side in range(2):
                r_all[side, at] = term[:, side * wide : (side + 1) * wide].reshape(
                    chips, strip, wide
                )
            red.near_copy(at).start()
            term = dot_rows(mlt[...], gpb[...].reshape(rows, block)).astype(bf16)
            for side in range(2):
                e_all[lax.div(at, 2), lax.rem(at, 2) * 2 + side] = term[
                    :, side * wide : (side + 1) * wide
                ].reshape(depth, quarter, wide)

            @pl.when(lax.div(at, 2) != core)
            def _():
                for side in range(2):
                    exp.near_copy(lax.rem(at, 2) * 2 + side).start()

            @pl.when(n > 0)
            def _():
                fold(n - 1)

    def first_norm(gb, n1, inv, ctx, ow, dsnd):
        later = [
            fetch(ctx_ref, ctx, 13),
            fetch(ow_ref, ow, 14),
            fetch(inv_ref, inv, 15),
        ]
        def n1_copy(j):
            return fetch(n1_ref.at[j], n1.at[j % 2], 16 + j % 2)

        def d_copy(j):
            return far_copy(dsnd.at[j], dbuf.at[core, j], (d_s, d_r), j, me.sibling())

        n1_copy(0).start()
        for copy in later:
            copy.start()
        fold(counts - 1)
        for copy in later:
            copy.wait()
        gain = vecs[3:4, :]
        for row in range(3, 8):
            vbuf[row : row + 1, :] = jnp.zeros((1, width), f32)
        for j in range(chips):
            n1_copy(j).wait()
            if j + 1 < chips:
                n1_copy(j + 1).start()
            grad = acc[j]
            normed = n1[j % 2]
            vbuf[3:4, :] += jnp.sum(grad * normed, axis=0, keepdims=True)
            vbuf[4:5, :] += jnp.sum(grad, axis=0, keepdims=True)
            scaled = grad * gain
            first = jnp.mean(scaled, axis=1, keepdims=True)
            second = jnp.mean(scaled * normed, axis=1, keepdims=True)
            grad = inv[j][:, :1] * (scaled - first - normed * second)
            acc[j] = grad
            low = grad.astype(bf16)
            gb[j] = low.reshape(per, cluster, width)
            vbuf[5:6, :] += jnp.sum(low.astype(f32), axis=0, keepdims=True)
            back = dot_lanes(low, ow[...].reshape(width, width)).astype(bf16)

            for c in range(2):
                piece = back[:, c * half : (c + 1) * half]

                @pl.when(core == c)
                def _():
                    dbuf[c, j] = piece.reshape(per, cluster, half)

                @pl.when(core != c)
                def _():
                    dsnd[j] = piece.reshape(per, cluster, half)

            d_copy(j).start()
        sums.send(0)
        term = dot_first(ctx[...].reshape(rows, width), gb[...].reshape(rows, width))
        for zz in range(depth):
            for c in range(2):
                for p in range(chips):
                    begin_at = zz * quarter + (c * chips + p) * eighth
                    o_all[c, p, zz] = term[begin_at : begin_at + eighth, :].astype(bf16)
        for p in range(chips):
            out.near_copy(p).start()
        for j in range(chips):
            d_copy(j).wait()
        for a in range(depth):
            red.near_copy(a).wait_send()
        for b in range(chips):
            exp.near_copy(b).wait_send()

    shape = (chips, per, cluster, width)
    vm = pltpu.VMEM

    def feed_back(gb):
        pl.run_scoped(
            functools.partial(chunks, gb),
            vm((width, rows), bf16),
            vm((width, rows), bf16),
            vm((2, chips, tile, block), bf16),
            vm((2, chips, tile, block), bf16),
            vm((2, blocks, block // blocks, width), bf16),
            vm((2, depth, quarter, block), bf16),
            vm(shape[:3] + (block,), bf16),
        )
        pl.run_scoped(
            functools.partial(first_norm, gb),
            vm((2, tile, width), f32),
            vm((chips, tile, 128), f32),
            vm(shape, bf16),
            vm((depth, 2, quarter // 2, width), bf16),
            vm((chips, per, cluster, half), bf16),
        )

    pl.run_scoped(feed_back, vm(shape, bf16))

    def attend_back(qs, ks, vs, ps, xbuf, wbuf, ds, gs, gbuf, tbuf, dw, dwp):
        atts = [
            Reducer(
                me,
                dwp.at[n],
                None,
                None,
                p_mid.at[n],
                p_last.at[n],
                p_done.at[n],
                groups[3 + n],
                n % 2 == 1,
            )
            for n in range(pairs)
        ]

        def loads(i, slot):
            span = pl.ds(i * pairs, pairs)
            pieces = (
                (q_ref.at[span], qs),
                (k_ref.at[span], ks),
                (v_ref.at[span], vs),
                (p_ref.at[span], ps),
            )
            return [fetch(src, dst.at[slot], slot * 4 + n) for n, (src, dst) in enumerate(pieces)]

        def load_x(i):
            return fetch(x_ref.at[:, :, i], xbuf, 8)

        load_w = fetch(aw_ref, wbuf, 9)
        for copy in loads(0, 0) + [load_x(0), load_w]:
            copy.start()
        bbuf[...] = jnp.zeros_like(bbuf)
        slots = lax.broadcasted_iota(jnp.int32, (cluster, cluster), 0)
        low = lax.broadcasted_iota(jnp.int32, (cluster, 128), 1) < size
        scale = size ** (-0.5)

        def tables(jj, i, pair, part):
            begin = part * heads + core * (heads // 2) + 2 * pair
            return [
                one_hot(posbuf[jj // chips, jj % chips, i, pl.ds(begin + h, 1), :], slots)
                for h in range(2)
            ]

        def clusters(i, slot, pair):
            lanes = pl.ds(multiple(pair * 128, 128), 128)
            for jj in range(blocks):
                tq = jnp.concatenate(tables(jj, i, pair, 0), axis=1)
                rows = stack_lanes(dbuf[jj // chips, jj % chips, i, :, lanes], low)
                ds[:, jj * share : (jj + 1) * share, :] = (
                    dot_rows(tq, rows).astype(bf16).reshape(blocks, share, 128)
                )
            for c in range(blocks):
                d = ds[c]
                probs = ps[slot, pair, c]
                slope = dot_lanes(d, stack_lanes(vs[slot, pair, c], low))
                broad = probs.astype(f32)
                halves = []
                for h in range(2):
                    span = slice(h * cluster, (h + 1) * cluster)
                    inner = jnp.sum(broad[:, span] * slope[:, span], axis=1, keepdims=True)
                    halves.append((broad[:, span] * (slope[:, span] - inner)).astype(bf16))
                grads = jnp.concatenate(halves, axis=1)
                gq = dot_rows(grads, stack_lanes(ks[slot, pair, c], low)) * scale
                gk = dot_first(grads, qs[slot, pair, c]) * scale
                gv = dot_first(probs, d)
                gs[0, c] = gq.astype(bf16)
                gs[1, c] = jnp.where(low, gk[:cluster], gk[cluster:]).astype(bf16)
                gs[2, c] = jnp.where(low, gv[:cluster], gv[cluster:]).astype(bf16)
            for jj in range(blocks):
                for part in range(3):
                    if part < 2:
                        table = jnp.concatenate(tables(jj, i, pair, part), axis=0)
                    rows = gs[part, :, jj * share : (jj + 1) * share, :].reshape(cluster, 128)
                    back = dot_first(table, stack_lanes(rows, low))
                    to = pl.ds(multiple(part * half + pair * 128, 128), 128)
                    gbuf[slot, jj // chips, jj % chips, :, to] = back.astype(bf16)

        def give(slot):
            return far_copy(gbuf.at[slot, 1 - core], gfar.at[slot], (g_s, g_r), slot, me.sibling())

        def token_copy(i, slot, k):
            return far_copy(
                tbuf.at[slot, me.chip_at(k)],
                token_out.at[chip * per + i],
                (t_s, t_r),
                i * (chips - 1) + k - 1,
                me.plane(k),
            )

        def token_keep(i, slot):
            return pltpu.make_async_copy(
                tbuf.at[slot, chip], token_out.at[chip * per + i], out_sem.at[1 + i]
            )

        def token_rows(i, slot):
            give(slot).wait()
            for j in range(chips):
                near = dot_lanes(gbuf[slot, core, j], wbuf[core])
                distant = dot_lanes(gfar[slot, j], wbuf[1 - core])
                resid = acc[j, i * cluster : (i + 1) * cluster, :]
                tbuf[slot, j] = (resid + near + distant).astype(bf16)
            token_keep(i, slot).start()
            for k in range(1, chips):
                token_copy(i, slot, k).start()

        ready = []

        def emit(src, dst):
            copy = pltpu.make_async_copy(src, dst, out_sem.at[1 + per + len(ready)])
            copy.start()
            ready.append(copy)

        def step_out_near():
            for p in range(chips):
                out.fold_near(p)
            out.send_mid()
            for p in range(chips):
                out.near_copy(p).wait_send()
            sums.fold(0)
            sums.send(1)

        def step_exp_mid():
            exp.fold_mid()
            exp.send_last()

        def step_red_mid():
            red.fold_mid()
            red.send_last()
            sums.fold(1)
            sums.send(2)

        def step_exp_last():
            exp.fold_last()
            exp.send_back()
            out.fold_mid()
            out.send_last()

        def step_red_last():
            red.fold_last()
            red.send_back()
            sums.fold(2)

        def step_out_last():
            out.fold_last()
            out.send_back()
            exp.send_side()

        def step_sides():
            red.send_side()

        hooks = {}
        steps = [
            (0, step_out_near),
            (1, step_exp_mid),
            (3, step_red_mid),
            (5, step_exp_last),
            (6, step_red_last),
            (7, step_out_last),
            (8, step_sides),
        ]
        for n, step in steps:
            hooks.setdefault(min(n, per * pairs - 1), []).append(step)
        depth_rows = quarter // chips

        def pair_grad(n, slot):
            lanes = [slice(p * half + n * 128, p * half + (n + 1) * 128) for p in range(3)]
            total = jnp.concatenate([dw[:, lane] for lane in lanes], axis=1)
            line = jnp.zeros((1, 384), f32)
            for b in range(2):
                x = jnp.concatenate([xbuf[b, j] for j in range(chips)], axis=0)
                g = jnp.concatenate(
                    [
                        jnp.concatenate([gbuf[slot, b, j, :, lane] for lane in lanes], axis=1)
                        for j in range(chips)
                    ],
                    axis=0,
                )
                total = total + dot_first(x, g)
                line = line + jnp.sum(g.astype(f32), axis=0, keepdims=True)
            for p, lane in enumerate(lanes):
                bbuf[0:1, lane] += line[:, p * 128 : (p + 1) * 128]
            low = total.astype(bf16)
            for a in range(depth):
                for b in range(chips):
                    begin = (a * chips + b) * depth_rows
                    piece = low[begin : begin + depth_rows]
                    if atts[n].tower_first:
                        dwp[n, a, b] = piece
                    else:
                        dwp[n, b, a] = piece
            atts[n].send_mid()

        dw[...] = jnp.zeros_like(dw)
        for i in range(per):
            slot = i % 2
            for copy in loads(i, slot):
                copy.wait()
            if i == 0:
                load_w.wait()
            if i >= 1:
                token_rows(i - 1, 1 - slot)
            if i + 1 < per:
                for copy in loads(i + 1, 1 - slot):
                    copy.start()
            if i == per - 1:
                load_x(i).wait()

            @pl.loop(0, pairs)
            def _(pair):
                clusters(i, slot, pair)
                for n in range(pairs):
                    if hooks.get(i * pairs + n) or i == per - 1:

                        @pl.when(pair == n)
                        def _():
                            if i == per - 1:
                                pair_grad(n, slot)
                            for step in hooks.get(i * pairs + n, ()):
                                step()

            if i >= 2:
                token_keep(i - 2, slot).wait()
                for k in range(1, chips):
                    token_copy(i - 2, slot, k).wait()
            give(slot).start()
            if i + 1 < per:
                load_x(i).wait()
                for b in range(2):
                    x = jnp.concatenate([xbuf[b, j] for j in range(chips)], axis=0)
                    g = jnp.concatenate([gbuf[slot, b, j] for j in range(chips)], axis=0)
                    dw[...] += dot_first(x, g)
                    bbuf[0:1, :] += jnp.sum(g.astype(f32), axis=0, keepdims=True)
                load_x(i + 1).start()

        biases.send(1)
        token_rows(per - 1, (per - 1) % 2)
        emit(vbuf, vec_out)
        out.send_side()
        for n in range(pairs - 1):
            atts[n].fold_mid()
            atts[n].send_last()
        biases.fold(1)
        biases.send(2)
        exp.finish()
        for c in range(2):
            for p in range(chips):
                emit(e_done.at[c, p], ew_out.at[:, pl.ds((c * chips + p) * wide, wide)])
        for n in range(pairs - 1, pairs):
            atts[n].fold_mid()
            atts[n].send_last()
        for n in range(pairs - 1):
            atts[n].fold_last()
            atts[n].send_back()
        red.finish()
        for c in range(2):
            emit(r_done.at[c], rw_out.at[:, :, pl.ds(c * wide, wide)])
        out.finish()
        emit(o_done, ow_out)
        biases.fold(2)
        share_bias = far_copy(bbuf, bias_out.at[core], (b_s, b_r), 0, me.sibling())
        share_bias.start()
        emit(bbuf, bias_out.at[core])
        for n in range(pairs - 1, pairs):
            atts[n].fold_last()
            atts[n].send_back()
        for n in range(pairs):
            atts[n].send_side()
        for n in range(pairs):
            atts[n].finish()
            for c in range(2):
                for part in range(3):
                    emit(
                        p_done.at[n, c, :, :, pl.ds(part * 128, 128)],
                        aw_out.at[:, :, pl.ds((2 * part + c) * half + n * 128, 128)],
                    )
        for i in range(max(per - 2, 0), per):
            token_keep(i, i % 2).wait()
            for k in range(1, chips):
                token_copy(i, i % 2, k).wait()
        share_bias.wait()
        for copy in ready:
            copy.wait()
        lo_keep.wait()
        for k in range(1, chips):
            lo_copy(k).wait()

    group = (2, pairs, blocks, cluster)
    pl.run_scoped(
        attend_back,
        vm(group + (128,), bf16),
        vm(group + (128,), bf16),
        vm(group + (128,), bf16),
        vm(group + (2 * cluster,), bf16),
        vm((2, chips, cluster, width), bf16),
        vm(aw_ref.shape, bf16),
        vm((blocks, cluster, 128), bf16),
        vm((3, blocks, cluster, 128), bf16),
        vm((2, 2, chips, cluster, 3 * half), bf16),
        vm((2, chips, cluster, width), bf16),
        vm((width, 3 * half), f32),
        vm((pairs, depth, chips, quarter // chips, 384), bf16),
    )


def back(arrays, depth, heads):
    chips, per, cluster, width = arrays[17].shape
    half, blocks = width // 2, 2 * chips
    dma = pltpu.SemaphoreType.DMA
    anywhere = pl.BlockSpec(memory_space=pl.ANY)
    quarter = width // depth
    hidden = arrays[15].shape[2]
    eighth, strip, wide = quarter // blocks, width // chips, hidden // blocks
    rows = quarter // chips
    c, t = chips - 1, depth - 1
    pairs = heads // 4
    shapes = [
        ((chips * per, cluster, width), bf16),
        ((chips * per, cluster, width), bf16),
        ((chips, rows, 3 * width), bf16),
        ((2, chips, eighth, width), bf16),
        ((quarter, hidden), bf16),
        ((chips, strip, 2 * wide), bf16),
        ((8 + blocks, width), f32),
        ((2, 8, 3 * half), f32),
    ]
    vm = pltpu.VMEM

    def reducing(near, first, second):
        return [
            dma((near,)), dma((near,)),
            dma((first,)), dma((first,)),
            dma((second,)), dma((second,)),
            dma((c,)), dma((c,)),
            dma((1,)), dma((1,)),
        ]

    return pl.pallas_call(
        functools.partial(back_kernel, chips, depth, heads),
        out_shape=[jax.ShapeDtypeStruct(*s) for s in shapes],
        in_specs=[anywhere] * len(arrays),
        out_specs=[anywhere] * len(shapes),
        scratch_shapes=[
            vm((2, chips, per, cluster, half), bf16),
            vm(arrays[4].shape, jnp.int32),
            vm((chips, per * cluster, width), f32),
            vm((2, chips, cluster, 3 * half), bf16),
            vm((pairs, t, chips, rows, 384), bf16),
            vm((pairs, t, rows, 384), bf16),
            vm((pairs, 2, chips, rows, 384), bf16),
            vm((2, chips, depth, eighth, width), bf16),
            vm((chips, depth, eighth, width), bf16),
            vm((c, depth, eighth, width), bf16),
            vm((t, eighth, width), bf16),
            vm((2, chips, eighth, width), bf16),
            vm((2, chips, depth, quarter, wide), bf16),
            vm((chips, depth, quarter, wide), bf16),
            vm((c, depth, quarter, wide), bf16),
            vm((t, quarter, wide), bf16),
            vm((2, chips, quarter, wide), bf16),
            vm((2, depth, chips, strip, wide), bf16),
            vm((depth, chips, strip, wide), bf16),
            vm((t, chips, strip, wide), bf16),
            vm((c, strip, wide), bf16),
            vm((2, chips, strip, wide), bf16),
            vm((8 + blocks, width), f32),
            vm((chips + t, 8 + blocks, width), f32),
            vm((8, 3 * half), f32),
            vm((chips + t, 8, 3 * half), f32),
            vm((8, width), f32),
            dma((chips,)), dma((chips,)), dma((2,)), dma((2,)),
            dma((per * c,)), dma((per * c,)),
            dma((c,)), dma((c,)),
            dma((19,)), dma((1 + per + 6 + blocks + 6 * pairs,)),
            dma((chips + t,)), dma((chips + t,)), dma((chips + t,)), dma((chips + t,)),
            *reducing(depth, t, c),
            *reducing(chips, c, t),
            *reducing(chips, c, t),
            *[sem for n in range(pairs) for sem in reducing(1, c, t)],
        ],
        compiler_params=pltpu.CompilerParams(
            collective_id=2, has_side_effects=True, vmem_limit_bytes=63 * 2**20
        ),
        name="back",
    )(*arrays)


def places(rank, cluster, share):
    seqs, rows, length = rank.shape
    clusters = cluster // share
    target = rank // cluster
    which = lax.broadcasted_iota(jnp.int32, (1, 1, clusters, 1), 2)
    inside = (target[:, :, None, :] == which).astype(bf16)
    first = lax.broadcasted_iota(jnp.int32, (length, length), 0)
    second = lax.broadcasted_iota(jnp.int32, (length, length), 1)
    before = (first < second).astype(bf16)
    count = lax.dot_general(
        inside.reshape(seqs * rows * clusters, length),
        before,
        (((1,), (0,)), ((), ())),
        preferred_element_type=f32,
    ).reshape(seqs, rows, clusters, length)
    spot = which.astype(f32) * share + count
    return jnp.sum(inside.astype(f32) * spot, axis=2).astype(jnp.int32)


def per_chip(
    tokens,
    attend_weight,
    query_bias,
    value_bias,
    output_weight,
    output_bias,
    first_gain,
    first_shift,
    expand_weight,
    expand_bias,
    reduce_weight,
    reduce_bias,
    second_gain,
    second_shift,
    query_rank,
    key_rank,
    cotangent,
):
    seqs, cluster, width = tokens.shape
    heads = query_rank.shape[1]
    owners = lax.axis_size("seq")
    depth = lax.axis_size("batch")
    chips = owners // 2
    half = width // 2
    share = cluster // owners
    pos = places(jnp.concatenate([query_rank, key_rank], axis=1), cluster, share)
    quarter = width // depth
    lines = [
        query_bias,
        value_bias,
        output_bias,
        first_gain,
        first_shift,
        reduce_bias,
        second_gain,
        second_shift,
    ]
    lines += [
        expand_bias[at : at + quarter] for at in range(0, expand_bias.shape[0], quarter)
    ]
    vectors = jnp.zeros((16 * 256,), f32)
    for row, v in enumerate(lines):
        vectors += jnp.pad(v.astype(f32), (row * 256, (16 - row) * 256 - quarter))
    vectors = vectors.reshape(16, 256)
    (
        x_all,
        context,
        qs,
        ks,
        vs,
        ps,
        pos_all,
        attend_all,
        vecs,
        out_all,
        exp_all,
        red_all,
        normed_one,
        inverse_one,
        middle_low,
        hidden,
        slope,
        layer_out,
        grad_resid_two,
        grad_branch_two,
        late_sums,
    ) = forward(
        tokens,
        pos,
        attend_weight,
        vectors,
        output_weight,
        expand_weight,
        reduce_weight,
        cotangent,
        chips,
        depth,
        heads,
    )
    token_grad, layer_out, aw_grad, ow_grad, ew_grad, rw_grad, vec_sum, bias_sum = back(
        (
            qs,
            ks,
            vs,
            ps,
            pos_all,
            x_all,
            attend_all,
            out_all,
            exp_all,
            red_all,
            vecs,
            context,
            normed_one,
            inverse_one,
            middle_low,
            hidden,
            slope,
            layer_out,
            grad_resid_two,
            grad_branch_two,
            late_sums,
        ),
        depth,
        heads,
    )
    z = lax.axis_index("batch")
    six = lax.dynamic_slice_in_dim(vec_sum[:6], z * quarter, quarter, 1)
    up = lax.dynamic_index_in_dim(vec_sum[8:], z, 0, keepdims=False)
    both = jnp.concatenate([bias_sum[0, 0], bias_sum[1, 0]]).reshape(2, 3, half)
    query_value = jnp.transpose(both, (1, 0, 2)).reshape(3, width)
    query_value = lax.dynamic_slice_in_dim(query_value, z * quarter, quarter, 1)
    return (
        layer_out,
        token_grad,
        aw_grad.reshape(quarter, 3 * width).astype(f32),
        query_value[0],
        query_value[2],
        ow_grad.reshape(quarter, width).astype(f32),
        six[5],
        six[3],
        six[4],
        ew_grad.astype(f32),
        up,
        jnp.transpose(rw_grad.reshape(width, -1)).astype(f32),
        six[2],
        six[0],
        six[1],
    )


def layer(mesh):
    def run(*arrays):
        seqs, cluster, width = arrays[0].shape
        heads = arrays[14].shape[1]
        owners, depth = mesh.shape["seq"], mesh.shape["batch"]
        chips = owners // 2
        fits = (
            owners % 2 == 0
            and chips > 1
            and depth == chips == 4
            and seqs % chips == 0
            and cluster == 128
            and heads % 4 == 0
            and width == heads * 64
            and cluster == 16 * owners
            and arrays[8].shape[1] == 4 * width
        )
        return (per_chip if fits else per_device)(*arrays)

    return run


def solution(mesh):
    in_specs = (
        P("batch", "seq", None),
        P("batch", None),
        P("batch"),
        P("batch"),
        P("batch", None),
        P("batch"),
        P("batch"),
        P("batch"),
        P("batch", None),
        P("batch"),
        P("batch", None),
        P("batch"),
        P("batch"),
        P("batch"),
        P("batch", None, "seq"),
        P("batch", None, "seq"),
        P("batch", "seq", None),
    )
    out_specs = (
        P("batch", "seq", None),
        P("batch", "seq", None),
        P("batch", None),
        P("batch"),
        P("batch"),
        P("batch", None),
        P("batch"),
        P("batch"),
        P("batch"),
        P("batch", None),
        P("batch"),
        P("batch", None),
        P("batch"),
        P("batch"),
        P("batch"),
    )
    return jax.shard_map(
        layer(mesh), mesh=mesh, in_specs=in_specs, out_specs=out_specs, check_vma=False
    )
```

```python
import functools
import math

import jax
import jax.numpy as jnp
from jax import lax
from jax.experimental import pallas as pl
from jax.experimental.pallas import tpu as pltpu
from jax.sharding import PartitionSpec as P

epsilon = 1e-05


def layer_norm(resid, gain, shift):
    center = jnp.mean(resid, axis=-1, keepdims=True)
    centered = resid - center
    spread = jnp.mean(centered * centered, axis=-1, keepdims=True)
    inverse = lax.rsqrt(spread + epsilon)
    normed = centered * inverse
    return (normed * gain + shift, normed, inverse)


def norm_back(upstream, normed, inverse, gain):
    scaled = upstream * gain
    first_mean = jnp.mean(scaled, axis=-1, keepdims=True)
    second_mean = jnp.mean(scaled * normed, axis=-1, keepdims=True)
    return inverse * (scaled - first_mean - normed * second_mean)


def gelu_slope(value):
    cumulative = 0.5 * (1.0 + lax.erf(value * 0.5**0.5))
    density = jnp.exp(-0.5 * value * value) * (2.0 * math.pi) ** (-0.5)
    return cumulative + value * density


def transpose_left(first, second):
    return lax.dot_general(
        first, second, (((0,), (0,)), ((), ())), preferred_element_type=jnp.float32
    )


def transpose_right(first, second):
    return lax.dot_general(
        first, second, (((1,), (1,)), ((), ())), preferred_element_type=jnp.float32
    )


def group_table(rank, cluster, owners):
    share = cluster // owners
    target = rank // cluster
    length = rank.shape[-1]
    places = lax.broadcasted_iota(jnp.int32, (length, length), 0)
    later = lax.broadcasted_iota(jnp.int32, (length, length), 1)
    before = (places < later)[None, None]
    same = target[..., :, None] == target[..., None, :]
    earlier = jnp.sum((same & before).astype(jnp.int32), axis=-2)
    position = target * share + earlier
    slots = lax.broadcasted_iota(jnp.int32, position.shape + (length,), 3)
    return (position[..., None] == slots).astype(jnp.bfloat16)


def sort_heads(rows, table, heads):
    seqs, length, width = rows.shape
    split = rows.reshape(seqs, length, heads, width // heads)
    moved = jnp.einsum("shtp,sthd->sphd", table, split, preferred_element_type=jnp.float32)
    return moved.astype(rows.dtype).reshape(seqs, length, width)


def unsort_heads(rows, table, heads):
    seqs, length, width = rows.shape
    split = rows.reshape(seqs, length, heads, width // heads)
    moved = jnp.einsum("shtp,sphd->sthd", table, split, preferred_element_type=jnp.float32)
    return moved.astype(rows.dtype).reshape(seqs, length, width)


def cluster_scores(queries, keys_rows, heads):
    items, length, width = queries.shape
    size = width // heads
    query_split = queries.reshape(items, length, heads, size)
    key_split = keys_rows.reshape(items, length, heads, size)
    scores = jnp.einsum(
        "sqhd,skhd->shqk", query_split, key_split, preferred_element_type=jnp.float32
    )
    return scores * size ** (-0.5)


def cluster_forward(queries, keys_rows, values_rows, heads):
    items, length, width = queries.shape
    scores = cluster_scores(queries, keys_rows, heads)
    top = jnp.max(scores, axis=-1, keepdims=True)
    weights = jnp.exp(scores - top)
    total = jnp.sum(weights, axis=-1, keepdims=True)
    probs = (weights / total).astype(jnp.bfloat16)
    value_split = values_rows.reshape(items, length, heads, width // heads)
    context = jnp.einsum("shqk,skhd->sqhd", probs, value_split, preferred_element_type=jnp.float32)
    return (
        context.reshape(items, length, width).astype(jnp.bfloat16),
        (top + jnp.log(total))[..., 0],
    )


def cluster_backward(scores, log_total, queries, keys_rows, values_rows, grad_context, heads):
    items, length, width = queries.shape
    size = width // heads
    query_split = queries.reshape(items, length, heads, size)
    key_split = keys_rows.reshape(items, length, heads, size)
    value_split = values_rows.reshape(items, length, heads, size)
    grad_split = grad_context.reshape(items, length, heads, size)
    probs = jnp.exp(scores - log_total[..., None])
    grad_probs = jnp.einsum(
        "sqhd,skhd->shqk", grad_split, value_split, preferred_element_type=jnp.float32
    )
    inner = jnp.sum(probs * grad_probs, axis=-1, keepdims=True)
    grad_scores = (probs * (grad_probs - inner)).astype(jnp.bfloat16)
    scale = size ** (-0.5)
    grad_query = (
        jnp.einsum("shqk,skhd->sqhd", grad_scores, key_split, preferred_element_type=jnp.float32)
        * scale
    )
    grad_key = (
        jnp.einsum("shqk,sqhd->skhd", grad_scores, query_split, preferred_element_type=jnp.float32)
        * scale
    )
    grad_value = jnp.einsum(
        "shqk,sqhd->skhd",
        probs.astype(jnp.bfloat16),
        grad_split,
        preferred_element_type=jnp.float32,
    )
    shape = (items, length, width)
    return (
        grad_query.reshape(shape).astype(jnp.bfloat16),
        grad_key.reshape(shape).astype(jnp.bfloat16),
        grad_value.reshape(shape).astype(jnp.bfloat16),
    )


def send_context(context):
    return lax.all_to_all(context, "seq", split_axis=1, concat_axis=1, tiled=True)


def send_grads(grads):
    return (
        lax.all_to_all(grads[0], "seq", split_axis=1, concat_axis=1, tiled=True),
        lax.all_to_all(grads[1], "seq", split_axis=1, concat_axis=1, tiled=True),
        lax.all_to_all(grads[2], "seq", split_axis=1, concat_axis=1, tiled=True),
    )


def make_step(left, pieces):
    total = jnp.dot(left, pieces[0], preferred_element_type=jnp.float32)
    stored = tuple(pieces[1:]) + ()
    placed = tuple((piece for piece in stored))
    return (total,) + placed


def make_hidden_step(before, pieces):
    section = before + pieces[1].astype(jnp.float32)
    activated = jax.nn.gelu(section, approximate=False).astype(jnp.bfloat16)
    total = jnp.dot(activated, pieces[0], preferred_element_type=jnp.float32)
    stored = ()
    return (total, section, activated) + stored


def per_device(
    tokens,
    attend_weight,
    query_bias,
    value_bias,
    output_weight,
    output_bias,
    first_gain,
    first_shift,
    expand_weight,
    expand_bias,
    reduce_weight,
    reduce_bias,
    second_gain,
    second_shift,
    query_rank,
    key_rank,
    cotangent,
):
    seqs, cluster, width = tokens.shape
    heads = query_rank.shape[1]
    rows = seqs * cluster
    owners = lax.axis_size("seq")
    flat = tokens.reshape(rows, width)
    attend_out = make_step(
        flat,
        (
            lax.all_gather(attend_weight, "batch", axis=0, tiled=True),
            lax.all_gather(query_bias, "batch", axis=0, tiled=True),
            lax.all_gather(value_bias, "batch", axis=0, tiled=True),
        ),
    )
    summed = attend_out[0]
    queries = (summed[:, :width] + attend_out[1].astype(jnp.float32)).astype(jnp.bfloat16)
    keys_rows = summed[:, width : 2 * width].astype(jnp.bfloat16)
    values_rows = (summed[:, 2 * width :] + attend_out[2].astype(jnp.float32)).astype(jnp.bfloat16)
    query_table = group_table(query_rank, cluster, owners)
    key_table = group_table(key_rank, cluster, owners)
    query_sorted = sort_heads(queries.reshape(seqs, cluster, width), query_table, heads)
    key_sorted = sort_heads(keys_rows.reshape(seqs, cluster, width), key_table, heads)
    value_sorted = sort_heads(values_rows.reshape(seqs, cluster, width), key_table, heads)
    received = (
        lax.all_to_all(query_sorted, "seq", split_axis=1, concat_axis=1, tiled=True),
        lax.all_to_all(key_sorted, "seq", split_axis=1, concat_axis=1, tiled=True),
        lax.all_to_all(value_sorted, "seq", split_axis=1, concat_axis=1, tiled=True),
    )
    context, log_total = cluster_forward(received[0], received[1], received[2], heads)
    forward_out = (send_context(context), log_total, received[0], received[1], received[2])
    context_rows = unsort_heads(forward_out[0], query_table, heads).reshape(rows, width)
    output_out = make_step(
        context_rows,
        (
            lax.all_gather(output_weight, "batch", axis=0, tiled=True),
            lax.all_gather(output_bias, "batch", axis=0, tiled=True),
            lax.all_gather(first_gain, "batch", axis=0, tiled=True),
            lax.all_gather(first_shift, "batch", axis=0, tiled=True),
        ),
    )
    resid_one = flat.astype(jnp.float32) + output_out[0] + output_out[1].astype(jnp.float32)
    gain_one = output_out[2].astype(jnp.float32)
    middle, normed_one, inverse_one = layer_norm(
        resid_one, gain_one, output_out[3].astype(jnp.float32)
    )
    middle_low = middle.astype(jnp.bfloat16)
    expand_out = make_step(
        middle_low,
        (
            lax.all_gather(expand_weight, "batch", axis=0, tiled=True),
            lax.all_gather(reduce_bias, "batch", axis=0, tiled=True),
            lax.all_gather(second_gain, "batch", axis=0, tiled=True),
            lax.all_gather(second_shift, "batch", axis=0, tiled=True),
        ),
    )
    hidden_out = make_hidden_step(
        expand_out[0],
        (
            lax.all_gather(reduce_weight, "batch", axis=0, tiled=True),
            lax.all_gather(expand_bias, "batch", axis=0, tiled=True),
        ),
    )
    pre_full, hidden_full = (hidden_out[1], hidden_out[2])
    resid_two = middle + hidden_out[0] + expand_out[1].astype(jnp.float32)
    gain_two = expand_out[2].astype(jnp.float32)
    final, normed_two, inverse_two = layer_norm(
        resid_two, gain_two, expand_out[3].astype(jnp.float32)
    )
    layer_out = final.astype(jnp.bfloat16).reshape(seqs, cluster, width)
    attend_full, output_full, expand_full, reduce_full = (
        lax.all_gather(attend_weight, "batch", axis=0, tiled=True),
        lax.all_gather(output_weight, "batch", axis=0, tiled=True),
        lax.all_gather(expand_weight, "batch", axis=0, tiled=True),
        lax.all_gather(reduce_weight, "batch", axis=0, tiled=True),
    )
    upstream = cotangent.reshape(rows, width).astype(jnp.float32)
    grad_second_gain = jnp.sum(upstream * normed_two, axis=0)
    grad_second_shift = jnp.sum(upstream, axis=0)
    grad_resid_two = norm_back(upstream, normed_two, inverse_two, gain_two)
    grad_branch_two = grad_resid_two.astype(jnp.bfloat16)
    grad_reduce_bias = jnp.sum(grad_branch_two, axis=0, dtype=jnp.float32)
    grad_reduce = transpose_left(hidden_full, grad_branch_two)
    grad_hidden = transpose_right(grad_branch_two, reduce_full)
    grad_pre = (grad_hidden * gelu_slope(pre_full)).astype(jnp.bfloat16)
    grad_expand_bias = jnp.sum(grad_pre, axis=0, dtype=jnp.float32)
    grad_expand = transpose_left(middle_low, grad_pre)
    grad_middle = grad_resid_two + transpose_right(grad_pre, expand_full)
    grad_first_gain = jnp.sum(grad_middle * normed_one, axis=0)
    grad_first_shift = jnp.sum(grad_middle, axis=0)
    grad_resid_one = norm_back(grad_middle, normed_one, inverse_one, gain_one)
    grad_branch_one = grad_resid_one.astype(jnp.bfloat16)
    grad_output_bias = jnp.sum(grad_branch_one, axis=0, dtype=jnp.float32)
    grad_output = transpose_left(context_rows, grad_branch_one)
    grad_context = transpose_right(grad_branch_one, output_full).astype(jnp.bfloat16)
    grad_sorted = sort_heads(grad_context.reshape(seqs, cluster, width), query_table, heads)
    grad_received = lax.all_to_all(grad_sorted, "seq", split_axis=1, concat_axis=1, tiled=True)
    kept_scores = cluster_scores(forward_out[2], forward_out[3], heads)
    home = send_grads(
        cluster_backward(
            kept_scores,
            forward_out[1],
            forward_out[2],
            forward_out[3],
            forward_out[4],
            grad_received,
            heads,
        )
    )
    grad_queries = unsort_heads(home[0], query_table, heads).reshape(rows, width)
    grad_keys = unsort_heads(home[1], key_table, heads).reshape(rows, width)
    grad_values = unsort_heads(home[2], key_table, heads).reshape(rows, width)
    grad_mixed = jnp.concatenate([grad_queries, grad_keys, grad_values], axis=1)
    grad_query_bias = jnp.sum(grad_queries, axis=0, dtype=jnp.float32)
    grad_value_bias = jnp.sum(grad_values, axis=0, dtype=jnp.float32)
    grad_attend = transpose_left(flat, grad_mixed)
    token_grad = (
        (grad_resid_one + transpose_right(grad_mixed, attend_full))
        .astype(jnp.bfloat16)
        .reshape(seqs, cluster, width)
    )
    owned = (
        lax.psum_scatter(
            grad_attend.astype(jnp.bfloat16), "batch", scatter_dimension=0, tiled=True
        ).astype(jnp.float32),
        lax.psum_scatter(
            grad_query_bias.astype(jnp.bfloat16), "batch", scatter_dimension=0, tiled=True
        ).astype(jnp.float32),
        lax.psum_scatter(
            grad_value_bias.astype(jnp.bfloat16), "batch", scatter_dimension=0, tiled=True
        ).astype(jnp.float32),
        lax.psum_scatter(
            grad_output.astype(jnp.bfloat16), "batch", scatter_dimension=0, tiled=True
        ).astype(jnp.float32),
        lax.psum_scatter(
            grad_output_bias.astype(jnp.bfloat16), "batch", scatter_dimension=0, tiled=True
        ).astype(jnp.float32),
        lax.psum_scatter(
            grad_first_gain.astype(jnp.bfloat16), "batch", scatter_dimension=0, tiled=True
        ).astype(jnp.float32),
        lax.psum_scatter(
            grad_first_shift.astype(jnp.bfloat16), "batch", scatter_dimension=0, tiled=True
        ).astype(jnp.float32),
        lax.psum_scatter(
            grad_expand.astype(jnp.bfloat16), "batch", scatter_dimension=0, tiled=True
        ).astype(jnp.float32),
        lax.psum_scatter(
            grad_expand_bias.astype(jnp.bfloat16), "batch", scatter_dimension=0, tiled=True
        ).astype(jnp.float32),
        lax.psum_scatter(
            grad_reduce.astype(jnp.bfloat16), "batch", scatter_dimension=0, tiled=True
        ).astype(jnp.float32),
        lax.psum_scatter(
            grad_reduce_bias.astype(jnp.bfloat16), "batch", scatter_dimension=0, tiled=True
        ).astype(jnp.float32),
        lax.psum_scatter(
            grad_second_gain.astype(jnp.bfloat16), "batch", scatter_dimension=0, tiled=True
        ).astype(jnp.float32),
        lax.psum_scatter(
            grad_second_shift.astype(jnp.bfloat16), "batch", scatter_dimension=0, tiled=True
        ).astype(jnp.float32),
    )
    shared = (
        lax.psum(owned[0].astype(jnp.bfloat16), "seq").astype(jnp.float32),
        lax.psum(owned[1].astype(jnp.bfloat16), "seq").astype(jnp.float32),
        lax.psum(owned[2].astype(jnp.bfloat16), "seq").astype(jnp.float32),
        lax.psum(owned[3].astype(jnp.bfloat16), "seq").astype(jnp.float32),
        lax.psum(owned[4].astype(jnp.bfloat16), "seq").astype(jnp.float32),
        lax.psum(owned[5].astype(jnp.bfloat16), "seq").astype(jnp.float32),
        lax.psum(owned[6].astype(jnp.bfloat16), "seq").astype(jnp.float32),
        lax.psum(owned[7].astype(jnp.bfloat16), "seq").astype(jnp.float32),
        lax.psum(owned[8].astype(jnp.bfloat16), "seq").astype(jnp.float32),
        lax.psum(owned[9].astype(jnp.bfloat16), "seq").astype(jnp.float32),
        lax.psum(owned[10].astype(jnp.bfloat16), "seq").astype(jnp.float32),
        lax.psum(owned[11].astype(jnp.bfloat16), "seq").astype(jnp.float32),
        lax.psum(owned[12].astype(jnp.bfloat16), "seq").astype(jnp.float32),
    )
    return (
        layer_out,
        token_grad,
        shared[0],
        shared[1],
        shared[2],
        shared[3],
        shared[4],
        shared[5],
        shared[6],
        shared[7],
        shared[8],
        shared[9],
        shared[10],
        shared[11],
        shared[12],
    )


MESH = pl.DeviceIdType.MESH
f32 = jnp.float32
bf16 = jnp.bfloat16


class Place:
    def __init__(self, chips, depth):
        self.chips, self.depth = chips, depth
        self.z = lax.axis_index("batch")
        spot = lax.axis_index("seq")
        self.chip, self.core = lax.div(spot, 2), lax.rem(spot, 2)

    def chip_at(self, k):
        return lax.rem(self.chip + k + self.chips, self.chips)

    def z_at(self, k):
        return lax.rem(self.z + k + self.depth, self.depth)

    def plane(self, k):
        return (self.z, self.chip_at(k) * 2 + self.core)

    def tower(self, k):
        return (self.z_at(k), self.chip * 2 + self.core)

    def sibling(self):
        return (self.z, self.chip * 2 + 1 - self.core)

    def greet(self):
        bell = pltpu.get_barrier_semaphore()
        others = [self.plane(k) for k in range(1, self.chips)]
        others += [self.tower(k) for k in range(1, self.depth)]
        others.append(self.sibling())
        for other in others:
            pl.semaphore_signal(bell, inc=1, device_id=other, device_id_type=MESH)
        pl.semaphore_wait(bell, len(others))


def far_copy(src, dst, sems, at, device):
    return pltpu.make_async_remote_copy(
        src_ref=src,
        dst_ref=dst,
        send_sem=sems[0].at[at],
        recv_sem=sems[1].at[at],
        device_id=device,
        device_id_type=MESH,
    )


def one_hot(row, slots):
    return jnp.where(slots == row, 1.0, 0.0).astype(bf16)


def split_lanes(tile, low):
    zero = jnp.zeros_like(tile)
    return jnp.where(low, tile, zero), jnp.where(low, zero, tile)


def stack_lanes(tile, low):
    first, second = split_lanes(tile, low)
    return jnp.concatenate([first, second], axis=0)


def dot_rows(a, b):
    return jnp.dot(a, b, preferred_element_type=f32)


def dot_lanes(a, b):
    return lax.dot_general(a, b, (((1,), (1,)), ((), ())), preferred_element_type=f32)


def dot_first(a, b):
    return lax.dot_general(a, b, (((0,), (0,)), ((), ())), preferred_element_type=f32)


def multiple(value, by):
    return pl.multiple_of(value, by)


def forward_kernel(
    chips,
    depth,
    heads,
    tok_ref,
    pos_ref,
    aw_ref,
    vec_ref,
    ow_ref,
    ew_ref,
    rw_ref,
    cot_ref,
    x_out,
    ctx_out,
    q_out,
    k_out,
    v_out,
    p_out,
    pos_out,
    aw_out,
    vec_out,
    ow_out,
    ew_out,
    rw_out,
    n1_out,
    inv_out,
    ml_out,
    hid_out,
    slope_out,
    lo_out,
    gr_out,
    gb_out,
    sum_out,
    xbuf,
    posbuf,
    wbuf,
    vbuf,
    bias,
    ctxb,
    ctxt,
    owbuf,
    ewbuf,
    rwbuf,
    cbuf,
    n1buf,
    invbuf,
    mlbuf,
    vecs,
    upb,
    sums,
    tok_s,
    tok_r,
    tokc_s,
    tokc_r,
    pos_s,
    pos_r,
    posc_s,
    posc_r,
    up_s,
    up_r,
    dn_s,
    dn_r,
    awc_s,
    awc_r,
    vec_s,
    vec_r,
    wz_s,
    wz_r,
    wp_s,
    wp_r,
    wd_s,
    wd_r,
    wc_s,
    wc_r,
    ctx_s,
    ctx_r,
    cot_s,
    cot_r,
    oc_s,
    oc_r,
    loc,
    out_sem,
    slope_sem,
    att_sem,
    late_sem,
):
    me = Place(chips, depth)
    z, chip, core = me.z, me.chip, me.core
    per = tok_ref.shape[0] // chips
    half = aw_ref.shape[1] // 6
    rows_z = aw_ref.shape[0]
    pairs = heads // 4
    size = half // (2 * pairs)
    me.greet()

    def aw_block(zz):
        return wbuf.at[pl.ds(multiple(zz * rows_z, 8), rows_z)]

    def up_copy(h):
        return far_copy(
            aw_block(z - h), aw_block(z - h), (up_s, up_r), h, (z + 1, chip * 2 + core)
        )

    def down_copy(h):
        return far_copy(
            aw_block(z + h), aw_block(z + h), (dn_s, dn_r), h, (z - 1, chip * 2 + core)
        )

    def up_got(h):
        return far_copy(
            aw_block(z - 1 - h), aw_block(z - 1 - h), (up_s, up_r), h, me.sibling()
        )

    def down_got(h):
        return far_copy(
            aw_block(z + 1 + h), aw_block(z + 1 + h), (dn_s, dn_r), h, me.sibling()
        )

    def pass_on():
        @pl.when(z < depth - 1)
        def _():
            up_copy(0).start()

        @pl.when(z > 0)
        def _():
            down_copy(0).start()

    def pass_rest(hops):
        for h in hops:

            @pl.when(z > h)
            def _():
                up_got(h).wait_recv()
                if h + 1 < depth - 1:

                    @pl.when(z < depth - 1)
                    def _():
                        up_copy(h + 1).start()

            @pl.when(z + 1 + h < depth)
            def _():
                down_got(h).wait_recv()
                if h + 1 < depth - 1:

                    @pl.when(z > 0)
                    def _():
                        down_copy(h + 1).start()

    def pass_end():
        for h in range(depth - 1):

            @pl.when((z >= h) & (z < depth - 1))
            def _():
                up_copy(h).wait_send()

            @pl.when((z + h < depth) & (z > 0))
            def _():
                down_copy(h).wait_send()

    def mine(ref, target):
        return ref.at[pl.ds(target * per, per)]

    def tok_copy(k):
        return far_copy(
            mine(tok_ref, me.chip_at(k)), xbuf.at[core, chip], (tok_s, tok_r), k - 1, me.plane(k)
        )

    def pos_copy(k):
        return far_copy(
            mine(pos_ref, me.chip_at(k)), posbuf.at[core, chip], (pos_s, pos_r), k - 1, me.plane(k)
        )

    def vec_copy(k):
        return far_copy(vec_ref, vbuf.at[z], (vec_s, vec_r), k - 1, me.tower(k))

    sends = []
    for k in range(1, chips):
        sends.append(pos_copy(k))
        sends[-1].start()
    for k in range(1, depth):
        sends.append(vec_copy(k))
        sends[-1].start()
    for k in range(1, chips):
        sends.append(tok_copy(k))
        sends[-1].start()
    local = []

    def keep(src, dst):
        copy = pltpu.make_async_copy(src, dst, loc.at[len(local)])
        copy.start()
        local.append(copy)

    for part in range(3):
        keep(
            aw_ref.at[:, pl.ds(multiple(part * 2 * half + core * half, 128), half)],
            wbuf.at[pl.ds(multiple(z * rows_z, 8), rows_z), pl.ds(part * half, half)],
        )
    keep(mine(tok_ref, chip), xbuf.at[core, chip])
    keep(mine(pos_ref, chip), posbuf.at[core, chip])
    keep(vec_ref, vbuf.at[z])
    for copy in local[:3]:
        copy.wait()
    pass_on()
    wide = ew_ref.shape[1] // (2 * chips)
    tall = rw_ref.shape[0] // (2 * chips)
    mid_rows = rows_z // 2
    mine_at = core * chips + chip

    def piece(kind):
        if kind == 0:
            return ow_ref.at[pl.ds(multiple(core * mid_rows, 8), mid_rows)]
        if kind == 1:
            return ew_ref.at[:, pl.ds(multiple(mine_at * wide, 128), wide)]
        return rw_ref.at[pl.ds(multiple(mine_at * tall, 8), tall)]

    def place(kind, zz):
        if kind == 0:
            return owbuf.at[zz, core]
        if kind == 1:
            return ewbuf.at[zz, :, pl.ds(multiple(mine_at * wide, 128), wide)]
        return rwbuf.at[zz, mine_at]

    def place_all(kind, at):
        if kind == 1:
            return ewbuf.at[:, :, pl.ds(multiple(at * wide, 128), wide)]
        return rwbuf.at[:, at]

    for kind in range(3):
        keep(piece(kind), place(kind, z))

    def wz_copy(kind, k):
        return far_copy(
            piece(kind),
            place(kind, z),
            (wz_s, wz_r),
            kind * (depth - 1) + k - 1,
            me.tower(k),
        )

    beside = (chip + 1 - 2 * lax.rem(chip, 2), lax.rem(chip + 2, chips))
    across = chips - 1 - chip

    def part_of(kind, origin, side):
        at = core * chips + origin
        span = pl.ds(side * (depth // 2), depth // 2)
        if kind == 1:
            return ewbuf.at[span, :, pl.ds(multiple(at * wide, 128), wide)]
        return rwbuf.at[span, at]

    def wp_copy(kind, d):
        spot = place_all(kind, mine_at)
        return far_copy(
            spot, spot, (wp_s, wp_r), (kind - 1) * 2 + d, (z, beside[d] * 2 + core)
        )

    def wd_copy(kind, d):
        spot = part_of(kind, beside[d], d)
        return far_copy(
            spot, spot, (wd_s, wd_r), (kind - 1) * 2 + d, (z, beside[1 - d] * 2 + core)
        )

    def wc_copy(kind, n):
        at = core * chips + (chip, beside[0], beside[1], across)[n]
        return far_copy(
            place_all(kind, at),
            place_all(kind, at),
            (wc_s, wc_r),
            (kind - 1) * chips + n,
            me.sibling(),
        )

    def tower_wait(kind):
        for k in range(1, depth):
            wz_copy(kind, k).wait_recv()

    def plane_first(kind):
        for d in range(2):
            wp_copy(kind, d).start()
        wc_copy(kind, 0).start()

    def plane_second(kind):
        for d in range(2):
            wp_copy(kind, d).wait_recv()
            wd_copy(kind, d).start()
            wc_copy(kind, 1 + d).start()

    def plane_last(kind):
        for d in range(2):
            wd_copy(kind, d).wait_recv()
        wc_copy(kind, 3).start()
        for n in range(chips):
            wc_copy(kind, n).wait()
        for d in range(2):
            wp_copy(kind, d).wait_send()
            wd_copy(kind, d).wait_send()

    def oc_copy():
        spot = owbuf.at[:, core]
        return far_copy(spot, spot, (oc_s, oc_r), 0, me.sibling())

    def cot_copy(n):
        target = (beside[0], beside[1], across)[n]
        return far_copy(
            mine(cot_ref, target),
            cbuf.at[chip],
            (cot_s, cot_r),
            n,
            (z, target * 2 + core),
        )

    keep(mine(cot_ref, chip), cbuf.at[chip])

    for copy in local[3:5]:
        copy.wait()

    def tokc_copy(k):
        source = me.chip_at(-k)
        return far_copy(
            xbuf.at[core, source], xbuf.at[core, source], (tokc_s, tokc_r), k, me.sibling()
        )

    def posc_copy(k):
        source = me.chip_at(-k)
        return far_copy(
            posbuf.at[core, source], posbuf.at[core, source], (posc_s, posc_r), k, me.sibling()
        )

    for k in range(1, depth):
        wz_copy(1, k).start()
        for kind in range(3):
            sends.append(wz_copy(kind, k))
    pass_rest(range(depth - 2))
    for k in range(chips):
        if k:
            pos_copy(k).wait_recv()
            tok_copy(k).wait_recv()
        for copy in (posc_copy(k), tokc_copy(k)):
            copy.start()
            sends.append(copy)
    for copy in local[5:]:
        copy.wait()
    tower_wait(1)
    plane_first(1)
    pass_rest(range(depth - 2, depth - 1))
    for k in range(1, depth):
        wz_copy(2, k).start()
    plane_second(1)
    for n in range(2):
        cot_copy(n).start()
    for k in range(1, depth):
        vec_copy(k).wait_recv()
    for k in range(chips):
        posc_copy(k).wait_recv()
        tokc_copy(k).wait_recv()

    outs = []

    def emit(src, dst):
        copy = pltpu.make_async_copy(src, dst, out_sem.at[len(outs)])
        copy.start()
        outs.append(copy)

    emit(xbuf, x_out)
    emit(posbuf, pos_out)
    emit(wbuf, aw_out.at[core])
    awc = far_copy(wbuf, aw_out.at[core], (awc_s, awc_r), 0, me.sibling())
    awc.start()
    sends.append(awc)

    quarter = rows_z
    for zz in range(depth):
        begin = zz * quarter
        for row, at in ((0, 0), (1, 2)):
            for side in range(2):
                lo = max(begin, side * half)
                hi = min(begin + quarter, (side + 1) * half)
                if lo < hi:
                    bias[side, 0:1, at * half + lo - side * half : at * half + hi - side * half] = (
                        vbuf[zz, row : row + 1, lo - begin : hi - begin]
                    )
    bias[0, 0:1, half : 2 * half] = jnp.zeros((1, half), f32)
    bias[1, 0:1, half : 2 * half] = jnp.zeros((1, half), f32)
    added = bias[core, 0:1, :]
    for zz in range(depth):
        for row in range(8):
            vecs[row : row + 1, zz * quarter : (zz + 1) * quarter] = vbuf[
                zz, row : row + 1, :quarter
            ]
        steps = upb.shape[1] // (depth * quarter)
        for row in range(steps):
            to = (zz * steps + row) * quarter
            upb[0:1, to : to + quarter] = vbuf[zz, 8 + row : 9 + row, :quarter]

    cluster = tok_ref.shape[1]
    blocks = 2 * chips
    share = cluster // blocks
    width = tok_ref.shape[2]

    slots = lax.broadcasted_iota(jnp.int32, (cluster, cluster), 0)
    low = lax.broadcasted_iota(jnp.int32, (cluster, 128), 1) < size
    scale = size ** (-0.5)

    def tables(jj, i, pair, part):
        first = part * heads + core * (heads // 2) + 2 * pair
        rows = [
            one_hot(posbuf[jj // chips, jj % chips, i, pl.ds(first + h, 1), :], slots)
            for h in range(2)
        ]
        return rows

    def hook(i, pair):
        step = i * pairs + pair
        last = per * pairs - 1

        @pl.when(step == min(2, last))
        def _():
            tower_wait(2)
            plane_first(2)
            for k in range(1, depth):
                wz_copy(0, k).start()

        @pl.when(step == last)
        def _():
            plane_second(2)
            cot_copy(2).start()

    def attention(qkv, qs, ks, vs, ps, os):
        def group_copies(i):
            span = pl.ds(i * pairs, pairs)
            pieces = ((qs, q_out), (ks, k_out), (vs, v_out), (ps, p_out))
            return [
                pltpu.make_async_copy(src.at[span], dst.at[span], att_sem.at[5 + 4 * i + n])
                for n, (src, dst) in enumerate(pieces)
            ]

        @pl.loop(0, blocks)
        def _(jj):
            x = xbuf[lax.div(jj, chips), lax.rem(jj, chips)].reshape(per * cluster, width)
            mixed = (dot_rows(x, wbuf[...]) + added).astype(bf16)
            for at in range(3 * pairs):
                qkv[at, jj] = mixed[:, at * 128 : (at + 1) * 128].reshape(per, cluster, 128)

        @pl.loop(0, per)
        def _(i):
            @pl.loop(0, pairs)
            def _(pair):
                at = i * pairs + pair
                for jj in range(blocks):
                    tq = jnp.concatenate(tables(jj, i, pair, 0), axis=1)
                    tk = jnp.concatenate(tables(jj, i, pair, 1), axis=1)
                    q = stack_lanes(qkv[pair, jj, i], low)
                    k = stack_lanes(qkv[pairs + pair, jj, i], low)
                    v = stack_lanes(qkv[2 * pairs + pair, jj, i], low)
                    span = slice(jj * share, (jj + 1) * share)
                    sq = dot_rows(tq, q).astype(bf16)
                    skv = dot_rows(tk, jnp.concatenate([k, v], axis=1)).astype(bf16)
                    qs[at, :, span, :] = sq.reshape(blocks, share, 128)
                    ks[at, :, span, :] = skv[:, :128].reshape(blocks, share, 128)
                    vs[at, :, span, :] = skv[:, 128:].reshape(blocks, share, 128)
                for c in range(blocks):
                    scores = dot_lanes(qs[at, c], stack_lanes(ks[at, c], low)) * scale
                    halves = []
                    for h in range(2):
                        s = scores[:, h * cluster : (h + 1) * cluster]
                        e = jnp.exp(s - jnp.max(s, axis=1, keepdims=True))
                        halves.append((e / jnp.sum(e, axis=1, keepdims=True)).astype(bf16))
                    probs = jnp.concatenate(halves, axis=1)
                    ps[at, c] = probs
                    o = dot_rows(probs, stack_lanes(vs[at, c], low)).astype(bf16)
                    os[c] = o
                for jj in range(blocks):
                    tq = jnp.concatenate(tables(jj, i, pair, 0), axis=0)
                    rows = os[:, jj * share : (jj + 1) * share, :].reshape(cluster, 128)
                    back = dot_first(tq, stack_lanes(rows, low)).astype(bf16)
                    ctxb[jj // chips, jj % chips, i, :, pl.ds(multiple(pair * 128, 128), 128)] = back
                hook(i, pair)

                @pl.when(pair == pairs - 1)
                def _():
                    for copy in group_copies(i):
                        copy.start()


        far, own = ctx_copies()
        for copy in (far, own):
            copy.start()
        for copy in (far, own):
            copy.wait()
        for i in range(per):
            for copy in group_copies(i):
                copy.wait()

    def ctx_copies():
        lanes = pl.ds(multiple(core * half, 128), half)
        far = far_copy(
            ctxb.at[1 - core], ctxt.at[:, :, :, lanes], (ctx_s, ctx_r), 0, me.sibling()
        )
        own = pltpu.make_async_copy(ctxb.at[core], ctxt.at[:, :, :, lanes], att_sem.at[4])
        return far, own

    group = (per * pairs, blocks, cluster, 128)
    pl.run_scoped(
        attention,
        pltpu.VMEM((3 * pairs, blocks, per, cluster, 128), bf16),
        pltpu.VMEM(group, bf16),
        pltpu.VMEM(group, bf16),
        pltpu.VMEM(group, bf16),
        pltpu.VMEM((per * pairs, blocks, cluster, 2 * cluster), bf16),
        pltpu.VMEM((blocks, cluster, 128), bf16),
    )

    tower_wait(0)
    oc_copy().start()
    oc_copy().wait()
    emit(ctxt, ctx_out)
    context_out = outs[-1]
    emit(owbuf, ow_out)
    tile = per * cluster
    hidden = upb.shape[1]
    eps = epsilon

    def moments(rows):
        center = jnp.mean(rows, axis=1, keepdims=True)
        centered = rows - center
        spread = jnp.mean(centered * centered, axis=1, keepdims=True)
        inverse = lax.rsqrt(spread + eps)
        return centered * inverse, inverse

    def slope_out_copy(j, slot):
        return pltpu.make_async_copy(sbuf.at[slot], slope_out.at[j], slope_sem.at[slot])

    def vec(row):
        return vecs[row : row + 1, :]

    def feed(hbuf, sbuf):
        step = sbuf.shape[3]

        def late_copies(j):
            pieces = ((cbuf, lo_out), (n1buf, gr_out), (ctxt, gb_out))
            return [
                pltpu.make_async_copy(src.at[j], dst.at[j], late_sem.at[3 * j + n])
                for n, (src, dst) in enumerate(pieces)
            ]

        def slope_copy(n):
            return pltpu.make_async_copy(
                sbuf.at[n % 2],
                slope_out.at[:, :, pl.ds(n * step, step)],
                slope_sem.at[n % 2],
            )

        @pl.loop(0, chips)
        def _(j):
            rows = ctxt[j].reshape(tile, width)
            branch = dot_rows(rows, owbuf[...].reshape(width, width))
            resid = xbuf[core, j].reshape(tile, width).astype(f32) + branch + vec(2)
            normed, inverse = moments(resid)
            n1buf[j] = normed
            invbuf[j] = jnp.broadcast_to(inverse, (tile, 128))
            mlbuf[j] = (normed * vec(3) + vec(4)).astype(bf16).reshape(per, cluster, width)

        plane_last(1)
        emit(ewbuf, ew_out)
        for n in range(hidden // step):
            lanes = slice(n * step, (n + 1) * step)
            if n >= 2:
                slope_copy(n - 2).wait()
            for j in range(chips):
                weight = ewbuf[:, :, lanes].reshape(width, step)
                pre = dot_rows(mlbuf[j].reshape(tile, width), weight) + upb[0:1, lanes]
                cumulative = 0.5 * (1.0 + lax.erf(pre * 0.5**0.5))
                density = jnp.exp(-0.5 * pre * pre) * (2.0 * math.pi) ** (-0.5)
                hbuf[j, :, lanes] = (pre * cumulative).astype(bf16)
                sbuf[n % 2, j] = (cumulative + pre * density).astype(bf16)
            slope_copy(n).start()

        emit(vecs, vec_out)
        held = len(outs)
        emit(n1buf, n1_out)
        emit(invbuf, inv_out)
        emit(mlbuf, ml_out)
        emit(hbuf, hid_out)
        plane_last(2)
        pass_end()
        emit(rwbuf, rw_out)
        for n in range(2):
            cot_copy(n).wait()
        sums[...] = jnp.zeros_like(sums)
        waited = (context_out, outs[held])
        for copy in waited:
            copy.wait()

        @pl.loop(0, chips)
        def _(n):
            j = 2 * lax.rem(lax.div(chip, 2) + lax.div(n, 2), 2)
            j = j + lax.rem(chip + n, 2)

            @pl.when(n == chips - 1)
            def _():
                cot_copy(2).wait()

            branch = vec(5)
            for zz in range(depth):
                span = hidden // depth
                branch = branch + dot_rows(
                    hbuf[j, :, zz * span : (zz + 1) * span], rwbuf[zz].reshape(span, width)
                )
            middle = n1buf[j] * vec(3) + vec(4)
            normed, inverse = moments(middle + branch)
            upstream = cbuf[j].reshape(tile, width).astype(f32)
            cbuf[j] = (normed * vec(6) + vec(7)).astype(bf16).reshape(per, cluster, width)
            sums[0:1, :] += jnp.sum(upstream * normed, axis=0, keepdims=True)
            sums[1:2, :] += jnp.sum(upstream, axis=0, keepdims=True)
            scaled = upstream * vec(6)
            first = jnp.mean(scaled, axis=1, keepdims=True)
            second = jnp.mean(scaled * normed, axis=1, keepdims=True)
            grad = inverse * (scaled - first - normed * second)
            n1buf[j] = grad
            low_grad = grad.astype(bf16)
            sums[2:3, :] += jnp.sum(low_grad.astype(f32), axis=0, keepdims=True)
            ctxt[j] = low_grad.reshape(per, cluster, width)
            for copy in late_copies(j):
                copy.start()

        emit(sums, sum_out)
        for j in range(chips):
            for copy in late_copies(j):
                copy.wait()
        for copy in sends:
            copy.wait_send()
        awc.wait_recv()
        for n in range(max(hidden // step - 2, 0), hidden // step):
            slope_copy(n).wait()
        for copy in outs:
            if not any(copy is other for other in waited):
                copy.wait()

    pl.run_scoped(
        feed,
        pltpu.VMEM((chips, tile, hidden), bf16),
        pltpu.VMEM((2, chips, tile, hidden // depth), bf16),
    )


def forward(
    tokens,
    pos,
    attend_weight,
    vectors,
    output_weight,
    expand_weight,
    reduce_weight,
    cotangent,
    chips,
    depth,
    heads,
):
    seqs, cluster, width = tokens.shape
    per, blocks, pairs = seqs // chips, 2 * chips, heads // 4
    half = width // 2
    rows_z = attend_weight.shape[0]
    hidden = expand_weight.shape[1]
    items = per * pairs
    tile = per * cluster
    dma = pltpu.SemaphoreType.DMA
    anywhere = pl.BlockSpec(memory_space=pl.ANY)
    tall = reduce_weight.shape[0] // blocks
    shapes = [
        ((2, chips, per, cluster, width), bf16),
        ((chips, per, cluster, width), bf16),
        ((items, blocks, cluster, 128), bf16),
        ((items, blocks, cluster, 128), bf16),
        ((items, blocks, cluster, 128), bf16),
        ((items, blocks, cluster, 2 * cluster), bf16),
        ((2, chips, per, 2 * heads, cluster), jnp.int32),
        ((2, depth * rows_z, 3 * half), bf16),
        ((8, width), f32),
        ((depth, 2, rows_z // 2, width), bf16),
        ((depth, rows_z, hidden), bf16),
        ((depth, blocks, tall, width), bf16),
        ((chips, tile, width), f32),
        ((chips, tile, 128), f32),
        ((chips, per, cluster, width), bf16),
        ((chips, tile, hidden), bf16),
        ((chips, tile, hidden), bf16),
        ((chips, per, cluster, width), bf16),
        ((chips, tile, width), f32),
        ((chips, per, cluster, width), bf16),
        ((8, width), f32),
    ]
    t, c = depth - 1, chips - 1
    vm = pltpu.VMEM
    return pl.pallas_call(
        functools.partial(forward_kernel, chips, depth, heads),
        out_shape=[jax.ShapeDtypeStruct(*s) for s in shapes],
        in_specs=[anywhere] * 8,
        out_specs=[anywhere] * len(shapes),
        scratch_shapes=[
            vm(shapes[0][0], bf16),
            vm(shapes[6][0], jnp.int32),
            vm(shapes[7][0][1:], bf16),
            vm((depth,) + vectors.shape, f32),
            vm((2, 8, 3 * half), f32),
            vm((2, chips, per, cluster, half), bf16),
            vm(shapes[1][0], bf16),
            vm(shapes[9][0], bf16),
            vm(shapes[10][0], bf16),
            vm(shapes[11][0], bf16),
            vm(shapes[17][0], bf16),
            vm(shapes[12][0], f32),
            vm(shapes[13][0], f32),
            vm(shapes[14][0], bf16),
            vm((8, width), f32),
            vm((8, hidden), f32),
            vm((8, width), f32),
            dma((c,)), dma((c,)), dma((chips,)), dma((chips,)),
            dma((c,)), dma((c,)), dma((chips,)), dma((chips,)),
            dma((t,)), dma((t,)), dma((t,)), dma((t,)), dma((1,)), dma((1,)),
            dma((t,)), dma((t,)),
            dma((3 * t,)), dma((3 * t,)),
            dma((4,)), dma((4,)), dma((4,)), dma((4,)),
            dma((2 * chips,)), dma((2 * chips,)),
            dma((1,)), dma((1,)),
            dma((c,)), dma((c,)),
            dma((1,)), dma((1,)),
            dma((12,)), dma((24,)), dma((2,)), dma((5 + 4 * per,)), dma((3 * chips,)),
        ],
        compiler_params=pltpu.CompilerParams(
            collective_id=1, has_side_effects=True, vmem_limit_bytes=63 * 2**20
        ),
        name="forward",
    )(
        tokens,
        pos,
        attend_weight,
        vectors,
        output_weight,
        expand_weight,
        reduce_weight,
        cotangent,
    )


def add_into(target, at, parts):
    total = target[at].astype(f32)
    for part in parts:
        total = total + part.astype(f32)
    target[at] = total.astype(target.dtype)


class Reducer:
    def __init__(self, me, own, other, near, mid, last, done, sems, tower_first):
        self.me, self.own, self.other = me, own, other
        self.near, self.mid, self.last, self.done = near, mid, last, done
        (self.near_s, self.near_r, self.mid_s, self.mid_r, self.last_s, self.last_r) = sems[:6]
        (self.back_s, self.back_r, self.side_s, self.side_r) = sems[6:10]
        self.tower_first = tower_first
        self.sizes = (mid.shape[0] + 1, last.shape[0] + 1)

    def spot(self, axis, k):
        me = self.me
        if self.tower_first == (axis == 0):
            return me.z_at(k), me.tower(k)
        return me.chip_at(k), me.plane(k)

    def near_copy(self, a):
        return far_copy(
            self.other.at[a], self.near.at[a], (self.near_s, self.near_r), a, self.me.sibling()
        )

    def fold_near(self, a):
        self.near_copy(a).wait_recv()
        for b in range(self.sizes[1]):
            add_into(self.own, (a, b), [self.near[a, b]])

    def mid_copy(self, k):
        where, device = self.spot(0, k)
        return far_copy(
            self.own.at[where], self.mid.at[k - 1], (self.mid_s, self.mid_r), k - 1, device
        )

    def send_mid(self):
        for k in range(1, self.sizes[0]):
            self.mid_copy(k).start()

    def fold_mid(self):
        for k in range(1, self.sizes[0]):
            self.mid_copy(k).wait()
        here = self.spot(0, 0)[0]
        for b in range(self.sizes[1]):
            add_into(self.own, (here, b), [self.mid[k - 1, b] for k in range(1, self.sizes[0])])

    def last_copy(self, k):
        here = self.spot(0, 0)[0]
        where, device = self.spot(1, k)
        return far_copy(
            self.own.at[here, where],
            self.last.at[k - 1],
            (self.last_s, self.last_r),
            k - 1,
            device,
        )

    def send_last(self):
        for k in range(1, self.sizes[1]):
            self.last_copy(k).start()

    def fold_last(self):
        me = self.me
        for k in range(1, self.sizes[1]):
            self.last_copy(k).wait()
        total = self.own[self.spot(0, 0)[0], self.spot(1, 0)[0]].astype(f32)
        for k in range(1, self.sizes[1]):
            total = total + self.last[k - 1].astype(f32)
        self.done[me.core, me.chip] = total.astype(bf16)

    def back_copy(self, k):
        me = self.me
        spot = self.done.at[me.core, me.chip]
        return far_copy(spot, spot, (self.back_s, self.back_r), k - 1, me.plane(k))

    def send_back(self):
        for k in range(1, self.done.shape[1]):
            self.back_copy(k).start()

    def side_copy(self):
        spot = self.done.at[self.me.core]
        return far_copy(spot, spot, (self.side_s, self.side_r), 0, self.me.sibling())

    def send_side(self):
        for k in range(1, self.done.shape[1]):
            self.back_copy(k).wait()
        self.side_copy().start()

    def finish(self):
        self.side_copy().wait()


class Sum:
    def __init__(self, me, vec, got, s, r):
        self.me, self.vec, self.got, self.s, self.r = me, vec, got, s, r

    def copies(self, hop):
        me = self.me
        if hop == 0:
            spots = [(0, me.sibling())]
        elif hop == 1:
            spots = [(k, me.plane(k)) for k in range(1, me.chips)]
        else:
            spots = [(me.chips + k - 1, me.tower(k)) for k in range(1, me.depth)]
        return [far_copy(self.vec, self.got.at[n], (self.s, self.r), n, d) for n, d in spots], spots

    def send(self, hop):
        for copy in self.copies(hop)[0]:
            copy.start()

    def fold(self, hop):
        copies, spots = self.copies(hop)
        for copy in copies:
            copy.wait()
        total = self.vec[...]
        for n, _ in spots:
            total = total + self.got[n]
        self.vec[...] = total


def back_kernel(
    chips,
    depth,
    heads,
    q_ref,
    k_ref,
    v_ref,
    p_ref,
    pos_ref,
    x_ref,
    aw_ref,
    ow_ref,
    ew_ref,
    rw_ref,
    vec_ref,
    ctx_ref,
    n1_ref,
    inv_ref,
    ml_ref,
    hid_ref,
    slope_ref,
    lo_ref,
    gr_ref,
    gb_ref,
    late_ref,
    token_out,
    layer_out,
    aw_out,
    ow_out,
    ew_out,
    rw_out,
    vec_out,
    bias_out,
    dbuf,
    posbuf,
    acc,
    gfar,
    p_mid,
    p_last,
    p_done,
    o_all,
    o_near,
    o_mid,
    o_last,
    o_done,
    e_all,
    e_near,
    e_mid,
    e_last,
    e_done,
    r_all,
    r_near,
    r_mid,
    r_last,
    r_done,
    vbuf,
    vgot,
    bbuf,
    bgot,
    vecs,
    d_s,
    d_r,
    g_s,
    g_r,
    t_s,
    t_r,
    lo_s,
    lo_r,
    load,
    out_sem,
    v_s,
    v_r,
    b_s,
    b_r,
    *sems,
):
    me = Place(chips, depth)
    z, core, chip = me.z, me.core, me.chip
    per, cluster, width = lo_ref.shape[1:]
    half = width // 2
    pairs = heads // 4
    size = half // (2 * pairs)
    blocks = 2 * chips
    share = cluster // blocks
    tile = per * cluster
    hidden = hid_ref.shape[2]
    wide = hidden // blocks
    strip = width // chips
    quarter = width // depth
    eighth = quarter // blocks
    rows = chips * tile
    me.greet()
    groups = [sems[n * 10 : (n + 1) * 10] for n in range(3 + heads // 4)]
    red = Reducer(
        me, r_all.at[core], r_all.at[1 - core], r_near, r_mid, r_last, r_done, groups[0], True
    )
    exp = Reducer(
        me, e_all.at[core], e_all.at[1 - core], e_near, e_mid, e_last, e_done, groups[1], False
    )
    out = Reducer(
        me, o_all.at[core], o_all.at[1 - core], o_near, o_mid, o_last, o_done, groups[2], False
    )
    sums = Sum(me, vbuf, vgot, v_s, v_r)
    biases = Sum(me, bbuf, bgot, b_s, b_r)

    def fetch(src, dst, at):
        return pltpu.make_async_copy(src, dst, load.at[at])

    def lo_copy(k):
        return far_copy(
            lo_ref.at[me.chip_at(k)],
            layer_out.at[pl.ds(chip * per, per)],
            (lo_s, lo_r),
            k - 1,
            me.plane(k),
        )

    lo_keep = pltpu.make_async_copy(
        lo_ref.at[chip], layer_out.at[pl.ds(chip * per, per)], out_sem.at[0]
    )

    block = 2 * wide
    counts = blocks // 2

    def order(n):
        return lax.rem(n + z + chip, counts)

    def fold_red(n):
        at = order(n)
        red.fold_near(at)
        k = lax.rem(at - z + depth, depth)

        @pl.when(k != 0)
        def _():
            red.mid_copy(k).start()

    def fold_exp(n):
        at = order(n)

        @pl.when(lax.div(at, 2) == core)
        def _():
            for side in range(2):
                b = lax.rem(at, 2) * 2 + side
                exp.fold_near(b)
                k = lax.rem(b - chip + chips, chips)

                @pl.when(k != 0)
                def _():
                    exp.mid_copy(k).start()

    def chunks(gb, gbt, mlt, hid, slope, rwc, ewc, gpb):
        def chunk(n, slot):
            at = order(n)
            lanes = pl.ds(multiple(at * block, 128), block)
            return [
                fetch(hid_ref.at[:, :, lanes], hid.at[slot], slot * 4),
                fetch(slope_ref.at[:, :, lanes], slope.at[slot], slot * 4 + 1),
                fetch(rw_ref.at[at], rwc.at[slot], slot * 4 + 2),
                fetch(ew_ref.at[:, :, lanes], ewc.at[slot], slot * 4 + 3),
            ]

        begin = [
            fetch(gb_ref, gb, 8),
            fetch(ml_ref, gpb, 9),
            fetch(gr_ref, acc, 10),
        ]
        later = [
            fetch(vec_ref, vecs, 11),
            fetch(late_ref, vbuf.at[pl.ds(0, 8)], 12),
            fetch(pos_ref, posbuf, 18),
        ]
        for copy in begin + chunk(0, 0) + later:
            copy.start()
        for k in range(1, chips):
            lo_copy(k).start()
        lo_keep.start()
        vbuf[8:, :] = jnp.zeros((blocks, width), f32)
        for copy in begin:
            copy.wait()
        for j in range(chips):
            span = slice(j * tile, (j + 1) * tile)
            mlt[:, span] = jnp.transpose(gpb[j].reshape(tile, width))
            gbt[:, span] = jnp.transpose(gb[j].reshape(tile, width))
        for copy in later:
            copy.wait()

        @pl.loop(0, counts)
        def _(n):
            slot = lax.rem(n, 2)
            at = order(n)
            for copy in chunk(n, slot):
                copy.wait()

            @pl.when(n + 1 < counts)
            def _():
                for copy in chunk(n + 1, 1 - slot):
                    copy.start()

            term = dot_rows(gbt[...], hid[slot].reshape(rows, block)).astype(bf16)
            for side in range(2):
                r_all[side, at] = term[:, side * wide : (side + 1) * wide].reshape(
                    chips, strip, wide
                )
            red.near_copy(at).start()

            @pl.when(n > 0)
            def _():
                fold_exp(n - 1)

            up = rwc[slot].reshape(block, width)
            down = ewc[slot].reshape(width, block)
            total = jnp.zeros((1, block), f32)
            for j in range(chips):
                grad = dot_lanes(gb[j].reshape(tile, width), up)
                low = (grad * slope[slot, j].astype(f32)).astype(bf16)
                gpb[j] = low.reshape(per, cluster, block)
                acc[j] += dot_lanes(low, down)
                total = total + jnp.sum(low.astype(f32), axis=0, keepdims=True)
            vbuf[pl.ds(8 + at, 1), :block] = total
            fold_red(n)
            term = dot_rows(mlt[...], gpb[...].reshape(rows, block)).astype(bf16)
            for side in range(2):
                e_all[lax.div(at, 2), lax.rem(at, 2) * 2 + side] = term[
                    :, side * wide : (side + 1) * wide
                ].reshape(depth, quarter, wide)

            @pl.when(lax.div(at, 2) != core)
            def _():
                for side in range(2):
                    exp.near_copy(lax.rem(at, 2) * 2 + side).start()

    def first_norm(gb, n1, inv, ctx, ow, dsnd):
        later = [
            fetch(ctx_ref, ctx, 13),
            fetch(ow_ref, ow, 14),
            fetch(inv_ref, inv, 15),
        ]
        def n1_copy(j):
            return fetch(n1_ref.at[j], n1.at[j % 2], 16 + j % 2)

        def d_copy(j):
            return far_copy(dsnd.at[j], dbuf.at[core, j], (d_s, d_r), j, me.sibling())

        n1_copy(0).start()
        for copy in later:
            copy.start()
        fold_exp(counts - 1)
        for copy in later:
            copy.wait()
        gain = vecs[3:4, :]
        for row in range(3, 8):
            vbuf[row : row + 1, :] = jnp.zeros((1, width), f32)
        for j in range(chips):
            n1_copy(j).wait()
            if j + 1 < chips:
                n1_copy(j + 1).start()
            grad = acc[j]
            normed = n1[j % 2]
            vbuf[3:4, :] += jnp.sum(grad * normed, axis=0, keepdims=True)
            vbuf[4:5, :] += jnp.sum(grad, axis=0, keepdims=True)
            scaled = grad * gain
            first = jnp.mean(scaled, axis=1, keepdims=True)
            second = jnp.mean(scaled * normed, axis=1, keepdims=True)
            grad = inv[j][:, :1] * (scaled - first - normed * second)
            acc[j] = grad
            low = grad.astype(bf16)
            gb[j] = low.reshape(per, cluster, width)
            vbuf[5:6, :] += jnp.sum(low.astype(f32), axis=0, keepdims=True)
            back = dot_lanes(low, ow[...].reshape(width, width)).astype(bf16)

            for c in range(2):
                piece = back[:, c * half : (c + 1) * half]

                @pl.when(core == c)
                def _():
                    dbuf[c, j] = piece.reshape(per, cluster, half)

                @pl.when(core != c)
                def _():
                    dsnd[j] = piece.reshape(per, cluster, half)

            d_copy(j).start()
        sums.send(0)
        term = dot_first(ctx[...].reshape(rows, width), gb[...].reshape(rows, width))
        for zz in range(depth):
            for c in range(2):
                for p in range(chips):
                    begin_at = zz * quarter + (c * chips + p) * eighth
                    o_all[c, p, zz] = term[begin_at : begin_at + eighth, :].astype(bf16)
        for p in range(chips):
            out.near_copy(p).start()
        for j in range(chips):
            d_copy(j).wait()
        for a in range(depth):
            red.near_copy(a).wait_send()
        for b in range(chips):
            exp.near_copy(b).wait_send()

    shape = (chips, per, cluster, width)
    vm = pltpu.VMEM

    def feed_back(gb):
        pl.run_scoped(
            functools.partial(chunks, gb),
            vm((width, rows), bf16),
            vm((width, rows), bf16),
            vm((2, chips, tile, block), bf16),
            vm((2, chips, tile, block), bf16),
            vm((2, blocks, block // blocks, width), bf16),
            vm((2, depth, quarter, block), bf16),
            vm(shape[:3] + (block,), bf16),
        )
        pl.run_scoped(
            functools.partial(first_norm, gb),
            vm((2, tile, width), f32),
            vm((chips, tile, 128), f32),
            vm(shape, bf16),
            vm((depth, 2, quarter // 2, width), bf16),
            vm((chips, per, cluster, half), bf16),
        )

    pl.run_scoped(feed_back, vm(shape, bf16))

    def attend_back(qs, ks, vs, ps, xbuf, wbuf, ds, gs, gbuf, tbuf, dw, dwp, turned):
        atts = [
            Reducer(
                me,
                dwp.at[n],
                None,
                None,
                p_mid.at[n],
                p_last.at[n],
                p_done.at[n],
                groups[3 + n],
                n % 2 == 1,
            )
            for n in range(pairs)
        ]

        def loads(i, slot):
            span = pl.ds(i * pairs, pairs)
            pieces = (
                (q_ref.at[span], qs),
                (k_ref.at[span], ks),
                (v_ref.at[span], vs),
                (p_ref.at[span], ps),
            )
            return [fetch(src, dst.at[slot], slot * 4 + n) for n, (src, dst) in enumerate(pieces)]

        def load_x(i):
            return fetch(x_ref.at[:, :, i], xbuf, 8)

        load_w = fetch(aw_ref, wbuf, 9)
        for copy in loads(0, 0) + [load_x(0), load_w]:
            copy.start()
        bbuf[...] = jnp.zeros_like(bbuf)
        slots = lax.broadcasted_iota(jnp.int32, (cluster, cluster), 0)
        low = lax.broadcasted_iota(jnp.int32, (cluster, 128), 1) < size
        scale = size ** (-0.5)

        def tables(jj, i, pair, part):
            begin = part * heads + core * (heads // 2) + 2 * pair
            return [
                one_hot(posbuf[jj // chips, jj % chips, i, pl.ds(begin + h, 1), :], slots)
                for h in range(2)
            ]

        def clusters(i, slot, pair):
            lanes = pl.ds(multiple(pair * 128, 128), 128)
            for jj in range(blocks):
                tq = jnp.concatenate(tables(jj, i, pair, 0), axis=1)
                rows = stack_lanes(dbuf[jj // chips, jj % chips, i, :, lanes], low)
                ds[:, jj * share : (jj + 1) * share, :] = (
                    dot_rows(tq, rows).astype(bf16).reshape(blocks, share, 128)
                )
            for c in range(blocks):
                d = ds[c]
                probs = ps[slot, pair, c]
                slope = dot_lanes(d, stack_lanes(vs[slot, pair, c], low))
                broad = probs.astype(f32)
                halves = []
                for h in range(2):
                    span = slice(h * cluster, (h + 1) * cluster)
                    inner = jnp.sum(broad[:, span] * slope[:, span], axis=1, keepdims=True)
                    halves.append((broad[:, span] * (slope[:, span] - inner)).astype(bf16))
                grads = jnp.concatenate(halves, axis=1)
                gq = dot_rows(grads, stack_lanes(ks[slot, pair, c], low)) * scale
                gk = dot_first(grads, qs[slot, pair, c]) * scale
                gv = dot_first(probs, d)
                gs[0, c] = gq.astype(bf16)
                gs[1, c] = jnp.where(low, gk[:cluster], gk[cluster:]).astype(bf16)
                gs[2, c] = jnp.where(low, gv[:cluster], gv[cluster:]).astype(bf16)
            for jj in range(blocks):
                for part in range(3):
                    if part < 2:
                        table = jnp.concatenate(tables(jj, i, pair, part), axis=0)
                    rows = gs[part, :, jj * share : (jj + 1) * share, :].reshape(cluster, 128)
                    back = dot_first(table, stack_lanes(rows, low))
                    to = pl.ds(multiple(part * half + pair * 128, 128), 128)
                    gbuf[slot, jj // chips, jj % chips, :, to] = back.astype(bf16)

        def give(slot):
            return far_copy(gbuf.at[slot, 1 - core], gfar.at[slot], (g_s, g_r), slot, me.sibling())

        def token_copy(i, slot, k):
            return far_copy(
                tbuf.at[slot, me.chip_at(k)],
                token_out.at[chip * per + i],
                (t_s, t_r),
                i * (chips - 1) + k - 1,
                me.plane(k),
            )

        def token_keep(i, slot):
            return pltpu.make_async_copy(
                tbuf.at[slot, chip], token_out.at[chip * per + i], out_sem.at[1 + i]
            )

        def token_rows(i, slot):
            give(slot).wait()
            for j in range(chips):
                near = dot_lanes(gbuf[slot, core, j], wbuf[core])
                distant = dot_lanes(gfar[slot, j], wbuf[1 - core])
                resid = acc[j, i * cluster : (i + 1) * cluster, :]
                tbuf[slot, j] = (resid + near + distant).astype(bf16)
            token_keep(i, slot).start()
            for k in range(1, chips):
                token_copy(i, slot, k).start()

        ready = []

        def emit(src, dst):
            copy = pltpu.make_async_copy(src, dst, out_sem.at[1 + per + len(ready)])
            copy.start()
            ready.append(copy)

        def step_out_near():
            for p in range(chips):
                out.fold_near(p)
            out.send_mid()
            for p in range(chips):
                out.near_copy(p).wait_send()
            sums.fold(0)
            sums.send(1)

        def step_exp_mid():
            exp.fold_mid()
            exp.send_last()

        def step_red_mid():
            red.fold_mid()
            red.send_last()
            sums.fold(1)
            sums.send(2)

        def step_exp_last():
            exp.fold_last()
            exp.send_back()
            out.fold_mid()
            out.send_last()

        def step_red_last():
            red.fold_last()
            red.send_back()
            sums.fold(2)

        def step_out_last():
            out.fold_last()
            out.send_back()
            exp.send_side()

        def step_sides():
            red.send_side()

        hooks = {}
        steps = [
            (0, step_out_near),
            (1, step_exp_mid),
            (3, step_red_mid),
            (5, step_exp_last),
            (6, step_red_last),
            (7, step_out_last),
            (8, step_sides),
        ]
        for n, step in steps:
            hooks.setdefault(min(n, per * pairs - 1), []).append(step)
        depth_rows = quarter // chips

        def pair_grad(n, slot):
            lanes = [slice(p * half + n * 128, p * half + (n + 1) * 128) for p in range(3)]
            total = jnp.concatenate([dw[:, lane] for lane in lanes], axis=1)
            line = jnp.zeros((1, 384), f32)
            for b in range(2):
                x = jnp.concatenate([xbuf[b, j] for j in range(chips)], axis=0)
                g = jnp.concatenate(
                    [
                        jnp.concatenate([gbuf[slot, b, j, :, lane] for lane in lanes], axis=1)
                        for j in range(chips)
                    ],
                    axis=0,
                )
                total = total + dot_first(x, g)
                line = line + jnp.sum(g.astype(f32), axis=0, keepdims=True)
            for p, lane in enumerate(lanes):
                bbuf[0:1, lane] += line[:, p * 128 : (p + 1) * 128]
            low = total.astype(bf16)
            for a in range(depth):
                for b in range(chips):
                    begin = (a * chips + b) * depth_rows
                    piece = low[begin : begin + depth_rows]
                    if atts[n].tower_first:
                        dwp[n, a, b] = piece
                    else:
                        dwp[n, b, a] = piece
            atts[n].send_mid()

        dw[...] = jnp.zeros_like(dw)
        for i in range(per):
            slot = i % 2
            for copy in loads(i, slot):
                copy.wait()
            if i == 0:
                load_w.wait()
            if i >= 1:
                token_rows(i - 1, 1 - slot)
            if i + 1 < per:
                for copy in loads(i + 1, 1 - slot):
                    copy.start()
            if i == per - 1:
                load_x(i).wait()

            @pl.loop(0, pairs)
            def _(pair):
                clusters(i, slot, pair)
                for n in range(pairs):
                    if hooks.get(i * pairs + n) or i == per - 1:

                        @pl.when(pair == n)
                        def _():
                            if i == per - 1:
                                pair_grad(n, slot)
                            for step in hooks.get(i * pairs + n, ()):
                                step()

            if i >= 2:
                token_keep(i - 2, slot).wait()
                for k in range(1, chips):
                    token_copy(i - 2, slot, k).wait()
            give(slot).start()
            if i + 1 < per:
                load_x(i).wait()
                for b in range(2):
                    x = jnp.concatenate([xbuf[b, j] for j in range(chips)], axis=0)
                    g = jnp.concatenate([gbuf[slot, b, j] for j in range(chips)], axis=0)
                    dw[...] += dot_first(x, g)
                    bbuf[0:1, :] += jnp.sum(g.astype(f32), axis=0, keepdims=True)
                load_x(i + 1).start()

        biases.send(1)
        token_rows(per - 1, (per - 1) % 2)
        emit(vbuf, vec_out)
        out.send_side()
        for n in range(pairs - 1):
            atts[n].fold_mid()
            atts[n].send_last()
        biases.fold(1)
        biases.send(2)
        exp.finish()
        for c in range(2):
            for p in range(chips):
                emit(e_done.at[c, p], ew_out.at[:, pl.ds((c * chips + p) * wide, wide)])
        for n in range(pairs - 1, pairs):
            atts[n].fold_mid()
            atts[n].send_last()
        for n in range(pairs - 1):
            atts[n].fold_last()
            atts[n].send_back()
        red.finish()
        for c in range(2):
            turned[c] = jnp.transpose(r_done[c].reshape(width, wide))
            emit(turned.at[c], rw_out.at[c])
        out.finish()
        emit(o_done, ow_out)
        biases.fold(2)
        share_bias = far_copy(bbuf, bias_out.at[core], (b_s, b_r), 0, me.sibling())
        share_bias.start()
        emit(bbuf, bias_out.at[core])
        for n in range(pairs - 1, pairs):
            atts[n].fold_last()
            atts[n].send_back()
        for n in range(pairs):
            atts[n].send_side()
        for n in range(pairs):
            atts[n].finish()
            for c in range(2):
                for part in range(3):
                    emit(
                        p_done.at[n, c, :, :, pl.ds(part * 128, 128)],
                        aw_out.at[:, :, pl.ds((2 * part + c) * half + n * 128, 128)],
                    )
        for i in range(max(per - 2, 0), per):
            token_keep(i, i % 2).wait()
            for k in range(1, chips):
                token_copy(i, i % 2, k).wait()
        share_bias.wait()
        for copy in ready:
            copy.wait()
        lo_keep.wait()
        for k in range(1, chips):
            lo_copy(k).wait()

    group = (2, pairs, blocks, cluster)
    pl.run_scoped(
        attend_back,
        vm(group + (128,), bf16),
        vm(group + (128,), bf16),
        vm(group + (128,), bf16),
        vm(group + (2 * cluster,), bf16),
        vm((2, chips, cluster, width), bf16),
        vm(aw_ref.shape, bf16),
        vm((blocks, cluster, 128), bf16),
        vm((3, blocks, cluster, 128), bf16),
        vm((2, 2, chips, cluster, 3 * half), bf16),
        vm((2, chips, cluster, width), bf16),
        vm((width, 3 * half), f32),
        vm((pairs, depth, chips, quarter // chips, 384), bf16),
        vm((2, wide, width), bf16),
    )


def back(arrays, depth, heads):
    chips, per, cluster, width = arrays[17].shape
    half, blocks = width // 2, 2 * chips
    dma = pltpu.SemaphoreType.DMA
    anywhere = pl.BlockSpec(memory_space=pl.ANY)
    quarter = width // depth
    hidden = arrays[15].shape[2]
    eighth, strip, wide = quarter // blocks, width // chips, hidden // blocks
    rows = quarter // chips
    c, t = chips - 1, depth - 1
    pairs = heads // 4
    shapes = [
        ((chips * per, cluster, width), bf16),
        ((chips * per, cluster, width), bf16),
        ((chips, rows, 3 * width), bf16),
        ((2, chips, eighth, width), bf16),
        ((quarter, hidden), bf16),
        ((2, wide, width), bf16),
        ((8 + blocks, width), f32),
        ((2, 8, 3 * half), f32),
    ]
    vm = pltpu.VMEM

    def reducing(near, first, second):
        return [
            dma((near,)), dma((near,)),
            dma((first,)), dma((first,)),
            dma((second,)), dma((second,)),
            dma((c,)), dma((c,)),
            dma((1,)), dma((1,)),
        ]

    return pl.pallas_call(
        functools.partial(back_kernel, chips, depth, heads),
        out_shape=[jax.ShapeDtypeStruct(*s) for s in shapes],
        in_specs=[anywhere] * len(arrays),
        out_specs=[anywhere] * len(shapes),
        scratch_shapes=[
            vm((2, chips, per, cluster, half), bf16),
            vm(arrays[4].shape, jnp.int32),
            vm((chips, per * cluster, width), f32),
            vm((2, chips, cluster, 3 * half), bf16),
            vm((pairs, t, chips, rows, 384), bf16),
            vm((pairs, t, rows, 384), bf16),
            vm((pairs, 2, chips, rows, 384), bf16),
            vm((2, chips, depth, eighth, width), bf16),
            vm((chips, depth, eighth, width), bf16),
            vm((c, depth, eighth, width), bf16),
            vm((t, eighth, width), bf16),
            vm((2, chips, eighth, width), bf16),
            vm((2, chips, depth, quarter, wide), bf16),
            vm((chips, depth, quarter, wide), bf16),
            vm((c, depth, quarter, wide), bf16),
            vm((t, quarter, wide), bf16),
            vm((2, chips, quarter, wide), bf16),
            vm((2, depth, chips, strip, wide), bf16),
            vm((depth, chips, strip, wide), bf16),
            vm((t, chips, strip, wide), bf16),
            vm((c, strip, wide), bf16),
            vm((2, chips, strip, wide), bf16),
            vm((8 + blocks, width), f32),
            vm((chips + t, 8 + blocks, width), f32),
            vm((8, 3 * half), f32),
            vm((chips + t, 8, 3 * half), f32),
            vm((8, width), f32),
            dma((chips,)), dma((chips,)), dma((2,)), dma((2,)),
            dma((per * c,)), dma((per * c,)),
            dma((c,)), dma((c,)),
            dma((19,)), dma((1 + per + 6 + blocks + 6 * pairs,)),
            dma((chips + t,)), dma((chips + t,)), dma((chips + t,)), dma((chips + t,)),
            *reducing(depth, t, c),
            *reducing(chips, c, t),
            *reducing(chips, c, t),
            *[sem for n in range(pairs) for sem in reducing(1, c, t)],
        ],
        compiler_params=pltpu.CompilerParams(
            collective_id=2, has_side_effects=True, vmem_limit_bytes=63 * 2**20
        ),
        name="back",
    )(*arrays)


def places(rank, cluster, share):
    seqs, rows, length = rank.shape
    clusters = cluster // share
    target = rank // cluster
    which = lax.broadcasted_iota(jnp.int32, (1, 1, clusters, 1), 2)
    inside = (target[:, :, None, :] == which).astype(bf16)
    first = lax.broadcasted_iota(jnp.int32, (length, length), 0)
    second = lax.broadcasted_iota(jnp.int32, (length, length), 1)
    before = (first < second).astype(bf16)
    count = lax.dot_general(
        inside.reshape(seqs * rows * clusters, length),
        before,
        (((1,), (0,)), ((), ())),
        preferred_element_type=f32,
    ).reshape(seqs, rows, clusters, length)
    spot = which.astype(f32) * share + count
    return jnp.sum(inside.astype(f32) * spot, axis=2).astype(jnp.int32)


def per_chip(
    tokens,
    attend_weight,
    query_bias,
    value_bias,
    output_weight,
    output_bias,
    first_gain,
    first_shift,
    expand_weight,
    expand_bias,
    reduce_weight,
    reduce_bias,
    second_gain,
    second_shift,
    query_rank,
    key_rank,
    cotangent,
):
    seqs, cluster, width = tokens.shape
    heads = query_rank.shape[1]
    owners = lax.axis_size("seq")
    depth = lax.axis_size("batch")
    chips = owners // 2
    half = width // 2
    share = cluster // owners
    pos = places(jnp.concatenate([query_rank, key_rank], axis=1), cluster, share)
    quarter = width // depth
    lines = [
        query_bias,
        value_bias,
        output_bias,
        first_gain,
        first_shift,
        reduce_bias,
        second_gain,
        second_shift,
    ]
    lines += [
        expand_bias[at : at + quarter] for at in range(0, expand_bias.shape[0], quarter)
    ]
    vectors = jnp.zeros((16 * 256,), f32)
    for row, v in enumerate(lines):
        vectors += jnp.pad(v.astype(f32), (row * 256, (16 - row) * 256 - quarter))
    vectors = vectors.reshape(16, 256)
    (
        x_all,
        context,
        qs,
        ks,
        vs,
        ps,
        pos_all,
        attend_all,
        vecs,
        out_all,
        exp_all,
        red_all,
        normed_one,
        inverse_one,
        middle_low,
        hidden,
        slope,
        layer_out,
        grad_resid_two,
        grad_branch_two,
        late_sums,
    ) = forward(
        tokens,
        pos,
        attend_weight,
        vectors,
        output_weight,
        expand_weight,
        reduce_weight,
        cotangent,
        chips,
        depth,
        heads,
    )
    token_grad, layer_out, aw_grad, ow_grad, ew_grad, rw_grad, vec_sum, bias_sum = back(
        (
            qs,
            ks,
            vs,
            ps,
            pos_all,
            x_all,
            attend_all,
            out_all,
            exp_all,
            red_all,
            vecs,
            context,
            normed_one,
            inverse_one,
            middle_low,
            hidden,
            slope,
            layer_out,
            grad_resid_two,
            grad_branch_two,
            late_sums,
        ),
        depth,
        heads,
    )
    z = lax.axis_index("batch")
    six = lax.dynamic_slice_in_dim(vec_sum[:6], z * quarter, quarter, 1)
    up = lax.dynamic_index_in_dim(vec_sum[8:], z, 0, keepdims=False)
    both = jnp.concatenate([bias_sum[0, 0], bias_sum[1, 0]]).reshape(2, 3, half)
    query_value = jnp.transpose(both, (1, 0, 2)).reshape(3, width)
    query_value = lax.dynamic_slice_in_dim(query_value, z * quarter, quarter, 1)
    return (
        layer_out,
        token_grad,
        aw_grad.reshape(quarter, 3 * width).astype(f32),
        query_value[0],
        query_value[2],
        ow_grad.reshape(quarter, width).astype(f32),
        six[5],
        six[3],
        six[4],
        ew_grad.astype(f32),
        up,
        rw_grad.reshape(-1, width).astype(f32),
        six[2],
        six[0],
        six[1],
    )


def layer(mesh):
    def run(*arrays):
        seqs, cluster, width = arrays[0].shape
        heads = arrays[14].shape[1]
        owners, depth = mesh.shape["seq"], mesh.shape["batch"]
        chips = owners // 2
        fits = (
            owners % 2 == 0
            and chips > 1
            and depth == chips == 4
            and seqs % chips == 0
            and cluster == 128
            and heads % 4 == 0
            and width == heads * 64
            and cluster == 16 * owners
            and arrays[8].shape[1] == 4 * width
        )
        return (per_chip if fits else per_device)(*arrays)

    return run


def solution(mesh):
    in_specs = (
        P("batch", "seq", None),
        P("batch", None),
        P("batch"),
        P("batch"),
        P("batch", None),
        P("batch"),
        P("batch"),
        P("batch"),
        P("batch", None),
        P("batch"),
        P("batch", None),
        P("batch"),
        P("batch"),
        P("batch"),
        P("batch", None, "seq"),
        P("batch", None, "seq"),
        P("batch", "seq", None),
    )
    out_specs = (
        P("batch", "seq", None),
        P("batch", "seq", None),
        P("batch", None),
        P("batch"),
        P("batch"),
        P("batch", None),
        P("batch"),
        P("batch"),
        P("batch"),
        P("batch", None),
        P("batch"),
        P("batch", None),
        P("batch"),
        P("batch"),
        P("batch"),
    )
    return jax.shard_map(
        layer(mesh), mesh=mesh, in_specs=in_specs, out_specs=out_specs, check_vma=False
    )
```

```python
import functools
import math

import jax
import jax.numpy as jnp
from jax import lax
from jax.experimental import pallas as pl
from jax.experimental.pallas import tpu as pltpu
from jax.sharding import PartitionSpec as P

epsilon = 1e-05


def layer_norm(resid, gain, shift):
    center = jnp.mean(resid, axis=-1, keepdims=True)
    centered = resid - center
    spread = jnp.mean(centered * centered, axis=-1, keepdims=True)
    inverse = lax.rsqrt(spread + epsilon)
    normed = centered * inverse
    return (normed * gain + shift, normed, inverse)


def norm_back(upstream, normed, inverse, gain):
    scaled = upstream * gain
    first_mean = jnp.mean(scaled, axis=-1, keepdims=True)
    second_mean = jnp.mean(scaled * normed, axis=-1, keepdims=True)
    return inverse * (scaled - first_mean - normed * second_mean)


def gelu_slope(value):
    cumulative = 0.5 * (1.0 + lax.erf(value * 0.5**0.5))
    density = jnp.exp(-0.5 * value * value) * (2.0 * math.pi) ** (-0.5)
    return cumulative + value * density


def transpose_left(first, second):
    return lax.dot_general(
        first, second, (((0,), (0,)), ((), ())), preferred_element_type=jnp.float32
    )


def transpose_right(first, second):
    return lax.dot_general(
        first, second, (((1,), (1,)), ((), ())), preferred_element_type=jnp.float32
    )


def group_table(rank, cluster, owners):
    share = cluster // owners
    target = rank // cluster
    length = rank.shape[-1]
    places = lax.broadcasted_iota(jnp.int32, (length, length), 0)
    later = lax.broadcasted_iota(jnp.int32, (length, length), 1)
    before = (places < later)[None, None]
    same = target[..., :, None] == target[..., None, :]
    earlier = jnp.sum((same & before).astype(jnp.int32), axis=-2)
    position = target * share + earlier
    slots = lax.broadcasted_iota(jnp.int32, position.shape + (length,), 3)
    return (position[..., None] == slots).astype(jnp.bfloat16)


def sort_heads(rows, table, heads):
    seqs, length, width = rows.shape
    split = rows.reshape(seqs, length, heads, width // heads)
    moved = jnp.einsum("shtp,sthd->sphd", table, split, preferred_element_type=jnp.float32)
    return moved.astype(rows.dtype).reshape(seqs, length, width)


def unsort_heads(rows, table, heads):
    seqs, length, width = rows.shape
    split = rows.reshape(seqs, length, heads, width // heads)
    moved = jnp.einsum("shtp,sphd->sthd", table, split, preferred_element_type=jnp.float32)
    return moved.astype(rows.dtype).reshape(seqs, length, width)


def cluster_scores(queries, keys_rows, heads):
    items, length, width = queries.shape
    size = width // heads
    query_split = queries.reshape(items, length, heads, size)
    key_split = keys_rows.reshape(items, length, heads, size)
    scores = jnp.einsum(
        "sqhd,skhd->shqk", query_split, key_split, preferred_element_type=jnp.float32
    )
    return scores * size ** (-0.5)


def cluster_forward(queries, keys_rows, values_rows, heads):
    items, length, width = queries.shape
    scores = cluster_scores(queries, keys_rows, heads)
    top = jnp.max(scores, axis=-1, keepdims=True)
    weights = jnp.exp(scores - top)
    total = jnp.sum(weights, axis=-1, keepdims=True)
    probs = (weights / total).astype(jnp.bfloat16)
    value_split = values_rows.reshape(items, length, heads, width // heads)
    context = jnp.einsum("shqk,skhd->sqhd", probs, value_split, preferred_element_type=jnp.float32)
    return (
        context.reshape(items, length, width).astype(jnp.bfloat16),
        (top + jnp.log(total))[..., 0],
    )


def cluster_backward(scores, log_total, queries, keys_rows, values_rows, grad_context, heads):
    items, length, width = queries.shape
    size = width // heads
    query_split = queries.reshape(items, length, heads, size)
    key_split = keys_rows.reshape(items, length, heads, size)
    value_split = values_rows.reshape(items, length, heads, size)
    grad_split = grad_context.reshape(items, length, heads, size)
    probs = jnp.exp(scores - log_total[..., None])
    grad_probs = jnp.einsum(
        "sqhd,skhd->shqk", grad_split, value_split, preferred_element_type=jnp.float32
    )
    inner = jnp.sum(probs * grad_probs, axis=-1, keepdims=True)
    grad_scores = (probs * (grad_probs - inner)).astype(jnp.bfloat16)
    scale = size ** (-0.5)
    grad_query = (
        jnp.einsum("shqk,skhd->sqhd", grad_scores, key_split, preferred_element_type=jnp.float32)
        * scale
    )
    grad_key = (
        jnp.einsum("shqk,sqhd->skhd", grad_scores, query_split, preferred_element_type=jnp.float32)
        * scale
    )
    grad_value = jnp.einsum(
        "shqk,sqhd->skhd",
        probs.astype(jnp.bfloat16),
        grad_split,
        preferred_element_type=jnp.float32,
    )
    shape = (items, length, width)
    return (
        grad_query.reshape(shape).astype(jnp.bfloat16),
        grad_key.reshape(shape).astype(jnp.bfloat16),
        grad_value.reshape(shape).astype(jnp.bfloat16),
    )


def send_context(context):
    return lax.all_to_all(context, "seq", split_axis=1, concat_axis=1, tiled=True)


def send_grads(grads):
    return (
        lax.all_to_all(grads[0], "seq", split_axis=1, concat_axis=1, tiled=True),
        lax.all_to_all(grads[1], "seq", split_axis=1, concat_axis=1, tiled=True),
        lax.all_to_all(grads[2], "seq", split_axis=1, concat_axis=1, tiled=True),
    )


def make_step(left, pieces):
    total = jnp.dot(left, pieces[0], preferred_element_type=jnp.float32)
    stored = tuple(pieces[1:]) + ()
    placed = tuple((piece for piece in stored))
    return (total,) + placed


def make_hidden_step(before, pieces):
    section = before + pieces[1].astype(jnp.float32)
    activated = jax.nn.gelu(section, approximate=False).astype(jnp.bfloat16)
    total = jnp.dot(activated, pieces[0], preferred_element_type=jnp.float32)
    stored = ()
    return (total, section, activated) + stored


def per_device(
    tokens,
    attend_weight,
    query_bias,
    value_bias,
    output_weight,
    output_bias,
    first_gain,
    first_shift,
    expand_weight,
    expand_bias,
    reduce_weight,
    reduce_bias,
    second_gain,
    second_shift,
    query_rank,
    key_rank,
    cotangent,
):
    seqs, cluster, width = tokens.shape
    heads = query_rank.shape[1]
    rows = seqs * cluster
    owners = lax.axis_size("seq")
    flat = tokens.reshape(rows, width)
    attend_out = make_step(
        flat,
        (
            lax.all_gather(attend_weight, "batch", axis=0, tiled=True),
            lax.all_gather(query_bias, "batch", axis=0, tiled=True),
            lax.all_gather(value_bias, "batch", axis=0, tiled=True),
        ),
    )
    summed = attend_out[0]
    queries = (summed[:, :width] + attend_out[1].astype(jnp.float32)).astype(jnp.bfloat16)
    keys_rows = summed[:, width : 2 * width].astype(jnp.bfloat16)
    values_rows = (summed[:, 2 * width :] + attend_out[2].astype(jnp.float32)).astype(jnp.bfloat16)
    query_table = group_table(query_rank, cluster, owners)
    key_table = group_table(key_rank, cluster, owners)
    query_sorted = sort_heads(queries.reshape(seqs, cluster, width), query_table, heads)
    key_sorted = sort_heads(keys_rows.reshape(seqs, cluster, width), key_table, heads)
    value_sorted = sort_heads(values_rows.reshape(seqs, cluster, width), key_table, heads)
    received = (
        lax.all_to_all(query_sorted, "seq", split_axis=1, concat_axis=1, tiled=True),
        lax.all_to_all(key_sorted, "seq", split_axis=1, concat_axis=1, tiled=True),
        lax.all_to_all(value_sorted, "seq", split_axis=1, concat_axis=1, tiled=True),
    )
    context, log_total = cluster_forward(received[0], received[1], received[2], heads)
    forward_out = (send_context(context), log_total, received[0], received[1], received[2])
    context_rows = unsort_heads(forward_out[0], query_table, heads).reshape(rows, width)
    output_out = make_step(
        context_rows,
        (
            lax.all_gather(output_weight, "batch", axis=0, tiled=True),
            lax.all_gather(output_bias, "batch", axis=0, tiled=True),
            lax.all_gather(first_gain, "batch", axis=0, tiled=True),
            lax.all_gather(first_shift, "batch", axis=0, tiled=True),
        ),
    )
    resid_one = flat.astype(jnp.float32) + output_out[0] + output_out[1].astype(jnp.float32)
    gain_one = output_out[2].astype(jnp.float32)
    middle, normed_one, inverse_one = layer_norm(
        resid_one, gain_one, output_out[3].astype(jnp.float32)
    )
    middle_low = middle.astype(jnp.bfloat16)
    expand_out = make_step(
        middle_low,
        (
            lax.all_gather(expand_weight, "batch", axis=0, tiled=True),
            lax.all_gather(reduce_bias, "batch", axis=0, tiled=True),
            lax.all_gather(second_gain, "batch", axis=0, tiled=True),
            lax.all_gather(second_shift, "batch", axis=0, tiled=True),
        ),
    )
    hidden_out = make_hidden_step(
        expand_out[0],
        (
            lax.all_gather(reduce_weight, "batch", axis=0, tiled=True),
            lax.all_gather(expand_bias, "batch", axis=0, tiled=True),
        ),
    )
    pre_full, hidden_full = (hidden_out[1], hidden_out[2])
    resid_two = middle + hidden_out[0] + expand_out[1].astype(jnp.float32)
    gain_two = expand_out[2].astype(jnp.float32)
    final, normed_two, inverse_two = layer_norm(
        resid_two, gain_two, expand_out[3].astype(jnp.float32)
    )
    layer_out = final.astype(jnp.bfloat16).reshape(seqs, cluster, width)
    attend_full, output_full, expand_full, reduce_full = (
        lax.all_gather(attend_weight, "batch", axis=0, tiled=True),
        lax.all_gather(output_weight, "batch", axis=0, tiled=True),
        lax.all_gather(expand_weight, "batch", axis=0, tiled=True),
        lax.all_gather(reduce_weight, "batch", axis=0, tiled=True),
    )
    upstream = cotangent.reshape(rows, width).astype(jnp.float32)
    grad_second_gain = jnp.sum(upstream * normed_two, axis=0)
    grad_second_shift = jnp.sum(upstream, axis=0)
    grad_resid_two = norm_back(upstream, normed_two, inverse_two, gain_two)
    grad_branch_two = grad_resid_two.astype(jnp.bfloat16)
    grad_reduce_bias = jnp.sum(grad_branch_two, axis=0, dtype=jnp.float32)
    grad_reduce = transpose_left(hidden_full, grad_branch_two)
    grad_hidden = transpose_right(grad_branch_two, reduce_full)
    grad_pre = (grad_hidden * gelu_slope(pre_full)).astype(jnp.bfloat16)
    grad_expand_bias = jnp.sum(grad_pre, axis=0, dtype=jnp.float32)
    grad_expand = transpose_left(middle_low, grad_pre)
    grad_middle = grad_resid_two + transpose_right(grad_pre, expand_full)
    grad_first_gain = jnp.sum(grad_middle * normed_one, axis=0)
    grad_first_shift = jnp.sum(grad_middle, axis=0)
    grad_resid_one = norm_back(grad_middle, normed_one, inverse_one, gain_one)
    grad_branch_one = grad_resid_one.astype(jnp.bfloat16)
    grad_output_bias = jnp.sum(grad_branch_one, axis=0, dtype=jnp.float32)
    grad_output = transpose_left(context_rows, grad_branch_one)
    grad_context = transpose_right(grad_branch_one, output_full).astype(jnp.bfloat16)
    grad_sorted = sort_heads(grad_context.reshape(seqs, cluster, width), query_table, heads)
    grad_received = lax.all_to_all(grad_sorted, "seq", split_axis=1, concat_axis=1, tiled=True)
    kept_scores = cluster_scores(forward_out[2], forward_out[3], heads)
    home = send_grads(
        cluster_backward(
            kept_scores,
            forward_out[1],
            forward_out[2],
            forward_out[3],
            forward_out[4],
            grad_received,
            heads,
        )
    )
    grad_queries = unsort_heads(home[0], query_table, heads).reshape(rows, width)
    grad_keys = unsort_heads(home[1], key_table, heads).reshape(rows, width)
    grad_values = unsort_heads(home[2], key_table, heads).reshape(rows, width)
    grad_mixed = jnp.concatenate([grad_queries, grad_keys, grad_values], axis=1)
    grad_query_bias = jnp.sum(grad_queries, axis=0, dtype=jnp.float32)
    grad_value_bias = jnp.sum(grad_values, axis=0, dtype=jnp.float32)
    grad_attend = transpose_left(flat, grad_mixed)
    token_grad = (
        (grad_resid_one + transpose_right(grad_mixed, attend_full))
        .astype(jnp.bfloat16)
        .reshape(seqs, cluster, width)
    )
    owned = (
        lax.psum_scatter(
            grad_attend.astype(jnp.bfloat16), "batch", scatter_dimension=0, tiled=True
        ).astype(jnp.float32),
        lax.psum_scatter(
            grad_query_bias.astype(jnp.bfloat16), "batch", scatter_dimension=0, tiled=True
        ).astype(jnp.float32),
        lax.psum_scatter(
            grad_value_bias.astype(jnp.bfloat16), "batch", scatter_dimension=0, tiled=True
        ).astype(jnp.float32),
        lax.psum_scatter(
            grad_output.astype(jnp.bfloat16), "batch", scatter_dimension=0, tiled=True
        ).astype(jnp.float32),
        lax.psum_scatter(
            grad_output_bias.astype(jnp.bfloat16), "batch", scatter_dimension=0, tiled=True
        ).astype(jnp.float32),
        lax.psum_scatter(
            grad_first_gain.astype(jnp.bfloat16), "batch", scatter_dimension=0, tiled=True
        ).astype(jnp.float32),
        lax.psum_scatter(
            grad_first_shift.astype(jnp.bfloat16), "batch", scatter_dimension=0, tiled=True
        ).astype(jnp.float32),
        lax.psum_scatter(
            grad_expand.astype(jnp.bfloat16), "batch", scatter_dimension=0, tiled=True
        ).astype(jnp.float32),
        lax.psum_scatter(
            grad_expand_bias.astype(jnp.bfloat16), "batch", scatter_dimension=0, tiled=True
        ).astype(jnp.float32),
        lax.psum_scatter(
            grad_reduce.astype(jnp.bfloat16), "batch", scatter_dimension=0, tiled=True
        ).astype(jnp.float32),
        lax.psum_scatter(
            grad_reduce_bias.astype(jnp.bfloat16), "batch", scatter_dimension=0, tiled=True
        ).astype(jnp.float32),
        lax.psum_scatter(
            grad_second_gain.astype(jnp.bfloat16), "batch", scatter_dimension=0, tiled=True
        ).astype(jnp.float32),
        lax.psum_scatter(
            grad_second_shift.astype(jnp.bfloat16), "batch", scatter_dimension=0, tiled=True
        ).astype(jnp.float32),
    )
    shared = (
        lax.psum(owned[0].astype(jnp.bfloat16), "seq").astype(jnp.float32),
        lax.psum(owned[1].astype(jnp.bfloat16), "seq").astype(jnp.float32),
        lax.psum(owned[2].astype(jnp.bfloat16), "seq").astype(jnp.float32),
        lax.psum(owned[3].astype(jnp.bfloat16), "seq").astype(jnp.float32),
        lax.psum(owned[4].astype(jnp.bfloat16), "seq").astype(jnp.float32),
        lax.psum(owned[5].astype(jnp.bfloat16), "seq").astype(jnp.float32),
        lax.psum(owned[6].astype(jnp.bfloat16), "seq").astype(jnp.float32),
        lax.psum(owned[7].astype(jnp.bfloat16), "seq").astype(jnp.float32),
        lax.psum(owned[8].astype(jnp.bfloat16), "seq").astype(jnp.float32),
        lax.psum(owned[9].astype(jnp.bfloat16), "seq").astype(jnp.float32),
        lax.psum(owned[10].astype(jnp.bfloat16), "seq").astype(jnp.float32),
        lax.psum(owned[11].astype(jnp.bfloat16), "seq").astype(jnp.float32),
        lax.psum(owned[12].astype(jnp.bfloat16), "seq").astype(jnp.float32),
    )
    return (
        layer_out,
        token_grad,
        shared[0],
        shared[1],
        shared[2],
        shared[3],
        shared[4],
        shared[5],
        shared[6],
        shared[7],
        shared[8],
        shared[9],
        shared[10],
        shared[11],
        shared[12],
    )


MESH = pl.DeviceIdType.MESH
f32 = jnp.float32
bf16 = jnp.bfloat16


class Place:
    def __init__(self, chips, depth):
        self.chips, self.depth = chips, depth
        self.z = lax.axis_index("batch")
        spot = lax.axis_index("seq")
        self.chip, self.core = lax.div(spot, 2), lax.rem(spot, 2)

    def chip_at(self, k):
        return lax.rem(self.chip + k + self.chips, self.chips)

    def z_at(self, k):
        return lax.rem(self.z + k + self.depth, self.depth)

    def plane(self, k):
        return (self.z, self.chip_at(k) * 2 + self.core)

    def tower(self, k):
        return (self.z_at(k), self.chip * 2 + self.core)

    def sibling(self):
        return (self.z, self.chip * 2 + 1 - self.core)

    def greet(self):
        bell = pltpu.get_barrier_semaphore()
        others = [self.plane(k) for k in range(1, self.chips)]
        others += [self.tower(k) for k in range(1, self.depth)]
        others.append(self.sibling())
        for other in others:
            pl.semaphore_signal(bell, inc=1, device_id=other, device_id_type=MESH)
        pl.semaphore_wait(bell, len(others))


def far_copy(src, dst, sems, at, device):
    return pltpu.make_async_remote_copy(
        src_ref=src,
        dst_ref=dst,
        send_sem=sems[0].at[at],
        recv_sem=sems[1].at[at],
        device_id=device,
        device_id_type=MESH,
    )


def one_hot(row, slots):
    return jnp.where(slots == row, 1.0, 0.0).astype(bf16)


def split_lanes(tile, low):
    zero = jnp.zeros_like(tile)
    return jnp.where(low, tile, zero), jnp.where(low, zero, tile)


def stack_lanes(tile, low):
    first, second = split_lanes(tile, low)
    return jnp.concatenate([first, second], axis=0)


def dot_rows(a, b):
    return jnp.dot(a, b, preferred_element_type=f32)


def dot_lanes(a, b):
    return lax.dot_general(a, b, (((1,), (1,)), ((), ())), preferred_element_type=f32)


def dot_first(a, b):
    return lax.dot_general(a, b, (((0,), (0,)), ((), ())), preferred_element_type=f32)


def multiple(value, by):
    return pl.multiple_of(value, by)


def forward_kernel(
    chips,
    depth,
    heads,
    tok_ref,
    pos_ref,
    aw_ref,
    vec_ref,
    ow_ref,
    ew_ref,
    rw_ref,
    cot_ref,
    x_out,
    ctx_out,
    q_out,
    k_out,
    v_out,
    p_out,
    pos_out,
    aw_out,
    vec_out,
    ow_out,
    ew_out,
    rw_out,
    n1_out,
    inv_out,
    ml_out,
    hid_out,
    slope_out,
    lo_out,
    gr_out,
    gb_out,
    sum_out,
    xbuf,
    posbuf,
    wbuf,
    vbuf,
    bias,
    ctxb,
    ctxt,
    owbuf,
    ewbuf,
    rwbuf,
    cbuf,
    n1buf,
    invbuf,
    mlbuf,
    vecs,
    upb,
    sums,
    tok_s,
    tok_r,
    tokc_s,
    tokc_r,
    pos_s,
    pos_r,
    posc_s,
    posc_r,
    up_s,
    up_r,
    dn_s,
    dn_r,
    awc_s,
    awc_r,
    vec_s,
    vec_r,
    wz_s,
    wz_r,
    wp_s,
    wp_r,
    wd_s,
    wd_r,
    wc_s,
    wc_r,
    ctx_s,
    ctx_r,
    cot_s,
    cot_r,
    oc_s,
    oc_r,
    loc,
    out_sem,
    slope_sem,
    att_sem,
    late_sem,
):
    me = Place(chips, depth)
    z, chip, core = me.z, me.chip, me.core
    per = tok_ref.shape[0] // chips
    half = aw_ref.shape[1] // 6
    rows_z = aw_ref.shape[0]
    pairs = heads // 4
    size = half // (2 * pairs)
    me.greet()

    def aw_block(zz):
        return wbuf.at[pl.ds(multiple(zz * rows_z, 8), rows_z)]

    def up_copy(h):
        return far_copy(
            aw_block(z - h), aw_block(z - h), (up_s, up_r), h, (z + 1, chip * 2 + core)
        )

    def down_copy(h):
        return far_copy(
            aw_block(z + h), aw_block(z + h), (dn_s, dn_r), h, (z - 1, chip * 2 + core)
        )

    def up_got(h):
        return far_copy(
            aw_block(z - 1 - h), aw_block(z - 1 - h), (up_s, up_r), h, me.sibling()
        )

    def down_got(h):
        return far_copy(
            aw_block(z + 1 + h), aw_block(z + 1 + h), (dn_s, dn_r), h, me.sibling()
        )

    def pass_on():
        @pl.when(z < depth - 1)
        def _():
            up_copy(0).start()

        @pl.when(z > 0)
        def _():
            down_copy(0).start()

    def pass_rest(hops):
        for h in hops:

            @pl.when(z > h)
            def _():
                up_got(h).wait_recv()
                if h + 1 < depth - 1:

                    @pl.when(z < depth - 1)
                    def _():
                        up_copy(h + 1).start()

            @pl.when(z + 1 + h < depth)
            def _():
                down_got(h).wait_recv()
                if h + 1 < depth - 1:

                    @pl.when(z > 0)
                    def _():
                        down_copy(h + 1).start()

    def pass_end():
        for h in range(depth - 1):

            @pl.when((z >= h) & (z < depth - 1))
            def _():
                up_copy(h).wait_send()

            @pl.when((z + h < depth) & (z > 0))
            def _():
                down_copy(h).wait_send()

    def mine(ref, target):
        return ref.at[pl.ds(target * per, per)]

    def tok_copy(k):
        return far_copy(
            mine(tok_ref, me.chip_at(k)), xbuf.at[core, chip], (tok_s, tok_r), k - 1, me.plane(k)
        )

    def pos_copy(k):
        return far_copy(
            mine(pos_ref, me.chip_at(k)), posbuf.at[core, chip], (pos_s, pos_r), k - 1, me.plane(k)
        )

    def vec_copy(k):
        return far_copy(vec_ref, vbuf.at[z], (vec_s, vec_r), k - 1, me.tower(k))

    sends = []
    for k in range(1, chips):
        sends.append(pos_copy(k))
        sends[-1].start()
    for k in range(1, depth):
        sends.append(vec_copy(k))
        sends[-1].start()
    for k in range(1, chips):
        sends.append(tok_copy(k))
        sends[-1].start()
    local = []

    def keep(src, dst):
        copy = pltpu.make_async_copy(src, dst, loc.at[len(local)])
        copy.start()
        local.append(copy)

    for part in range(3):
        keep(
            aw_ref.at[:, pl.ds(multiple(part * 2 * half + core * half, 128), half)],
            wbuf.at[pl.ds(multiple(z * rows_z, 8), rows_z), pl.ds(part * half, half)],
        )
    keep(mine(tok_ref, chip), xbuf.at[core, chip])
    keep(mine(pos_ref, chip), posbuf.at[core, chip])
    keep(vec_ref, vbuf.at[z])
    for copy in local[:3]:
        copy.wait()
    pass_on()
    wide = ew_ref.shape[1] // (2 * chips)
    tall = rw_ref.shape[0] // (2 * chips)
    mid_rows = rows_z // 2
    mine_at = core * chips + chip

    def piece(kind):
        if kind == 0:
            return ow_ref.at[pl.ds(multiple(core * mid_rows, 8), mid_rows)]
        if kind == 1:
            return ew_ref.at[:, pl.ds(multiple(mine_at * wide, 128), wide)]
        return rw_ref.at[pl.ds(multiple(mine_at * tall, 8), tall)]

    def place(kind, zz):
        if kind == 0:
            return owbuf.at[zz, core]
        if kind == 1:
            return ewbuf.at[zz, :, pl.ds(multiple(mine_at * wide, 128), wide)]
        return rwbuf.at[zz, mine_at]

    def place_all(kind, at):
        if kind == 1:
            return ewbuf.at[:, :, pl.ds(multiple(at * wide, 128), wide)]
        return rwbuf.at[:, at]

    for kind in range(3):
        keep(piece(kind), place(kind, z))

    def wz_copy(kind, k):
        return far_copy(
            piece(kind),
            place(kind, z),
            (wz_s, wz_r),
            kind * (depth - 1) + k - 1,
            me.tower(k),
        )

    beside = (chip + 1 - 2 * lax.rem(chip, 2), lax.rem(chip + 2, chips))
    across = chips - 1 - chip

    def part_of(kind, origin, side):
        at = core * chips + origin
        span = pl.ds(side * (depth // 2), depth // 2)
        if kind == 1:
            return ewbuf.at[span, :, pl.ds(multiple(at * wide, 128), wide)]
        return rwbuf.at[span, at]

    def wp_copy(kind, d):
        spot = place_all(kind, mine_at)
        return far_copy(
            spot, spot, (wp_s, wp_r), (kind - 1) * 2 + d, (z, beside[d] * 2 + core)
        )

    def wd_copy(kind, d):
        spot = part_of(kind, beside[d], d)
        return far_copy(
            spot, spot, (wd_s, wd_r), (kind - 1) * 2 + d, (z, beside[1 - d] * 2 + core)
        )

    def wc_copy(kind, n):
        at = core * chips + (chip, beside[0], beside[1], across)[n]
        return far_copy(
            place_all(kind, at),
            place_all(kind, at),
            (wc_s, wc_r),
            (kind - 1) * chips + n,
            me.sibling(),
        )

    def tower_wait(kind):
        for k in range(1, depth):
            wz_copy(kind, k).wait_recv()

    def plane_first(kind):
        for d in range(2):
            wp_copy(kind, d).start()
        wc_copy(kind, 0).start()

    def plane_second(kind):
        for d in range(2):
            wp_copy(kind, d).wait_recv()
            wd_copy(kind, d).start()
            wc_copy(kind, 1 + d).start()

    def plane_last(kind):
        for d in range(2):
            wd_copy(kind, d).wait_recv()
        wc_copy(kind, 3).start()
        for n in range(chips):
            wc_copy(kind, n).wait()
        for d in range(2):
            wp_copy(kind, d).wait_send()
            wd_copy(kind, d).wait_send()

    def oc_copy():
        spot = owbuf.at[:, core]
        return far_copy(spot, spot, (oc_s, oc_r), 0, me.sibling())

    def cot_copy(n):
        target = (beside[0], beside[1], across)[n]
        return far_copy(
            mine(cot_ref, target),
            cbuf.at[chip],
            (cot_s, cot_r),
            n,
            (z, target * 2 + core),
        )

    keep(mine(cot_ref, chip), cbuf.at[chip])

    for copy in local[3:5]:
        copy.wait()

    def tokc_copy(k):
        source = me.chip_at(-k)
        return far_copy(
            xbuf.at[core, source], xbuf.at[core, source], (tokc_s, tokc_r), k, me.sibling()
        )

    def posc_copy(k):
        source = me.chip_at(-k)
        return far_copy(
            posbuf.at[core, source], posbuf.at[core, source], (posc_s, posc_r), k, me.sibling()
        )

    for k in range(1, depth):
        wz_copy(1, k).start()
        for kind in range(3):
            sends.append(wz_copy(kind, k))
    pass_rest(range(depth - 2))
    for k in range(chips):
        if k:
            pos_copy(k).wait_recv()
            tok_copy(k).wait_recv()
        for copy in (posc_copy(k), tokc_copy(k)):
            copy.start()
            sends.append(copy)
    for copy in local[5:]:
        copy.wait()
    tower_wait(1)
    plane_first(1)
    pass_rest(range(depth - 2, depth - 1))
    for k in range(1, depth):
        wz_copy(2, k).start()
    plane_second(1)
    for n in range(2):
        cot_copy(n).start()
    for k in range(1, depth):
        vec_copy(k).wait_recv()
    for k in range(chips):
        posc_copy(k).wait_recv()
        tokc_copy(k).wait_recv()

    outs = []

    def emit(src, dst):
        copy = pltpu.make_async_copy(src, dst, out_sem.at[len(outs)])
        copy.start()
        outs.append(copy)

    emit(xbuf, x_out)
    emit(posbuf, pos_out)
    emit(wbuf, aw_out.at[core])
    awc = far_copy(wbuf, aw_out.at[core], (awc_s, awc_r), 0, me.sibling())
    awc.start()
    sends.append(awc)

    quarter = rows_z
    for zz in range(depth):
        begin = zz * quarter
        for row, at in ((0, 0), (1, 2)):
            for side in range(2):
                lo = max(begin, side * half)
                hi = min(begin + quarter, (side + 1) * half)
                if lo < hi:
                    bias[side, 0:1, at * half + lo - side * half : at * half + hi - side * half] = (
                        vbuf[zz, row : row + 1, lo - begin : hi - begin]
                    )
    bias[0, 0:1, half : 2 * half] = jnp.zeros((1, half), f32)
    bias[1, 0:1, half : 2 * half] = jnp.zeros((1, half), f32)
    added = bias[core, 0:1, :]
    for zz in range(depth):
        for row in range(8):
            vecs[row : row + 1, zz * quarter : (zz + 1) * quarter] = vbuf[
                zz, row : row + 1, :quarter
            ]
        steps = upb.shape[1] // (depth * quarter)
        for row in range(steps):
            to = (zz * steps + row) * quarter
            upb[0:1, to : to + quarter] = vbuf[zz, 8 + row : 9 + row, :quarter]

    cluster = tok_ref.shape[1]
    blocks = 2 * chips
    share = cluster // blocks
    width = tok_ref.shape[2]

    slots = lax.broadcasted_iota(jnp.int32, (cluster, cluster), 0)
    low = lax.broadcasted_iota(jnp.int32, (cluster, 128), 1) < size
    scale = size ** (-0.5)

    def tables(jj, i, pair, part):
        first = part * heads + core * (heads // 2) + 2 * pair
        rows = [
            one_hot(posbuf[jj // chips, jj % chips, i, pl.ds(first + h, 1), :], slots)
            for h in range(2)
        ]
        return rows

    def hook(i, pair):
        step = i * pairs + pair
        last = per * pairs - 1

        @pl.when(step == min(2, last))
        def _():
            tower_wait(2)
            plane_first(2)
            for k in range(1, depth):
                wz_copy(0, k).start()

        @pl.when(step == last)
        def _():
            plane_second(2)

    def attention(qkv, qs, ks, vs, ps, os):
        def group_copies(i):
            span = pl.ds(i * pairs, pairs)
            pieces = ((qs, q_out), (ks, k_out), (vs, v_out), (ps, p_out))
            return [
                pltpu.make_async_copy(src.at[span], dst.at[span], att_sem.at[5 + 4 * i + n])
                for n, (src, dst) in enumerate(pieces)
            ]

        @pl.loop(0, blocks)
        def _(jj):
            x = xbuf[lax.div(jj, chips), lax.rem(jj, chips)].reshape(per * cluster, width)
            mixed = (dot_rows(x, wbuf[...]) + added).astype(bf16)
            for at in range(3 * pairs):
                qkv[at, jj] = mixed[:, at * 128 : (at + 1) * 128].reshape(per, cluster, 128)

        @pl.loop(0, per)
        def _(i):
            @pl.loop(0, pairs)
            def _(pair):
                at = i * pairs + pair
                for jj in range(blocks):
                    tq = jnp.concatenate(tables(jj, i, pair, 0), axis=1)
                    tk = jnp.concatenate(tables(jj, i, pair, 1), axis=1)
                    q = stack_lanes(qkv[pair, jj, i], low)
                    k = stack_lanes(qkv[pairs + pair, jj, i], low)
                    v = stack_lanes(qkv[2 * pairs + pair, jj, i], low)
                    span = slice(jj * share, (jj + 1) * share)
                    sq = dot_rows(tq, q).astype(bf16)
                    skv = dot_rows(tk, jnp.concatenate([k, v], axis=1)).astype(bf16)
                    qs[at, :, span, :] = sq.reshape(blocks, share, 128)
                    ks[at, :, span, :] = skv[:, :128].reshape(blocks, share, 128)
                    vs[at, :, span, :] = skv[:, 128:].reshape(blocks, share, 128)
                for c in range(blocks):
                    scores = dot_lanes(qs[at, c], stack_lanes(ks[at, c], low)) * scale
                    halves = []
                    for h in range(2):
                        s = scores[:, h * cluster : (h + 1) * cluster]
                        e = jnp.exp(s - jnp.max(s, axis=1, keepdims=True))
                        halves.append((e / jnp.sum(e, axis=1, keepdims=True)).astype(bf16))
                    probs = jnp.concatenate(halves, axis=1)
                    ps[at, c] = probs
                    o = dot_rows(probs, stack_lanes(vs[at, c], low)).astype(bf16)
                    os[c] = o
                for jj in range(blocks):
                    tq = jnp.concatenate(tables(jj, i, pair, 0), axis=0)
                    rows = os[:, jj * share : (jj + 1) * share, :].reshape(cluster, 128)
                    back = dot_first(tq, stack_lanes(rows, low)).astype(bf16)
                    ctxb[jj // chips, jj % chips, i, :, pl.ds(multiple(pair * 128, 128), 128)] = back
                hook(i, pair)

                @pl.when(pair == pairs - 1)
                def _():
                    for copy in group_copies(i):
                        copy.start()


        far, own = ctx_copies()
        for copy in (far, own):
            copy.start()
        for copy in (far, own):
            copy.wait()
        for i in range(per):
            for copy in group_copies(i):
                copy.wait()

    def ctx_copies():
        lanes = pl.ds(multiple(core * half, 128), half)
        far = far_copy(
            ctxb.at[1 - core], ctxt.at[:, :, :, lanes], (ctx_s, ctx_r), 0, me.sibling()
        )
        own = pltpu.make_async_copy(ctxb.at[core], ctxt.at[:, :, :, lanes], att_sem.at[4])
        return far, own

    group = (per * pairs, blocks, cluster, 128)
    pl.run_scoped(
        attention,
        pltpu.VMEM((3 * pairs, blocks, per, cluster, 128), bf16),
        pltpu.VMEM(group, bf16),
        pltpu.VMEM(group, bf16),
        pltpu.VMEM(group, bf16),
        pltpu.VMEM((per * pairs, blocks, cluster, 2 * cluster), bf16),
        pltpu.VMEM((blocks, cluster, 128), bf16),
    )

    tower_wait(0)
    oc_copy().start()
    oc_copy().wait()
    emit(ctxt, ctx_out)
    context_out = outs[-1]
    emit(owbuf, ow_out)
    tile = per * cluster
    hidden = upb.shape[1]
    eps = epsilon

    def moments(rows):
        center = jnp.mean(rows, axis=1, keepdims=True)
        centered = rows - center
        spread = jnp.mean(centered * centered, axis=1, keepdims=True)
        inverse = lax.rsqrt(spread + eps)
        return centered * inverse, inverse

    def slope_out_copy(j, slot):
        return pltpu.make_async_copy(sbuf.at[slot], slope_out.at[j], slope_sem.at[slot])

    def vec(row):
        return vecs[row : row + 1, :]

    def feed(hbuf, sbuf):
        step = sbuf.shape[3]

        def late_copies(j):
            pieces = ((cbuf, lo_out), (n1buf, gr_out), (ctxt, gb_out))
            return [
                pltpu.make_async_copy(src.at[j], dst.at[j], late_sem.at[3 * j + n])
                for n, (src, dst) in enumerate(pieces)
            ]

        def slope_copy(n):
            return pltpu.make_async_copy(
                sbuf.at[n % 2],
                slope_out.at[:, :, pl.ds(n * step, step)],
                slope_sem.at[n % 2],
            )

        @pl.loop(0, chips)
        def _(j):
            rows = ctxt[j].reshape(tile, width)
            branch = dot_rows(rows, owbuf[...].reshape(width, width))
            resid = xbuf[core, j].reshape(tile, width).astype(f32) + branch + vec(2)
            normed, inverse = moments(resid)
            n1buf[j] = normed
            invbuf[j] = jnp.broadcast_to(inverse, (tile, 128))
            mlbuf[j] = (normed * vec(3) + vec(4)).astype(bf16).reshape(per, cluster, width)

        cot_copy(2).start()
        plane_last(1)
        emit(ewbuf, ew_out)
        for n in range(hidden // step):
            lanes = slice(n * step, (n + 1) * step)
            if n >= 2:
                slope_copy(n - 2).wait()
            for j in range(chips):
                weight = ewbuf[:, :, lanes].reshape(width, step)
                pre = dot_rows(mlbuf[j].reshape(tile, width), weight) + upb[0:1, lanes]
                cumulative = 0.5 * (1.0 + lax.erf(pre * 0.5**0.5))
                density = jnp.exp(-0.5 * pre * pre) * (2.0 * math.pi) ** (-0.5)
                hbuf[j, :, lanes] = (pre * cumulative).astype(bf16)
                sbuf[n % 2, j] = (cumulative + pre * density).astype(bf16)
            slope_copy(n).start()

        emit(vecs, vec_out)
        held = len(outs)
        emit(n1buf, n1_out)
        emit(invbuf, inv_out)
        emit(mlbuf, ml_out)
        emit(hbuf, hid_out)
        plane_last(2)
        pass_end()
        emit(rwbuf, rw_out)
        for n in range(2):
            cot_copy(n).wait()
        sums[...] = jnp.zeros_like(sums)
        waited = (context_out, outs[held])
        for copy in waited:
            copy.wait()

        @pl.loop(0, chips)
        def _(n):
            j = 2 * lax.rem(lax.div(chip, 2) + lax.div(n, 2), 2)
            j = j + lax.rem(chip + n, 2)

            @pl.when(n == chips - 1)
            def _():
                cot_copy(2).wait()

            branch = vec(5)
            for zz in range(depth):
                span = hidden // depth
                branch = branch + dot_rows(
                    hbuf[j, :, zz * span : (zz + 1) * span], rwbuf[zz].reshape(span, width)
                )
            middle = n1buf[j] * vec(3) + vec(4)
            normed, inverse = moments(middle + branch)
            upstream = cbuf[j].reshape(tile, width).astype(f32)
            cbuf[j] = (normed * vec(6) + vec(7)).astype(bf16).reshape(per, cluster, width)
            sums[0:1, :] += jnp.sum(upstream * normed, axis=0, keepdims=True)
            sums[1:2, :] += jnp.sum(upstream, axis=0, keepdims=True)
            scaled = upstream * vec(6)
            first = jnp.mean(scaled, axis=1, keepdims=True)
            second = jnp.mean(scaled * normed, axis=1, keepdims=True)
            grad = inverse * (scaled - first - normed * second)
            n1buf[j] = grad
            low_grad = grad.astype(bf16)
            sums[2:3, :] += jnp.sum(low_grad.astype(f32), axis=0, keepdims=True)
            ctxt[j] = low_grad.reshape(per, cluster, width)
            for copy in late_copies(j):
                copy.start()

        emit(sums, sum_out)
        for j in range(chips):
            for copy in late_copies(j):
                copy.wait()
        for copy in sends:
            copy.wait_send()
        awc.wait_recv()
        for n in range(max(hidden // step - 2, 0), hidden // step):
            slope_copy(n).wait()
        for copy in outs:
            if not any(copy is other for other in waited):
                copy.wait()

    pl.run_scoped(
        feed,
        pltpu.VMEM((chips, tile, hidden), bf16),
        pltpu.VMEM((2, chips, tile, hidden // depth), bf16),
    )


def forward(
    tokens,
    pos,
    attend_weight,
    vectors,
    output_weight,
    expand_weight,
    reduce_weight,
    cotangent,
    chips,
    depth,
    heads,
):
    seqs, cluster, width = tokens.shape
    per, blocks, pairs = seqs // chips, 2 * chips, heads // 4
    half = width // 2
    rows_z = attend_weight.shape[0]
    hidden = expand_weight.shape[1]
    items = per * pairs
    tile = per * cluster
    dma = pltpu.SemaphoreType.DMA
    anywhere = pl.BlockSpec(memory_space=pl.ANY)
    tall = reduce_weight.shape[0] // blocks
    shapes = [
        ((2, chips, per, cluster, width), bf16),
        ((chips, per, cluster, width), bf16),
        ((items, blocks, cluster, 128), bf16),
        ((items, blocks, cluster, 128), bf16),
        ((items, blocks, cluster, 128), bf16),
        ((items, blocks, cluster, 2 * cluster), bf16),
        ((2, chips, per, 2 * heads, cluster), jnp.int32),
        ((2, depth * rows_z, 3 * half), bf16),
        ((8, width), f32),
        ((depth, 2, rows_z // 2, width), bf16),
        ((depth, rows_z, hidden), bf16),
        ((depth, blocks, tall, width), bf16),
        ((chips, tile, width), f32),
        ((chips, tile, 128), f32),
        ((chips, per, cluster, width), bf16),
        ((chips, tile, hidden), bf16),
        ((chips, tile, hidden), bf16),
        ((chips, per, cluster, width), bf16),
        ((chips, tile, width), f32),
        ((chips, per, cluster, width), bf16),
        ((8, width), f32),
    ]
    t, c = depth - 1, chips - 1
    vm = pltpu.VMEM
    return pl.pallas_call(
        functools.partial(forward_kernel, chips, depth, heads),
        out_shape=[jax.ShapeDtypeStruct(*s) for s in shapes],
        in_specs=[anywhere] * 8,
        out_specs=[anywhere] * len(shapes),
        scratch_shapes=[
            vm(shapes[0][0], bf16),
            vm(shapes[6][0], jnp.int32),
            vm(shapes[7][0][1:], bf16),
            vm((depth,) + vectors.shape, f32),
            vm((2, 8, 3 * half), f32),
            vm((2, chips, per, cluster, half), bf16),
            vm(shapes[1][0], bf16),
            vm(shapes[9][0], bf16),
            vm(shapes[10][0], bf16),
            vm(shapes[11][0], bf16),
            vm(shapes[17][0], bf16),
            vm(shapes[12][0], f32),
            vm(shapes[13][0], f32),
            vm(shapes[14][0], bf16),
            vm((8, width), f32),
            vm((8, hidden), f32),
            vm((8, width), f32),
            dma((c,)), dma((c,)), dma((chips,)), dma((chips,)),
            dma((c,)), dma((c,)), dma((chips,)), dma((chips,)),
            dma((t,)), dma((t,)), dma((t,)), dma((t,)), dma((1,)), dma((1,)),
            dma((t,)), dma((t,)),
            dma((3 * t,)), dma((3 * t,)),
            dma((4,)), dma((4,)), dma((4,)), dma((4,)),
            dma((2 * chips,)), dma((2 * chips,)),
            dma((1,)), dma((1,)),
            dma((c,)), dma((c,)),
            dma((1,)), dma((1,)),
            dma((12,)), dma((24,)), dma((2,)), dma((5 + 4 * per,)), dma((3 * chips,)),
        ],
        compiler_params=pltpu.CompilerParams(
            collective_id=1, has_side_effects=True, vmem_limit_bytes=63 * 2**20
        ),
        name="forward",
    )(
        tokens,
        pos,
        attend_weight,
        vectors,
        output_weight,
        expand_weight,
        reduce_weight,
        cotangent,
    )


def add_into(target, at, parts):
    total = target[at].astype(f32)
    for part in parts:
        total = total + part.astype(f32)
    target[at] = total.astype(target.dtype)


class Reducer:
    def __init__(self, me, own, other, near, mid, last, done, sems, tower_first):
        self.me, self.own, self.other = me, own, other
        self.near, self.mid, self.last, self.done = near, mid, last, done
        (self.near_s, self.near_r, self.mid_s, self.mid_r, self.last_s, self.last_r) = sems[:6]
        (self.back_s, self.back_r, self.side_s, self.side_r) = sems[6:10]
        self.tower_first = tower_first
        self.sizes = (mid.shape[0] + 1, last.shape[0] + 1)

    def spot(self, axis, k):
        me = self.me
        if self.tower_first == (axis == 0):
            return me.z_at(k), me.tower(k)
        return me.chip_at(k), me.plane(k)

    def near_copy(self, a):
        return far_copy(
            self.other.at[a], self.near.at[a], (self.near_s, self.near_r), a, self.me.sibling()
        )

    def fold_near(self, a):
        self.near_copy(a).wait_recv()
        for b in range(self.sizes[1]):
            add_into(self.own, (a, b), [self.near[a, b]])

    def mid_copy(self, k):
        where, device = self.spot(0, k)
        return far_copy(
            self.own.at[where], self.mid.at[k - 1], (self.mid_s, self.mid_r), k - 1, device
        )

    def send_mid(self):
        for k in range(1, self.sizes[0]):
            self.mid_copy(k).start()

    def fold_mid(self):
        for k in range(1, self.sizes[0]):
            self.mid_copy(k).wait()
        here = self.spot(0, 0)[0]
        for b in range(self.sizes[1]):
            add_into(self.own, (here, b), [self.mid[k - 1, b] for k in range(1, self.sizes[0])])

    def last_copy(self, k):
        here = self.spot(0, 0)[0]
        where, device = self.spot(1, k)
        return far_copy(
            self.own.at[here, where],
            self.last.at[k - 1],
            (self.last_s, self.last_r),
            k - 1,
            device,
        )

    def send_last(self):
        for k in range(1, self.sizes[1]):
            self.last_copy(k).start()

    def fold_last(self):
        me = self.me
        for k in range(1, self.sizes[1]):
            self.last_copy(k).wait()
        total = self.own[self.spot(0, 0)[0], self.spot(1, 0)[0]].astype(f32)
        for k in range(1, self.sizes[1]):
            total = total + self.last[k - 1].astype(f32)
        self.done[me.core, me.chip] = total.astype(bf16)

    def back_copy(self, k):
        me = self.me
        spot = self.done.at[me.core, me.chip]
        return far_copy(spot, spot, (self.back_s, self.back_r), k - 1, me.plane(k))

    def send_back(self):
        for k in range(1, self.done.shape[1]):
            self.back_copy(k).start()

    def side_copy(self):
        spot = self.done.at[self.me.core]
        return far_copy(spot, spot, (self.side_s, self.side_r), 0, self.me.sibling())

    def send_side(self):
        for k in range(1, self.done.shape[1]):
            self.back_copy(k).wait()
        self.side_copy().start()

    def finish(self):
        self.side_copy().wait()


class Sum:
    def __init__(self, me, vec, got, s, r):
        self.me, self.vec, self.got, self.s, self.r = me, vec, got, s, r

    def copies(self, hop):
        me = self.me
        if hop == 0:
            spots = [(0, me.sibling())]
        elif hop == 1:
            spots = [(k, me.plane(k)) for k in range(1, me.chips)]
        else:
            spots = [(me.chips + k - 1, me.tower(k)) for k in range(1, me.depth)]
        return [far_copy(self.vec, self.got.at[n], (self.s, self.r), n, d) for n, d in spots], spots

    def send(self, hop):
        for copy in self.copies(hop)[0]:
            copy.start()

    def fold(self, hop):
        copies, spots = self.copies(hop)
        for copy in copies:
            copy.wait()
        total = self.vec[...]
        for n, _ in spots:
            total = total + self.got[n]
        self.vec[...] = total


def back_kernel(
    chips,
    depth,
    heads,
    q_ref,
    k_ref,
    v_ref,
    p_ref,
    pos_ref,
    x_ref,
    aw_ref,
    ow_ref,
    ew_ref,
    rw_ref,
    vec_ref,
    ctx_ref,
    n1_ref,
    inv_ref,
    ml_ref,
    hid_ref,
    slope_ref,
    lo_ref,
    gr_ref,
    gb_ref,
    late_ref,
    token_out,
    layer_out,
    aw_out,
    ow_out,
    ew_out,
    rw_out,
    vec_out,
    bias_out,
    dbuf,
    posbuf,
    acc,
    gfar,
    p_mid,
    p_last,
    p_done,
    o_all,
    o_near,
    o_mid,
    o_last,
    o_done,
    e_all,
    e_near,
    e_mid,
    e_last,
    e_done,
    r_all,
    r_near,
    r_mid,
    r_last,
    r_done,
    vbuf,
    vgot,
    bbuf,
    bgot,
    vecs,
    d_s,
    d_r,
    g_s,
    g_r,
    t_s,
    t_r,
    lo_s,
    lo_r,
    load,
    out_sem,
    v_s,
    v_r,
    b_s,
    b_r,
    *sems,
):
    me = Place(chips, depth)
    z, core, chip = me.z, me.core, me.chip
    per, cluster, width = lo_ref.shape[1:]
    half = width // 2
    pairs = heads // 4
    size = half // (2 * pairs)
    blocks = 2 * chips
    share = cluster // blocks
    tile = per * cluster
    hidden = hid_ref.shape[2]
    wide = hidden // blocks
    strip = width // chips
    quarter = width // depth
    eighth = quarter // blocks
    rows = chips * tile
    me.greet()
    groups = [sems[n * 10 : (n + 1) * 10] for n in range(3 + heads // 4)]
    red = Reducer(
        me, r_all.at[core], r_all.at[1 - core], r_near, r_mid, r_last, r_done, groups[0], True
    )
    exp = Reducer(
        me, e_all.at[core], e_all.at[1 - core], e_near, e_mid, e_last, e_done, groups[1], False
    )
    out = Reducer(
        me, o_all.at[core], o_all.at[1 - core], o_near, o_mid, o_last, o_done, groups[2], False
    )
    sums = Sum(me, vbuf, vgot, v_s, v_r)
    biases = Sum(me, bbuf, bgot, b_s, b_r)

    def fetch(src, dst, at):
        return pltpu.make_async_copy(src, dst, load.at[at])

    def lo_copy(k):
        return far_copy(
            lo_ref.at[me.chip_at(k)],
            layer_out.at[pl.ds(chip * per, per)],
            (lo_s, lo_r),
            k - 1,
            me.plane(k),
        )

    lo_keep = pltpu.make_async_copy(
        lo_ref.at[chip], layer_out.at[pl.ds(chip * per, per)], out_sem.at[0]
    )

    block = 2 * wide
    counts = blocks // 2

    def order(n):
        return lax.rem(n + z + chip, counts)

    def fold_red(n):
        at = order(n)
        red.fold_near(at)
        k = lax.rem(at - z + depth, depth)

        @pl.when(k != 0)
        def _():
            red.mid_copy(k).start()

    def fold_exp(n):
        at = order(n)

        @pl.when(lax.div(at, 2) == core)
        def _():
            for side in range(2):
                b = lax.rem(at, 2) * 2 + side
                exp.fold_near(b)
                k = lax.rem(b - chip + chips, chips)

                @pl.when(k != 0)
                def _():
                    exp.mid_copy(k).start()

    def chunks(gb, gbt, mlt, hid, slope, rwc, ewc, gpb):
        def chunk(n, slot):
            at = order(n)
            lanes = pl.ds(multiple(at * block, 128), block)
            return [
                fetch(hid_ref.at[:, :, lanes], hid.at[slot], slot * 4),
                fetch(slope_ref.at[:, :, lanes], slope.at[slot], slot * 4 + 1),
                fetch(rw_ref.at[at], rwc.at[slot], slot * 4 + 2),
                fetch(ew_ref.at[:, :, lanes], ewc.at[slot], slot * 4 + 3),
            ]

        begin = [
            fetch(gb_ref, gb, 8),
            fetch(ml_ref, gpb, 9),
            fetch(gr_ref, acc, 10),
        ]
        later = [
            fetch(vec_ref, vecs, 11),
            fetch(late_ref, vbuf.at[pl.ds(0, 8)], 12),
            fetch(pos_ref, posbuf, 18),
        ]
        for copy in begin[:1] + chunk(0, 0) + begin[1:] + later:
            copy.start()
        for k in range(1, chips):
            lo_copy(k).start()
        lo_keep.start()
        vbuf[8:, :] = jnp.zeros((blocks, width), f32)
        begin[0].wait()
        for j in range(chips):
            gbt[:, j * tile : (j + 1) * tile] = jnp.transpose(gb[j].reshape(tile, width))

        def settle():
            for copy in begin[1:] + later:
                copy.wait()
            for j in range(chips):
                mlt[:, j * tile : (j + 1) * tile] = jnp.transpose(gpb[j].reshape(tile, width))

        @pl.loop(0, counts)
        def _(n):
            slot = lax.rem(n, 2)
            at = order(n)
            for copy in chunk(n, slot):
                copy.wait()

            @pl.when(n + 1 < counts)
            def _():
                for copy in chunk(n + 1, 1 - slot):
                    copy.start()

            term = dot_rows(gbt[...], hid[slot].reshape(rows, block)).astype(bf16)
            for side in range(2):
                r_all[side, at] = term[:, side * wide : (side + 1) * wide].reshape(
                    chips, strip, wide
                )
            red.near_copy(at).start()

            @pl.when(n == 0)
            def _():
                settle()

            @pl.when(n > 0)
            def _():
                fold_exp(n - 1)

            up = rwc[slot].reshape(block, width)
            down = ewc[slot].reshape(width, block)
            total = jnp.zeros((1, block), f32)
            for j in range(chips):
                grad = dot_lanes(gb[j].reshape(tile, width), up)
                low = (grad * slope[slot, j].astype(f32)).astype(bf16)
                gpb[j] = low.reshape(per, cluster, block)
                acc[j] += dot_lanes(low, down)
                total = total + jnp.sum(low.astype(f32), axis=0, keepdims=True)
            vbuf[pl.ds(8 + at, 1), :block] = total
            fold_red(n)
            term = dot_rows(mlt[...], gpb[...].reshape(rows, block)).astype(bf16)
            for side in range(2):
                e_all[lax.div(at, 2), lax.rem(at, 2) * 2 + side] = term[
                    :, side * wide : (side + 1) * wide
                ].reshape(depth, quarter, wide)

            @pl.when(lax.div(at, 2) != core)
            def _():
                for side in range(2):
                    exp.near_copy(lax.rem(at, 2) * 2 + side).start()

    def first_norm(gb, n1, inv, ctx, ow, dsnd):
        later = [
            fetch(ctx_ref, ctx, 13),
            fetch(ow_ref, ow, 14),
            fetch(inv_ref, inv, 15),
        ]
        def n1_copy(j):
            return fetch(n1_ref.at[j], n1.at[j % 2], 16 + j % 2)

        def d_copy(j):
            return far_copy(dsnd.at[j], dbuf.at[core, j], (d_s, d_r), j, me.sibling())

        n1_copy(0).start()
        for copy in later:
            copy.start()
        fold_exp(counts - 1)
        for copy in later:
            copy.wait()
        gain = vecs[3:4, :]
        for row in range(3, 8):
            vbuf[row : row + 1, :] = jnp.zeros((1, width), f32)
        for j in range(chips):
            n1_copy(j).wait()
            if j + 1 < chips:
                n1_copy(j + 1).start()
            grad = acc[j]
            normed = n1[j % 2]
            vbuf[3:4, :] += jnp.sum(grad * normed, axis=0, keepdims=True)
            vbuf[4:5, :] += jnp.sum(grad, axis=0, keepdims=True)
            scaled = grad * gain
            first = jnp.mean(scaled, axis=1, keepdims=True)
            second = jnp.mean(scaled * normed, axis=1, keepdims=True)
            grad = inv[j][:, :1] * (scaled - first - normed * second)
            acc[j] = grad
            low = grad.astype(bf16)
            gb[j] = low.reshape(per, cluster, width)
            vbuf[5:6, :] += jnp.sum(low.astype(f32), axis=0, keepdims=True)
            back = dot_lanes(low, ow[...].reshape(width, width)).astype(bf16)

            for c in range(2):
                piece = back[:, c * half : (c + 1) * half]

                @pl.when(core == c)
                def _():
                    dbuf[c, j] = piece.reshape(per, cluster, half)

                @pl.when(core != c)
                def _():
                    dsnd[j] = piece.reshape(per, cluster, half)

            d_copy(j).start()
        sums.send(0)
        term = dot_first(ctx[...].reshape(rows, width), gb[...].reshape(rows, width))
        for zz in range(depth):
            for c in range(2):
                for p in range(chips):
                    begin_at = zz * quarter + (c * chips + p) * eighth
                    o_all[c, p, zz] = term[begin_at : begin_at + eighth, :].astype(bf16)
        for p in range(chips):
            out.near_copy(p).start()
        for j in range(chips):
            d_copy(j).wait()
        for a in range(depth):
            red.near_copy(a).wait_send()
        for b in range(chips):
            exp.near_copy(b).wait_send()

    shape = (chips, per, cluster, width)
    vm = pltpu.VMEM

    def feed_back(gb):
        pl.run_scoped(
            functools.partial(chunks, gb),
            vm((width, rows), bf16),
            vm((width, rows), bf16),
            vm((2, chips, tile, block), bf16),
            vm((2, chips, tile, block), bf16),
            vm((2, blocks, block // blocks, width), bf16),
            vm((2, depth, quarter, block), bf16),
            vm(shape[:3] + (block,), bf16),
        )
        pl.run_scoped(
            functools.partial(first_norm, gb),
            vm((2, tile, width), f32),
            vm((chips, tile, 128), f32),
            vm(shape, bf16),
            vm((depth, 2, quarter // 2, width), bf16),
            vm((chips, per, cluster, half), bf16),
        )

    pl.run_scoped(feed_back, vm(shape, bf16))

    def attend_back(qs, ks, vs, ps, xbuf, wbuf, ds, gs, gbuf, tbuf, dw, dwp, turned):
        atts = [
            Reducer(
                me,
                dwp.at[n],
                None,
                None,
                p_mid.at[n],
                p_last.at[n],
                p_done.at[n],
                groups[3 + n],
                n % 2 == 1,
            )
            for n in range(pairs)
        ]

        def loads(i, slot):
            span = pl.ds(i * pairs, pairs)
            pieces = (
                (q_ref.at[span], qs),
                (k_ref.at[span], ks),
                (v_ref.at[span], vs),
                (p_ref.at[span], ps),
            )
            return [fetch(src, dst.at[slot], slot * 4 + n) for n, (src, dst) in enumerate(pieces)]

        def load_x(i):
            return fetch(x_ref.at[:, :, i], xbuf, 8)

        load_w = fetch(aw_ref, wbuf, 9)
        for copy in loads(0, 0) + [load_x(0), load_w]:
            copy.start()
        bbuf[...] = jnp.zeros_like(bbuf)
        slots = lax.broadcasted_iota(jnp.int32, (cluster, cluster), 0)
        low = lax.broadcasted_iota(jnp.int32, (cluster, 128), 1) < size
        scale = size ** (-0.5)

        def tables(jj, i, pair, part):
            begin = part * heads + core * (heads // 2) + 2 * pair
            return [
                one_hot(posbuf[jj // chips, jj % chips, i, pl.ds(begin + h, 1), :], slots)
                for h in range(2)
            ]

        def clusters(i, slot, pair):
            lanes = pl.ds(multiple(pair * 128, 128), 128)
            for jj in range(blocks):
                tq = jnp.concatenate(tables(jj, i, pair, 0), axis=1)
                rows = stack_lanes(dbuf[jj // chips, jj % chips, i, :, lanes], low)
                ds[:, jj * share : (jj + 1) * share, :] = (
                    dot_rows(tq, rows).astype(bf16).reshape(blocks, share, 128)
                )
            for c in range(blocks):
                d = ds[c]
                probs = ps[slot, pair, c]
                slope = dot_lanes(d, stack_lanes(vs[slot, pair, c], low))
                broad = probs.astype(f32)
                halves = []
                for h in range(2):
                    span = slice(h * cluster, (h + 1) * cluster)
                    inner = jnp.sum(broad[:, span] * slope[:, span], axis=1, keepdims=True)
                    halves.append((broad[:, span] * (slope[:, span] - inner)).astype(bf16))
                grads = jnp.concatenate(halves, axis=1)
                gq = dot_rows(grads, stack_lanes(ks[slot, pair, c], low)) * scale
                gk = dot_first(grads, qs[slot, pair, c]) * scale
                gv = dot_first(probs, d)
                gs[0, c] = gq.astype(bf16)
                gs[1, c] = jnp.where(low, gk[:cluster], gk[cluster:]).astype(bf16)
                gs[2, c] = jnp.where(low, gv[:cluster], gv[cluster:]).astype(bf16)
            for jj in range(blocks):
                for part in range(3):
                    if part < 2:
                        table = jnp.concatenate(tables(jj, i, pair, part), axis=0)
                    rows = gs[part, :, jj * share : (jj + 1) * share, :].reshape(cluster, 128)
                    back = dot_first(table, stack_lanes(rows, low))
                    to = pl.ds(multiple(part * half + pair * 128, 128), 128)
                    gbuf[slot, jj // chips, jj % chips, :, to] = back.astype(bf16)

        def give(slot):
            return far_copy(gbuf.at[slot, 1 - core], gfar.at[slot], (g_s, g_r), slot, me.sibling())

        def token_copy(i, slot, k):
            return far_copy(
                tbuf.at[slot, me.chip_at(k)],
                token_out.at[chip * per + i],
                (t_s, t_r),
                i * (chips - 1) + k - 1,
                me.plane(k),
            )

        def token_keep(i, slot):
            return pltpu.make_async_copy(
                tbuf.at[slot, chip], token_out.at[chip * per + i], out_sem.at[1 + i]
            )

        def token_rows(i, slot):
            give(slot).wait()
            near = dot_lanes(gbuf[slot, core].reshape(chips * cluster, 3 * half), wbuf[core])
            distant = dot_lanes(gfar[slot].reshape(chips * cluster, 3 * half), wbuf[1 - core])
            resid = acc[:, i * cluster : (i + 1) * cluster, :].reshape(chips * cluster, width)
            tbuf[slot] = (resid + near + distant).astype(bf16).reshape(chips, cluster, width)
            token_keep(i, slot).start()
            for k in range(1, chips):
                token_copy(i, slot, k).start()

        ready = []

        def emit(src, dst):
            copy = pltpu.make_async_copy(src, dst, out_sem.at[1 + per + len(ready)])
            copy.start()
            ready.append(copy)

        def step_out_near():
            for p in range(chips):
                out.fold_near(p)
            out.send_mid()
            for p in range(chips):
                out.near_copy(p).wait_send()
            sums.fold(0)
            sums.send(1)

        def step_exp_mid():
            exp.fold_mid()
            exp.send_last()

        def step_red_mid():
            red.fold_mid()
            red.send_last()
            sums.fold(1)
            sums.send(2)

        def step_exp_last():
            exp.fold_last()
            exp.send_back()
            out.fold_mid()
            out.send_last()

        def step_red_last():
            red.fold_last()
            red.send_back()
            sums.fold(2)

        def step_out_last():
            out.fold_last()
            out.send_back()
            exp.send_side()

        def step_sides():
            red.send_side()

        hooks = {}
        steps = [
            (0, step_out_near),
            (1, step_exp_mid),
            (3, step_red_mid),
            (5, step_exp_last),
            (6, step_red_last),
            (7, step_out_last),
            (8, step_sides),
        ]
        for n, step in steps:
            hooks.setdefault(min(n, per * pairs - 1), []).append(step)
        depth_rows = quarter // chips

        def pair_grad(n, slot):
            lanes = [slice(p * half + n * 128, p * half + (n + 1) * 128) for p in range(3)]
            total = jnp.concatenate([dw[:, lane] for lane in lanes], axis=1)
            line = jnp.zeros((1, 384), f32)
            for b in range(2):
                x = jnp.concatenate([xbuf[b, j] for j in range(chips)], axis=0)
                g = jnp.concatenate(
                    [
                        jnp.concatenate([gbuf[slot, b, j, :, lane] for lane in lanes], axis=1)
                        for j in range(chips)
                    ],
                    axis=0,
                )
                total = total + dot_first(x, g)
                line = line + jnp.sum(g.astype(f32), axis=0, keepdims=True)
            for p, lane in enumerate(lanes):
                bbuf[0:1, lane] += line[:, p * 128 : (p + 1) * 128]
            low = total.astype(bf16)
            for a in range(depth):
                for b in range(chips):
                    begin = (a * chips + b) * depth_rows
                    piece = low[begin : begin + depth_rows]
                    if atts[n].tower_first:
                        dwp[n, a, b] = piece
                    else:
                        dwp[n, b, a] = piece
            atts[n].send_mid()

        dw[...] = jnp.zeros_like(dw)
        for i in range(per):
            slot = i % 2
            for copy in loads(i, slot):
                copy.wait()
            if i == 0:
                load_w.wait()
            if i >= 1:
                token_rows(i - 1, 1 - slot)
            if i + 1 < per:
                for copy in loads(i + 1, 1 - slot):
                    copy.start()
            if i == per - 1:
                load_x(i).wait()

            @pl.loop(0, pairs)
            def _(pair):
                clusters(i, slot, pair)
                for n in range(pairs):
                    if hooks.get(i * pairs + n) or i == per - 1:

                        @pl.when(pair == n)
                        def _():
                            if i == per - 1:
                                pair_grad(n, slot)
                            for step in hooks.get(i * pairs + n, ()):
                                step()

            if i >= 2:
                token_keep(i - 2, slot).wait()
                for k in range(1, chips):
                    token_copy(i - 2, slot, k).wait()
            give(slot).start()
            if i + 1 < per:
                load_x(i).wait()
                for b in range(2):
                    x = jnp.concatenate([xbuf[b, j] for j in range(chips)], axis=0)
                    g = jnp.concatenate([gbuf[slot, b, j] for j in range(chips)], axis=0)
                    dw[...] += dot_first(x, g)
                    bbuf[0:1, :] += jnp.sum(g.astype(f32), axis=0, keepdims=True)
                load_x(i + 1).start()

        biases.send(1)
        token_rows(per - 1, (per - 1) % 2)
        emit(vbuf, vec_out)
        out.send_side()
        for n in range(pairs - 1):
            atts[n].fold_mid()
            atts[n].send_last()
        biases.fold(1)
        biases.send(2)
        exp.finish()
        for c in range(2):
            for p in range(chips):
                emit(e_done.at[c, p], ew_out.at[:, pl.ds((c * chips + p) * wide, wide)])
        for n in range(pairs - 1, pairs):
            atts[n].fold_mid()
            atts[n].send_last()
        for n in range(pairs - 1):
            atts[n].fold_last()
            atts[n].send_back()
        red.finish()
        for c in range(2):
            turned[c] = jnp.transpose(r_done[c].reshape(width, wide))
            emit(turned.at[c], rw_out.at[c])
        out.finish()
        emit(o_done, ow_out)
        biases.fold(2)
        share_bias = far_copy(bbuf, bias_out.at[core], (b_s, b_r), 0, me.sibling())
        share_bias.start()
        emit(bbuf, bias_out.at[core])
        for n in range(pairs - 1, pairs):
            atts[n].fold_last()
            atts[n].send_back()
        for n in range(pairs):
            atts[n].send_side()
        for n in range(pairs):
            atts[n].finish()
            for c in range(2):
                for part in range(3):
                    emit(
                        p_done.at[n, c, :, :, pl.ds(part * 128, 128)],
                        aw_out.at[:, :, pl.ds((2 * part + c) * half + n * 128, 128)],
                    )
        for i in range(max(per - 2, 0), per):
            token_keep(i, i % 2).wait()
            for k in range(1, chips):
                token_copy(i, i % 2, k).wait()
        share_bias.wait()
        for copy in ready:
            copy.wait()
        lo_keep.wait()
        for k in range(1, chips):
            lo_copy(k).wait()

    group = (2, pairs, blocks, cluster)
    pl.run_scoped(
        attend_back,
        vm(group + (128,), bf16),
        vm(group + (128,), bf16),
        vm(group + (128,), bf16),
        vm(group + (2 * cluster,), bf16),
        vm((2, chips, cluster, width), bf16),
        vm(aw_ref.shape, bf16),
        vm((blocks, cluster, 128), bf16),
        vm((3, blocks, cluster, 128), bf16),
        vm((2, 2, chips, cluster, 3 * half), bf16),
        vm((2, chips, cluster, width), bf16),
        vm((width, 3 * half), f32),
        vm((pairs, depth, chips, quarter // chips, 384), bf16),
        vm((2, wide, width), bf16),
    )


def back(arrays, depth, heads):
    chips, per, cluster, width = arrays[17].shape
    half, blocks = width // 2, 2 * chips
    dma = pltpu.SemaphoreType.DMA
    anywhere = pl.BlockSpec(memory_space=pl.ANY)
    quarter = width // depth
    hidden = arrays[15].shape[2]
    eighth, strip, wide = quarter // blocks, width // chips, hidden // blocks
    rows = quarter // chips
    c, t = chips - 1, depth - 1
    pairs = heads // 4
    shapes = [
        ((chips * per, cluster, width), bf16),
        ((chips * per, cluster, width), bf16),
        ((chips, rows, 3 * width), bf16),
        ((2, chips, eighth, width), bf16),
        ((quarter, hidden), bf16),
        ((2, wide, width), bf16),
        ((8 + blocks, width), f32),
        ((2, 8, 3 * half), f32),
    ]
    vm = pltpu.VMEM

    def reducing(near, first, second):
        return [
            dma((near,)), dma((near,)),
            dma((first,)), dma((first,)),
            dma((second,)), dma((second,)),
            dma((c,)), dma((c,)),
            dma((1,)), dma((1,)),
        ]

    return pl.pallas_call(
        functools.partial(back_kernel, chips, depth, heads),
        out_shape=[jax.ShapeDtypeStruct(*s) for s in shapes],
        in_specs=[anywhere] * len(arrays),
        out_specs=[anywhere] * len(shapes),
        scratch_shapes=[
            vm((2, chips, per, cluster, half), bf16),
            vm(arrays[4].shape, jnp.int32),
            vm((chips, per * cluster, width), f32),
            vm((2, chips, cluster, 3 * half), bf16),
            vm((pairs, t, chips, rows, 384), bf16),
            vm((pairs, t, rows, 384), bf16),
            vm((pairs, 2, chips, rows, 384), bf16),
            vm((2, chips, depth, eighth, width), bf16),
            vm((chips, depth, eighth, width), bf16),
            vm((c, depth, eighth, width), bf16),
            vm((t, eighth, width), bf16),
            vm((2, chips, eighth, width), bf16),
            vm((2, chips, depth, quarter, wide), bf16),
            vm((chips, depth, quarter, wide), bf16),
            vm((c, depth, quarter, wide), bf16),
            vm((t, quarter, wide), bf16),
            vm((2, chips, quarter, wide), bf16),
            vm((2, depth, chips, strip, wide), bf16),
            vm((depth, chips, strip, wide), bf16),
            vm((t, chips, strip, wide), bf16),
            vm((c, strip, wide), bf16),
            vm((2, chips, strip, wide), bf16),
            vm((8 + blocks, width), f32),
            vm((chips + t, 8 + blocks, width), f32),
            vm((8, 3 * half), f32),
            vm((chips + t, 8, 3 * half), f32),
            vm((8, width), f32),
            dma((chips,)), dma((chips,)), dma((2,)), dma((2,)),
            dma((per * c,)), dma((per * c,)),
            dma((c,)), dma((c,)),
            dma((19,)), dma((1 + per + 6 + blocks + 6 * pairs,)),
            dma((chips + t,)), dma((chips + t,)), dma((chips + t,)), dma((chips + t,)),
            *reducing(depth, t, c),
            *reducing(chips, c, t),
            *reducing(chips, c, t),
            *[sem for n in range(pairs) for sem in reducing(1, c, t)],
        ],
        compiler_params=pltpu.CompilerParams(
            collective_id=2, has_side_effects=True, vmem_limit_bytes=63 * 2**20
        ),
        name="back",
    )(*arrays)


def places(rank, cluster, share):
    seqs, rows, length = rank.shape
    clusters = cluster // share
    target = rank // cluster
    which = lax.broadcasted_iota(jnp.int32, (1, 1, clusters, 1), 2)
    inside = (target[:, :, None, :] == which).astype(bf16)
    first = lax.broadcasted_iota(jnp.int32, (length, length), 0)
    second = lax.broadcasted_iota(jnp.int32, (length, length), 1)
    before = (first < second).astype(bf16)
    count = lax.dot_general(
        inside.reshape(seqs * rows * clusters, length),
        before,
        (((1,), (0,)), ((), ())),
        preferred_element_type=f32,
    ).reshape(seqs, rows, clusters, length)
    spot = which.astype(f32) * share + count
    return jnp.sum(inside.astype(f32) * spot, axis=2).astype(jnp.int32)


def per_chip(
    tokens,
    attend_weight,
    query_bias,
    value_bias,
    output_weight,
    output_bias,
    first_gain,
    first_shift,
    expand_weight,
    expand_bias,
    reduce_weight,
    reduce_bias,
    second_gain,
    second_shift,
    query_rank,
    key_rank,
    cotangent,
):
    seqs, cluster, width = tokens.shape
    heads = query_rank.shape[1]
    owners = lax.axis_size("seq")
    depth = lax.axis_size("batch")
    chips = owners // 2
    half = width // 2
    share = cluster // owners
    pos = places(jnp.concatenate([query_rank, key_rank], axis=1), cluster, share)
    quarter = width // depth
    lines = [
        query_bias,
        value_bias,
        output_bias,
        first_gain,
        first_shift,
        reduce_bias,
        second_gain,
        second_shift,
    ]
    lines += [
        expand_bias[at : at + quarter] for at in range(0, expand_bias.shape[0], quarter)
    ]
    vectors = jnp.zeros((16 * 256,), f32)
    for row, v in enumerate(lines):
        vectors += jnp.pad(v.astype(f32), (row * 256, (16 - row) * 256 - quarter))
    vectors = vectors.reshape(16, 256)
    (
        x_all,
        context,
        qs,
        ks,
        vs,
        ps,
        pos_all,
        attend_all,
        vecs,
        out_all,
        exp_all,
        red_all,
        normed_one,
        inverse_one,
        middle_low,
        hidden,
        slope,
        layer_out,
        grad_resid_two,
        grad_branch_two,
        late_sums,
    ) = forward(
        tokens,
        pos,
        attend_weight,
        vectors,
        output_weight,
        expand_weight,
        reduce_weight,
        cotangent,
        chips,
        depth,
        heads,
    )
    token_grad, layer_out, aw_grad, ow_grad, ew_grad, rw_grad, vec_sum, bias_sum = back(
        (
            qs,
            ks,
            vs,
            ps,
            pos_all,
            x_all,
            attend_all,
            out_all,
            exp_all,
            red_all,
            vecs,
            context,
            normed_one,
            inverse_one,
            middle_low,
            hidden,
            slope,
            layer_out,
            grad_resid_two,
            grad_branch_two,
            late_sums,
        ),
        depth,
        heads,
    )
    z = lax.axis_index("batch")
    six = lax.dynamic_slice_in_dim(vec_sum[:6], z * quarter, quarter, 1)
    up = lax.dynamic_index_in_dim(vec_sum[8:], z, 0, keepdims=False)
    both = jnp.concatenate([bias_sum[0, 0], bias_sum[1, 0]]).reshape(2, 3, half)
    query_value = jnp.transpose(both, (1, 0, 2)).reshape(3, width)
    query_value = lax.dynamic_slice_in_dim(query_value, z * quarter, quarter, 1)
    return (
        layer_out,
        token_grad,
        aw_grad.reshape(quarter, 3 * width).astype(f32),
        query_value[0],
        query_value[2],
        ow_grad.reshape(quarter, width).astype(f32),
        six[5],
        six[3],
        six[4],
        ew_grad.astype(f32),
        up,
        rw_grad.reshape(-1, width).astype(f32),
        six[2],
        six[0],
        six[1],
    )


def layer(mesh):
    def run(*arrays):
        seqs, cluster, width = arrays[0].shape
        heads = arrays[14].shape[1]
        owners, depth = mesh.shape["seq"], mesh.shape["batch"]
        chips = owners // 2
        fits = (
            owners % 2 == 0
            and chips > 1
            and depth == chips == 4
            and seqs % chips == 0
            and cluster == 128
            and heads % 4 == 0
            and width == heads * 64
            and cluster == 16 * owners
            and arrays[8].shape[1] == 4 * width
        )
        return (per_chip if fits else per_device)(*arrays)

    return run


def solution(mesh):
    in_specs = (
        P("batch", "seq", None),
        P("batch", None),
        P("batch"),
        P("batch"),
        P("batch", None),
        P("batch"),
        P("batch"),
        P("batch"),
        P("batch", None),
        P("batch"),
        P("batch", None),
        P("batch"),
        P("batch"),
        P("batch"),
        P("batch", None, "seq"),
        P("batch", None, "seq"),
        P("batch", "seq", None),
    )
    out_specs = (
        P("batch", "seq", None),
        P("batch", "seq", None),
        P("batch", None),
        P("batch"),
        P("batch"),
        P("batch", None),
        P("batch"),
        P("batch"),
        P("batch"),
        P("batch", None),
        P("batch"),
        P("batch", None),
        P("batch"),
        P("batch"),
        P("batch"),
    )
    return jax.shard_map(
        layer(mesh), mesh=mesh, in_specs=in_specs, out_specs=out_specs, check_vma=False
    )
```

```python
import functools
import math

import jax
import jax.numpy as jnp
from jax import lax
from jax.experimental import pallas as pl
from jax.experimental.pallas import tpu as pltpu
from jax.sharding import PartitionSpec as P

epsilon = 1e-05


def layer_norm(resid, gain, shift):
    center = jnp.mean(resid, axis=-1, keepdims=True)
    centered = resid - center
    spread = jnp.mean(centered * centered, axis=-1, keepdims=True)
    inverse = lax.rsqrt(spread + epsilon)
    normed = centered * inverse
    return (normed * gain + shift, normed, inverse)


def norm_back(upstream, normed, inverse, gain):
    scaled = upstream * gain
    first_mean = jnp.mean(scaled, axis=-1, keepdims=True)
    second_mean = jnp.mean(scaled * normed, axis=-1, keepdims=True)
    return inverse * (scaled - first_mean - normed * second_mean)


def gelu_slope(value):
    cumulative = 0.5 * (1.0 + lax.erf(value * 0.5**0.5))
    density = jnp.exp(-0.5 * value * value) * (2.0 * math.pi) ** (-0.5)
    return cumulative + value * density


def transpose_left(first, second):
    return lax.dot_general(
        first, second, (((0,), (0,)), ((), ())), preferred_element_type=jnp.float32
    )


def transpose_right(first, second):
    return lax.dot_general(
        first, second, (((1,), (1,)), ((), ())), preferred_element_type=jnp.float32
    )


def group_table(rank, cluster, owners):
    share = cluster // owners
    target = rank // cluster
    length = rank.shape[-1]
    places = lax.broadcasted_iota(jnp.int32, (length, length), 0)
    later = lax.broadcasted_iota(jnp.int32, (length, length), 1)
    before = (places < later)[None, None]
    same = target[..., :, None] == target[..., None, :]
    earlier = jnp.sum((same & before).astype(jnp.int32), axis=-2)
    position = target * share + earlier
    slots = lax.broadcasted_iota(jnp.int32, position.shape + (length,), 3)
    return (position[..., None] == slots).astype(jnp.bfloat16)


def sort_heads(rows, table, heads):
    seqs, length, width = rows.shape
    split = rows.reshape(seqs, length, heads, width // heads)
    moved = jnp.einsum("shtp,sthd->sphd", table, split, preferred_element_type=jnp.float32)
    return moved.astype(rows.dtype).reshape(seqs, length, width)


def unsort_heads(rows, table, heads):
    seqs, length, width = rows.shape
    split = rows.reshape(seqs, length, heads, width // heads)
    moved = jnp.einsum("shtp,sphd->sthd", table, split, preferred_element_type=jnp.float32)
    return moved.astype(rows.dtype).reshape(seqs, length, width)


def cluster_scores(queries, keys_rows, heads):
    items, length, width = queries.shape
    size = width // heads
    query_split = queries.reshape(items, length, heads, size)
    key_split = keys_rows.reshape(items, length, heads, size)
    scores = jnp.einsum(
        "sqhd,skhd->shqk", query_split, key_split, preferred_element_type=jnp.float32
    )
    return scores * size ** (-0.5)


def cluster_forward(queries, keys_rows, values_rows, heads):
    items, length, width = queries.shape
    scores = cluster_scores(queries, keys_rows, heads)
    top = jnp.max(scores, axis=-1, keepdims=True)
    weights = jnp.exp(scores - top)
    total = jnp.sum(weights, axis=-1, keepdims=True)
    probs = (weights / total).astype(jnp.bfloat16)
    value_split = values_rows.reshape(items, length, heads, width // heads)
    context = jnp.einsum("shqk,skhd->sqhd", probs, value_split, preferred_element_type=jnp.float32)
    return (
        context.reshape(items, length, width).astype(jnp.bfloat16),
        (top + jnp.log(total))[..., 0],
    )


def cluster_backward(scores, log_total, queries, keys_rows, values_rows, grad_context, heads):
    items, length, width = queries.shape
    size = width // heads
    query_split = queries.reshape(items, length, heads, size)
    key_split = keys_rows.reshape(items, length, heads, size)
    value_split = values_rows.reshape(items, length, heads, size)
    grad_split = grad_context.reshape(items, length, heads, size)
    probs = jnp.exp(scores - log_total[..., None])
    grad_probs = jnp.einsum(
        "sqhd,skhd->shqk", grad_split, value_split, preferred_element_type=jnp.float32
    )
    inner = jnp.sum(probs * grad_probs, axis=-1, keepdims=True)
    grad_scores = (probs * (grad_probs - inner)).astype(jnp.bfloat16)
    scale = size ** (-0.5)
    grad_query = (
        jnp.einsum("shqk,skhd->sqhd", grad_scores, key_split, preferred_element_type=jnp.float32)
        * scale
    )
    grad_key = (
        jnp.einsum("shqk,sqhd->skhd", grad_scores, query_split, preferred_element_type=jnp.float32)
        * scale
    )
    grad_value = jnp.einsum(
        "shqk,sqhd->skhd",
        probs.astype(jnp.bfloat16),
        grad_split,
        preferred_element_type=jnp.float32,
    )
    shape = (items, length, width)
    return (
        grad_query.reshape(shape).astype(jnp.bfloat16),
        grad_key.reshape(shape).astype(jnp.bfloat16),
        grad_value.reshape(shape).astype(jnp.bfloat16),
    )


def send_context(context):
    return lax.all_to_all(context, "seq", split_axis=1, concat_axis=1, tiled=True)


def send_grads(grads):
    return (
        lax.all_to_all(grads[0], "seq", split_axis=1, concat_axis=1, tiled=True),
        lax.all_to_all(grads[1], "seq", split_axis=1, concat_axis=1, tiled=True),
        lax.all_to_all(grads[2], "seq", split_axis=1, concat_axis=1, tiled=True),
    )


def make_step(left, pieces):
    total = jnp.dot(left, pieces[0], preferred_element_type=jnp.float32)
    stored = tuple(pieces[1:]) + ()
    placed = tuple((piece for piece in stored))
    return (total,) + placed


def make_hidden_step(before, pieces):
    section = before + pieces[1].astype(jnp.float32)
    activated = jax.nn.gelu(section, approximate=False).astype(jnp.bfloat16)
    total = jnp.dot(activated, pieces[0], preferred_element_type=jnp.float32)
    stored = ()
    return (total, section, activated) + stored


def per_device(
    tokens,
    attend_weight,
    query_bias,
    value_bias,
    output_weight,
    output_bias,
    first_gain,
    first_shift,
    expand_weight,
    expand_bias,
    reduce_weight,
    reduce_bias,
    second_gain,
    second_shift,
    query_rank,
    key_rank,
    cotangent,
):
    seqs, cluster, width = tokens.shape
    heads = query_rank.shape[1]
    rows = seqs * cluster
    owners = lax.axis_size("seq")
    flat = tokens.reshape(rows, width)
    attend_out = make_step(
        flat,
        (
            lax.all_gather(attend_weight, "batch", axis=0, tiled=True),
            lax.all_gather(query_bias, "batch", axis=0, tiled=True),
            lax.all_gather(value_bias, "batch", axis=0, tiled=True),
        ),
    )
    summed = attend_out[0]
    queries = (summed[:, :width] + attend_out[1].astype(jnp.float32)).astype(jnp.bfloat16)
    keys_rows = summed[:, width : 2 * width].astype(jnp.bfloat16)
    values_rows = (summed[:, 2 * width :] + attend_out[2].astype(jnp.float32)).astype(jnp.bfloat16)
    query_table = group_table(query_rank, cluster, owners)
    key_table = group_table(key_rank, cluster, owners)
    query_sorted = sort_heads(queries.reshape(seqs, cluster, width), query_table, heads)
    key_sorted = sort_heads(keys_rows.reshape(seqs, cluster, width), key_table, heads)
    value_sorted = sort_heads(values_rows.reshape(seqs, cluster, width), key_table, heads)
    received = (
        lax.all_to_all(query_sorted, "seq", split_axis=1, concat_axis=1, tiled=True),
        lax.all_to_all(key_sorted, "seq", split_axis=1, concat_axis=1, tiled=True),
        lax.all_to_all(value_sorted, "seq", split_axis=1, concat_axis=1, tiled=True),
    )
    context, log_total = cluster_forward(received[0], received[1], received[2], heads)
    forward_out = (send_context(context), log_total, received[0], received[1], received[2])
    context_rows = unsort_heads(forward_out[0], query_table, heads).reshape(rows, width)
    output_out = make_step(
        context_rows,
        (
            lax.all_gather(output_weight, "batch", axis=0, tiled=True),
            lax.all_gather(output_bias, "batch", axis=0, tiled=True),
            lax.all_gather(first_gain, "batch", axis=0, tiled=True),
            lax.all_gather(first_shift, "batch", axis=0, tiled=True),
        ),
    )
    resid_one = flat.astype(jnp.float32) + output_out[0] + output_out[1].astype(jnp.float32)
    gain_one = output_out[2].astype(jnp.float32)
    middle, normed_one, inverse_one = layer_norm(
        resid_one, gain_one, output_out[3].astype(jnp.float32)
    )
    middle_low = middle.astype(jnp.bfloat16)
    expand_out = make_step(
        middle_low,
        (
            lax.all_gather(expand_weight, "batch", axis=0, tiled=True),
            lax.all_gather(reduce_bias, "batch", axis=0, tiled=True),
            lax.all_gather(second_gain, "batch", axis=0, tiled=True),
            lax.all_gather(second_shift, "batch", axis=0, tiled=True),
        ),
    )
    hidden_out = make_hidden_step(
        expand_out[0],
        (
            lax.all_gather(reduce_weight, "batch", axis=0, tiled=True),
            lax.all_gather(expand_bias, "batch", axis=0, tiled=True),
        ),
    )
    pre_full, hidden_full = (hidden_out[1], hidden_out[2])
    resid_two = middle + hidden_out[0] + expand_out[1].astype(jnp.float32)
    gain_two = expand_out[2].astype(jnp.float32)
    final, normed_two, inverse_two = layer_norm(
        resid_two, gain_two, expand_out[3].astype(jnp.float32)
    )
    layer_out = final.astype(jnp.bfloat16).reshape(seqs, cluster, width)
    attend_full, output_full, expand_full, reduce_full = (
        lax.all_gather(attend_weight, "batch", axis=0, tiled=True),
        lax.all_gather(output_weight, "batch", axis=0, tiled=True),
        lax.all_gather(expand_weight, "batch", axis=0, tiled=True),
        lax.all_gather(reduce_weight, "batch", axis=0, tiled=True),
    )
    upstream = cotangent.reshape(rows, width).astype(jnp.float32)
    grad_second_gain = jnp.sum(upstream * normed_two, axis=0)
    grad_second_shift = jnp.sum(upstream, axis=0)
    grad_resid_two = norm_back(upstream, normed_two, inverse_two, gain_two)
    grad_branch_two = grad_resid_two.astype(jnp.bfloat16)
    grad_reduce_bias = jnp.sum(grad_branch_two, axis=0, dtype=jnp.float32)
    grad_reduce = transpose_left(hidden_full, grad_branch_two)
    grad_hidden = transpose_right(grad_branch_two, reduce_full)
    grad_pre = (grad_hidden * gelu_slope(pre_full)).astype(jnp.bfloat16)
    grad_expand_bias = jnp.sum(grad_pre, axis=0, dtype=jnp.float32)
    grad_expand = transpose_left(middle_low, grad_pre)
    grad_middle = grad_resid_two + transpose_right(grad_pre, expand_full)
    grad_first_gain = jnp.sum(grad_middle * normed_one, axis=0)
    grad_first_shift = jnp.sum(grad_middle, axis=0)
    grad_resid_one = norm_back(grad_middle, normed_one, inverse_one, gain_one)
    grad_branch_one = grad_resid_one.astype(jnp.bfloat16)
    grad_output_bias = jnp.sum(grad_branch_one, axis=0, dtype=jnp.float32)
    grad_output = transpose_left(context_rows, grad_branch_one)
    grad_context = transpose_right(grad_branch_one, output_full).astype(jnp.bfloat16)
    grad_sorted = sort_heads(grad_context.reshape(seqs, cluster, width), query_table, heads)
    grad_received = lax.all_to_all(grad_sorted, "seq", split_axis=1, concat_axis=1, tiled=True)
    kept_scores = cluster_scores(forward_out[2], forward_out[3], heads)
    home = send_grads(
        cluster_backward(
            kept_scores,
            forward_out[1],
            forward_out[2],
            forward_out[3],
            forward_out[4],
            grad_received,
            heads,
        )
    )
    grad_queries = unsort_heads(home[0], query_table, heads).reshape(rows, width)
    grad_keys = unsort_heads(home[1], key_table, heads).reshape(rows, width)
    grad_values = unsort_heads(home[2], key_table, heads).reshape(rows, width)
    grad_mixed = jnp.concatenate([grad_queries, grad_keys, grad_values], axis=1)
    grad_query_bias = jnp.sum(grad_queries, axis=0, dtype=jnp.float32)
    grad_value_bias = jnp.sum(grad_values, axis=0, dtype=jnp.float32)
    grad_attend = transpose_left(flat, grad_mixed)
    token_grad = (
        (grad_resid_one + transpose_right(grad_mixed, attend_full))
        .astype(jnp.bfloat16)
        .reshape(seqs, cluster, width)
    )
    owned = (
        lax.psum_scatter(
            grad_attend.astype(jnp.bfloat16), "batch", scatter_dimension=0, tiled=True
        ).astype(jnp.float32),
        lax.psum_scatter(
            grad_query_bias.astype(jnp.bfloat16), "batch", scatter_dimension=0, tiled=True
        ).astype(jnp.float32),
        lax.psum_scatter(
            grad_value_bias.astype(jnp.bfloat16), "batch", scatter_dimension=0, tiled=True
        ).astype(jnp.float32),
        lax.psum_scatter(
            grad_output.astype(jnp.bfloat16), "batch", scatter_dimension=0, tiled=True
        ).astype(jnp.float32),
        lax.psum_scatter(
            grad_output_bias.astype(jnp.bfloat16), "batch", scatter_dimension=0, tiled=True
        ).astype(jnp.float32),
        lax.psum_scatter(
            grad_first_gain.astype(jnp.bfloat16), "batch", scatter_dimension=0, tiled=True
        ).astype(jnp.float32),
        lax.psum_scatter(
            grad_first_shift.astype(jnp.bfloat16), "batch", scatter_dimension=0, tiled=True
        ).astype(jnp.float32),
        lax.psum_scatter(
            grad_expand.astype(jnp.bfloat16), "batch", scatter_dimension=0, tiled=True
        ).astype(jnp.float32),
        lax.psum_scatter(
            grad_expand_bias.astype(jnp.bfloat16), "batch", scatter_dimension=0, tiled=True
        ).astype(jnp.float32),
        lax.psum_scatter(
            grad_reduce.astype(jnp.bfloat16), "batch", scatter_dimension=0, tiled=True
        ).astype(jnp.float32),
        lax.psum_scatter(
            grad_reduce_bias.astype(jnp.bfloat16), "batch", scatter_dimension=0, tiled=True
        ).astype(jnp.float32),
        lax.psum_scatter(
            grad_second_gain.astype(jnp.bfloat16), "batch", scatter_dimension=0, tiled=True
        ).astype(jnp.float32),
        lax.psum_scatter(
            grad_second_shift.astype(jnp.bfloat16), "batch", scatter_dimension=0, tiled=True
        ).astype(jnp.float32),
    )
    shared = (
        lax.psum(owned[0].astype(jnp.bfloat16), "seq").astype(jnp.float32),
        lax.psum(owned[1].astype(jnp.bfloat16), "seq").astype(jnp.float32),
        lax.psum(owned[2].astype(jnp.bfloat16), "seq").astype(jnp.float32),
        lax.psum(owned[3].astype(jnp.bfloat16), "seq").astype(jnp.float32),
        lax.psum(owned[4].astype(jnp.bfloat16), "seq").astype(jnp.float32),
        lax.psum(owned[5].astype(jnp.bfloat16), "seq").astype(jnp.float32),
        lax.psum(owned[6].astype(jnp.bfloat16), "seq").astype(jnp.float32),
        lax.psum(owned[7].astype(jnp.bfloat16), "seq").astype(jnp.float32),
        lax.psum(owned[8].astype(jnp.bfloat16), "seq").astype(jnp.float32),
        lax.psum(owned[9].astype(jnp.bfloat16), "seq").astype(jnp.float32),
        lax.psum(owned[10].astype(jnp.bfloat16), "seq").astype(jnp.float32),
        lax.psum(owned[11].astype(jnp.bfloat16), "seq").astype(jnp.float32),
        lax.psum(owned[12].astype(jnp.bfloat16), "seq").astype(jnp.float32),
    )
    return (
        layer_out,
        token_grad,
        shared[0],
        shared[1],
        shared[2],
        shared[3],
        shared[4],
        shared[5],
        shared[6],
        shared[7],
        shared[8],
        shared[9],
        shared[10],
        shared[11],
        shared[12],
    )


MESH = pl.DeviceIdType.MESH
f32 = jnp.float32
bf16 = jnp.bfloat16


class Place:
    def __init__(self, chips, depth):
        self.chips, self.depth = chips, depth
        self.z = lax.axis_index("batch")
        spot = lax.axis_index("seq")
        self.chip, self.core = lax.div(spot, 2), lax.rem(spot, 2)

    def chip_at(self, k):
        return lax.rem(self.chip + k + self.chips, self.chips)

    def z_at(self, k):
        return lax.rem(self.z + k + self.depth, self.depth)

    def plane(self, k):
        return (self.z, self.chip_at(k) * 2 + self.core)

    def tower(self, k):
        return (self.z_at(k), self.chip * 2 + self.core)

    def sibling(self):
        return (self.z, self.chip * 2 + 1 - self.core)

    def greet(self):
        bell = pltpu.get_barrier_semaphore()
        others = [self.plane(k) for k in range(1, self.chips)]
        others += [self.tower(k) for k in range(1, self.depth)]
        others.append(self.sibling())
        for other in others:
            pl.semaphore_signal(bell, inc=1, device_id=other, device_id_type=MESH)
        pl.semaphore_wait(bell, len(others))


def far_copy(src, dst, sems, at, device):
    return pltpu.make_async_remote_copy(
        src_ref=src,
        dst_ref=dst,
        send_sem=sems[0].at[at],
        recv_sem=sems[1].at[at],
        device_id=device,
        device_id_type=MESH,
    )


def one_hot(row, slots):
    return jnp.where(slots == row, 1.0, 0.0).astype(bf16)


def split_lanes(tile, low):
    zero = jnp.zeros_like(tile)
    return jnp.where(low, tile, zero), jnp.where(low, zero, tile)


def stack_lanes(tile, low):
    first, second = split_lanes(tile, low)
    return jnp.concatenate([first, second], axis=0)


def dot_rows(a, b):
    return jnp.dot(a, b, preferred_element_type=f32)


def dot_lanes(a, b):
    return lax.dot_general(a, b, (((1,), (1,)), ((), ())), preferred_element_type=f32)


def dot_first(a, b):
    return lax.dot_general(a, b, (((0,), (0,)), ((), ())), preferred_element_type=f32)


def multiple(value, by):
    return pl.multiple_of(value, by)


def forward_kernel(
    chips,
    depth,
    heads,
    tok_ref,
    pos_ref,
    aw_ref,
    vec_ref,
    ow_ref,
    ew_ref,
    rw_ref,
    cot_ref,
    x_out,
    ctx_out,
    q_out,
    k_out,
    v_out,
    p_out,
    pos_out,
    aw_out,
    vec_out,
    ow_out,
    ew_out,
    rw_out,
    n1_out,
    inv_out,
    ml_out,
    hid_out,
    slope_out,
    lo_out,
    gb_out,
    sum_out,
    xbuf,
    posbuf,
    wbuf,
    vbuf,
    bias,
    ctxb,
    ctxt,
    owbuf,
    ewbuf,
    rwbuf,
    cbuf,
    n1buf,
    invbuf,
    mlbuf,
    vecs,
    upb,
    sums,
    tok_s,
    tok_r,
    tokc_s,
    tokc_r,
    pos_s,
    pos_r,
    posc_s,
    posc_r,
    up_s,
    up_r,
    dn_s,
    dn_r,
    awc_s,
    awc_r,
    vec_s,
    vec_r,
    wz_s,
    wz_r,
    wp_s,
    wp_r,
    wd_s,
    wd_r,
    wc_s,
    wc_r,
    ctx_s,
    ctx_r,
    cot_s,
    cot_r,
    oc_s,
    oc_r,
    loc,
    out_sem,
    slope_sem,
    att_sem,
    late_sem,
):
    me = Place(chips, depth)
    z, chip, core = me.z, me.chip, me.core
    per = tok_ref.shape[0] // chips
    half = aw_ref.shape[1] // 6
    rows_z = aw_ref.shape[0]
    pairs = heads // 4
    size = half // (2 * pairs)
    me.greet()

    def aw_block(zz):
        return wbuf.at[pl.ds(multiple(zz * rows_z, 8), rows_z)]

    def up_copy(h):
        return far_copy(
            aw_block(z - h), aw_block(z - h), (up_s, up_r), h, (z + 1, chip * 2 + core)
        )

    def down_copy(h):
        return far_copy(
            aw_block(z + h), aw_block(z + h), (dn_s, dn_r), h, (z - 1, chip * 2 + core)
        )

    def up_got(h):
        return far_copy(
            aw_block(z - 1 - h), aw_block(z - 1 - h), (up_s, up_r), h, me.sibling()
        )

    def down_got(h):
        return far_copy(
            aw_block(z + 1 + h), aw_block(z + 1 + h), (dn_s, dn_r), h, me.sibling()
        )

    def pass_on():
        @pl.when(z < depth - 1)
        def _():
            up_copy(0).start()

        @pl.when(z > 0)
        def _():
            down_copy(0).start()

    def pass_rest(hops):
        for h in hops:

            @pl.when(z > h)
            def _():
                up_got(h).wait_recv()
                if h + 1 < depth - 1:

                    @pl.when(z < depth - 1)
                    def _():
                        up_copy(h + 1).start()

            @pl.when(z + 1 + h < depth)
            def _():
                down_got(h).wait_recv()
                if h + 1 < depth - 1:

                    @pl.when(z > 0)
                    def _():
                        down_copy(h + 1).start()

    def pass_end():
        for h in range(depth - 1):

            @pl.when((z >= h) & (z < depth - 1))
            def _():
                up_copy(h).wait_send()

            @pl.when((z + h < depth) & (z > 0))
            def _():
                down_copy(h).wait_send()

    def mine(ref, target):
        return ref.at[pl.ds(target * per, per)]

    def tok_copy(k):
        return far_copy(
            mine(tok_ref, me.chip_at(k)), xbuf.at[core, chip], (tok_s, tok_r), k - 1, me.plane(k)
        )

    def pos_copy(k):
        return far_copy(
            mine(pos_ref, me.chip_at(k)), posbuf.at[core, chip], (pos_s, pos_r), k - 1, me.plane(k)
        )

    def vec_copy(k):
        return far_copy(vec_ref, vbuf.at[z], (vec_s, vec_r), k - 1, me.tower(k))

    sends = []
    for k in range(1, chips):
        sends.append(pos_copy(k))
        sends[-1].start()
    for k in range(1, depth):
        sends.append(vec_copy(k))
        sends[-1].start()
    for k in range(1, chips):
        sends.append(tok_copy(k))
        sends[-1].start()
    local = []

    def keep(src, dst):
        copy = pltpu.make_async_copy(src, dst, loc.at[len(local)])
        copy.start()
        local.append(copy)

    for part in range(3):
        keep(
            aw_ref.at[:, pl.ds(multiple(part * 2 * half + core * half, 128), half)],
            wbuf.at[pl.ds(multiple(z * rows_z, 8), rows_z), pl.ds(part * half, half)],
        )
    keep(mine(tok_ref, chip), xbuf.at[core, chip])
    keep(mine(pos_ref, chip), posbuf.at[core, chip])
    keep(vec_ref, vbuf.at[z])
    for copy in local[:3]:
        copy.wait()
    pass_on()
    wide = ew_ref.shape[1] // (2 * chips)
    tall = rw_ref.shape[0] // (2 * chips)
    mid_rows = rows_z // 2
    mine_at = core * chips + chip

    def piece(kind):
        if kind == 0:
            return ow_ref.at[pl.ds(multiple(core * mid_rows, 8), mid_rows)]
        if kind == 1:
            return ew_ref.at[:, pl.ds(multiple(mine_at * wide, 128), wide)]
        return rw_ref.at[pl.ds(multiple(mine_at * tall, 8), tall)]

    def place(kind, zz):
        if kind == 0:
            return owbuf.at[zz, core]
        if kind == 1:
            return ewbuf.at[zz, :, pl.ds(multiple(mine_at * wide, 128), wide)]
        return rwbuf.at[zz, mine_at]

    def place_all(kind, at):
        if kind == 1:
            return ewbuf.at[:, :, pl.ds(multiple(at * wide, 128), wide)]
        return rwbuf.at[:, at]

    for kind in range(3):
        keep(piece(kind), place(kind, z))

    def wz_copy(kind, k):
        return far_copy(
            piece(kind),
            place(kind, z),
            (wz_s, wz_r),
            kind * (depth - 1) + k - 1,
            me.tower(k),
        )

    beside = (chip + 1 - 2 * lax.rem(chip, 2), lax.rem(chip + 2, chips))
    across = chips - 1 - chip

    def part_of(kind, origin, side):
        at = core * chips + origin
        span = pl.ds(side * (depth // 2), depth // 2)
        if kind == 1:
            return ewbuf.at[span, :, pl.ds(multiple(at * wide, 128), wide)]
        return rwbuf.at[span, at]

    def wp_copy(kind, d):
        spot = place_all(kind, mine_at)
        return far_copy(
            spot, spot, (wp_s, wp_r), (kind - 1) * 2 + d, (z, beside[d] * 2 + core)
        )

    def wd_copy(kind, d):
        spot = part_of(kind, beside[d], d)
        return far_copy(
            spot, spot, (wd_s, wd_r), (kind - 1) * 2 + d, (z, beside[1 - d] * 2 + core)
        )

    def wc_copy(kind, n):
        at = core * chips + (chip, beside[0], beside[1], across)[n]
        return far_copy(
            place_all(kind, at),
            place_all(kind, at),
            (wc_s, wc_r),
            (kind - 1) * chips + n,
            me.sibling(),
        )

    def tower_wait(kind):
        for k in range(1, depth):
            wz_copy(kind, k).wait_recv()

    def plane_first(kind):
        for d in range(2):
            wp_copy(kind, d).start()
        wc_copy(kind, 0).start()

    def plane_second(kind):
        for d in range(2):
            wp_copy(kind, d).wait_recv()
            wd_copy(kind, d).start()
            wc_copy(kind, 1 + d).start()

    def plane_last(kind):
        for d in range(2):
            wd_copy(kind, d).wait_recv()
        wc_copy(kind, 3).start()
        for n in range(chips):
            wc_copy(kind, n).wait()
        for d in range(2):
            wp_copy(kind, d).wait_send()
            wd_copy(kind, d).wait_send()

    def oc_copy():
        spot = owbuf.at[:, core]
        return far_copy(spot, spot, (oc_s, oc_r), 0, me.sibling())

    def cot_copy(n):
        target = (beside[0], beside[1], across)[n]
        return far_copy(
            mine(cot_ref, target),
            cbuf.at[chip],
            (cot_s, cot_r),
            n,
            (z, target * 2 + core),
        )

    keep(mine(cot_ref, chip), cbuf.at[chip])

    for copy in local[3:5]:
        copy.wait()

    def tokc_copy(k):
        source = me.chip_at(-k)
        return far_copy(
            xbuf.at[core, source], xbuf.at[core, source], (tokc_s, tokc_r), k, me.sibling()
        )

    def posc_copy(k):
        source = me.chip_at(-k)
        return far_copy(
            posbuf.at[core, source], posbuf.at[core, source], (posc_s, posc_r), k, me.sibling()
        )

    for k in range(1, depth):
        wz_copy(1, k).start()
        for kind in range(3):
            sends.append(wz_copy(kind, k))
    pass_rest(range(depth - 2))
    for k in range(chips):
        if k:
            pos_copy(k).wait_recv()
            tok_copy(k).wait_recv()
        for copy in (posc_copy(k), tokc_copy(k)):
            copy.start()
            sends.append(copy)
    for copy in local[5:]:
        copy.wait()
    tower_wait(1)
    plane_first(1)
    pass_rest(range(depth - 2, depth - 1))
    for k in range(1, depth):
        wz_copy(2, k).start()
    plane_second(1)
    for n in range(2):
        cot_copy(n).start()
    for k in range(1, depth):
        vec_copy(k).wait_recv()
    for k in range(chips):
        posc_copy(k).wait_recv()
        tokc_copy(k).wait_recv()

    outs = []

    def emit(src, dst):
        copy = pltpu.make_async_copy(src, dst, out_sem.at[len(outs)])
        copy.start()
        outs.append(copy)

    emit(xbuf, x_out)
    emit(posbuf, pos_out)
    emit(wbuf, aw_out.at[core])
    awc = far_copy(wbuf, aw_out.at[core], (awc_s, awc_r), 0, me.sibling())
    awc.start()
    sends.append(awc)

    quarter = rows_z
    for zz in range(depth):
        begin = zz * quarter
        for row, at in ((0, 0), (1, 2)):
            for side in range(2):
                lo = max(begin, side * half)
                hi = min(begin + quarter, (side + 1) * half)
                if lo < hi:
                    bias[side, 0:1, at * half + lo - side * half : at * half + hi - side * half] = (
                        vbuf[zz, row : row + 1, lo - begin : hi - begin]
                    )
    bias[0, 0:1, half : 2 * half] = jnp.zeros((1, half), f32)
    bias[1, 0:1, half : 2 * half] = jnp.zeros((1, half), f32)
    added = bias[core, 0:1, :]
    for zz in range(depth):
        for row in range(8):
            vecs[row : row + 1, zz * quarter : (zz + 1) * quarter] = vbuf[
                zz, row : row + 1, :quarter
            ]
        steps = upb.shape[1] // (depth * quarter)
        for row in range(steps):
            to = (zz * steps + row) * quarter
            upb[0:1, to : to + quarter] = vbuf[zz, 8 + row : 9 + row, :quarter]

    cluster = tok_ref.shape[1]
    blocks = 2 * chips
    share = cluster // blocks
    width = tok_ref.shape[2]

    slots = lax.broadcasted_iota(jnp.int32, (cluster, cluster), 0)
    low = lax.broadcasted_iota(jnp.int32, (cluster, 128), 1) < size
    scale = size ** (-0.5)

    def tables(jj, i, pair, part):
        first = part * heads + core * (heads // 2) + 2 * pair
        rows = [
            one_hot(posbuf[jj // chips, jj % chips, i, pl.ds(first + h, 1), :], slots)
            for h in range(2)
        ]
        return rows

    def hook(i, pair):
        step = i * pairs + pair
        last = per * pairs - 1

        @pl.when(step == min(2, last))
        def _():
            tower_wait(2)
            plane_first(2)
            for k in range(1, depth):
                wz_copy(0, k).start()

        @pl.when(step == last)
        def _():
            plane_second(2)

    def attention(qkv, qs, ks, vs, ps, os):
        def group_copies(i):
            span = pl.ds(i * pairs, pairs)
            pieces = ((qs, q_out), (ks, k_out), (vs, v_out), (ps, p_out))
            return [
                pltpu.make_async_copy(src.at[span], dst.at[span], att_sem.at[5 + 4 * i + n])
                for n, (src, dst) in enumerate(pieces)
            ]

        @pl.loop(0, blocks)
        def _(jj):
            x = xbuf[lax.div(jj, chips), lax.rem(jj, chips)].reshape(per * cluster, width)
            mixed = (dot_rows(x, wbuf[...]) + added).astype(bf16)
            for at in range(3 * pairs):
                qkv[at, jj] = mixed[:, at * 128 : (at + 1) * 128].reshape(per, cluster, 128)

        @pl.loop(0, per)
        def _(i):
            @pl.loop(0, pairs)
            def _(pair):
                at = i * pairs + pair
                for jj in range(blocks):
                    tq = jnp.concatenate(tables(jj, i, pair, 0), axis=1)
                    tk = jnp.concatenate(tables(jj, i, pair, 1), axis=1)
                    q = stack_lanes(qkv[pair, jj, i], low)
                    k = stack_lanes(qkv[pairs + pair, jj, i], low)
                    v = stack_lanes(qkv[2 * pairs + pair, jj, i], low)
                    span = slice(jj * share, (jj + 1) * share)
                    sq = dot_rows(tq, q).astype(bf16)
                    skv = dot_rows(tk, jnp.concatenate([k, v], axis=1)).astype(bf16)
                    qs[at, :, span, :] = sq.reshape(blocks, share, 128)
                    ks[at, :, span, :] = skv[:, :128].reshape(blocks, share, 128)
                    vs[at, :, span, :] = skv[:, 128:].reshape(blocks, share, 128)
                for c in range(blocks):
                    scores = dot_lanes(qs[at, c], stack_lanes(ks[at, c], low)) * scale
                    halves = []
                    for h in range(2):
                        s = scores[:, h * cluster : (h + 1) * cluster]
                        e = jnp.exp(s - jnp.max(s, axis=1, keepdims=True))
                        halves.append((e / jnp.sum(e, axis=1, keepdims=True)).astype(bf16))
                    probs = jnp.concatenate(halves, axis=1)
                    ps[at, c] = probs
                    o = dot_rows(probs, stack_lanes(vs[at, c], low)).astype(bf16)
                    os[c] = o
                for jj in range(blocks):
                    tq = jnp.concatenate(tables(jj, i, pair, 0), axis=0)
                    rows = os[:, jj * share : (jj + 1) * share, :].reshape(cluster, 128)
                    back = dot_first(tq, stack_lanes(rows, low)).astype(bf16)
                    ctxb[jj // chips, jj % chips, i, :, pl.ds(multiple(pair * 128, 128), 128)] = back
                hook(i, pair)

                @pl.when(pair == pairs - 1)
                def _():
                    for copy in group_copies(i):
                        copy.start()


        far, own = ctx_copies()
        for copy in (far, own):
            copy.start()
        for copy in (far, own):
            copy.wait()
        for i in range(per):
            for copy in group_copies(i):
                copy.wait()

    def ctx_copies():
        lanes = pl.ds(multiple(core * half, 128), half)
        far = far_copy(
            ctxb.at[1 - core], ctxt.at[:, :, :, lanes], (ctx_s, ctx_r), 0, me.sibling()
        )
        own = pltpu.make_async_copy(ctxb.at[core], ctxt.at[:, :, :, lanes], att_sem.at[4])
        return far, own

    group = (per * pairs, blocks, cluster, 128)
    pl.run_scoped(
        attention,
        pltpu.VMEM((3 * pairs, blocks, per, cluster, 128), bf16),
        pltpu.VMEM(group, bf16),
        pltpu.VMEM(group, bf16),
        pltpu.VMEM(group, bf16),
        pltpu.VMEM((per * pairs, blocks, cluster, 2 * cluster), bf16),
        pltpu.VMEM((blocks, cluster, 128), bf16),
    )

    tower_wait(0)
    oc_copy().start()
    oc_copy().wait()
    emit(ctxt, ctx_out)
    context_out = outs[-1]
    emit(owbuf, ow_out)
    tile = per * cluster
    hidden = upb.shape[1]
    eps = epsilon

    def moments(rows):
        center = jnp.mean(rows, axis=1, keepdims=True)
        centered = rows - center
        spread = jnp.mean(centered * centered, axis=1, keepdims=True)
        inverse = lax.rsqrt(spread + eps)
        return centered * inverse, inverse

    def slope_out_copy(j, slot):
        return pltpu.make_async_copy(sbuf.at[slot], slope_out.at[j], slope_sem.at[slot])

    def vec(row):
        return vecs[row : row + 1, :]

    def feed(hbuf, sbuf):
        step = sbuf.shape[3]

        def late_copies(j):
            pieces = ((cbuf, lo_out), (ctxt, gb_out))
            return [
                pltpu.make_async_copy(src.at[j], dst.at[j], late_sem.at[2 * j + n])
                for n, (src, dst) in enumerate(pieces)
            ]

        def slope_copy(n):
            return pltpu.make_async_copy(
                sbuf.at[n % 2],
                slope_out.at[:, :, pl.ds(n * step, step)],
                slope_sem.at[n % 2],
            )

        @pl.loop(0, chips)
        def _(j):
            rows = ctxt[j].reshape(tile, width)
            branch = dot_rows(rows, owbuf[...].reshape(width, width))
            resid = xbuf[core, j].reshape(tile, width).astype(f32) + branch + vec(2)
            normed, inverse = moments(resid)
            n1buf[j] = normed
            invbuf[j] = jnp.broadcast_to(inverse, (tile, 128))
            mlbuf[j] = (normed * vec(3) + vec(4)).astype(bf16).reshape(per, cluster, width)

        cot_copy(2).start()
        plane_last(1)
        emit(ewbuf, ew_out)
        for n in range(hidden // step):
            lanes = slice(n * step, (n + 1) * step)
            if n >= 2:
                slope_copy(n - 2).wait()
            for j in range(chips):
                weight = ewbuf[:, :, lanes].reshape(width, step)
                pre = dot_rows(mlbuf[j].reshape(tile, width), weight) + upb[0:1, lanes]
                cumulative = 0.5 * (1.0 + lax.erf(pre * 0.5**0.5))
                density = jnp.exp(-0.5 * pre * pre) * (2.0 * math.pi) ** (-0.5)
                hbuf[j, :, lanes] = (pre * cumulative).astype(bf16)
                sbuf[n % 2, j] = (cumulative + pre * density).astype(bf16)
            slope_copy(n).start()

        emit(vecs, vec_out)
        emit(n1buf, n1_out)
        emit(invbuf, inv_out)
        emit(mlbuf, ml_out)
        emit(hbuf, hid_out)
        plane_last(2)
        pass_end()
        emit(rwbuf, rw_out)
        for n in range(2):
            cot_copy(n).wait()
        sums[...] = jnp.zeros_like(sums)
        waited = (context_out,)
        for copy in waited:
            copy.wait()

        @pl.loop(0, chips)
        def _(n):
            j = 2 * lax.rem(lax.div(chip, 2) + lax.div(n, 2), 2)
            j = j + lax.rem(chip + n, 2)

            @pl.when(n == chips - 1)
            def _():
                cot_copy(2).wait()

            branch = vec(5)
            for zz in range(depth):
                span = hidden // depth
                branch = branch + dot_rows(
                    hbuf[j, :, zz * span : (zz + 1) * span], rwbuf[zz].reshape(span, width)
                )
            middle = n1buf[j] * vec(3) + vec(4)
            normed, inverse = moments(middle + branch)
            upstream = cbuf[j].reshape(tile, width).astype(f32)
            cbuf[j] = (normed * vec(6) + vec(7)).astype(bf16).reshape(per, cluster, width)
            sums[0:1, :] += jnp.sum(upstream * normed, axis=0, keepdims=True)
            sums[1:2, :] += jnp.sum(upstream, axis=0, keepdims=True)
            scaled = upstream * vec(6)
            first = jnp.mean(scaled, axis=1, keepdims=True)
            second = jnp.mean(scaled * normed, axis=1, keepdims=True)
            grad = inverse * (scaled - first - normed * second)
            low_grad = grad.astype(bf16)
            sums[2:3, :] += jnp.sum(low_grad.astype(f32), axis=0, keepdims=True)
            ctxt[j] = low_grad.reshape(per, cluster, width)
            for copy in late_copies(j):
                copy.start()

        emit(sums, sum_out)
        for j in range(chips):
            for copy in late_copies(j):
                copy.wait()
        for copy in sends:
            copy.wait_send()
        awc.wait_recv()
        for n in range(max(hidden // step - 2, 0), hidden // step):
            slope_copy(n).wait()
        for copy in outs:
            if not any(copy is other for other in waited):
                copy.wait()

    pl.run_scoped(
        feed,
        pltpu.VMEM((chips, tile, hidden), bf16),
        pltpu.VMEM((2, chips, tile, hidden // depth), bf16),
    )


def forward(
    tokens,
    pos,
    attend_weight,
    vectors,
    output_weight,
    expand_weight,
    reduce_weight,
    cotangent,
    chips,
    depth,
    heads,
):
    seqs, cluster, width = tokens.shape
    per, blocks, pairs = seqs // chips, 2 * chips, heads // 4
    half = width // 2
    rows_z = attend_weight.shape[0]
    hidden = expand_weight.shape[1]
    items = per * pairs
    tile = per * cluster
    dma = pltpu.SemaphoreType.DMA
    anywhere = pl.BlockSpec(memory_space=pl.ANY)
    tall = reduce_weight.shape[0] // blocks
    shapes = [
        ((2, chips, per, cluster, width), bf16),
        ((chips, per, cluster, width), bf16),
        ((items, blocks, cluster, 128), bf16),
        ((items, blocks, cluster, 128), bf16),
        ((items, blocks, cluster, 128), bf16),
        ((items, blocks, cluster, 2 * cluster), bf16),
        ((2, chips, per, 2 * heads, cluster), jnp.int32),
        ((2, depth * rows_z, 3 * half), bf16),
        ((8, width), f32),
        ((depth, 2, rows_z // 2, width), bf16),
        ((depth, rows_z, hidden), bf16),
        ((depth, blocks, tall, width), bf16),
        ((chips, tile, width), f32),
        ((chips, tile, 128), f32),
        ((chips, per, cluster, width), bf16),
        ((chips, tile, hidden), bf16),
        ((chips, tile, hidden), bf16),
        ((chips, per, cluster, width), bf16),
        ((chips, per, cluster, width), bf16),
        ((8, width), f32),
    ]
    t, c = depth - 1, chips - 1
    vm = pltpu.VMEM
    return pl.pallas_call(
        functools.partial(forward_kernel, chips, depth, heads),
        out_shape=[jax.ShapeDtypeStruct(*s) for s in shapes],
        in_specs=[anywhere] * 8,
        out_specs=[anywhere] * len(shapes),
        scratch_shapes=[
            vm(shapes[0][0], bf16),
            vm(shapes[6][0], jnp.int32),
            vm(shapes[7][0][1:], bf16),
            vm((depth,) + vectors.shape, f32),
            vm((2, 8, 3 * half), f32),
            vm((2, chips, per, cluster, half), bf16),
            vm(shapes[1][0], bf16),
            vm(shapes[9][0], bf16),
            vm(shapes[10][0], bf16),
            vm(shapes[11][0], bf16),
            vm(shapes[17][0], bf16),
            vm(shapes[12][0], f32),
            vm(shapes[13][0], f32),
            vm(shapes[14][0], bf16),
            vm((8, width), f32),
            vm((8, hidden), f32),
            vm((8, width), f32),
            dma((c,)), dma((c,)), dma((chips,)), dma((chips,)),
            dma((c,)), dma((c,)), dma((chips,)), dma((chips,)),
            dma((t,)), dma((t,)), dma((t,)), dma((t,)), dma((1,)), dma((1,)),
            dma((t,)), dma((t,)),
            dma((3 * t,)), dma((3 * t,)),
            dma((4,)), dma((4,)), dma((4,)), dma((4,)),
            dma((2 * chips,)), dma((2 * chips,)),
            dma((1,)), dma((1,)),
            dma((c,)), dma((c,)),
            dma((1,)), dma((1,)),
            dma((12,)), dma((24,)), dma((2,)), dma((5 + 4 * per,)), dma((2 * chips,)),
        ],
        compiler_params=pltpu.CompilerParams(
            collective_id=1, has_side_effects=True, vmem_limit_bytes=63 * 2**20
        ),
        name="forward",
    )(
        tokens,
        pos,
        attend_weight,
        vectors,
        output_weight,
        expand_weight,
        reduce_weight,
        cotangent,
    )


def add_into(target, at, parts):
    total = target[at].astype(f32)
    for part in parts:
        total = total + part.astype(f32)
    target[at] = total.astype(target.dtype)


class Reducer:
    def __init__(self, me, own, other, near, mid, last, done, sems, tower_first):
        self.me, self.own, self.other = me, own, other
        self.near, self.mid, self.last, self.done = near, mid, last, done
        (self.near_s, self.near_r, self.mid_s, self.mid_r, self.last_s, self.last_r) = sems[:6]
        (self.back_s, self.back_r, self.side_s, self.side_r) = sems[6:10]
        self.tower_first = tower_first
        self.sizes = (mid.shape[0] + 1, last.shape[0] + 1)

    def spot(self, axis, k):
        me = self.me
        if self.tower_first == (axis == 0):
            return me.z_at(k), me.tower(k)
        return me.chip_at(k), me.plane(k)

    def near_copy(self, a):
        return far_copy(
            self.other.at[a], self.near.at[a], (self.near_s, self.near_r), a, self.me.sibling()
        )

    def fold_near(self, a):
        self.near_copy(a).wait_recv()
        for b in range(self.sizes[1]):
            add_into(self.own, (a, b), [self.near[a, b]])

    def mid_copy(self, k):
        where, device = self.spot(0, k)
        return far_copy(
            self.own.at[where], self.mid.at[k - 1], (self.mid_s, self.mid_r), k - 1, device
        )

    def send_mid(self):
        for k in range(1, self.sizes[0]):
            self.mid_copy(k).start()

    def fold_mid(self):
        for k in range(1, self.sizes[0]):
            self.mid_copy(k).wait()
        here = self.spot(0, 0)[0]
        for b in range(self.sizes[1]):
            add_into(self.own, (here, b), [self.mid[k - 1, b] for k in range(1, self.sizes[0])])

    def last_copy(self, k):
        here = self.spot(0, 0)[0]
        where, device = self.spot(1, k)
        return far_copy(
            self.own.at[here, where],
            self.last.at[k - 1],
            (self.last_s, self.last_r),
            k - 1,
            device,
        )

    def send_last(self):
        for k in range(1, self.sizes[1]):
            self.last_copy(k).start()

    def fold_last(self):
        me = self.me
        for k in range(1, self.sizes[1]):
            self.last_copy(k).wait()
        total = self.own[self.spot(0, 0)[0], self.spot(1, 0)[0]].astype(f32)
        for k in range(1, self.sizes[1]):
            total = total + self.last[k - 1].astype(f32)
        self.done[me.core, me.chip] = total.astype(bf16)

    def back_copy(self, k):
        me = self.me
        spot = self.done.at[me.core, me.chip]
        return far_copy(spot, spot, (self.back_s, self.back_r), k - 1, me.plane(k))

    def send_back(self):
        for k in range(1, self.done.shape[1]):
            self.back_copy(k).start()

    def side_copy(self):
        spot = self.done.at[self.me.core]
        return far_copy(spot, spot, (self.side_s, self.side_r), 0, self.me.sibling())

    def send_side(self):
        for k in range(1, self.done.shape[1]):
            self.back_copy(k).wait()
        self.side_copy().start()

    def finish(self):
        self.side_copy().wait()


class Sum:
    def __init__(self, me, vec, got, s, r):
        self.me, self.vec, self.got, self.s, self.r = me, vec, got, s, r

    def copies(self, hop):
        me = self.me
        if hop == 0:
            spots = [(0, me.sibling())]
        elif hop == 1:
            spots = [(k, me.plane(k)) for k in range(1, me.chips)]
        else:
            spots = [(me.chips + k - 1, me.tower(k)) for k in range(1, me.depth)]
        return [far_copy(self.vec, self.got.at[n], (self.s, self.r), n, d) for n, d in spots], spots

    def send(self, hop):
        for copy in self.copies(hop)[0]:
            copy.start()

    def fold(self, hop):
        copies, spots = self.copies(hop)
        for copy in copies:
            copy.wait()
        total = self.vec[...]
        for n, _ in spots:
            total = total + self.got[n]
        self.vec[...] = total


def back_kernel(
    chips,
    depth,
    heads,
    q_ref,
    k_ref,
    v_ref,
    p_ref,
    pos_ref,
    x_ref,
    aw_ref,
    ow_ref,
    ew_ref,
    rw_ref,
    vec_ref,
    ctx_ref,
    n1_ref,
    inv_ref,
    ml_ref,
    hid_ref,
    slope_ref,
    lo_ref,
    gb_ref,
    late_ref,
    token_out,
    layer_out,
    aw_out,
    ow_out,
    ew_out,
    rw_out,
    vec_out,
    bias_out,
    dbuf,
    posbuf,
    acc,
    gfar,
    p_mid,
    p_last,
    p_done,
    o_all,
    o_near,
    o_mid,
    o_last,
    o_done,
    e_all,
    e_near,
    e_mid,
    e_last,
    e_done,
    r_all,
    r_near,
    r_mid,
    r_last,
    r_done,
    vbuf,
    vgot,
    bbuf,
    bgot,
    vecs,
    d_s,
    d_r,
    g_s,
    g_r,
    t_s,
    t_r,
    lo_s,
    lo_r,
    load,
    out_sem,
    v_s,
    v_r,
    b_s,
    b_r,
    *sems,
):
    me = Place(chips, depth)
    z, core, chip = me.z, me.core, me.chip
    per, cluster, width = lo_ref.shape[1:]
    half = width // 2
    pairs = heads // 4
    size = half // (2 * pairs)
    blocks = 2 * chips
    share = cluster // blocks
    tile = per * cluster
    hidden = hid_ref.shape[2]
    wide = hidden // blocks
    strip = width // chips
    quarter = width // depth
    eighth = quarter // blocks
    rows = chips * tile
    me.greet()
    groups = [sems[n * 10 : (n + 1) * 10] for n in range(3 + heads // 4)]
    red = Reducer(
        me, r_all.at[core], r_all.at[1 - core], r_near, r_mid, r_last, r_done, groups[0], True
    )
    exp = Reducer(
        me, e_all.at[core], e_all.at[1 - core], e_near, e_mid, e_last, e_done, groups[1], False
    )
    out = Reducer(
        me, o_all.at[core], o_all.at[1 - core], o_near, o_mid, o_last, o_done, groups[2], False
    )
    sums = Sum(me, vbuf, vgot, v_s, v_r)
    biases = Sum(me, bbuf, bgot, b_s, b_r)

    def fetch(src, dst, at):
        return pltpu.make_async_copy(src, dst, load.at[at])

    def lo_copy(k):
        return far_copy(
            lo_ref.at[me.chip_at(k)],
            layer_out.at[pl.ds(chip * per, per)],
            (lo_s, lo_r),
            k - 1,
            me.plane(k),
        )

    lo_keep = pltpu.make_async_copy(
        lo_ref.at[chip], layer_out.at[pl.ds(chip * per, per)], out_sem.at[0]
    )

    block = 2 * wide
    counts = blocks // 2

    def order(n):
        return lax.rem(n + z + chip, counts)

    def fold_red(n):
        at = order(n)
        red.fold_near(at)
        k = lax.rem(at - z + depth, depth)

        @pl.when(k != 0)
        def _():
            red.mid_copy(k).start()

    def fold_exp(n):
        at = order(n)

        @pl.when(lax.div(at, 2) == core)
        def _():
            for side in range(2):
                b = lax.rem(at, 2) * 2 + side
                exp.fold_near(b)
                k = lax.rem(b - chip + chips, chips)

                @pl.when(k != 0)
                def _():
                    exp.mid_copy(k).start()

    def chunks(gb, gbt, mlt, hid, slope, rwc, ewc, gpb):
        def chunk(n, slot):
            at = order(n)
            lanes = pl.ds(multiple(at * block, 128), block)
            return [
                fetch(hid_ref.at[:, :, lanes], hid.at[slot], slot * 4),
                fetch(slope_ref.at[:, :, lanes], slope.at[slot], slot * 4 + 1),
                fetch(rw_ref.at[at], rwc.at[slot], slot * 4 + 2),
                fetch(ew_ref.at[:, :, lanes], ewc.at[slot], slot * 4 + 3),
            ]

        begin = [
            fetch(gb_ref, gb, 8),
            fetch(ml_ref, gpb, 9),
        ]
        later = [
            fetch(vec_ref, vecs, 11),
            fetch(late_ref, vbuf.at[pl.ds(0, 8)], 12),
            fetch(pos_ref, posbuf, 18),
        ]
        for copy in begin[:1] + chunk(0, 0) + begin[1:] + later:
            copy.start()
        for k in range(1, chips):
            lo_copy(k).start()
        lo_keep.start()
        vbuf[8:, :] = jnp.zeros((blocks, width), f32)
        begin[0].wait()
        for j in range(chips):
            gbt[:, j * tile : (j + 1) * tile] = jnp.transpose(gb[j].reshape(tile, width))

        def settle():
            for copy in begin[1:] + later:
                copy.wait()
            for j in range(chips):
                mlt[:, j * tile : (j + 1) * tile] = jnp.transpose(gpb[j].reshape(tile, width))
                acc[j] = gb[j].reshape(tile, width).astype(f32)

        @pl.loop(0, counts)
        def _(n):
            slot = lax.rem(n, 2)
            at = order(n)
            for copy in chunk(n, slot):
                copy.wait()

            @pl.when(n + 1 < counts)
            def _():
                for copy in chunk(n + 1, 1 - slot):
                    copy.start()

            term = dot_rows(gbt[...], hid[slot].reshape(rows, block)).astype(bf16)
            for side in range(2):
                r_all[side, at] = term[:, side * wide : (side + 1) * wide].reshape(
                    chips, strip, wide
                )
            red.near_copy(at).start()

            @pl.when(n == 0)
            def _():
                settle()

            @pl.when(n > 0)
            def _():
                fold_exp(n - 1)

            up = rwc[slot].reshape(block, width)
            down = ewc[slot].reshape(width, block)
            total = jnp.zeros((1, block), f32)
            for j in range(chips):
                grad = dot_lanes(gb[j].reshape(tile, width), up)
                low = (grad * slope[slot, j].astype(f32)).astype(bf16)
                gpb[j] = low.reshape(per, cluster, block)
                acc[j] += dot_lanes(low, down)
                total = total + jnp.sum(low.astype(f32), axis=0, keepdims=True)
            vbuf[pl.ds(8 + at, 1), :block] = total
            fold_red(n)
            term = dot_rows(mlt[...], gpb[...].reshape(rows, block)).astype(bf16)
            for side in range(2):
                e_all[lax.div(at, 2), lax.rem(at, 2) * 2 + side] = term[
                    :, side * wide : (side + 1) * wide
                ].reshape(depth, quarter, wide)

            @pl.when(lax.div(at, 2) != core)
            def _():
                for side in range(2):
                    exp.near_copy(lax.rem(at, 2) * 2 + side).start()

    def first_norm(gb, n1, inv, ctx, ow, dsnd):
        later = [
            fetch(ctx_ref, ctx, 13),
            fetch(ow_ref, ow, 14),
            fetch(inv_ref, inv, 15),
        ]
        def n1_copy(j):
            return fetch(n1_ref.at[j], n1.at[j % 2], 16 + j % 2)

        def d_copy(j):
            return far_copy(dsnd.at[j], dbuf.at[core, j], (d_s, d_r), j, me.sibling())

        n1_copy(0).start()
        for copy in later:
            copy.start()
        fold_exp(counts - 1)
        for copy in later:
            copy.wait()
        gain = vecs[3:4, :]
        for row in range(3, 8):
            vbuf[row : row + 1, :] = jnp.zeros((1, width), f32)
        for j in range(chips):
            n1_copy(j).wait()
            if j + 1 < chips:
                n1_copy(j + 1).start()
            grad = acc[j]
            normed = n1[j % 2]
            vbuf[3:4, :] += jnp.sum(grad * normed, axis=0, keepdims=True)
            vbuf[4:5, :] += jnp.sum(grad, axis=0, keepdims=True)
            scaled = grad * gain
            first = jnp.mean(scaled, axis=1, keepdims=True)
            second = jnp.mean(scaled * normed, axis=1, keepdims=True)
            grad = inv[j][:, :1] * (scaled - first - normed * second)
            acc[j] = grad
            low = grad.astype(bf16)
            gb[j] = low.reshape(per, cluster, width)
            vbuf[5:6, :] += jnp.sum(low.astype(f32), axis=0, keepdims=True)
            back = dot_lanes(low, ow[...].reshape(width, width)).astype(bf16)

            for c in range(2):
                piece = back[:, c * half : (c + 1) * half]

                @pl.when(core == c)
                def _():
                    dbuf[c, j] = piece.reshape(per, cluster, half)

                @pl.when(core != c)
                def _():
                    dsnd[j] = piece.reshape(per, cluster, half)

            d_copy(j).start()
        sums.send(0)
        term = dot_first(ctx[...].reshape(rows, width), gb[...].reshape(rows, width))
        for zz in range(depth):
            for c in range(2):
                for p in range(chips):
                    begin_at = zz * quarter + (c * chips + p) * eighth
                    o_all[c, p, zz] = term[begin_at : begin_at + eighth, :].astype(bf16)
        for p in range(chips):
            out.near_copy(p).start()
        for j in range(chips):
            d_copy(j).wait()
        for a in range(depth):
            red.near_copy(a).wait_send()
        for b in range(chips):
            exp.near_copy(b).wait_send()

    shape = (chips, per, cluster, width)
    vm = pltpu.VMEM

    def feed_back(gb):
        pl.run_scoped(
            functools.partial(chunks, gb),
            vm((width, rows), bf16),
            vm((width, rows), bf16),
            vm((2, chips, tile, block), bf16),
            vm((2, chips, tile, block), bf16),
            vm((2, blocks, block // blocks, width), bf16),
            vm((2, depth, quarter, block), bf16),
            vm(shape[:3] + (block,), bf16),
        )
        pl.run_scoped(
            functools.partial(first_norm, gb),
            vm((2, tile, width), f32),
            vm((chips, tile, 128), f32),
            vm(shape, bf16),
            vm((depth, 2, quarter // 2, width), bf16),
            vm((chips, per, cluster, half), bf16),
        )

    pl.run_scoped(feed_back, vm(shape, bf16))

    def attend_back(qs, ks, vs, ps, xbuf, wbuf, ds, gs, gbuf, tbuf, dw, dwp, turned):
        atts = [
            Reducer(
                me,
                dwp.at[n],
                None,
                None,
                p_mid.at[n],
                p_last.at[n],
                p_done.at[n],
                groups[3 + n],
                n % 2 == 1,
            )
            for n in range(pairs)
        ]

        def loads(i, slot):
            span = pl.ds(i * pairs, pairs)
            pieces = (
                (q_ref.at[span], qs),
                (k_ref.at[span], ks),
                (v_ref.at[span], vs),
                (p_ref.at[span], ps),
            )
            return [fetch(src, dst.at[slot], slot * 4 + n) for n, (src, dst) in enumerate(pieces)]

        def load_x(i):
            return fetch(x_ref.at[:, :, i], xbuf, 8)

        load_w = fetch(aw_ref, wbuf, 9)
        for copy in loads(0, 0) + [load_x(0), load_w]:
            copy.start()
        bbuf[...] = jnp.zeros_like(bbuf)
        slots = lax.broadcasted_iota(jnp.int32, (cluster, cluster), 0)
        low = lax.broadcasted_iota(jnp.int32, (cluster, 128), 1) < size
        scale = size ** (-0.5)

        def tables(jj, i, pair, part):
            begin = part * heads + core * (heads // 2) + 2 * pair
            return [
                one_hot(posbuf[jj // chips, jj % chips, i, pl.ds(begin + h, 1), :], slots)
                for h in range(2)
            ]

        def clusters(i, slot, pair):
            lanes = pl.ds(multiple(pair * 128, 128), 128)
            for jj in range(blocks):
                tq = jnp.concatenate(tables(jj, i, pair, 0), axis=1)
                rows = stack_lanes(dbuf[jj // chips, jj % chips, i, :, lanes], low)
                ds[:, jj * share : (jj + 1) * share, :] = (
                    dot_rows(tq, rows).astype(bf16).reshape(blocks, share, 128)
                )
            for c in range(blocks):
                d = ds[c]
                probs = ps[slot, pair, c]
                slope = dot_lanes(d, stack_lanes(vs[slot, pair, c], low))
                broad = probs.astype(f32)
                halves = []
                for h in range(2):
                    span = slice(h * cluster, (h + 1) * cluster)
                    inner = jnp.sum(broad[:, span] * slope[:, span], axis=1, keepdims=True)
                    halves.append((broad[:, span] * (slope[:, span] - inner)).astype(bf16))
                grads = jnp.concatenate(halves, axis=1)
                gq = dot_rows(grads, stack_lanes(ks[slot, pair, c], low)) * scale
                gk = dot_first(grads, qs[slot, pair, c]) * scale
                gv = dot_first(probs, d)
                gs[0, c] = gq.astype(bf16)
                gs[1, c] = jnp.where(low, gk[:cluster], gk[cluster:]).astype(bf16)
                gs[2, c] = jnp.where(low, gv[:cluster], gv[cluster:]).astype(bf16)
            for jj in range(blocks):
                for part in range(3):
                    if part < 2:
                        table = jnp.concatenate(tables(jj, i, pair, part), axis=0)
                    rows = gs[part, :, jj * share : (jj + 1) * share, :].reshape(cluster, 128)
                    back = dot_first(table, stack_lanes(rows, low))
                    to = pl.ds(multiple(part * half + pair * 128, 128), 128)
                    gbuf[slot, jj // chips, jj % chips, :, to] = back.astype(bf16)

        def give(slot):
            return far_copy(gbuf.at[slot, 1 - core], gfar.at[slot], (g_s, g_r), slot, me.sibling())

        def token_copy(i, slot, k):
            return far_copy(
                tbuf.at[slot, me.chip_at(k)],
                token_out.at[chip * per + i],
                (t_s, t_r),
                i * (chips - 1) + k - 1,
                me.plane(k),
            )

        def token_keep(i, slot):
            return pltpu.make_async_copy(
                tbuf.at[slot, chip], token_out.at[chip * per + i], out_sem.at[1 + i]
            )

        def token_rows(i, slot):
            give(slot).wait()
            near = dot_lanes(gbuf[slot, core].reshape(chips * cluster, 3 * half), wbuf[core])
            distant = dot_lanes(gfar[slot].reshape(chips * cluster, 3 * half), wbuf[1 - core])
            resid = acc[:, i * cluster : (i + 1) * cluster, :].reshape(chips * cluster, width)
            tbuf[slot] = (resid + near + distant).astype(bf16).reshape(chips, cluster, width)
            token_keep(i, slot).start()
            for k in range(1, chips):
                token_copy(i, slot, k).start()

        ready = []

        def emit(src, dst):
            copy = pltpu.make_async_copy(src, dst, out_sem.at[1 + per + len(ready)])
            copy.start()
            ready.append(copy)

        def step_out_near():
            for p in range(chips):
                out.fold_near(p)
            out.send_mid()
            for p in range(chips):
                out.near_copy(p).wait_send()
            sums.fold(0)
            sums.send(1)

        def step_exp_mid():
            exp.fold_mid()
            exp.send_last()

        def step_red_mid():
            red.fold_mid()
            red.send_last()
            sums.fold(1)
            sums.send(2)

        def step_exp_last():
            exp.fold_last()
            exp.send_back()
            out.fold_mid()
            out.send_last()

        def step_red_last():
            red.fold_last()
            red.send_back()
            sums.fold(2)

        def step_out_last():
            out.fold_last()
            out.send_back()
            exp.send_side()

        def step_sides():
            red.send_side()

        hooks = {}
        steps = [
            (0, step_out_near),
            (1, step_exp_mid),
            (3, step_red_mid),
            (5, step_exp_last),
            (6, step_red_last),
            (7, step_out_last),
            (8, step_sides),
        ]
        for n, step in steps:
            hooks.setdefault(min(n, per * pairs - 1), []).append(step)
        depth_rows = quarter // chips

        def pair_grad(n, slot):
            lanes = [slice(p * half + n * 128, p * half + (n + 1) * 128) for p in range(3)]
            total = jnp.concatenate([dw[:, lane] for lane in lanes], axis=1)
            line = jnp.zeros((1, 384), f32)
            for b in range(2):
                x = jnp.concatenate([xbuf[b, j] for j in range(chips)], axis=0)
                g = jnp.concatenate(
                    [
                        jnp.concatenate([gbuf[slot, b, j, :, lane] for lane in lanes], axis=1)
                        for j in range(chips)
                    ],
                    axis=0,
                )
                total = total + dot_first(x, g)
                line = line + jnp.sum(g.astype(f32), axis=0, keepdims=True)
            for p, lane in enumerate(lanes):
                bbuf[0:1, lane] += line[:, p * 128 : (p + 1) * 128]
            low = total.astype(bf16)
            for a in range(depth):
                for b in range(chips):
                    begin = (a * chips + b) * depth_rows
                    piece = low[begin : begin + depth_rows]
                    if atts[n].tower_first:
                        dwp[n, a, b] = piece
                    else:
                        dwp[n, b, a] = piece
            atts[n].send_mid()

        dw[...] = jnp.zeros_like(dw)
        for i in range(per):
            slot = i % 2
            for copy in loads(i, slot):
                copy.wait()
            if i == 0:
                load_w.wait()
            if i >= 1:
                token_rows(i - 1, 1 - slot)
            if i + 1 < per:
                for copy in loads(i + 1, 1 - slot):
                    copy.start()
            if i == per - 1:
                load_x(i).wait()

            @pl.loop(0, pairs)
            def _(pair):
                clusters(i, slot, pair)
                for n in range(pairs):
                    if hooks.get(i * pairs + n) or i == per - 1:

                        @pl.when(pair == n)
                        def _():
                            if i == per - 1:
                                pair_grad(n, slot)
                            for step in hooks.get(i * pairs + n, ()):
                                step()

            if i >= 2:
                token_keep(i - 2, slot).wait()
                for k in range(1, chips):
                    token_copy(i - 2, slot, k).wait()
            give(slot).start()
            if i + 1 < per:
                load_x(i).wait()
                for b in range(2):
                    x = jnp.concatenate([xbuf[b, j] for j in range(chips)], axis=0)
                    g = jnp.concatenate([gbuf[slot, b, j] for j in range(chips)], axis=0)
                    dw[...] += dot_first(x, g)
                    bbuf[0:1, :] += jnp.sum(g.astype(f32), axis=0, keepdims=True)
                load_x(i + 1).start()

        biases.send(1)
        token_rows(per - 1, (per - 1) % 2)
        emit(vbuf, vec_out)
        out.send_side()
        for n in range(pairs - 1):
            atts[n].fold_mid()
            atts[n].send_last()
        biases.fold(1)
        biases.send(2)
        exp.finish()
        for c in range(2):
            for p in range(chips):
                emit(e_done.at[c, p], ew_out.at[:, pl.ds((c * chips + p) * wide, wide)])
        for n in range(pairs - 1, pairs):
            atts[n].fold_mid()
            atts[n].send_last()
        for n in range(pairs - 1):
            atts[n].fold_last()
            atts[n].send_back()
        red.finish()
        for c in range(2):
            turned[c] = jnp.transpose(r_done[c].reshape(width, wide))
            emit(turned.at[c], rw_out.at[c])
        out.finish()
        emit(o_done, ow_out)
        biases.fold(2)
        share_bias = far_copy(bbuf, bias_out.at[core], (b_s, b_r), 0, me.sibling())
        share_bias.start()
        emit(bbuf, bias_out.at[core])
        for n in range(pairs - 1, pairs):
            atts[n].fold_last()
            atts[n].send_back()
        for n in range(pairs):
            atts[n].send_side()
        for n in range(pairs):
            atts[n].finish()
            for c in range(2):
                for part in range(3):
                    emit(
                        p_done.at[n, c, :, :, pl.ds(part * 128, 128)],
                        aw_out.at[:, :, pl.ds((2 * part + c) * half + n * 128, 128)],
                    )
        for i in range(max(per - 2, 0), per):
            token_keep(i, i % 2).wait()
            for k in range(1, chips):
                token_copy(i, i % 2, k).wait()
        share_bias.wait()
        for copy in ready:
            copy.wait()
        lo_keep.wait()
        for k in range(1, chips):
            lo_copy(k).wait()

    group = (2, pairs, blocks, cluster)
    pl.run_scoped(
        attend_back,
        vm(group + (128,), bf16),
        vm(group + (128,), bf16),
        vm(group + (128,), bf16),
        vm(group + (2 * cluster,), bf16),
        vm((2, chips, cluster, width), bf16),
        vm(aw_ref.shape, bf16),
        vm((blocks, cluster, 128), bf16),
        vm((3, blocks, cluster, 128), bf16),
        vm((2, 2, chips, cluster, 3 * half), bf16),
        vm((2, chips, cluster, width), bf16),
        vm((width, 3 * half), f32),
        vm((pairs, depth, chips, quarter // chips, 384), bf16),
        vm((2, wide, width), bf16),
    )


def back(arrays, depth, heads):
    chips, per, cluster, width = arrays[17].shape
    half, blocks = width // 2, 2 * chips
    dma = pltpu.SemaphoreType.DMA
    anywhere = pl.BlockSpec(memory_space=pl.ANY)
    quarter = width // depth
    hidden = arrays[15].shape[2]
    eighth, strip, wide = quarter // blocks, width // chips, hidden // blocks
    rows = quarter // chips
    c, t = chips - 1, depth - 1
    pairs = heads // 4
    shapes = [
        ((chips * per, cluster, width), bf16),
        ((chips * per, cluster, width), bf16),
        ((chips, rows, 3 * width), bf16),
        ((2, chips, eighth, width), bf16),
        ((quarter, hidden), bf16),
        ((2, wide, width), bf16),
        ((8 + blocks, width), f32),
        ((2, 8, 3 * half), f32),
    ]
    vm = pltpu.VMEM

    def reducing(near, first, second):
        return [
            dma((near,)), dma((near,)),
            dma((first,)), dma((first,)),
            dma((second,)), dma((second,)),
            dma((c,)), dma((c,)),
            dma((1,)), dma((1,)),
        ]

    return pl.pallas_call(
        functools.partial(back_kernel, chips, depth, heads),
        out_shape=[jax.ShapeDtypeStruct(*s) for s in shapes],
        in_specs=[anywhere] * len(arrays),
        out_specs=[anywhere] * len(shapes),
        scratch_shapes=[
            vm((2, chips, per, cluster, half), bf16),
            vm(arrays[4].shape, jnp.int32),
            vm((chips, per * cluster, width), f32),
            vm((2, chips, cluster, 3 * half), bf16),
            vm((pairs, t, chips, rows, 384), bf16),
            vm((pairs, t, rows, 384), bf16),
            vm((pairs, 2, chips, rows, 384), bf16),
            vm((2, chips, depth, eighth, width), bf16),
            vm((chips, depth, eighth, width), bf16),
            vm((c, depth, eighth, width), bf16),
            vm((t, eighth, width), bf16),
            vm((2, chips, eighth, width), bf16),
            vm((2, chips, depth, quarter, wide), bf16),
            vm((chips, depth, quarter, wide), bf16),
            vm((c, depth, quarter, wide), bf16),
            vm((t, quarter, wide), bf16),
            vm((2, chips, quarter, wide), bf16),
            vm((2, depth, chips, strip, wide), bf16),
            vm((depth, chips, strip, wide), bf16),
            vm((t, chips, strip, wide), bf16),
            vm((c, strip, wide), bf16),
            vm((2, chips, strip, wide), bf16),
            vm((8 + blocks, width), f32),
            vm((chips + t, 8 + blocks, width), f32),
            vm((8, 3 * half), f32),
            vm((chips + t, 8, 3 * half), f32),
            vm((8, width), f32),
            dma((chips,)), dma((chips,)), dma((2,)), dma((2,)),
            dma((per * c,)), dma((per * c,)),
            dma((c,)), dma((c,)),
            dma((19,)), dma((1 + per + 6 + blocks + 6 * pairs,)),
            dma((chips + t,)), dma((chips + t,)), dma((chips + t,)), dma((chips + t,)),
            *reducing(depth, t, c),
            *reducing(chips, c, t),
            *reducing(chips, c, t),
            *[sem for n in range(pairs) for sem in reducing(1, c, t)],
        ],
        compiler_params=pltpu.CompilerParams(
            collective_id=2, has_side_effects=True, vmem_limit_bytes=63 * 2**20
        ),
        name="back",
    )(*arrays)


def places(rank, cluster, share):
    seqs, rows, length = rank.shape
    clusters = cluster // share
    target = rank // cluster
    which = lax.broadcasted_iota(jnp.int32, (1, 1, clusters, 1), 2)
    inside = (target[:, :, None, :] == which).astype(bf16)
    first = lax.broadcasted_iota(jnp.int32, (length, length), 0)
    second = lax.broadcasted_iota(jnp.int32, (length, length), 1)
    before = (first < second).astype(bf16)
    count = lax.dot_general(
        inside.reshape(seqs * rows * clusters, length),
        before,
        (((1,), (0,)), ((), ())),
        preferred_element_type=f32,
    ).reshape(seqs, rows, clusters, length)
    spot = which.astype(f32) * share + count
    return jnp.sum(inside.astype(f32) * spot, axis=2).astype(jnp.int32)


def per_chip(
    tokens,
    attend_weight,
    query_bias,
    value_bias,
    output_weight,
    output_bias,
    first_gain,
    first_shift,
    expand_weight,
    expand_bias,
    reduce_weight,
    reduce_bias,
    second_gain,
    second_shift,
    query_rank,
    key_rank,
    cotangent,
):
    seqs, cluster, width = tokens.shape
    heads = query_rank.shape[1]
    owners = lax.axis_size("seq")
    depth = lax.axis_size("batch")
    chips = owners // 2
    half = width // 2
    share = cluster // owners
    pos = places(jnp.concatenate([query_rank, key_rank], axis=1), cluster, share)
    quarter = width // depth
    lines = [
        query_bias,
        value_bias,
        output_bias,
        first_gain,
        first_shift,
        reduce_bias,
        second_gain,
        second_shift,
    ]
    lines += [
        expand_bias[at : at + quarter] for at in range(0, expand_bias.shape[0], quarter)
    ]
    vectors = jnp.zeros((16 * 256,), f32)
    for row, v in enumerate(lines):
        vectors += jnp.pad(v.astype(f32), (row * 256, (16 - row) * 256 - quarter))
    vectors = vectors.reshape(16, 256)
    (
        x_all,
        context,
        qs,
        ks,
        vs,
        ps,
        pos_all,
        attend_all,
        vecs,
        out_all,
        exp_all,
        red_all,
        normed_one,
        inverse_one,
        middle_low,
        hidden,
        slope,
        layer_out,
        grad_branch_two,
        late_sums,
    ) = forward(
        tokens,
        pos,
        attend_weight,
        vectors,
        output_weight,
        expand_weight,
        reduce_weight,
        cotangent,
        chips,
        depth,
        heads,
    )
    token_grad, layer_out, aw_grad, ow_grad, ew_grad, rw_grad, vec_sum, bias_sum = back(
        (
            qs,
            ks,
            vs,
            ps,
            pos_all,
            x_all,
            attend_all,
            out_all,
            exp_all,
            red_all,
            vecs,
            context,
            normed_one,
            inverse_one,
            middle_low,
            hidden,
            slope,
            layer_out,
            grad_branch_two,
            late_sums,
        ),
        depth,
        heads,
    )
    z = lax.axis_index("batch")
    six = lax.dynamic_slice_in_dim(vec_sum[:6], z * quarter, quarter, 1)
    up = lax.dynamic_index_in_dim(vec_sum[8:], z, 0, keepdims=False)
    both = jnp.concatenate([bias_sum[0, 0], bias_sum[1, 0]]).reshape(2, 3, half)
    query_value = jnp.transpose(both, (1, 0, 2)).reshape(3, width)
    query_value = lax.dynamic_slice_in_dim(query_value, z * quarter, quarter, 1)
    return (
        layer_out,
        token_grad,
        aw_grad.reshape(quarter, 3 * width).astype(f32),
        query_value[0],
        query_value[2],
        ow_grad.reshape(quarter, width).astype(f32),
        six[5],
        six[3],
        six[4],
        ew_grad.astype(f32),
        up,
        rw_grad.reshape(-1, width).astype(f32),
        six[2],
        six[0],
        six[1],
    )


def layer(mesh):
    def run(*arrays):
        seqs, cluster, width = arrays[0].shape
        heads = arrays[14].shape[1]
        owners, depth = mesh.shape["seq"], mesh.shape["batch"]
        chips = owners // 2
        fits = (
            owners % 2 == 0
            and chips > 1
            and depth == chips == 4
            and seqs % chips == 0
            and cluster == 128
            and heads % 4 == 0
            and width == heads * 64
            and cluster == 16 * owners
            and arrays[8].shape[1] == 4 * width
        )
        return (per_chip if fits else per_device)(*arrays)

    return run


def solution(mesh):
    in_specs = (
        P("batch", "seq", None),
        P("batch", None),
        P("batch"),
        P("batch"),
        P("batch", None),
        P("batch"),
        P("batch"),
        P("batch"),
        P("batch", None),
        P("batch"),
        P("batch", None),
        P("batch"),
        P("batch"),
        P("batch"),
        P("batch", None, "seq"),
        P("batch", None, "seq"),
        P("batch", "seq", None),
    )
    out_specs = (
        P("batch", "seq", None),
        P("batch", "seq", None),
        P("batch", None),
        P("batch"),
        P("batch"),
        P("batch", None),
        P("batch"),
        P("batch"),
        P("batch"),
        P("batch", None),
        P("batch"),
        P("batch", None),
        P("batch"),
        P("batch"),
        P("batch"),
    )
    return jax.shard_map(
        layer(mesh), mesh=mesh, in_specs=in_specs, out_specs=out_specs, check_vma=False
    )
```

```python
import functools
import math

import jax
import jax.numpy as jnp
from jax import lax
from jax.experimental import pallas as pl
from jax.experimental.pallas import tpu as pltpu
from jax.sharding import PartitionSpec as P

epsilon = 1e-05


def layer_norm(resid, gain, shift):
    center = jnp.mean(resid, axis=-1, keepdims=True)
    centered = resid - center
    spread = jnp.mean(centered * centered, axis=-1, keepdims=True)
    inverse = lax.rsqrt(spread + epsilon)
    normed = centered * inverse
    return (normed * gain + shift, normed, inverse)


def norm_back(upstream, normed, inverse, gain):
    scaled = upstream * gain
    first_mean = jnp.mean(scaled, axis=-1, keepdims=True)
    second_mean = jnp.mean(scaled * normed, axis=-1, keepdims=True)
    return inverse * (scaled - first_mean - normed * second_mean)


def gelu_slope(value):
    cumulative = 0.5 * (1.0 + lax.erf(value * 0.5**0.5))
    density = jnp.exp(-0.5 * value * value) * (2.0 * math.pi) ** (-0.5)
    return cumulative + value * density


def transpose_left(first, second):
    return lax.dot_general(
        first, second, (((0,), (0,)), ((), ())), preferred_element_type=jnp.float32
    )


def transpose_right(first, second):
    return lax.dot_general(
        first, second, (((1,), (1,)), ((), ())), preferred_element_type=jnp.float32
    )


def group_table(rank, cluster, owners):
    share = cluster // owners
    target = rank // cluster
    length = rank.shape[-1]
    places = lax.broadcasted_iota(jnp.int32, (length, length), 0)
    later = lax.broadcasted_iota(jnp.int32, (length, length), 1)
    before = (places < later)[None, None]
    same = target[..., :, None] == target[..., None, :]
    earlier = jnp.sum((same & before).astype(jnp.int32), axis=-2)
    position = target * share + earlier
    slots = lax.broadcasted_iota(jnp.int32, position.shape + (length,), 3)
    return (position[..., None] == slots).astype(jnp.bfloat16)


def sort_heads(rows, table, heads):
    seqs, length, width = rows.shape
    split = rows.reshape(seqs, length, heads, width // heads)
    moved = jnp.einsum("shtp,sthd->sphd", table, split, preferred_element_type=jnp.float32)
    return moved.astype(rows.dtype).reshape(seqs, length, width)


def unsort_heads(rows, table, heads):
    seqs, length, width = rows.shape
    split = rows.reshape(seqs, length, heads, width // heads)
    moved = jnp.einsum("shtp,sphd->sthd", table, split, preferred_element_type=jnp.float32)
    return moved.astype(rows.dtype).reshape(seqs, length, width)


def cluster_scores(queries, keys_rows, heads):
    items, length, width = queries.shape
    size = width // heads
    query_split = queries.reshape(items, length, heads, size)
    key_split = keys_rows.reshape(items, length, heads, size)
    scores = jnp.einsum(
        "sqhd,skhd->shqk", query_split, key_split, preferred_element_type=jnp.float32
    )
    return scores * size ** (-0.5)


def cluster_forward(queries, keys_rows, values_rows, heads):
    items, length, width = queries.shape
    scores = cluster_scores(queries, keys_rows, heads)
    top = jnp.max(scores, axis=-1, keepdims=True)
    weights = jnp.exp(scores - top)
    total = jnp.sum(weights, axis=-1, keepdims=True)
    probs = (weights / total).astype(jnp.bfloat16)
    value_split = values_rows.reshape(items, length, heads, width // heads)
    context = jnp.einsum("shqk,skhd->sqhd", probs, value_split, preferred_element_type=jnp.float32)
    return (
        context.reshape(items, length, width).astype(jnp.bfloat16),
        (top + jnp.log(total))[..., 0],
    )


def cluster_backward(scores, log_total, queries, keys_rows, values_rows, grad_context, heads):
    items, length, width = queries.shape
    size = width // heads
    query_split = queries.reshape(items, length, heads, size)
    key_split = keys_rows.reshape(items, length, heads, size)
    value_split = values_rows.reshape(items, length, heads, size)
    grad_split = grad_context.reshape(items, length, heads, size)
    probs = jnp.exp(scores - log_total[..., None])
    grad_probs = jnp.einsum(
        "sqhd,skhd->shqk", grad_split, value_split, preferred_element_type=jnp.float32
    )
    inner = jnp.sum(probs * grad_probs, axis=-1, keepdims=True)
    grad_scores = (probs * (grad_probs - inner)).astype(jnp.bfloat16)
    scale = size ** (-0.5)
    grad_query = (
        jnp.einsum("shqk,skhd->sqhd", grad_scores, key_split, preferred_element_type=jnp.float32)
        * scale
    )
    grad_key = (
        jnp.einsum("shqk,sqhd->skhd", grad_scores, query_split, preferred_element_type=jnp.float32)
        * scale
    )
    grad_value = jnp.einsum(
        "shqk,sqhd->skhd",
        probs.astype(jnp.bfloat16),
        grad_split,
        preferred_element_type=jnp.float32,
    )
    shape = (items, length, width)
    return (
        grad_query.reshape(shape).astype(jnp.bfloat16),
        grad_key.reshape(shape).astype(jnp.bfloat16),
        grad_value.reshape(shape).astype(jnp.bfloat16),
    )


def send_context(context):
    return lax.all_to_all(context, "seq", split_axis=1, concat_axis=1, tiled=True)


def send_grads(grads):
    return (
        lax.all_to_all(grads[0], "seq", split_axis=1, concat_axis=1, tiled=True),
        lax.all_to_all(grads[1], "seq", split_axis=1, concat_axis=1, tiled=True),
        lax.all_to_all(grads[2], "seq", split_axis=1, concat_axis=1, tiled=True),
    )


def make_step(left, pieces):
    total = jnp.dot(left, pieces[0], preferred_element_type=jnp.float32)
    stored = tuple(pieces[1:]) + ()
    placed = tuple((piece for piece in stored))
    return (total,) + placed


def make_hidden_step(before, pieces):
    section = before + pieces[1].astype(jnp.float32)
    activated = jax.nn.gelu(section, approximate=False).astype(jnp.bfloat16)
    total = jnp.dot(activated, pieces[0], preferred_element_type=jnp.float32)
    stored = ()
    return (total, section, activated) + stored


def per_device(
    tokens,
    attend_weight,
    query_bias,
    value_bias,
    output_weight,
    output_bias,
    first_gain,
    first_shift,
    expand_weight,
    expand_bias,
    reduce_weight,
    reduce_bias,
    second_gain,
    second_shift,
    query_rank,
    key_rank,
    cotangent,
):
    seqs, cluster, width = tokens.shape
    heads = query_rank.shape[1]
    rows = seqs * cluster
    owners = lax.axis_size("seq")
    flat = tokens.reshape(rows, width)
    attend_out = make_step(
        flat,
        (
            lax.all_gather(attend_weight, "batch", axis=0, tiled=True),
            lax.all_gather(query_bias, "batch", axis=0, tiled=True),
            lax.all_gather(value_bias, "batch", axis=0, tiled=True),
        ),
    )
    summed = attend_out[0]
    queries = (summed[:, :width] + attend_out[1].astype(jnp.float32)).astype(jnp.bfloat16)
    keys_rows = summed[:, width : 2 * width].astype(jnp.bfloat16)
    values_rows = (summed[:, 2 * width :] + attend_out[2].astype(jnp.float32)).astype(jnp.bfloat16)
    query_table = group_table(query_rank, cluster, owners)
    key_table = group_table(key_rank, cluster, owners)
    query_sorted = sort_heads(queries.reshape(seqs, cluster, width), query_table, heads)
    key_sorted = sort_heads(keys_rows.reshape(seqs, cluster, width), key_table, heads)
    value_sorted = sort_heads(values_rows.reshape(seqs, cluster, width), key_table, heads)
    received = (
        lax.all_to_all(query_sorted, "seq", split_axis=1, concat_axis=1, tiled=True),
        lax.all_to_all(key_sorted, "seq", split_axis=1, concat_axis=1, tiled=True),
        lax.all_to_all(value_sorted, "seq", split_axis=1, concat_axis=1, tiled=True),
    )
    context, log_total = cluster_forward(received[0], received[1], received[2], heads)
    forward_out = (send_context(context), log_total, received[0], received[1], received[2])
    context_rows = unsort_heads(forward_out[0], query_table, heads).reshape(rows, width)
    output_out = make_step(
        context_rows,
        (
            lax.all_gather(output_weight, "batch", axis=0, tiled=True),
            lax.all_gather(output_bias, "batch", axis=0, tiled=True),
            lax.all_gather(first_gain, "batch", axis=0, tiled=True),
            lax.all_gather(first_shift, "batch", axis=0, tiled=True),
        ),
    )
    resid_one = flat.astype(jnp.float32) + output_out[0] + output_out[1].astype(jnp.float32)
    gain_one = output_out[2].astype(jnp.float32)
    middle, normed_one, inverse_one = layer_norm(
        resid_one, gain_one, output_out[3].astype(jnp.float32)
    )
    middle_low = middle.astype(jnp.bfloat16)
    expand_out = make_step(
        middle_low,
        (
            lax.all_gather(expand_weight, "batch", axis=0, tiled=True),
            lax.all_gather(reduce_bias, "batch", axis=0, tiled=True),
            lax.all_gather(second_gain, "batch", axis=0, tiled=True),
            lax.all_gather(second_shift, "batch", axis=0, tiled=True),
        ),
    )
    hidden_out = make_hidden_step(
        expand_out[0],
        (
            lax.all_gather(reduce_weight, "batch", axis=0, tiled=True),
            lax.all_gather(expand_bias, "batch", axis=0, tiled=True),
        ),
    )
    pre_full, hidden_full = (hidden_out[1], hidden_out[2])
    resid_two = middle + hidden_out[0] + expand_out[1].astype(jnp.float32)
    gain_two = expand_out[2].astype(jnp.float32)
    final, normed_two, inverse_two = layer_norm(
        resid_two, gain_two, expand_out[3].astype(jnp.float32)
    )
    layer_out = final.astype(jnp.bfloat16).reshape(seqs, cluster, width)
    attend_full, output_full, expand_full, reduce_full = (
        lax.all_gather(attend_weight, "batch", axis=0, tiled=True),
        lax.all_gather(output_weight, "batch", axis=0, tiled=True),
        lax.all_gather(expand_weight, "batch", axis=0, tiled=True),
        lax.all_gather(reduce_weight, "batch", axis=0, tiled=True),
    )
    upstream = cotangent.reshape(rows, width).astype(jnp.float32)
    grad_second_gain = jnp.sum(upstream * normed_two, axis=0)
    grad_second_shift = jnp.sum(upstream, axis=0)
    grad_resid_two = norm_back(upstream, normed_two, inverse_two, gain_two)
    grad_branch_two = grad_resid_two.astype(jnp.bfloat16)
    grad_reduce_bias = jnp.sum(grad_branch_two, axis=0, dtype=jnp.float32)
    grad_reduce = transpose_left(hidden_full, grad_branch_two)
    grad_hidden = transpose_right(grad_branch_two, reduce_full)
    grad_pre = (grad_hidden * gelu_slope(pre_full)).astype(jnp.bfloat16)
    grad_expand_bias = jnp.sum(grad_pre, axis=0, dtype=jnp.float32)
    grad_expand = transpose_left(middle_low, grad_pre)
    grad_middle = grad_resid_two + transpose_right(grad_pre, expand_full)
    grad_first_gain = jnp.sum(grad_middle * normed_one, axis=0)
    grad_first_shift = jnp.sum(grad_middle, axis=0)
    grad_resid_one = norm_back(grad_middle, normed_one, inverse_one, gain_one)
    grad_branch_one = grad_resid_one.astype(jnp.bfloat16)
    grad_output_bias = jnp.sum(grad_branch_one, axis=0, dtype=jnp.float32)
    grad_output = transpose_left(context_rows, grad_branch_one)
    grad_context = transpose_right(grad_branch_one, output_full).astype(jnp.bfloat16)
    grad_sorted = sort_heads(grad_context.reshape(seqs, cluster, width), query_table, heads)
    grad_received = lax.all_to_all(grad_sorted, "seq", split_axis=1, concat_axis=1, tiled=True)
    kept_scores = cluster_scores(forward_out[2], forward_out[3], heads)
    home = send_grads(
        cluster_backward(
            kept_scores,
            forward_out[1],
            forward_out[2],
            forward_out[3],
            forward_out[4],
            grad_received,
            heads,
        )
    )
    grad_queries = unsort_heads(home[0], query_table, heads).reshape(rows, width)
    grad_keys = unsort_heads(home[1], key_table, heads).reshape(rows, width)
    grad_values = unsort_heads(home[2], key_table, heads).reshape(rows, width)
    grad_mixed = jnp.concatenate([grad_queries, grad_keys, grad_values], axis=1)
    grad_query_bias = jnp.sum(grad_queries, axis=0, dtype=jnp.float32)
    grad_value_bias = jnp.sum(grad_values, axis=0, dtype=jnp.float32)
    grad_attend = transpose_left(flat, grad_mixed)
    token_grad = (
        (grad_resid_one + transpose_right(grad_mixed, attend_full))
        .astype(jnp.bfloat16)
        .reshape(seqs, cluster, width)
    )
    owned = (
        lax.psum_scatter(
            grad_attend.astype(jnp.bfloat16), "batch", scatter_dimension=0, tiled=True
        ).astype(jnp.float32),
        lax.psum_scatter(
            grad_query_bias.astype(jnp.bfloat16), "batch", scatter_dimension=0, tiled=True
        ).astype(jnp.float32),
        lax.psum_scatter(
            grad_value_bias.astype(jnp.bfloat16), "batch", scatter_dimension=0, tiled=True
        ).astype(jnp.float32),
        lax.psum_scatter(
            grad_output.astype(jnp.bfloat16), "batch", scatter_dimension=0, tiled=True
        ).astype(jnp.float32),
        lax.psum_scatter(
            grad_output_bias.astype(jnp.bfloat16), "batch", scatter_dimension=0, tiled=True
        ).astype(jnp.float32),
        lax.psum_scatter(
            grad_first_gain.astype(jnp.bfloat16), "batch", scatter_dimension=0, tiled=True
        ).astype(jnp.float32),
        lax.psum_scatter(
            grad_first_shift.astype(jnp.bfloat16), "batch", scatter_dimension=0, tiled=True
        ).astype(jnp.float32),
        lax.psum_scatter(
            grad_expand.astype(jnp.bfloat16), "batch", scatter_dimension=0, tiled=True
        ).astype(jnp.float32),
        lax.psum_scatter(
            grad_expand_bias.astype(jnp.bfloat16), "batch", scatter_dimension=0, tiled=True
        ).astype(jnp.float32),
        lax.psum_scatter(
            grad_reduce.astype(jnp.bfloat16), "batch", scatter_dimension=0, tiled=True
        ).astype(jnp.float32),
        lax.psum_scatter(
            grad_reduce_bias.astype(jnp.bfloat16), "batch", scatter_dimension=0, tiled=True
        ).astype(jnp.float32),
        lax.psum_scatter(
            grad_second_gain.astype(jnp.bfloat16), "batch", scatter_dimension=0, tiled=True
        ).astype(jnp.float32),
        lax.psum_scatter(
            grad_second_shift.astype(jnp.bfloat16), "batch", scatter_dimension=0, tiled=True
        ).astype(jnp.float32),
    )
    shared = (
        lax.psum(owned[0].astype(jnp.bfloat16), "seq").astype(jnp.float32),
        lax.psum(owned[1].astype(jnp.bfloat16), "seq").astype(jnp.float32),
        lax.psum(owned[2].astype(jnp.bfloat16), "seq").astype(jnp.float32),
        lax.psum(owned[3].astype(jnp.bfloat16), "seq").astype(jnp.float32),
        lax.psum(owned[4].astype(jnp.bfloat16), "seq").astype(jnp.float32),
        lax.psum(owned[5].astype(jnp.bfloat16), "seq").astype(jnp.float32),
        lax.psum(owned[6].astype(jnp.bfloat16), "seq").astype(jnp.float32),
        lax.psum(owned[7].astype(jnp.bfloat16), "seq").astype(jnp.float32),
        lax.psum(owned[8].astype(jnp.bfloat16), "seq").astype(jnp.float32),
        lax.psum(owned[9].astype(jnp.bfloat16), "seq").astype(jnp.float32),
        lax.psum(owned[10].astype(jnp.bfloat16), "seq").astype(jnp.float32),
        lax.psum(owned[11].astype(jnp.bfloat16), "seq").astype(jnp.float32),
        lax.psum(owned[12].astype(jnp.bfloat16), "seq").astype(jnp.float32),
    )
    return (
        layer_out,
        token_grad,
        shared[0],
        shared[1],
        shared[2],
        shared[3],
        shared[4],
        shared[5],
        shared[6],
        shared[7],
        shared[8],
        shared[9],
        shared[10],
        shared[11],
        shared[12],
    )


MESH = pl.DeviceIdType.MESH
f32 = jnp.float32
bf16 = jnp.bfloat16


class Place:
    def __init__(self, chips, depth):
        self.chips, self.depth = chips, depth
        self.z = lax.axis_index("batch")
        spot = lax.axis_index("seq")
        self.chip, self.core = lax.div(spot, 2), lax.rem(spot, 2)

    def chip_at(self, k):
        return lax.rem(self.chip + k + self.chips, self.chips)

    def z_at(self, k):
        return lax.rem(self.z + k + self.depth, self.depth)

    def plane(self, k):
        return (self.z, self.chip_at(k) * 2 + self.core)

    def tower(self, k):
        return (self.z_at(k), self.chip * 2 + self.core)

    def sibling(self):
        return (self.z, self.chip * 2 + 1 - self.core)

    def greet(self):
        bell = pltpu.get_barrier_semaphore()
        others = [self.plane(k) for k in range(1, self.chips)]
        others += [self.tower(k) for k in range(1, self.depth)]
        others.append(self.sibling())
        for other in others:
            pl.semaphore_signal(bell, inc=1, device_id=other, device_id_type=MESH)
        pl.semaphore_wait(bell, len(others))


def far_copy(src, dst, sems, at, device):
    return pltpu.make_async_remote_copy(
        src_ref=src,
        dst_ref=dst,
        send_sem=sems[0].at[at],
        recv_sem=sems[1].at[at],
        device_id=device,
        device_id_type=MESH,
    )


def one_hot(row, slots):
    return jnp.where(slots == row, 1.0, 0.0).astype(bf16)


def split_lanes(tile, low):
    zero = jnp.zeros_like(tile)
    return jnp.where(low, tile, zero), jnp.where(low, zero, tile)


def stack_lanes(tile, low):
    first, second = split_lanes(tile, low)
    return jnp.concatenate([first, second], axis=0)


def dot_rows(a, b):
    return jnp.dot(a, b, preferred_element_type=f32)


def dot_lanes(a, b):
    return lax.dot_general(a, b, (((1,), (1,)), ((), ())), preferred_element_type=f32)


def dot_first(a, b):
    return lax.dot_general(a, b, (((0,), (0,)), ((), ())), preferred_element_type=f32)


def multiple(value, by):
    return pl.multiple_of(value, by)


def forward_kernel(
    chips,
    depth,
    heads,
    tok_ref,
    pos_ref,
    aw_ref,
    vec_ref,
    ow_ref,
    ew_ref,
    rw_ref,
    cot_ref,
    x_out,
    ctx_out,
    q_out,
    k_out,
    v_out,
    p_out,
    pos_out,
    aw_out,
    vec_out,
    ow_out,
    ew_out,
    rw_out,
    n1_out,
    inv_out,
    ml_out,
    hid_out,
    slope_out,
    lo_out,
    gb_out,
    sum_out,
    xbuf,
    posbuf,
    wbuf,
    vbuf,
    bias,
    ctxb,
    ctxt,
    owbuf,
    ewbuf,
    rwbuf,
    cbuf,
    n1buf,
    invbuf,
    mlbuf,
    vecs,
    upb,
    sums,
    tok_s,
    tok_r,
    tokc_s,
    tokc_r,
    pos_s,
    pos_r,
    posc_s,
    posc_r,
    up_s,
    up_r,
    dn_s,
    dn_r,
    awc_s,
    awc_r,
    vec_s,
    vec_r,
    wz_s,
    wz_r,
    wp_s,
    wp_r,
    wd_s,
    wd_r,
    wc_s,
    wc_r,
    ctx_s,
    ctx_r,
    cot_s,
    cot_r,
    oc_s,
    oc_r,
    loc,
    out_sem,
    slope_sem,
    att_sem,
    late_sem,
):
    me = Place(chips, depth)
    z, chip, core = me.z, me.chip, me.core
    per = tok_ref.shape[0] // chips
    half = aw_ref.shape[1] // 6
    rows_z = aw_ref.shape[0]
    pairs = heads // 4
    size = half // (2 * pairs)
    me.greet()

    def aw_block(zz):
        return wbuf.at[pl.ds(multiple(zz * rows_z, 8), rows_z)]

    def up_copy(h):
        return far_copy(
            aw_block(z - h), aw_block(z - h), (up_s, up_r), h, (z + 1, chip * 2 + core)
        )

    def down_copy(h):
        return far_copy(
            aw_block(z + h), aw_block(z + h), (dn_s, dn_r), h, (z - 1, chip * 2 + core)
        )

    def up_got(h):
        return far_copy(
            aw_block(z - 1 - h), aw_block(z - 1 - h), (up_s, up_r), h, me.sibling()
        )

    def down_got(h):
        return far_copy(
            aw_block(z + 1 + h), aw_block(z + 1 + h), (dn_s, dn_r), h, me.sibling()
        )

    def pass_on():
        @pl.when(z < depth - 1)
        def _():
            up_copy(0).start()

        @pl.when(z > 0)
        def _():
            down_copy(0).start()

    def pass_rest(hops):
        for h in hops:

            @pl.when(z > h)
            def _():
                up_got(h).wait_recv()
                if h + 1 < depth - 1:

                    @pl.when(z < depth - 1)
                    def _():
                        up_copy(h + 1).start()

            @pl.when(z + 1 + h < depth)
            def _():
                down_got(h).wait_recv()
                if h + 1 < depth - 1:

                    @pl.when(z > 0)
                    def _():
                        down_copy(h + 1).start()

    def pass_end():
        for h in range(depth - 1):

            @pl.when((z >= h) & (z < depth - 1))
            def _():
                up_copy(h).wait_send()

            @pl.when((z + h < depth) & (z > 0))
            def _():
                down_copy(h).wait_send()

    def mine(ref, target):
        return ref.at[pl.ds(target * per, per)]

    def tok_copy(k):
        return far_copy(
            mine(tok_ref, me.chip_at(k)), xbuf.at[core, chip], (tok_s, tok_r), k - 1, me.plane(k)
        )

    def pos_copy(k):
        return far_copy(
            mine(pos_ref, me.chip_at(k)), posbuf.at[core, chip], (pos_s, pos_r), k - 1, me.plane(k)
        )

    def vec_copy(k):
        return far_copy(vec_ref, vbuf.at[z], (vec_s, vec_r), k - 1, me.tower(k))

    sends = []
    for k in range(1, chips):
        sends.append(pos_copy(k))
        sends[-1].start()
    for k in range(1, depth):
        sends.append(vec_copy(k))
        sends[-1].start()
    for k in range(1, chips):
        sends.append(tok_copy(k))
        sends[-1].start()
    local = []

    def keep(src, dst):
        copy = pltpu.make_async_copy(src, dst, loc.at[len(local)])
        copy.start()
        local.append(copy)

    for part in range(3):
        keep(
            aw_ref.at[:, pl.ds(multiple(part * 2 * half + core * half, 128), half)],
            wbuf.at[pl.ds(multiple(z * rows_z, 8), rows_z), pl.ds(part * half, half)],
        )
    keep(mine(tok_ref, chip), xbuf.at[core, chip])
    keep(mine(pos_ref, chip), posbuf.at[core, chip])
    keep(vec_ref, vbuf.at[z])
    for copy in local[:3]:
        copy.wait()
    pass_on()
    wide = ew_ref.shape[1] // (2 * chips)
    tall = rw_ref.shape[0] // (2 * chips)
    mid_rows = rows_z // 2
    mine_at = core * chips + chip

    def piece(kind):
        if kind == 0:
            return ow_ref.at[pl.ds(multiple(core * mid_rows, 8), mid_rows)]
        if kind == 1:
            return ew_ref.at[:, pl.ds(multiple(mine_at * wide, 128), wide)]
        return rw_ref.at[pl.ds(multiple(mine_at * tall, 8), tall)]

    def place(kind, zz):
        if kind == 0:
            return owbuf.at[zz, core]
        if kind == 1:
            return ewbuf.at[zz, :, pl.ds(multiple(mine_at * wide, 128), wide)]
        return rwbuf.at[zz, mine_at]

    def place_all(kind, at):
        if kind == 1:
            return ewbuf.at[:, :, pl.ds(multiple(at * wide, 128), wide)]
        return rwbuf.at[:, at]

    for kind in range(3):
        keep(piece(kind), place(kind, z))

    def wz_copy(kind, k):
        return far_copy(
            piece(kind),
            place(kind, z),
            (wz_s, wz_r),
            kind * (depth - 1) + k - 1,
            me.tower(k),
        )

    beside = (chip + 1 - 2 * lax.rem(chip, 2), lax.rem(chip + 2, chips))
    across = chips - 1 - chip

    def part_of(kind, origin, side):
        at = core * chips + origin
        span = pl.ds(side * (depth // 2), depth // 2)
        if kind == 1:
            return ewbuf.at[span, :, pl.ds(multiple(at * wide, 128), wide)]
        return rwbuf.at[span, at]

    def wp_copy(kind, d):
        spot = place_all(kind, mine_at)
        return far_copy(
            spot, spot, (wp_s, wp_r), (kind - 1) * 2 + d, (z, beside[d] * 2 + core)
        )

    def wd_copy(kind, d):
        spot = part_of(kind, beside[d], d)
        return far_copy(
            spot, spot, (wd_s, wd_r), (kind - 1) * 2 + d, (z, beside[1 - d] * 2 + core)
        )

    def wc_copy(kind, n):
        at = core * chips + (chip, beside[0], beside[1], across)[n]
        return far_copy(
            place_all(kind, at),
            place_all(kind, at),
            (wc_s, wc_r),
            (kind - 1) * chips + n,
            me.sibling(),
        )

    def tower_wait(kind):
        for k in range(1, depth):
            wz_copy(kind, k).wait_recv()

    def plane_first(kind):
        for d in range(2):
            wp_copy(kind, d).start()
        wc_copy(kind, 0).start()

    def plane_second(kind):
        for d in range(2):
            wp_copy(kind, d).wait_recv()
            wd_copy(kind, d).start()
            wc_copy(kind, 1 + d).start()

    def plane_last(kind):
        for d in range(2):
            wd_copy(kind, d).wait_recv()
        wc_copy(kind, 3).start()
        for n in range(chips):
            wc_copy(kind, n).wait()
        for d in range(2):
            wp_copy(kind, d).wait_send()
            wd_copy(kind, d).wait_send()

    def oc_copy():
        spot = owbuf.at[:, core]
        return far_copy(spot, spot, (oc_s, oc_r), 0, me.sibling())

    def cot_copy(n):
        target = (beside[0], beside[1], across)[n]
        return far_copy(
            mine(cot_ref, target),
            cbuf.at[chip],
            (cot_s, cot_r),
            n,
            (z, target * 2 + core),
        )

    keep(mine(cot_ref, chip), cbuf.at[chip])

    for copy in local[3:5]:
        copy.wait()

    def tokc_copy(k):
        source = me.chip_at(-k)
        return far_copy(
            xbuf.at[core, source], xbuf.at[core, source], (tokc_s, tokc_r), k, me.sibling()
        )

    def posc_copy(k):
        source = me.chip_at(-k)
        return far_copy(
            posbuf.at[core, source], posbuf.at[core, source], (posc_s, posc_r), k, me.sibling()
        )

    for k in range(1, depth):
        wz_copy(1, k).start()
        for kind in range(3):
            sends.append(wz_copy(kind, k))
    pass_rest(range(depth - 2))
    for k in range(chips):
        if k:
            pos_copy(k).wait_recv()
            tok_copy(k).wait_recv()
        for copy in (posc_copy(k), tokc_copy(k)):
            copy.start()
            sends.append(copy)
    for copy in local[5:]:
        copy.wait()
    tower_wait(1)
    plane_first(1)
    pass_rest(range(depth - 2, depth - 1))
    for k in range(1, depth):
        wz_copy(2, k).start()
    plane_second(1)
    for n in range(2):
        cot_copy(n).start()
    for k in range(1, depth):
        vec_copy(k).wait_recv()
    for k in range(chips):
        posc_copy(k).wait_recv()
        tokc_copy(k).wait_recv()

    outs = []

    def emit(src, dst):
        copy = pltpu.make_async_copy(src, dst, out_sem.at[len(outs)])
        copy.start()
        outs.append(copy)

    emit(xbuf, x_out)
    emit(posbuf, pos_out)
    emit(wbuf, aw_out.at[core])
    awc = far_copy(wbuf, aw_out.at[core], (awc_s, awc_r), 0, me.sibling())
    awc.start()
    sends.append(awc)

    quarter = rows_z
    for zz in range(depth):
        begin = zz * quarter
        for row, at in ((0, 0), (1, 2)):
            for side in range(2):
                lo = max(begin, side * half)
                hi = min(begin + quarter, (side + 1) * half)
                if lo < hi:
                    bias[side, 0:1, at * half + lo - side * half : at * half + hi - side * half] = (
                        vbuf[zz, row : row + 1, lo - begin : hi - begin]
                    )
    bias[0, 0:1, half : 2 * half] = jnp.zeros((1, half), f32)
    bias[1, 0:1, half : 2 * half] = jnp.zeros((1, half), f32)
    added = bias[core, 0:1, :]
    for zz in range(depth):
        for row in range(8):
            vecs[row : row + 1, zz * quarter : (zz + 1) * quarter] = vbuf[
                zz, row : row + 1, :quarter
            ]
        steps = upb.shape[1] // (depth * quarter)
        for row in range(steps):
            to = (zz * steps + row) * quarter
            upb[0:1, to : to + quarter] = vbuf[zz, 8 + row : 9 + row, :quarter]

    cluster = tok_ref.shape[1]
    blocks = 2 * chips
    share = cluster // blocks
    width = tok_ref.shape[2]

    slots = lax.broadcasted_iota(jnp.int32, (cluster, cluster), 0)
    low = lax.broadcasted_iota(jnp.int32, (cluster, 128), 1) < size
    scale = size ** (-0.5)

    def tables(jj, i, pair, part):
        first = part * heads + core * (heads // 2) + 2 * pair
        rows = [
            one_hot(posbuf[jj // chips, jj % chips, i, pl.ds(first + h, 1), :], slots)
            for h in range(2)
        ]
        return rows

    def hook(i, pair):
        step = i * pairs + pair
        last = per * pairs - 1

        @pl.when(step == min(2, last))
        def _():
            tower_wait(2)
            plane_first(2)
            for k in range(1, depth):
                wz_copy(0, k).start()

        @pl.when(step == last)
        def _():
            plane_second(2)

    def attention(qkv, qs, ks, vs, ps, os):
        def group_copies(i):
            span = pl.ds(i * pairs, pairs)
            pieces = ((qs, q_out), (ks, k_out), (vs, v_out), (ps, p_out))
            return [
                pltpu.make_async_copy(src.at[span], dst.at[span], att_sem.at[5 + 4 * i + n])
                for n, (src, dst) in enumerate(pieces)
            ]

        @pl.loop(0, blocks)
        def _(jj):
            x = xbuf[lax.div(jj, chips), lax.rem(jj, chips)].reshape(per * cluster, width)
            mixed = (dot_rows(x, wbuf[...]) + added).astype(bf16)
            for at in range(3 * pairs):
                qkv[at, jj] = mixed[:, at * 128 : (at + 1) * 128].reshape(per, cluster, 128)

        @pl.loop(0, per)
        def _(i):
            @pl.loop(0, pairs)
            def _(pair):
                at = i * pairs + pair
                for jj in range(blocks):
                    tq = jnp.concatenate(tables(jj, i, pair, 0), axis=1)
                    tk = jnp.concatenate(tables(jj, i, pair, 1), axis=1)
                    q = stack_lanes(qkv[pair, jj, i], low)
                    k = stack_lanes(qkv[pairs + pair, jj, i], low)
                    v = stack_lanes(qkv[2 * pairs + pair, jj, i], low)
                    span = slice(jj * share, (jj + 1) * share)
                    sq = dot_rows(tq, q).astype(bf16)
                    skv = dot_rows(tk, jnp.concatenate([k, v], axis=1)).astype(bf16)
                    qs[at, :, span, :] = sq.reshape(blocks, share, 128)
                    ks[at, :, span, :] = skv[:, :128].reshape(blocks, share, 128)
                    vs[at, :, span, :] = skv[:, 128:].reshape(blocks, share, 128)
                for c in range(blocks):
                    scores = dot_lanes(qs[at, c], stack_lanes(ks[at, c], low)) * scale
                    halves = []
                    for h in range(2):
                        s = scores[:, h * cluster : (h + 1) * cluster]
                        e = jnp.exp(s - jnp.max(s, axis=1, keepdims=True))
                        halves.append((e / jnp.sum(e, axis=1, keepdims=True)).astype(bf16))
                    probs = jnp.concatenate(halves, axis=1)
                    ps[at, c] = probs
                    o = dot_rows(probs, stack_lanes(vs[at, c], low)).astype(bf16)
                    os[c] = o
                for jj in range(blocks):
                    tq = jnp.concatenate(tables(jj, i, pair, 0), axis=0)
                    rows = os[:, jj * share : (jj + 1) * share, :].reshape(cluster, 128)
                    back = dot_first(tq, stack_lanes(rows, low)).astype(bf16)
                    ctxb[jj // chips, jj % chips, i, :, pl.ds(multiple(pair * 128, 128), 128)] = back
                hook(i, pair)

                @pl.when(pair == pairs - 1)
                def _():
                    for copy in group_copies(i):
                        copy.start()


        far, own = ctx_copies()
        for copy in (far, own):
            copy.start()
        for copy in (far, own):
            copy.wait()
        for i in range(per):
            for copy in group_copies(i):
                copy.wait()

    def ctx_copies():
        lanes = pl.ds(multiple(core * half, 128), half)
        far = far_copy(
            ctxb.at[1 - core], ctxt.at[:, :, :, lanes], (ctx_s, ctx_r), 0, me.sibling()
        )
        own = pltpu.make_async_copy(ctxb.at[core], ctxt.at[:, :, :, lanes], att_sem.at[4])
        return far, own

    group = (per * pairs, blocks, cluster, 128)
    pl.run_scoped(
        attention,
        pltpu.VMEM((3 * pairs, blocks, per, cluster, 128), bf16),
        pltpu.VMEM(group, bf16),
        pltpu.VMEM(group, bf16),
        pltpu.VMEM(group, bf16),
        pltpu.VMEM((per * pairs, blocks, cluster, 2 * cluster), bf16),
        pltpu.VMEM((blocks, cluster, 128), bf16),
    )

    tower_wait(0)
    oc_copy().start()
    oc_copy().wait()
    emit(ctxt, ctx_out)
    context_out = outs[-1]
    emit(owbuf, ow_out)
    tile = per * cluster
    hidden = upb.shape[1]
    eps = epsilon

    def moments(rows):
        center = jnp.mean(rows, axis=1, keepdims=True)
        centered = rows - center
        spread = jnp.mean(centered * centered, axis=1, keepdims=True)
        inverse = lax.rsqrt(spread + eps)
        return centered * inverse, inverse

    def slope_out_copy(j, slot):
        return pltpu.make_async_copy(sbuf.at[slot], slope_out.at[j], slope_sem.at[slot])

    def vec(row):
        return vecs[row : row + 1, :]

    def feed(hbuf, sbuf):
        step = sbuf.shape[3]

        def late_copies(j):
            pieces = ((cbuf, lo_out), (ctxt, gb_out))
            return [
                pltpu.make_async_copy(src.at[j], dst.at[j], late_sem.at[2 * j + n])
                for n, (src, dst) in enumerate(pieces)
            ]

        def slope_copy(n):
            return pltpu.make_async_copy(
                sbuf.at[n % 2],
                slope_out.at[:, :, pl.ds(n * step, step)],
                slope_sem.at[n % 2],
            )

        for j in range(chips):
            rows = ctxt[j].reshape(tile, width)
            branch = dot_rows(rows, owbuf[...].reshape(width, width))
            resid = xbuf[core, j].reshape(tile, width).astype(f32) + branch + vec(2)
            normed, inverse = moments(resid)
            n1buf[j] = normed
            invbuf[j] = jnp.broadcast_to(inverse, (tile, 128))
            mlbuf[j] = (normed * vec(3) + vec(4)).astype(bf16).reshape(per, cluster, width)

        cot_copy(2).start()
        plane_last(1)
        emit(ewbuf, ew_out)
        for n in range(hidden // step):
            lanes = slice(n * step, (n + 1) * step)
            if n >= 2:
                slope_copy(n - 2).wait()
            for j in range(chips):
                weight = ewbuf[:, :, lanes].reshape(width, step)
                pre = dot_rows(mlbuf[j].reshape(tile, width), weight) + upb[0:1, lanes]
                cumulative = 0.5 * (1.0 + lax.erf(pre * 0.5**0.5))
                density = jnp.exp(-0.5 * pre * pre) * (2.0 * math.pi) ** (-0.5)
                hbuf[j, :, lanes] = (pre * cumulative).astype(bf16)
                sbuf[n % 2, j] = (cumulative + pre * density).astype(bf16)
            slope_copy(n).start()

        emit(vecs, vec_out)
        emit(n1buf, n1_out)
        emit(invbuf, inv_out)
        emit(mlbuf, ml_out)
        emit(hbuf, hid_out)
        plane_last(2)
        pass_end()
        emit(rwbuf, rw_out)
        for n in range(2):
            cot_copy(n).wait()
        sums[...] = jnp.zeros_like(sums)
        waited = (context_out,)
        for copy in waited:
            copy.wait()

        for n in range(chips):
            j = 2 * lax.rem(lax.div(chip, 2) + n // 2, 2)
            j = j + lax.rem(chip + n, 2)

            if n == chips - 1:
                cot_copy(2).wait()

            branch = vec(5)
            for zz in range(depth):
                span = hidden // depth
                branch = branch + dot_rows(
                    hbuf[j, :, zz * span : (zz + 1) * span], rwbuf[zz].reshape(span, width)
                )
            middle = n1buf[j] * vec(3) + vec(4)
            normed, inverse = moments(middle + branch)
            upstream = cbuf[j].reshape(tile, width).astype(f32)
            cbuf[j] = (normed * vec(6) + vec(7)).astype(bf16).reshape(per, cluster, width)
            sums[0:1, :] += jnp.sum(upstream * normed, axis=0, keepdims=True)
            sums[1:2, :] += jnp.sum(upstream, axis=0, keepdims=True)
            scaled = upstream * vec(6)
            first = jnp.mean(scaled, axis=1, keepdims=True)
            second = jnp.mean(scaled * normed, axis=1, keepdims=True)
            grad = inverse * (scaled - first - normed * second)
            low_grad = grad.astype(bf16)
            sums[2:3, :] += jnp.sum(low_grad.astype(f32), axis=0, keepdims=True)
            ctxt[j] = low_grad.reshape(per, cluster, width)
            for copy in late_copies(j):
                copy.start()

        emit(sums, sum_out)
        for j in range(chips):
            for copy in late_copies(j):
                copy.wait()
        for copy in sends:
            copy.wait_send()
        awc.wait_recv()
        for n in range(max(hidden // step - 2, 0), hidden // step):
            slope_copy(n).wait()
        for copy in outs:
            if not any(copy is other for other in waited):
                copy.wait()

    pl.run_scoped(
        feed,
        pltpu.VMEM((chips, tile, hidden), bf16),
        pltpu.VMEM((2, chips, tile, hidden // depth), bf16),
    )


def forward(
    tokens,
    pos,
    attend_weight,
    vectors,
    output_weight,
    expand_weight,
    reduce_weight,
    cotangent,
    chips,
    depth,
    heads,
):
    seqs, cluster, width = tokens.shape
    per, blocks, pairs = seqs // chips, 2 * chips, heads // 4
    half = width // 2
    rows_z = attend_weight.shape[0]
    hidden = expand_weight.shape[1]
    items = per * pairs
    tile = per * cluster
    dma = pltpu.SemaphoreType.DMA
    anywhere = pl.BlockSpec(memory_space=pl.ANY)
    tall = reduce_weight.shape[0] // blocks
    shapes = [
        ((2, chips, per, cluster, width), bf16),
        ((chips, per, cluster, width), bf16),
        ((items, blocks, cluster, 128), bf16),
        ((items, blocks, cluster, 128), bf16),
        ((items, blocks, cluster, 128), bf16),
        ((items, blocks, cluster, 2 * cluster), bf16),
        ((2, chips, per, 2 * heads, cluster), jnp.int32),
        ((2, depth * rows_z, 3 * half), bf16),
        ((8, width), f32),
        ((depth, 2, rows_z // 2, width), bf16),
        ((depth, rows_z, hidden), bf16),
        ((depth, blocks, tall, width), bf16),
        ((chips, tile, width), f32),
        ((chips, tile, 128), f32),
        ((chips, per, cluster, width), bf16),
        ((chips, tile, hidden), bf16),
        ((chips, tile, hidden), bf16),
        ((chips, per, cluster, width), bf16),
        ((chips, per, cluster, width), bf16),
        ((8, width), f32),
    ]
    t, c = depth - 1, chips - 1
    vm = pltpu.VMEM
    return pl.pallas_call(
        functools.partial(forward_kernel, chips, depth, heads),
        out_shape=[jax.ShapeDtypeStruct(*s) for s in shapes],
        in_specs=[anywhere] * 8,
        out_specs=[anywhere] * len(shapes),
        scratch_shapes=[
            vm(shapes[0][0], bf16),
            vm(shapes[6][0], jnp.int32),
            vm(shapes[7][0][1:], bf16),
            vm((depth,) + vectors.shape, f32),
            vm((2, 8, 3 * half), f32),
            vm((2, chips, per, cluster, half), bf16),
            vm(shapes[1][0], bf16),
            vm(shapes[9][0], bf16),
            vm(shapes[10][0], bf16),
            vm(shapes[11][0], bf16),
            vm(shapes[17][0], bf16),
            vm(shapes[12][0], f32),
            vm(shapes[13][0], f32),
            vm(shapes[14][0], bf16),
            vm((8, width), f32),
            vm((8, hidden), f32),
            vm((8, width), f32),
            dma((c,)), dma((c,)), dma((chips,)), dma((chips,)),
            dma((c,)), dma((c,)), dma((chips,)), dma((chips,)),
            dma((t,)), dma((t,)), dma((t,)), dma((t,)), dma((1,)), dma((1,)),
            dma((t,)), dma((t,)),
            dma((3 * t,)), dma((3 * t,)),
            dma((4,)), dma((4,)), dma((4,)), dma((4,)),
            dma((2 * chips,)), dma((2 * chips,)),
            dma((1,)), dma((1,)),
            dma((c,)), dma((c,)),
            dma((1,)), dma((1,)),
            dma((12,)), dma((24,)), dma((2,)), dma((5 + 4 * per,)), dma((2 * chips,)),
        ],
        compiler_params=pltpu.CompilerParams(
            collective_id=1, has_side_effects=True, vmem_limit_bytes=63 * 2**20
        ),
        name="forward",
    )(
        tokens,
        pos,
        attend_weight,
        vectors,
        output_weight,
        expand_weight,
        reduce_weight,
        cotangent,
    )


def add_into(target, at, parts):
    total = target[at].astype(f32)
    for part in parts:
        total = total + part.astype(f32)
    target[at] = total.astype(target.dtype)


class Reducer:
    def __init__(self, me, own, other, near, mid, last, done, sems, tower_first):
        self.me, self.own, self.other = me, own, other
        self.near, self.mid, self.last, self.done = near, mid, last, done
        (self.near_s, self.near_r, self.mid_s, self.mid_r, self.last_s, self.last_r) = sems[:6]
        (self.back_s, self.back_r, self.side_s, self.side_r) = sems[6:10]
        self.tower_first = tower_first
        self.sizes = (mid.shape[0] + 1, last.shape[0] + 1)

    def spot(self, axis, k):
        me = self.me
        if self.tower_first == (axis == 0):
            return me.z_at(k), me.tower(k)
        return me.chip_at(k), me.plane(k)

    def near_copy(self, a):
        return far_copy(
            self.other.at[a], self.near.at[a], (self.near_s, self.near_r), a, self.me.sibling()
        )

    def fold_near(self, a):
        self.near_copy(a).wait_recv()
        for b in range(self.sizes[1]):
            add_into(self.own, (a, b), [self.near[a, b]])

    def mid_copy(self, k):
        where, device = self.spot(0, k)
        return far_copy(
            self.own.at[where], self.mid.at[k - 1], (self.mid_s, self.mid_r), k - 1, device
        )

    def send_mid(self):
        for k in range(1, self.sizes[0]):
            self.mid_copy(k).start()

    def fold_mid(self):
        for k in range(1, self.sizes[0]):
            self.mid_copy(k).wait()
        here = self.spot(0, 0)[0]
        for b in range(self.sizes[1]):
            add_into(self.own, (here, b), [self.mid[k - 1, b] for k in range(1, self.sizes[0])])

    def last_copy(self, k):
        here = self.spot(0, 0)[0]
        where, device = self.spot(1, k)
        return far_copy(
            self.own.at[here, where],
            self.last.at[k - 1],
            (self.last_s, self.last_r),
            k - 1,
            device,
        )

    def send_last(self):
        for k in range(1, self.sizes[1]):
            self.last_copy(k).start()

    def fold_last(self):
        me = self.me
        for k in range(1, self.sizes[1]):
            self.last_copy(k).wait()
        total = self.own[self.spot(0, 0)[0], self.spot(1, 0)[0]].astype(f32)
        for k in range(1, self.sizes[1]):
            total = total + self.last[k - 1].astype(f32)
        self.done[me.core, me.chip] = total.astype(bf16)

    def back_copy(self, k):
        me = self.me
        spot = self.done.at[me.core, me.chip]
        return far_copy(spot, spot, (self.back_s, self.back_r), k - 1, me.plane(k))

    def send_back(self):
        for k in range(1, self.done.shape[1]):
            self.back_copy(k).start()

    def side_copy(self):
        spot = self.done.at[self.me.core]
        return far_copy(spot, spot, (self.side_s, self.side_r), 0, self.me.sibling())

    def send_side(self):
        for k in range(1, self.done.shape[1]):
            self.back_copy(k).wait()
        self.side_copy().start()

    def finish(self):
        self.side_copy().wait()


class Sum:
    def __init__(self, me, vec, got, s, r):
        self.me, self.vec, self.got, self.s, self.r = me, vec, got, s, r

    def copies(self, hop):
        me = self.me
        if hop == 0:
            spots = [(0, me.sibling())]
        elif hop == 1:
            spots = [(k, me.plane(k)) for k in range(1, me.chips)]
        else:
            spots = [(me.chips + k - 1, me.tower(k)) for k in range(1, me.depth)]
        return [far_copy(self.vec, self.got.at[n], (self.s, self.r), n, d) for n, d in spots], spots

    def send(self, hop):
        for copy in self.copies(hop)[0]:
            copy.start()

    def fold(self, hop):
        copies, spots = self.copies(hop)
        for copy in copies:
            copy.wait()
        total = self.vec[...]
        for n, _ in spots:
            total = total + self.got[n]
        self.vec[...] = total


def back_kernel(
    chips,
    depth,
    heads,
    q_ref,
    k_ref,
    v_ref,
    p_ref,
    pos_ref,
    x_ref,
    aw_ref,
    ow_ref,
    ew_ref,
    rw_ref,
    vec_ref,
    ctx_ref,
    n1_ref,
    inv_ref,
    ml_ref,
    hid_ref,
    slope_ref,
    lo_ref,
    gb_ref,
    late_ref,
    token_out,
    layer_out,
    aw_out,
    ow_out,
    ew_out,
    rw_out,
    vec_out,
    bias_out,
    dbuf,
    posbuf,
    acc,
    gfar,
    p_mid,
    p_last,
    p_done,
    o_all,
    o_near,
    o_mid,
    o_last,
    o_done,
    e_all,
    e_near,
    e_mid,
    e_last,
    e_done,
    r_all,
    r_near,
    r_mid,
    r_last,
    r_done,
    vbuf,
    vgot,
    bbuf,
    bgot,
    vecs,
    d_s,
    d_r,
    g_s,
    g_r,
    t_s,
    t_r,
    lo_s,
    lo_r,
    load,
    out_sem,
    v_s,
    v_r,
    b_s,
    b_r,
    *sems,
):
    me = Place(chips, depth)
    z, core, chip = me.z, me.core, me.chip
    per, cluster, width = lo_ref.shape[1:]
    half = width // 2
    pairs = heads // 4
    size = half // (2 * pairs)
    blocks = 2 * chips
    share = cluster // blocks
    tile = per * cluster
    hidden = hid_ref.shape[2]
    wide = hidden // blocks
    strip = width // chips
    quarter = width // depth
    eighth = quarter // blocks
    rows = chips * tile
    me.greet()
    groups = [sems[n * 10 : (n + 1) * 10] for n in range(3 + heads // 4)]
    red = Reducer(
        me, r_all.at[core], r_all.at[1 - core], r_near, r_mid, r_last, r_done, groups[0], True
    )
    exp = Reducer(
        me, e_all.at[core], e_all.at[1 - core], e_near, e_mid, e_last, e_done, groups[1], False
    )
    out = Reducer(
        me, o_all.at[core], o_all.at[1 - core], o_near, o_mid, o_last, o_done, groups[2], False
    )
    sums = Sum(me, vbuf, vgot, v_s, v_r)
    biases = Sum(me, bbuf, bgot, b_s, b_r)

    def fetch(src, dst, at):
        return pltpu.make_async_copy(src, dst, load.at[at])

    def lo_copy(k):
        return far_copy(
            lo_ref.at[me.chip_at(k)],
            layer_out.at[pl.ds(chip * per, per)],
            (lo_s, lo_r),
            k - 1,
            me.plane(k),
        )

    lo_keep = pltpu.make_async_copy(
        lo_ref.at[chip], layer_out.at[pl.ds(chip * per, per)], out_sem.at[0]
    )

    block = 2 * wide
    counts = blocks // 2

    def order(n):
        return lax.rem(n + z + chip, counts)

    def fold_red(n):
        at = order(n)
        red.fold_near(at)
        k = lax.rem(at - z + depth, depth)

        @pl.when(k != 0)
        def _():
            red.mid_copy(k).start()

    def fold_exp(n):
        at = order(n)

        @pl.when(lax.div(at, 2) == core)
        def _():
            for side in range(2):
                b = lax.rem(at, 2) * 2 + side
                exp.fold_near(b)
                k = lax.rem(b - chip + chips, chips)

                @pl.when(k != 0)
                def _():
                    exp.mid_copy(k).start()

    def chunks(gb, gbt, mlt, hid, slope, rwc, ewc, gpb):
        def chunk(n, slot):
            at = order(n)
            lanes = pl.ds(multiple(at * block, 128), block)
            return [
                fetch(hid_ref.at[:, :, lanes], hid.at[slot], slot * 4),
                fetch(slope_ref.at[:, :, lanes], slope.at[slot], slot * 4 + 1),
                fetch(rw_ref.at[at], rwc.at[slot], slot * 4 + 2),
                fetch(ew_ref.at[:, :, lanes], ewc.at[slot], slot * 4 + 3),
            ]

        begin = [
            fetch(gb_ref, gb, 8),
            fetch(ml_ref, gpb, 9),
        ]
        later = [
            fetch(vec_ref, vecs, 11),
            fetch(late_ref, vbuf.at[pl.ds(0, 8)], 12),
            fetch(pos_ref, posbuf, 18),
        ]
        for copy in begin[:1] + chunk(0, 0) + begin[1:] + later:
            copy.start()
        for k in range(1, chips):
            lo_copy(k).start()
        lo_keep.start()
        vbuf[8:, :] = jnp.zeros((blocks, width), f32)
        begin[0].wait()
        for j in range(chips):
            gbt[:, j * tile : (j + 1) * tile] = jnp.transpose(gb[j].reshape(tile, width))

        def settle():
            for copy in begin[1:] + later:
                copy.wait()
            for j in range(chips):
                mlt[:, j * tile : (j + 1) * tile] = jnp.transpose(gpb[j].reshape(tile, width))
                acc[j] = gb[j].reshape(tile, width).astype(f32)

        @pl.loop(0, counts)
        def _(n):
            slot = lax.rem(n, 2)
            at = order(n)
            for copy in chunk(n, slot):
                copy.wait()

            @pl.when(n + 1 < counts)
            def _():
                for copy in chunk(n + 1, 1 - slot):
                    copy.start()

            term = dot_rows(gbt[...], hid[slot].reshape(rows, block)).astype(bf16)
            for side in range(2):
                r_all[side, at] = term[:, side * wide : (side + 1) * wide].reshape(
                    chips, strip, wide
                )
            red.near_copy(at).start()

            @pl.when(n == 0)
            def _():
                settle()

            @pl.when(n > 0)
            def _():
                fold_exp(n - 1)

            up = rwc[slot].reshape(block, width)
            down = ewc[slot].reshape(width, block)
            total = jnp.zeros((1, block), f32)
            for j in range(chips):
                grad = dot_lanes(gb[j].reshape(tile, width), up)
                low = (grad * slope[slot, j].astype(f32)).astype(bf16)
                gpb[j] = low.reshape(per, cluster, block)
                acc[j] += dot_lanes(low, down)
                total = total + jnp.sum(low.astype(f32), axis=0, keepdims=True)
            vbuf[pl.ds(8 + at, 1), :block] = total
            fold_red(n)
            term = dot_rows(mlt[...], gpb[...].reshape(rows, block)).astype(bf16)
            for side in range(2):
                e_all[lax.div(at, 2), lax.rem(at, 2) * 2 + side] = term[
                    :, side * wide : (side + 1) * wide
                ].reshape(depth, quarter, wide)

            @pl.when(lax.div(at, 2) != core)
            def _():
                for side in range(2):
                    exp.near_copy(lax.rem(at, 2) * 2 + side).start()

    def first_norm(gb, n1, inv, ctx, ow, dsnd):
        later = [
            fetch(ctx_ref, ctx, 13),
            fetch(ow_ref, ow, 14),
            fetch(inv_ref, inv, 15),
        ]
        def n1_copy(j):
            return fetch(n1_ref.at[j], n1.at[j % 2], 16 + j % 2)

        def d_copy(j):
            return far_copy(dsnd.at[j], dbuf.at[core, j], (d_s, d_r), j, me.sibling())

        n1_copy(0).start()
        for copy in later:
            copy.start()
        fold_exp(counts - 1)
        for copy in later:
            copy.wait()
        gain = vecs[3:4, :]
        for row in range(3, 8):
            vbuf[row : row + 1, :] = jnp.zeros((1, width), f32)
        for j in range(chips):
            n1_copy(j).wait()
            if j + 1 < chips:
                n1_copy(j + 1).start()
            grad = acc[j]
            normed = n1[j % 2]
            vbuf[3:4, :] += jnp.sum(grad * normed, axis=0, keepdims=True)
            vbuf[4:5, :] += jnp.sum(grad, axis=0, keepdims=True)
            scaled = grad * gain
            first = jnp.mean(scaled, axis=1, keepdims=True)
            second = jnp.mean(scaled * normed, axis=1, keepdims=True)
            grad = inv[j][:, :1] * (scaled - first - normed * second)
            acc[j] = grad
            low = grad.astype(bf16)
            gb[j] = low.reshape(per, cluster, width)
            vbuf[5:6, :] += jnp.sum(low.astype(f32), axis=0, keepdims=True)
            back = dot_lanes(low, ow[...].reshape(width, width)).astype(bf16)

            for c in range(2):
                piece = back[:, c * half : (c + 1) * half]

                @pl.when(core == c)
                def _():
                    dbuf[c, j] = piece.reshape(per, cluster, half)

                @pl.when(core != c)
                def _():
                    dsnd[j] = piece.reshape(per, cluster, half)

            d_copy(j).start()
        sums.send(0)
        term = dot_first(ctx[...].reshape(rows, width), gb[...].reshape(rows, width))
        for zz in range(depth):
            for c in range(2):
                for p in range(chips):
                    begin_at = zz * quarter + (c * chips + p) * eighth
                    o_all[c, p, zz] = term[begin_at : begin_at + eighth, :].astype(bf16)
        for p in range(chips):
            out.near_copy(p).start()
        for j in range(chips):
            d_copy(j).wait()
        for a in range(depth):
            red.near_copy(a).wait_send()
        for b in range(chips):
            exp.near_copy(b).wait_send()

    shape = (chips, per, cluster, width)
    vm = pltpu.VMEM

    def feed_back(gb):
        pl.run_scoped(
            functools.partial(chunks, gb),
            vm((width, rows), bf16),
            vm((width, rows), bf16),
            vm((2, chips, tile, block), bf16),
            vm((2, chips, tile, block), bf16),
            vm((2, blocks, block // blocks, width), bf16),
            vm((2, depth, quarter, block), bf16),
            vm(shape[:3] + (block,), bf16),
        )
        pl.run_scoped(
            functools.partial(first_norm, gb),
            vm((2, tile, width), f32),
            vm((chips, tile, 128), f32),
            vm(shape, bf16),
            vm((depth, 2, quarter // 2, width), bf16),
            vm((chips, per, cluster, half), bf16),
        )

    pl.run_scoped(feed_back, vm(shape, bf16))

    def attend_back(qs, ks, vs, ps, xbuf, wbuf, ds, gs, gbuf, tbuf, dw, dwp, turned):
        atts = [
            Reducer(
                me,
                dwp.at[n],
                None,
                None,
                p_mid.at[n],
                p_last.at[n],
                p_done.at[n],
                groups[3 + n],
                n % 2 == 1,
            )
            for n in range(pairs)
        ]

        def loads(i, slot):
            span = pl.ds(i * pairs, pairs)
            pieces = (
                (q_ref.at[span], qs),
                (k_ref.at[span], ks),
                (v_ref.at[span], vs),
                (p_ref.at[span], ps),
            )
            return [fetch(src, dst.at[slot], slot * 4 + n) for n, (src, dst) in enumerate(pieces)]

        def load_x(i):
            return fetch(x_ref.at[:, :, i], xbuf, 8)

        load_w = fetch(aw_ref, wbuf, 9)
        for copy in loads(0, 0) + [load_x(0), load_w]:
            copy.start()
        bbuf[...] = jnp.zeros_like(bbuf)
        slots = lax.broadcasted_iota(jnp.int32, (cluster, cluster), 0)
        low = lax.broadcasted_iota(jnp.int32, (cluster, 128), 1) < size
        scale = size ** (-0.5)

        def tables(jj, i, pair, part):
            begin = part * heads + core * (heads // 2) + 2 * pair
            return [
                one_hot(posbuf[jj // chips, jj % chips, i, pl.ds(begin + h, 1), :], slots)
                for h in range(2)
            ]

        def clusters(i, slot, pair):
            lanes = pl.ds(multiple(pair * 128, 128), 128)
            for jj in range(blocks):
                tq = jnp.concatenate(tables(jj, i, pair, 0), axis=1)
                rows = stack_lanes(dbuf[jj // chips, jj % chips, i, :, lanes], low)
                ds[:, jj * share : (jj + 1) * share, :] = (
                    dot_rows(tq, rows).astype(bf16).reshape(blocks, share, 128)
                )
            for c in range(blocks):
                d = ds[c]
                probs = ps[slot, pair, c]
                slope = dot_lanes(d, stack_lanes(vs[slot, pair, c], low))
                broad = probs.astype(f32)
                halves = []
                for h in range(2):
                    span = slice(h * cluster, (h + 1) * cluster)
                    inner = jnp.sum(broad[:, span] * slope[:, span], axis=1, keepdims=True)
                    halves.append((broad[:, span] * (slope[:, span] - inner)).astype(bf16))
                grads = jnp.concatenate(halves, axis=1)
                gq = dot_rows(grads, stack_lanes(ks[slot, pair, c], low)) * scale
                gk = dot_first(grads, qs[slot, pair, c]) * scale
                gv = dot_first(probs, d)
                gs[0, c] = gq.astype(bf16)
                gs[1, c] = jnp.where(low, gk[:cluster], gk[cluster:]).astype(bf16)
                gs[2, c] = jnp.where(low, gv[:cluster], gv[cluster:]).astype(bf16)
            for jj in range(blocks):
                for part in range(3):
                    if part < 2:
                        table = jnp.concatenate(tables(jj, i, pair, part), axis=0)
                    rows = gs[part, :, jj * share : (jj + 1) * share, :].reshape(cluster, 128)
                    back = dot_first(table, stack_lanes(rows, low))
                    to = pl.ds(multiple(part * half + pair * 128, 128), 128)
                    gbuf[slot, jj // chips, jj % chips, :, to] = back.astype(bf16)

        def give(slot):
            return far_copy(gbuf.at[slot, 1 - core], gfar.at[slot], (g_s, g_r), slot, me.sibling())

        def token_copy(i, slot, k):
            return far_copy(
                tbuf.at[slot, me.chip_at(k)],
                token_out.at[chip * per + i],
                (t_s, t_r),
                i * (chips - 1) + k - 1,
                me.plane(k),
            )

        def token_keep(i, slot):
            return pltpu.make_async_copy(
                tbuf.at[slot, chip], token_out.at[chip * per + i], out_sem.at[1 + i]
            )

        def token_rows(i, slot):
            give(slot).wait()
            near = dot_lanes(gbuf[slot, core].reshape(chips * cluster, 3 * half), wbuf[core])
            distant = dot_lanes(gfar[slot].reshape(chips * cluster, 3 * half), wbuf[1 - core])
            resid = acc[:, i * cluster : (i + 1) * cluster, :].reshape(chips * cluster, width)
            tbuf[slot] = (resid + near + distant).astype(bf16).reshape(chips, cluster, width)
            token_keep(i, slot).start()
            for k in range(1, chips):
                token_copy(i, slot, k).start()

        ready = []

        def emit(src, dst):
            copy = pltpu.make_async_copy(src, dst, out_sem.at[1 + per + len(ready)])
            copy.start()
            ready.append(copy)

        def step_out_near():
            for p in range(chips):
                out.fold_near(p)
            out.send_mid()
            for p in range(chips):
                out.near_copy(p).wait_send()
            sums.fold(0)
            sums.send(1)

        def step_exp_mid():
            exp.fold_mid()
            exp.send_last()

        def step_red_mid():
            red.fold_mid()
            red.send_last()
            sums.fold(1)
            sums.send(2)

        def step_exp_last():
            exp.fold_last()
            exp.send_back()
            out.fold_mid()
            out.send_last()

        def step_red_last():
            red.fold_last()
            red.send_back()
            sums.fold(2)

        def step_out_last():
            out.fold_last()
            out.send_back()
            exp.send_side()

        def step_sides():
            red.send_side()

        hooks = {}
        steps = [
            (0, step_out_near),
            (1, step_exp_mid),
            (3, step_red_mid),
            (5, step_exp_last),
            (6, step_red_last),
            (7, step_out_last),
            (8, step_sides),
        ]
        for n, step in steps:
            hooks.setdefault(min(n, per * pairs - 1), []).append(step)
        depth_rows = quarter // chips

        def pair_grad(n, slot):
            lanes = [slice(p * half + n * 128, p * half + (n + 1) * 128) for p in range(3)]
            total = jnp.concatenate([dw[:, lane] for lane in lanes], axis=1)
            line = jnp.zeros((1, 384), f32)
            for b in range(2):
                x = jnp.concatenate([xbuf[b, j] for j in range(chips)], axis=0)
                g = jnp.concatenate(
                    [
                        jnp.concatenate([gbuf[slot, b, j, :, lane] for lane in lanes], axis=1)
                        for j in range(chips)
                    ],
                    axis=0,
                )
                total = total + dot_first(x, g)
                line = line + jnp.sum(g.astype(f32), axis=0, keepdims=True)
            for p, lane in enumerate(lanes):
                bbuf[0:1, lane] += line[:, p * 128 : (p + 1) * 128]
            low = total.astype(bf16)
            for a in range(depth):
                for b in range(chips):
                    begin = (a * chips + b) * depth_rows
                    piece = low[begin : begin + depth_rows]
                    if atts[n].tower_first:
                        dwp[n, a, b] = piece
                    else:
                        dwp[n, b, a] = piece
            atts[n].send_mid()

        dw[...] = jnp.zeros_like(dw)
        for i in range(per):
            slot = i % 2
            for copy in loads(i, slot):
                copy.wait()
            if i == min(1, per - 1):
                load_w.wait()
            if i >= 1:
                token_rows(i - 1, 1 - slot)
            if i + 1 < per:
                for copy in loads(i + 1, 1 - slot):
                    copy.start()
            if i == per - 1:
                load_x(i).wait()

            @pl.loop(0, pairs)
            def _(pair):
                clusters(i, slot, pair)
                for n in range(pairs):
                    if hooks.get(i * pairs + n) or i == per - 1:

                        @pl.when(pair == n)
                        def _():
                            if i == per - 1:
                                pair_grad(n, slot)
                            for step in hooks.get(i * pairs + n, ()):
                                step()

            if i >= 2:
                token_keep(i - 2, slot).wait()
                for k in range(1, chips):
                    token_copy(i - 2, slot, k).wait()
            give(slot).start()
            if i + 1 < per:
                load_x(i).wait()
                for b in range(2):
                    x = jnp.concatenate([xbuf[b, j] for j in range(chips)], axis=0)
                    g = jnp.concatenate([gbuf[slot, b, j] for j in range(chips)], axis=0)
                    dw[...] += dot_first(x, g)
                    bbuf[0:1, :] += jnp.sum(g.astype(f32), axis=0, keepdims=True)
                load_x(i + 1).start()

        biases.send(1)
        token_rows(per - 1, (per - 1) % 2)
        emit(vbuf, vec_out)
        out.send_side()
        for n in range(pairs - 1):
            atts[n].fold_mid()
            atts[n].send_last()
        biases.fold(1)
        biases.send(2)
        exp.finish()
        for c in range(2):
            for p in range(chips):
                emit(e_done.at[c, p], ew_out.at[:, pl.ds((c * chips + p) * wide, wide)])
        for n in range(pairs - 1, pairs):
            atts[n].fold_mid()
            atts[n].send_last()
        for n in range(pairs - 1):
            atts[n].fold_last()
            atts[n].send_back()
        red.finish()
        for c in range(2):
            turned[c] = jnp.transpose(r_done[c].reshape(width, wide))
            emit(turned.at[c], rw_out.at[c])
        out.finish()
        emit(o_done, ow_out)
        biases.fold(2)
        share_bias = far_copy(bbuf, bias_out.at[core], (b_s, b_r), 0, me.sibling())
        share_bias.start()
        emit(bbuf, bias_out.at[core])
        for n in range(pairs - 1, pairs):
            atts[n].fold_last()
            atts[n].send_back()
        for n in range(pairs):
            atts[n].send_side()
        for n in range(pairs):
            atts[n].finish()
            for c in range(2):
                for part in range(3):
                    emit(
                        p_done.at[n, c, :, :, pl.ds(part * 128, 128)],
                        aw_out.at[:, :, pl.ds((2 * part + c) * half + n * 128, 128)],
                    )
        for i in range(max(per - 2, 0), per):
            token_keep(i, i % 2).wait()
            for k in range(1, chips):
                token_copy(i, i % 2, k).wait()
        share_bias.wait()
        for copy in ready:
            copy.wait()
        lo_keep.wait()
        for k in range(1, chips):
            lo_copy(k).wait()

    group = (2, pairs, blocks, cluster)
    pl.run_scoped(
        attend_back,
        vm(group + (128,), bf16),
        vm(group + (128,), bf16),
        vm(group + (128,), bf16),
        vm(group + (2 * cluster,), bf16),
        vm((2, chips, cluster, width), bf16),
        vm(aw_ref.shape, bf16),
        vm((blocks, cluster, 128), bf16),
        vm((3, blocks, cluster, 128), bf16),
        vm((2, 2, chips, cluster, 3 * half), bf16),
        vm((2, chips, cluster, width), bf16),
        vm((width, 3 * half), f32),
        vm((pairs, depth, chips, quarter // chips, 384), bf16),
        vm((2, wide, width), bf16),
    )


def back(arrays, depth, heads):
    chips, per, cluster, width = arrays[17].shape
    half, blocks = width // 2, 2 * chips
    dma = pltpu.SemaphoreType.DMA
    anywhere = pl.BlockSpec(memory_space=pl.ANY)
    quarter = width // depth
    hidden = arrays[15].shape[2]
    eighth, strip, wide = quarter // blocks, width // chips, hidden // blocks
    rows = quarter // chips
    c, t = chips - 1, depth - 1
    pairs = heads // 4
    shapes = [
        ((chips * per, cluster, width), bf16),
        ((chips * per, cluster, width), bf16),
        ((chips, rows, 3 * width), bf16),
        ((2, chips, eighth, width), bf16),
        ((quarter, hidden), bf16),
        ((2, wide, width), bf16),
        ((8 + blocks, width), f32),
        ((2, 8, 3 * half), f32),
    ]
    vm = pltpu.VMEM

    def reducing(near, first, second):
        return [
            dma((near,)), dma((near,)),
            dma((first,)), dma((first,)),
            dma((second,)), dma((second,)),
            dma((c,)), dma((c,)),
            dma((1,)), dma((1,)),
        ]

    return pl.pallas_call(
        functools.partial(back_kernel, chips, depth, heads),
        out_shape=[jax.ShapeDtypeStruct(*s) for s in shapes],
        in_specs=[anywhere] * len(arrays),
        out_specs=[anywhere] * len(shapes),
        scratch_shapes=[
            vm((2, chips, per, cluster, half), bf16),
            vm(arrays[4].shape, jnp.int32),
            vm((chips, per * cluster, width), f32),
            vm((2, chips, cluster, 3 * half), bf16),
            vm((pairs, t, chips, rows, 384), bf16),
            vm((pairs, t, rows, 384), bf16),
            vm((pairs, 2, chips, rows, 384), bf16),
            vm((2, chips, depth, eighth, width), bf16),
            vm((chips, depth, eighth, width), bf16),
            vm((c, depth, eighth, width), bf16),
            vm((t, eighth, width), bf16),
            vm((2, chips, eighth, width), bf16),
            vm((2, chips, depth, quarter, wide), bf16),
            vm((chips, depth, quarter, wide), bf16),
            vm((c, depth, quarter, wide), bf16),
            vm((t, quarter, wide), bf16),
            vm((2, chips, quarter, wide), bf16),
            vm((2, depth, chips, strip, wide), bf16),
            vm((depth, chips, strip, wide), bf16),
            vm((t, chips, strip, wide), bf16),
            vm((c, strip, wide), bf16),
            vm((2, chips, strip, wide), bf16),
            vm((8 + blocks, width), f32),
            vm((chips + t, 8 + blocks, width), f32),
            vm((8, 3 * half), f32),
            vm((chips + t, 8, 3 * half), f32),
            vm((8, width), f32),
            dma((chips,)), dma((chips,)), dma((2,)), dma((2,)),
            dma((per * c,)), dma((per * c,)),
            dma((c,)), dma((c,)),
            dma((19,)), dma((1 + per + 6 + blocks + 6 * pairs,)),
            dma((chips + t,)), dma((chips + t,)), dma((chips + t,)), dma((chips + t,)),
            *reducing(depth, t, c),
            *reducing(chips, c, t),
            *reducing(chips, c, t),
            *[sem for n in range(pairs) for sem in reducing(1, c, t)],
        ],
        compiler_params=pltpu.CompilerParams(
            collective_id=2, has_side_effects=True, vmem_limit_bytes=63 * 2**20
        ),
        name="back",
    )(*arrays)


def places(rank, cluster, share):
    seqs, rows, length = rank.shape
    clusters = cluster // share
    target = rank // cluster
    which = lax.broadcasted_iota(jnp.int32, (1, 1, clusters, 1), 2)
    inside = (target[:, :, None, :] == which).astype(bf16)
    first = lax.broadcasted_iota(jnp.int32, (length, length), 0)
    second = lax.broadcasted_iota(jnp.int32, (length, length), 1)
    before = (first < second).astype(bf16)
    count = lax.dot_general(
        inside.reshape(seqs * rows * clusters, length),
        before,
        (((1,), (0,)), ((), ())),
        preferred_element_type=f32,
    ).reshape(seqs, rows, clusters, length)
    spot = which.astype(f32) * share + count
    return jnp.sum(inside.astype(f32) * spot, axis=2).astype(jnp.int32)


def per_chip(
    tokens,
    attend_weight,
    query_bias,
    value_bias,
    output_weight,
    output_bias,
    first_gain,
    first_shift,
    expand_weight,
    expand_bias,
    reduce_weight,
    reduce_bias,
    second_gain,
    second_shift,
    query_rank,
    key_rank,
    cotangent,
):
    seqs, cluster, width = tokens.shape
    heads = query_rank.shape[1]
    owners = lax.axis_size("seq")
    depth = lax.axis_size("batch")
    chips = owners // 2
    half = width // 2
    share = cluster // owners
    pos = places(jnp.concatenate([query_rank, key_rank], axis=1), cluster, share)
    quarter = width // depth
    lines = [
        query_bias,
        value_bias,
        output_bias,
        first_gain,
        first_shift,
        reduce_bias,
        second_gain,
        second_shift,
    ]
    lines += [
        expand_bias[at : at + quarter] for at in range(0, expand_bias.shape[0], quarter)
    ]
    vectors = jnp.zeros((16 * 256,), f32)
    for row, v in enumerate(lines):
        vectors += jnp.pad(v.astype(f32), (row * 256, (16 - row) * 256 - quarter))
    vectors = vectors.reshape(16, 256)
    (
        x_all,
        context,
        qs,
        ks,
        vs,
        ps,
        pos_all,
        attend_all,
        vecs,
        out_all,
        exp_all,
        red_all,
        normed_one,
        inverse_one,
        middle_low,
        hidden,
        slope,
        layer_out,
        grad_branch_two,
        late_sums,
    ) = forward(
        tokens,
        pos,
        attend_weight,
        vectors,
        output_weight,
        expand_weight,
        reduce_weight,
        cotangent,
        chips,
        depth,
        heads,
    )
    token_grad, layer_out, aw_grad, ow_grad, ew_grad, rw_grad, vec_sum, bias_sum = back(
        (
            qs,
            ks,
            vs,
            ps,
            pos_all,
            x_all,
            attend_all,
            out_all,
            exp_all,
            red_all,
            vecs,
            context,
            normed_one,
            inverse_one,
            middle_low,
            hidden,
            slope,
            layer_out,
            grad_branch_two,
            late_sums,
        ),
        depth,
        heads,
    )
    z = lax.axis_index("batch")
    six = lax.dynamic_slice_in_dim(vec_sum[:6], z * quarter, quarter, 1)
    up = lax.dynamic_index_in_dim(vec_sum[8:], z, 0, keepdims=False)
    both = jnp.concatenate([bias_sum[0, 0], bias_sum[1, 0]]).reshape(2, 3, half)
    query_value = jnp.transpose(both, (1, 0, 2)).reshape(3, width)
    query_value = lax.dynamic_slice_in_dim(query_value, z * quarter, quarter, 1)
    return (
        layer_out,
        token_grad,
        aw_grad.reshape(quarter, 3 * width).astype(f32),
        query_value[0],
        query_value[2],
        ow_grad.reshape(quarter, width).astype(f32),
        six[5],
        six[3],
        six[4],
        ew_grad.astype(f32),
        up,
        rw_grad.reshape(-1, width).astype(f32),
        six[2],
        six[0],
        six[1],
    )


def layer(mesh):
    def run(*arrays):
        seqs, cluster, width = arrays[0].shape
        heads = arrays[14].shape[1]
        owners, depth = mesh.shape["seq"], mesh.shape["batch"]
        chips = owners // 2
        fits = (
            owners % 2 == 0
            and chips > 1
            and depth == chips == 4
            and seqs % chips == 0
            and cluster == 128
            and heads % 4 == 0
            and width == heads * 64
            and cluster == 16 * owners
            and arrays[8].shape[1] == 4 * width
        )
        return (per_chip if fits else per_device)(*arrays)

    return run


def solution(mesh):
    in_specs = (
        P("batch", "seq", None),
        P("batch", None),
        P("batch"),
        P("batch"),
        P("batch", None),
        P("batch"),
        P("batch"),
        P("batch"),
        P("batch", None),
        P("batch"),
        P("batch", None),
        P("batch"),
        P("batch"),
        P("batch"),
        P("batch", None, "seq"),
        P("batch", None, "seq"),
        P("batch", "seq", None),
    )
    out_specs = (
        P("batch", "seq", None),
        P("batch", "seq", None),
        P("batch", None),
        P("batch"),
        P("batch"),
        P("batch", None),
        P("batch"),
        P("batch"),
        P("batch"),
        P("batch", None),
        P("batch"),
        P("batch", None),
        P("batch"),
        P("batch"),
        P("batch"),
    )
    return jax.shard_map(
        layer(mesh), mesh=mesh, in_specs=in_specs, out_specs=out_specs, check_vma=False
    )
```

```python
import functools
import math

import jax
import jax.numpy as jnp
from jax import lax
from jax.experimental import pallas as pl
from jax.experimental.pallas import tpu as pltpu
from jax.sharding import PartitionSpec as P

epsilon = 1e-05


def layer_norm(resid, gain, shift):
    center = jnp.mean(resid, axis=-1, keepdims=True)
    centered = resid - center
    spread = jnp.mean(centered * centered, axis=-1, keepdims=True)
    inverse = lax.rsqrt(spread + epsilon)
    normed = centered * inverse
    return (normed * gain + shift, normed, inverse)


def norm_back(upstream, normed, inverse, gain):
    scaled = upstream * gain
    first_mean = jnp.mean(scaled, axis=-1, keepdims=True)
    second_mean = jnp.mean(scaled * normed, axis=-1, keepdims=True)
    return inverse * (scaled - first_mean - normed * second_mean)


def gelu_slope(value):
    cumulative = 0.5 * (1.0 + lax.erf(value * 0.5**0.5))
    density = jnp.exp(-0.5 * value * value) * (2.0 * math.pi) ** (-0.5)
    return cumulative + value * density


def transpose_left(first, second):
    return lax.dot_general(
        first, second, (((0,), (0,)), ((), ())), preferred_element_type=jnp.float32
    )


def transpose_right(first, second):
    return lax.dot_general(
        first, second, (((1,), (1,)), ((), ())), preferred_element_type=jnp.float32
    )


def group_table(rank, cluster, owners):
    share = cluster // owners
    target = rank // cluster
    length = rank.shape[-1]
    places = lax.broadcasted_iota(jnp.int32, (length, length), 0)
    later = lax.broadcasted_iota(jnp.int32, (length, length), 1)
    before = (places < later)[None, None]
    same = target[..., :, None] == target[..., None, :]
    earlier = jnp.sum((same & before).astype(jnp.int32), axis=-2)
    position = target * share + earlier
    slots = lax.broadcasted_iota(jnp.int32, position.shape + (length,), 3)
    return (position[..., None] == slots).astype(jnp.bfloat16)


def sort_heads(rows, table, heads):
    seqs, length, width = rows.shape
    split = rows.reshape(seqs, length, heads, width // heads)
    moved = jnp.einsum("shtp,sthd->sphd", table, split, preferred_element_type=jnp.float32)
    return moved.astype(rows.dtype).reshape(seqs, length, width)


def unsort_heads(rows, table, heads):
    seqs, length, width = rows.shape
    split = rows.reshape(seqs, length, heads, width // heads)
    moved = jnp.einsum("shtp,sphd->sthd", table, split, preferred_element_type=jnp.float32)
    return moved.astype(rows.dtype).reshape(seqs, length, width)


def cluster_scores(queries, keys_rows, heads):
    items, length, width = queries.shape
    size = width // heads
    query_split = queries.reshape(items, length, heads, size)
    key_split = keys_rows.reshape(items, length, heads, size)
    scores = jnp.einsum(
        "sqhd,skhd->shqk", query_split, key_split, preferred_element_type=jnp.float32
    )
    return scores * size ** (-0.5)


def cluster_forward(queries, keys_rows, values_rows, heads):
    items, length, width = queries.shape
    scores = cluster_scores(queries, keys_rows, heads)
    top = jnp.max(scores, axis=-1, keepdims=True)
    weights = jnp.exp(scores - top)
    total = jnp.sum(weights, axis=-1, keepdims=True)
    probs = (weights / total).astype(jnp.bfloat16)
    value_split = values_rows.reshape(items, length, heads, width // heads)
    context = jnp.einsum("shqk,skhd->sqhd", probs, value_split, preferred_element_type=jnp.float32)
    return (
        context.reshape(items, length, width).astype(jnp.bfloat16),
        (top + jnp.log(total))[..., 0],
    )


def cluster_backward(scores, log_total, queries, keys_rows, values_rows, grad_context, heads):
    items, length, width = queries.shape
    size = width // heads
    query_split = queries.reshape(items, length, heads, size)
    key_split = keys_rows.reshape(items, length, heads, size)
    value_split = values_rows.reshape(items, length, heads, size)
    grad_split = grad_context.reshape(items, length, heads, size)
    probs = jnp.exp(scores - log_total[..., None])
    grad_probs = jnp.einsum(
        "sqhd,skhd->shqk", grad_split, value_split, preferred_element_type=jnp.float32
    )
    inner = jnp.sum(probs * grad_probs, axis=-1, keepdims=True)
    grad_scores = (probs * (grad_probs - inner)).astype(jnp.bfloat16)
    scale = size ** (-0.5)
    grad_query = (
        jnp.einsum("shqk,skhd->sqhd", grad_scores, key_split, preferred_element_type=jnp.float32)
        * scale
    )
    grad_key = (
        jnp.einsum("shqk,sqhd->skhd", grad_scores, query_split, preferred_element_type=jnp.float32)
        * scale
    )
    grad_value = jnp.einsum(
        "shqk,sqhd->skhd",
        probs.astype(jnp.bfloat16),
        grad_split,
        preferred_element_type=jnp.float32,
    )
    shape = (items, length, width)
    return (
        grad_query.reshape(shape).astype(jnp.bfloat16),
        grad_key.reshape(shape).astype(jnp.bfloat16),
        grad_value.reshape(shape).astype(jnp.bfloat16),
    )


def send_context(context):
    return lax.all_to_all(context, "seq", split_axis=1, concat_axis=1, tiled=True)


def send_grads(grads):
    return (
        lax.all_to_all(grads[0], "seq", split_axis=1, concat_axis=1, tiled=True),
        lax.all_to_all(grads[1], "seq", split_axis=1, concat_axis=1, tiled=True),
        lax.all_to_all(grads[2], "seq", split_axis=1, concat_axis=1, tiled=True),
    )


def make_step(left, pieces):
    total = jnp.dot(left, pieces[0], preferred_element_type=jnp.float32)
    stored = tuple(pieces[1:]) + ()
    placed = tuple((piece for piece in stored))
    return (total,) + placed


def make_hidden_step(before, pieces):
    section = before + pieces[1].astype(jnp.float32)
    activated = jax.nn.gelu(section, approximate=False).astype(jnp.bfloat16)
    total = jnp.dot(activated, pieces[0], preferred_element_type=jnp.float32)
    stored = ()
    return (total, section, activated) + stored


def per_device(
    tokens,
    attend_weight,
    query_bias,
    value_bias,
    output_weight,
    output_bias,
    first_gain,
    first_shift,
    expand_weight,
    expand_bias,
    reduce_weight,
    reduce_bias,
    second_gain,
    second_shift,
    query_rank,
    key_rank,
    cotangent,
):
    seqs, cluster, width = tokens.shape
    heads = query_rank.shape[1]
    rows = seqs * cluster
    owners = lax.axis_size("seq")
    flat = tokens.reshape(rows, width)
    attend_out = make_step(
        flat,
        (
            lax.all_gather(attend_weight, "batch", axis=0, tiled=True),
            lax.all_gather(query_bias, "batch", axis=0, tiled=True),
            lax.all_gather(value_bias, "batch", axis=0, tiled=True),
        ),
    )
    summed = attend_out[0]
    queries = (summed[:, :width] + attend_out[1].astype(jnp.float32)).astype(jnp.bfloat16)
    keys_rows = summed[:, width : 2 * width].astype(jnp.bfloat16)
    values_rows = (summed[:, 2 * width :] + attend_out[2].astype(jnp.float32)).astype(jnp.bfloat16)
    query_table = group_table(query_rank, cluster, owners)
    key_table = group_table(key_rank, cluster, owners)
    query_sorted = sort_heads(queries.reshape(seqs, cluster, width), query_table, heads)
    key_sorted = sort_heads(keys_rows.reshape(seqs, cluster, width), key_table, heads)
    value_sorted = sort_heads(values_rows.reshape(seqs, cluster, width), key_table, heads)
    received = (
        lax.all_to_all(query_sorted, "seq", split_axis=1, concat_axis=1, tiled=True),
        lax.all_to_all(key_sorted, "seq", split_axis=1, concat_axis=1, tiled=True),
        lax.all_to_all(value_sorted, "seq", split_axis=1, concat_axis=1, tiled=True),
    )
    context, log_total = cluster_forward(received[0], received[1], received[2], heads)
    forward_out = (send_context(context), log_total, received[0], received[1], received[2])
    context_rows = unsort_heads(forward_out[0], query_table, heads).reshape(rows, width)
    output_out = make_step(
        context_rows,
        (
            lax.all_gather(output_weight, "batch", axis=0, tiled=True),
            lax.all_gather(output_bias, "batch", axis=0, tiled=True),
            lax.all_gather(first_gain, "batch", axis=0, tiled=True),
            lax.all_gather(first_shift, "batch", axis=0, tiled=True),
        ),
    )
    resid_one = flat.astype(jnp.float32) + output_out[0] + output_out[1].astype(jnp.float32)
    gain_one = output_out[2].astype(jnp.float32)
    middle, normed_one, inverse_one = layer_norm(
        resid_one, gain_one, output_out[3].astype(jnp.float32)
    )
    middle_low = middle.astype(jnp.bfloat16)
    expand_out = make_step(
        middle_low,
        (
            lax.all_gather(expand_weight, "batch", axis=0, tiled=True),
            lax.all_gather(reduce_bias, "batch", axis=0, tiled=True),
            lax.all_gather(second_gain, "batch", axis=0, tiled=True),
            lax.all_gather(second_shift, "batch", axis=0, tiled=True),
        ),
    )
    hidden_out = make_hidden_step(
        expand_out[0],
        (
            lax.all_gather(reduce_weight, "batch", axis=0, tiled=True),
            lax.all_gather(expand_bias, "batch", axis=0, tiled=True),
        ),
    )
    pre_full, hidden_full = (hidden_out[1], hidden_out[2])
    resid_two = middle + hidden_out[0] + expand_out[1].astype(jnp.float32)
    gain_two = expand_out[2].astype(jnp.float32)
    final, normed_two, inverse_two = layer_norm(
        resid_two, gain_two, expand_out[3].astype(jnp.float32)
    )
    layer_out = final.astype(jnp.bfloat16).reshape(seqs, cluster, width)
    attend_full, output_full, expand_full, reduce_full = (
        lax.all_gather(attend_weight, "batch", axis=0, tiled=True),
        lax.all_gather(output_weight, "batch", axis=0, tiled=True),
        lax.all_gather(expand_weight, "batch", axis=0, tiled=True),
        lax.all_gather(reduce_weight, "batch", axis=0, tiled=True),
    )
    upstream = cotangent.reshape(rows, width).astype(jnp.float32)
    grad_second_gain = jnp.sum(upstream * normed_two, axis=0)
    grad_second_shift = jnp.sum(upstream, axis=0)
    grad_resid_two = norm_back(upstream, normed_two, inverse_two, gain_two)
    grad_branch_two = grad_resid_two.astype(jnp.bfloat16)
    grad_reduce_bias = jnp.sum(grad_branch_two, axis=0, dtype=jnp.float32)
    grad_reduce = transpose_left(hidden_full, grad_branch_two)
    grad_hidden = transpose_right(grad_branch_two, reduce_full)
    grad_pre = (grad_hidden * gelu_slope(pre_full)).astype(jnp.bfloat16)
    grad_expand_bias = jnp.sum(grad_pre, axis=0, dtype=jnp.float32)
    grad_expand = transpose_left(middle_low, grad_pre)
    grad_middle = grad_resid_two + transpose_right(grad_pre, expand_full)
    grad_first_gain = jnp.sum(grad_middle * normed_one, axis=0)
    grad_first_shift = jnp.sum(grad_middle, axis=0)
    grad_resid_one = norm_back(grad_middle, normed_one, inverse_one, gain_one)
    grad_branch_one = grad_resid_one.astype(jnp.bfloat16)
    grad_output_bias = jnp.sum(grad_branch_one, axis=0, dtype=jnp.float32)
    grad_output = transpose_left(context_rows, grad_branch_one)
    grad_context = transpose_right(grad_branch_one, output_full).astype(jnp.bfloat16)
    grad_sorted = sort_heads(grad_context.reshape(seqs, cluster, width), query_table, heads)
    grad_received = lax.all_to_all(grad_sorted, "seq", split_axis=1, concat_axis=1, tiled=True)
    kept_scores = cluster_scores(forward_out[2], forward_out[3], heads)
    home = send_grads(
        cluster_backward(
            kept_scores,
            forward_out[1],
            forward_out[2],
            forward_out[3],
            forward_out[4],
            grad_received,
            heads,
        )
    )
    grad_queries = unsort_heads(home[0], query_table, heads).reshape(rows, width)
    grad_keys = unsort_heads(home[1], key_table, heads).reshape(rows, width)
    grad_values = unsort_heads(home[2], key_table, heads).reshape(rows, width)
    grad_mixed = jnp.concatenate([grad_queries, grad_keys, grad_values], axis=1)
    grad_query_bias = jnp.sum(grad_queries, axis=0, dtype=jnp.float32)
    grad_value_bias = jnp.sum(grad_values, axis=0, dtype=jnp.float32)
    grad_attend = transpose_left(flat, grad_mixed)
    token_grad = (
        (grad_resid_one + transpose_right(grad_mixed, attend_full))
        .astype(jnp.bfloat16)
        .reshape(seqs, cluster, width)
    )
    owned = (
        lax.psum_scatter(
            grad_attend.astype(jnp.bfloat16), "batch", scatter_dimension=0, tiled=True
        ).astype(jnp.float32),
        lax.psum_scatter(
            grad_query_bias.astype(jnp.bfloat16), "batch", scatter_dimension=0, tiled=True
        ).astype(jnp.float32),
        lax.psum_scatter(
            grad_value_bias.astype(jnp.bfloat16), "batch", scatter_dimension=0, tiled=True
        ).astype(jnp.float32),
        lax.psum_scatter(
            grad_output.astype(jnp.bfloat16), "batch", scatter_dimension=0, tiled=True
        ).astype(jnp.float32),
        lax.psum_scatter(
            grad_output_bias.astype(jnp.bfloat16), "batch", scatter_dimension=0, tiled=True
        ).astype(jnp.float32),
        lax.psum_scatter(
            grad_first_gain.astype(jnp.bfloat16), "batch", scatter_dimension=0, tiled=True
        ).astype(jnp.float32),
        lax.psum_scatter(
            grad_first_shift.astype(jnp.bfloat16), "batch", scatter_dimension=0, tiled=True
        ).astype(jnp.float32),
        lax.psum_scatter(
            grad_expand.astype(jnp.bfloat16), "batch", scatter_dimension=0, tiled=True
        ).astype(jnp.float32),
        lax.psum_scatter(
            grad_expand_bias.astype(jnp.bfloat16), "batch", scatter_dimension=0, tiled=True
        ).astype(jnp.float32),
        lax.psum_scatter(
            grad_reduce.astype(jnp.bfloat16), "batch", scatter_dimension=0, tiled=True
        ).astype(jnp.float32),
        lax.psum_scatter(
            grad_reduce_bias.astype(jnp.bfloat16), "batch", scatter_dimension=0, tiled=True
        ).astype(jnp.float32),
        lax.psum_scatter(
            grad_second_gain.astype(jnp.bfloat16), "batch", scatter_dimension=0, tiled=True
        ).astype(jnp.float32),
        lax.psum_scatter(
            grad_second_shift.astype(jnp.bfloat16), "batch", scatter_dimension=0, tiled=True
        ).astype(jnp.float32),
    )
    shared = (
        lax.psum(owned[0].astype(jnp.bfloat16), "seq").astype(jnp.float32),
        lax.psum(owned[1].astype(jnp.bfloat16), "seq").astype(jnp.float32),
        lax.psum(owned[2].astype(jnp.bfloat16), "seq").astype(jnp.float32),
        lax.psum(owned[3].astype(jnp.bfloat16), "seq").astype(jnp.float32),
        lax.psum(owned[4].astype(jnp.bfloat16), "seq").astype(jnp.float32),
        lax.psum(owned[5].astype(jnp.bfloat16), "seq").astype(jnp.float32),
        lax.psum(owned[6].astype(jnp.bfloat16), "seq").astype(jnp.float32),
        lax.psum(owned[7].astype(jnp.bfloat16), "seq").astype(jnp.float32),
        lax.psum(owned[8].astype(jnp.bfloat16), "seq").astype(jnp.float32),
        lax.psum(owned[9].astype(jnp.bfloat16), "seq").astype(jnp.float32),
        lax.psum(owned[10].astype(jnp.bfloat16), "seq").astype(jnp.float32),
        lax.psum(owned[11].astype(jnp.bfloat16), "seq").astype(jnp.float32),
        lax.psum(owned[12].astype(jnp.bfloat16), "seq").astype(jnp.float32),
    )
    return (
        layer_out,
        token_grad,
        shared[0],
        shared[1],
        shared[2],
        shared[3],
        shared[4],
        shared[5],
        shared[6],
        shared[7],
        shared[8],
        shared[9],
        shared[10],
        shared[11],
        shared[12],
    )


MESH = pl.DeviceIdType.MESH
f32 = jnp.float32
bf16 = jnp.bfloat16


class Place:
    def __init__(self, chips, depth):
        self.chips, self.depth = chips, depth
        self.z = lax.axis_index("batch")
        spot = lax.axis_index("seq")
        self.chip, self.core = lax.div(spot, 2), lax.rem(spot, 2)

    def chip_at(self, k):
        return lax.rem(self.chip + k + self.chips, self.chips)

    def z_at(self, k):
        return lax.rem(self.z + k + self.depth, self.depth)

    def plane(self, k):
        return (self.z, self.chip_at(k) * 2 + self.core)

    def tower(self, k):
        return (self.z_at(k), self.chip * 2 + self.core)

    def sibling(self):
        return (self.z, self.chip * 2 + 1 - self.core)

    def greet(self):
        bell = pltpu.get_barrier_semaphore()
        others = [self.plane(k) for k in range(1, self.chips)]
        others += [self.tower(k) for k in range(1, self.depth)]
        others.append(self.sibling())
        for other in others:
            pl.semaphore_signal(bell, inc=1, device_id=other, device_id_type=MESH)
        pl.semaphore_wait(bell, len(others))


def far_copy(src, dst, sems, at, device):
    return pltpu.make_async_remote_copy(
        src_ref=src,
        dst_ref=dst,
        send_sem=sems[0].at[at],
        recv_sem=sems[1].at[at],
        device_id=device,
        device_id_type=MESH,
    )


def one_hot(row, slots):
    return jnp.where(slots == row, 1.0, 0.0).astype(bf16)


def split_lanes(tile, low):
    zero = jnp.zeros_like(tile)
    return jnp.where(low, tile, zero), jnp.where(low, zero, tile)


def stack_lanes(tile, low):
    first, second = split_lanes(tile, low)
    return jnp.concatenate([first, second], axis=0)


def dot_rows(a, b):
    return jnp.dot(a, b, preferred_element_type=f32)


def dot_lanes(a, b):
    return lax.dot_general(a, b, (((1,), (1,)), ((), ())), preferred_element_type=f32)


def dot_first(a, b):
    return lax.dot_general(a, b, (((0,), (0,)), ((), ())), preferred_element_type=f32)


def multiple(value, by):
    return pl.multiple_of(value, by)


def forward_kernel(
    chips,
    depth,
    heads,
    tok_ref,
    pos_ref,
    aw_ref,
    vec_ref,
    ow_ref,
    ew_ref,
    rw_ref,
    cot_ref,
    x_out,
    ctx_out,
    q_out,
    k_out,
    v_out,
    p_out,
    pos_out,
    aw_out,
    vec_out,
    ow_out,
    ew_out,
    rw_out,
    n1_out,
    inv_out,
    ml_out,
    hid_out,
    slope_out,
    lo_out,
    gb_out,
    sum_out,
    xbuf,
    posbuf,
    wbuf,
    vbuf,
    bias,
    ctxb,
    ctxt,
    owbuf,
    ewbuf,
    rwbuf,
    cbuf,
    n1buf,
    invbuf,
    mlbuf,
    vecs,
    upb,
    sums,
    tok_s,
    tok_r,
    tokc_s,
    tokc_r,
    pos_s,
    pos_r,
    posc_s,
    posc_r,
    up_s,
    up_r,
    dn_s,
    dn_r,
    awc_s,
    awc_r,
    vec_s,
    vec_r,
    wz_s,
    wz_r,
    wp_s,
    wp_r,
    wd_s,
    wd_r,
    wc_s,
    wc_r,
    ctx_s,
    ctx_r,
    cot_s,
    cot_r,
    oc_s,
    oc_r,
    loc,
    out_sem,
    slope_sem,
    att_sem,
    late_sem,
):
    me = Place(chips, depth)
    z, chip, core = me.z, me.chip, me.core
    per = tok_ref.shape[0] // chips
    half = aw_ref.shape[1] // 6
    rows_z = aw_ref.shape[0]
    pairs = heads // 4
    size = half // (2 * pairs)
    me.greet()

    def aw_block(zz):
        return wbuf.at[pl.ds(multiple(zz * rows_z, 8), rows_z)]

    def up_copy(h):
        return far_copy(
            aw_block(z - h), aw_block(z - h), (up_s, up_r), h, (z + 1, chip * 2 + core)
        )

    def down_copy(h):
        return far_copy(
            aw_block(z + h), aw_block(z + h), (dn_s, dn_r), h, (z - 1, chip * 2 + core)
        )

    def up_got(h):
        return far_copy(
            aw_block(z - 1 - h), aw_block(z - 1 - h), (up_s, up_r), h, me.sibling()
        )

    def down_got(h):
        return far_copy(
            aw_block(z + 1 + h), aw_block(z + 1 + h), (dn_s, dn_r), h, me.sibling()
        )

    def pass_on():
        @pl.when(z < depth - 1)
        def _():
            up_copy(0).start()

        @pl.when(z > 0)
        def _():
            down_copy(0).start()

    def pass_rest(hops):
        for h in hops:

            @pl.when(z > h)
            def _():
                up_got(h).wait_recv()
                if h + 1 < depth - 1:

                    @pl.when(z < depth - 1)
                    def _():
                        up_copy(h + 1).start()

            @pl.when(z + 1 + h < depth)
            def _():
                down_got(h).wait_recv()
                if h + 1 < depth - 1:

                    @pl.when(z > 0)
                    def _():
                        down_copy(h + 1).start()

    def pass_end():
        for h in range(depth - 1):

            @pl.when((z >= h) & (z < depth - 1))
            def _():
                up_copy(h).wait_send()

            @pl.when((z + h < depth) & (z > 0))
            def _():
                down_copy(h).wait_send()

    def mine(ref, target):
        return ref.at[pl.ds(target * per, per)]

    def tok_copy(k):
        return far_copy(
            mine(tok_ref, me.chip_at(k)), xbuf.at[core, chip], (tok_s, tok_r), k - 1, me.plane(k)
        )

    def pos_copy(k):
        return far_copy(
            mine(pos_ref, me.chip_at(k)), posbuf.at[core, chip], (pos_s, pos_r), k - 1, me.plane(k)
        )

    def vec_copy(k):
        return far_copy(vec_ref, vbuf.at[z], (vec_s, vec_r), k - 1, me.tower(k))

    sends = []
    for k in range(1, chips):
        sends.append(pos_copy(k))
        sends[-1].start()
    for k in range(1, depth):
        sends.append(vec_copy(k))
        sends[-1].start()
    for k in range(1, chips):
        sends.append(tok_copy(k))
        sends[-1].start()
    local = []

    def keep(src, dst):
        copy = pltpu.make_async_copy(src, dst, loc.at[len(local)])
        copy.start()
        local.append(copy)

    for part in range(3):
        keep(
            aw_ref.at[:, pl.ds(multiple(part * 2 * half + core * half, 128), half)],
            wbuf.at[pl.ds(multiple(z * rows_z, 8), rows_z), pl.ds(part * half, half)],
        )
    keep(mine(tok_ref, chip), xbuf.at[core, chip])
    keep(mine(pos_ref, chip), posbuf.at[core, chip])
    keep(vec_ref, vbuf.at[z])
    for copy in local[:3]:
        copy.wait()
    pass_on()
    wide = ew_ref.shape[1] // (2 * chips)
    tall = rw_ref.shape[0] // (2 * chips)
    mid_rows = rows_z // 2
    mine_at = core * chips + chip

    def piece(kind):
        if kind == 0:
            return ow_ref.at[pl.ds(multiple(core * mid_rows, 8), mid_rows)]
        if kind == 1:
            return ew_ref.at[:, pl.ds(multiple(mine_at * wide, 128), wide)]
        return rw_ref.at[pl.ds(multiple(mine_at * tall, 8), tall)]

    def place(kind, zz):
        if kind == 0:
            return owbuf.at[zz, core]
        if kind == 1:
            return ewbuf.at[zz, :, pl.ds(multiple(mine_at * wide, 128), wide)]
        return rwbuf.at[zz, mine_at]

    def place_all(kind, at):
        if kind == 1:
            return ewbuf.at[:, :, pl.ds(multiple(at * wide, 128), wide)]
        return rwbuf.at[:, at]

    for kind in range(3):
        keep(piece(kind), place(kind, z))

    def wz_copy(kind, k):
        return far_copy(
            piece(kind),
            place(kind, z),
            (wz_s, wz_r),
            kind * (depth - 1) + k - 1,
            me.tower(k),
        )

    beside = (chip + 1 - 2 * lax.rem(chip, 2), lax.rem(chip + 2, chips))
    across = chips - 1 - chip

    def part_of(kind, origin, side):
        at = core * chips + origin
        span = pl.ds(side * (depth // 2), depth // 2)
        if kind == 1:
            return ewbuf.at[span, :, pl.ds(multiple(at * wide, 128), wide)]
        return rwbuf.at[span, at]

    def wp_copy(kind, d):
        spot = place_all(kind, mine_at)
        return far_copy(
            spot, spot, (wp_s, wp_r), (kind - 1) * 2 + d, (z, beside[d] * 2 + core)
        )

    def wd_copy(kind, d):
        spot = part_of(kind, beside[d], d)
        return far_copy(
            spot, spot, (wd_s, wd_r), (kind - 1) * 2 + d, (z, beside[1 - d] * 2 + core)
        )

    def wc_copy(kind, n):
        at = core * chips + (chip, beside[0], beside[1], across)[n]
        return far_copy(
            place_all(kind, at),
            place_all(kind, at),
            (wc_s, wc_r),
            (kind - 1) * chips + n,
            me.sibling(),
        )

    def tower_wait(kind):
        for k in range(1, depth):
            wz_copy(kind, k).wait_recv()

    def plane_first(kind):
        for d in range(2):
            wp_copy(kind, d).start()
        wc_copy(kind, 0).start()

    def plane_second(kind):
        for d in range(2):
            wp_copy(kind, d).wait_recv()
            wd_copy(kind, d).start()
            wc_copy(kind, 1 + d).start()

    def plane_last(kind):
        for d in range(2):
            wd_copy(kind, d).wait_recv()
        wc_copy(kind, 3).start()
        for n in range(chips):
            wc_copy(kind, n).wait()
        for d in range(2):
            wp_copy(kind, d).wait_send()
            wd_copy(kind, d).wait_send()

    def oc_copy():
        spot = owbuf.at[:, core]
        return far_copy(spot, spot, (oc_s, oc_r), 0, me.sibling())

    def cot_copy(n):
        target = (beside[0], beside[1], across)[n]
        return far_copy(
            mine(cot_ref, target),
            cbuf.at[chip],
            (cot_s, cot_r),
            n,
            (z, target * 2 + core),
        )

    keep(mine(cot_ref, chip), cbuf.at[chip])

    for copy in local[3:5]:
        copy.wait()

    def tokc_copy(k):
        source = me.chip_at(-k)
        return far_copy(
            xbuf.at[core, source], xbuf.at[core, source], (tokc_s, tokc_r), k, me.sibling()
        )

    def posc_copy(k):
        source = me.chip_at(-k)
        return far_copy(
            posbuf.at[core, source], posbuf.at[core, source], (posc_s, posc_r), k, me.sibling()
        )

    for k in range(1, depth):
        wz_copy(1, k).start()
        for kind in range(3):
            sends.append(wz_copy(kind, k))
    pass_rest(range(depth - 2))
    for k in range(chips):
        if k:
            pos_copy(k).wait_recv()
            tok_copy(k).wait_recv()
        for copy in (posc_copy(k), tokc_copy(k)):
            copy.start()
            sends.append(copy)
    for copy in local[5:]:
        copy.wait()
    tower_wait(1)
    plane_first(1)
    pass_rest(range(depth - 2, depth - 1))
    for k in range(1, depth):
        wz_copy(2, k).start()
    plane_second(1)
    for n in range(2):
        cot_copy(n).start()
    for k in range(1, depth):
        vec_copy(k).wait_recv()
    for k in range(chips):
        posc_copy(k).wait_recv()
        tokc_copy(k).wait_recv()

    outs = []

    def emit(src, dst):
        copy = pltpu.make_async_copy(src, dst, out_sem.at[len(outs)])
        copy.start()
        outs.append(copy)

    emit(xbuf, x_out)
    emit(posbuf, pos_out)
    emit(wbuf, aw_out.at[core])
    awc = far_copy(wbuf, aw_out.at[core], (awc_s, awc_r), 0, me.sibling())
    awc.start()
    sends.append(awc)

    quarter = rows_z
    for zz in range(depth):
        begin = zz * quarter
        for row, at in ((0, 0), (1, 2)):
            for side in range(2):
                lo = max(begin, side * half)
                hi = min(begin + quarter, (side + 1) * half)
                if lo < hi:
                    bias[side, 0:1, at * half + lo - side * half : at * half + hi - side * half] = (
                        vbuf[zz, row : row + 1, lo - begin : hi - begin]
                    )
    bias[0, 0:1, half : 2 * half] = jnp.zeros((1, half), f32)
    bias[1, 0:1, half : 2 * half] = jnp.zeros((1, half), f32)
    added = bias[core, 0:1, :]
    for zz in range(depth):
        for row in range(8):
            vecs[row : row + 1, zz * quarter : (zz + 1) * quarter] = vbuf[
                zz, row : row + 1, :quarter
            ]
        steps = upb.shape[1] // (depth * quarter)
        for row in range(steps):
            to = (zz * steps + row) * quarter
            upb[0:1, to : to + quarter] = vbuf[zz, 8 + row : 9 + row, :quarter]

    cluster = tok_ref.shape[1]
    blocks = 2 * chips
    share = cluster // blocks
    width = tok_ref.shape[2]

    slots = lax.broadcasted_iota(jnp.int32, (cluster, cluster), 0)
    low = lax.broadcasted_iota(jnp.int32, (cluster, 128), 1) < size
    scale = size ** (-0.5)

    def tables(jj, i, pair, part):
        first = part * heads + core * (heads // 2) + 2 * pair
        rows = [
            one_hot(posbuf[jj // chips, jj % chips, i, pl.ds(first + h, 1), :], slots)
            for h in range(2)
        ]
        return rows

    def hook(i, pair):
        step = i * pairs + pair
        last = per * pairs - 1

        @pl.when(step == min(2, last))
        def _():
            tower_wait(2)
            plane_first(2)
            for k in range(1, depth):
                wz_copy(0, k).start()

        @pl.when(step == last)
        def _():
            plane_second(2)

    def attention(qkv, qs, ks, vs, ps, os):
        def group_copies(i):
            span = pl.ds(i * pairs, pairs)
            pieces = ((qs, q_out), (ks, k_out), (vs, v_out), (ps, p_out))
            return [
                pltpu.make_async_copy(src.at[span], dst.at[span], att_sem.at[5 + 4 * i + n])
                for n, (src, dst) in enumerate(pieces)
            ]

        @pl.loop(0, blocks)
        def _(jj):
            x = xbuf[lax.div(jj, chips), lax.rem(jj, chips)].reshape(per * cluster, width)
            mixed = (dot_rows(x, wbuf[...]) + added).astype(bf16)
            for at in range(3 * pairs):
                qkv[at, jj] = mixed[:, at * 128 : (at + 1) * 128].reshape(per, cluster, 128)

        @pl.loop(0, per)
        def _(i):
            @pl.loop(0, pairs)
            def _(pair):
                at = i * pairs + pair
                for jj in range(blocks):
                    tq = jnp.concatenate(tables(jj, i, pair, 0), axis=1)
                    tk = jnp.concatenate(tables(jj, i, pair, 1), axis=1)
                    q = stack_lanes(qkv[pair, jj, i], low)
                    k = stack_lanes(qkv[pairs + pair, jj, i], low)
                    v = stack_lanes(qkv[2 * pairs + pair, jj, i], low)
                    span = slice(jj * share, (jj + 1) * share)
                    sq = dot_rows(tq, q).astype(bf16)
                    skv = dot_rows(tk, jnp.concatenate([k, v], axis=1)).astype(bf16)
                    qs[at, :, span, :] = sq.reshape(blocks, share, 128)
                    ks[at, :, span, :] = skv[:, :128].reshape(blocks, share, 128)
                    vs[at, :, span, :] = skv[:, 128:].reshape(blocks, share, 128)
                for c in range(blocks):
                    scores = dot_lanes(qs[at, c], stack_lanes(ks[at, c], low)) * scale
                    halves = []
                    for h in range(2):
                        s = scores[:, h * cluster : (h + 1) * cluster]
                        e = jnp.exp(s - jnp.max(s, axis=1, keepdims=True))
                        halves.append((e / jnp.sum(e, axis=1, keepdims=True)).astype(bf16))
                    probs = jnp.concatenate(halves, axis=1)
                    ps[at, c] = probs
                    o = dot_rows(probs, stack_lanes(vs[at, c], low)).astype(bf16)
                    os[c] = o
                for jj in range(blocks):
                    tq = jnp.concatenate(tables(jj, i, pair, 0), axis=0)
                    rows = os[:, jj * share : (jj + 1) * share, :].reshape(cluster, 128)
                    back = dot_first(tq, stack_lanes(rows, low)).astype(bf16)
                    ctxb[jj // chips, jj % chips, i, :, pl.ds(multiple(pair * 128, 128), 128)] = back
                hook(i, pair)

                @pl.when(pair == pairs - 1)
                def _():
                    for copy in group_copies(i):
                        copy.start()


        far, own = ctx_copies()
        for copy in (far, own):
            copy.start()
        for copy in (far, own):
            copy.wait()
        for i in range(per):
            for copy in group_copies(i):
                copy.wait()

    def ctx_copies():
        lanes = pl.ds(multiple(core * half, 128), half)
        far = far_copy(
            ctxb.at[1 - core], ctxt.at[:, :, :, lanes], (ctx_s, ctx_r), 0, me.sibling()
        )
        own = pltpu.make_async_copy(ctxb.at[core], ctxt.at[:, :, :, lanes], att_sem.at[4])
        return far, own

    group = (per * pairs, blocks, cluster, 128)
    pl.run_scoped(
        attention,
        pltpu.VMEM((3 * pairs, blocks, per, cluster, 128), bf16),
        pltpu.VMEM(group, bf16),
        pltpu.VMEM(group, bf16),
        pltpu.VMEM(group, bf16),
        pltpu.VMEM((per * pairs, blocks, cluster, 2 * cluster), bf16),
        pltpu.VMEM((blocks, cluster, 128), bf16),
    )

    tower_wait(0)
    oc_copy().start()
    oc_copy().wait()
    emit(ctxt, ctx_out)
    context_out = outs[-1]
    emit(owbuf, ow_out)
    tile = per * cluster
    hidden = upb.shape[1]
    eps = epsilon

    def moments(rows):
        center = jnp.mean(rows, axis=1, keepdims=True)
        centered = rows - center
        spread = jnp.mean(centered * centered, axis=1, keepdims=True)
        inverse = lax.rsqrt(spread + eps)
        return centered * inverse, inverse

    def slope_out_copy(j, slot):
        return pltpu.make_async_copy(sbuf.at[slot], slope_out.at[j], slope_sem.at[slot])

    def vec(row):
        return vecs[row : row + 1, :]

    def feed(hbuf, sbuf):
        step = sbuf.shape[3]

        def late_copies(j):
            pieces = ((cbuf, lo_out), (ctxt, gb_out))
            return [
                pltpu.make_async_copy(src.at[j], dst.at[j], late_sem.at[2 * j + n])
                for n, (src, dst) in enumerate(pieces)
            ]

        def slope_copy(n):
            return pltpu.make_async_copy(
                sbuf.at[n % 2],
                slope_out.at[:, :, pl.ds(n * step, step)],
                slope_sem.at[n % 2],
            )

        @pl.loop(0, chips)
        def _(j):
            rows = ctxt[j].reshape(tile, width)
            branch = dot_rows(rows, owbuf[...].reshape(width, width))
            resid = xbuf[core, j].reshape(tile, width).astype(f32) + branch + vec(2)
            normed, inverse = moments(resid)
            n1buf[j] = normed
            invbuf[j] = jnp.broadcast_to(inverse, (tile, 128))
            mlbuf[j] = (normed * vec(3) + vec(4)).astype(bf16).reshape(per, cluster, width)

        cot_copy(2).start()
        plane_last(1)
        emit(ewbuf, ew_out)
        for n in range(hidden // step):
            lanes = slice(n * step, (n + 1) * step)
            if n >= 2:
                slope_copy(n - 2).wait()
            for j in range(chips):
                weight = ewbuf[:, :, lanes].reshape(width, step)
                pre = dot_rows(mlbuf[j].reshape(tile, width), weight) + upb[0:1, lanes]
                cumulative = 0.5 * (1.0 + lax.erf(pre * 0.5**0.5))
                density = jnp.exp(-0.5 * pre * pre) * (2.0 * math.pi) ** (-0.5)
                hbuf[j, :, lanes] = (pre * cumulative).astype(bf16)
                sbuf[n % 2, j] = (cumulative + pre * density).astype(bf16)
            slope_copy(n).start()

        emit(vecs, vec_out)
        emit(n1buf, n1_out)
        emit(invbuf, inv_out)
        emit(mlbuf, ml_out)
        emit(hbuf, hid_out)
        plane_last(2)
        pass_end()
        emit(rwbuf, rw_out)
        for n in range(2):
            cot_copy(n).wait()
        sums[...] = jnp.zeros_like(sums)
        waited = (context_out,)
        for copy in waited:
            copy.wait()

        @pl.loop(0, chips)
        def _(n):
            j = 2 * lax.rem(lax.div(chip, 2) + lax.div(n, 2), 2)
            j = j + lax.rem(chip + n, 2)

            @pl.when(n == chips - 1)
            def _():
                cot_copy(2).wait()

            branch = vec(5)
            for zz in range(depth):
                span = hidden // depth
                branch = branch + dot_rows(
                    hbuf[j, :, zz * span : (zz + 1) * span], rwbuf[zz].reshape(span, width)
                )
            middle = n1buf[j] * vec(3) + vec(4)
            normed, inverse = moments(middle + branch)
            upstream = cbuf[j].reshape(tile, width).astype(f32)
            cbuf[j] = (normed * vec(6) + vec(7)).astype(bf16).reshape(per, cluster, width)
            sums[0:1, :] += jnp.sum(upstream * normed, axis=0, keepdims=True)
            sums[1:2, :] += jnp.sum(upstream, axis=0, keepdims=True)
            scaled = upstream * vec(6)
            first = jnp.mean(scaled, axis=1, keepdims=True)
            second = jnp.mean(scaled * normed, axis=1, keepdims=True)
            grad = inverse * (scaled - first - normed * second)
            low_grad = grad.astype(bf16)
            sums[2:3, :] += jnp.sum(low_grad.astype(f32), axis=0, keepdims=True)
            ctxt[j] = low_grad.reshape(per, cluster, width)
            for copy in late_copies(j):
                copy.start()

        emit(sums, sum_out)
        for j in range(chips):
            for copy in late_copies(j):
                copy.wait()
        for copy in sends:
            copy.wait_send()
        awc.wait_recv()
        for n in range(max(hidden // step - 2, 0), hidden // step):
            slope_copy(n).wait()
        for copy in outs:
            if not any(copy is other for other in waited):
                copy.wait()

    pl.run_scoped(
        feed,
        pltpu.VMEM((chips, tile, hidden), bf16),
        pltpu.VMEM((2, chips, tile, hidden // depth), bf16),
    )


def forward(
    tokens,
    pos,
    attend_weight,
    vectors,
    output_weight,
    expand_weight,
    reduce_weight,
    cotangent,
    chips,
    depth,
    heads,
):
    seqs, cluster, width = tokens.shape
    per, blocks, pairs = seqs // chips, 2 * chips, heads // 4
    half = width // 2
    rows_z = attend_weight.shape[0]
    hidden = expand_weight.shape[1]
    items = per * pairs
    tile = per * cluster
    dma = pltpu.SemaphoreType.DMA
    anywhere = pl.BlockSpec(memory_space=pl.ANY)
    tall = reduce_weight.shape[0] // blocks
    shapes = [
        ((2, chips, per, cluster, width), bf16),
        ((chips, per, cluster, width), bf16),
        ((items, blocks, cluster, 128), bf16),
        ((items, blocks, cluster, 128), bf16),
        ((items, blocks, cluster, 128), bf16),
        ((items, blocks, cluster, 2 * cluster), bf16),
        ((2, chips, per, 2 * heads, cluster), jnp.int32),
        ((2, depth * rows_z, 3 * half), bf16),
        ((8, width), f32),
        ((depth, 2, rows_z // 2, width), bf16),
        ((depth, rows_z, hidden), bf16),
        ((depth, blocks, tall, width), bf16),
        ((chips, tile, width), f32),
        ((chips, tile, 128), f32),
        ((chips, per, cluster, width), bf16),
        ((chips, tile, hidden), bf16),
        ((chips, tile, hidden), bf16),
        ((chips, per, cluster, width), bf16),
        ((chips, per, cluster, width), bf16),
        ((8, width), f32),
    ]
    t, c = depth - 1, chips - 1
    vm = pltpu.VMEM
    return pl.pallas_call(
        functools.partial(forward_kernel, chips, depth, heads),
        out_shape=[jax.ShapeDtypeStruct(*s) for s in shapes],
        in_specs=[anywhere] * 8,
        out_specs=[anywhere] * len(shapes),
        scratch_shapes=[
            vm(shapes[0][0], bf16),
            vm(shapes[6][0], jnp.int32),
            vm(shapes[7][0][1:], bf16),
            vm((depth,) + vectors.shape, f32),
            vm((2, 8, 3 * half), f32),
            vm((2, chips, per, cluster, half), bf16),
            vm(shapes[1][0], bf16),
            vm(shapes[9][0], bf16),
            vm(shapes[10][0], bf16),
            vm(shapes[11][0], bf16),
            vm(shapes[17][0], bf16),
            vm(shapes[12][0], f32),
            vm(shapes[13][0], f32),
            vm(shapes[14][0], bf16),
            vm((8, width), f32),
            vm((8, hidden), f32),
            vm((8, width), f32),
            dma((c,)), dma((c,)), dma((chips,)), dma((chips,)),
            dma((c,)), dma((c,)), dma((chips,)), dma((chips,)),
            dma((t,)), dma((t,)), dma((t,)), dma((t,)), dma((1,)), dma((1,)),
            dma((t,)), dma((t,)),
            dma((3 * t,)), dma((3 * t,)),
            dma((4,)), dma((4,)), dma((4,)), dma((4,)),
            dma((2 * chips,)), dma((2 * chips,)),
            dma((1,)), dma((1,)),
            dma((c,)), dma((c,)),
            dma((1,)), dma((1,)),
            dma((12,)), dma((24,)), dma((2,)), dma((5 + 4 * per,)), dma((2 * chips,)),
        ],
        compiler_params=pltpu.CompilerParams(
            collective_id=1, has_side_effects=True, vmem_limit_bytes=63 * 2**20
        ),
        name="forward",
    )(
        tokens,
        pos,
        attend_weight,
        vectors,
        output_weight,
        expand_weight,
        reduce_weight,
        cotangent,
    )


def add_into(target, at, parts):
    total = target[at].astype(f32)
    for part in parts:
        total = total + part.astype(f32)
    target[at] = total.astype(target.dtype)


class Reducer:
    def __init__(self, me, own, other, near, mid, last, done, sems, tower_first):
        self.me, self.own, self.other = me, own, other
        self.near, self.mid, self.last, self.done = near, mid, last, done
        (self.near_s, self.near_r, self.mid_s, self.mid_r, self.last_s, self.last_r) = sems[:6]
        (self.back_s, self.back_r, self.side_s, self.side_r) = sems[6:10]
        self.tower_first = tower_first
        self.sizes = (mid.shape[0] + 1, last.shape[0] + 1)

    def spot(self, axis, k):
        me = self.me
        if self.tower_first == (axis == 0):
            return me.z_at(k), me.tower(k)
        return me.chip_at(k), me.plane(k)

    def near_copy(self, a):
        return far_copy(
            self.other.at[a], self.near.at[a], (self.near_s, self.near_r), a, self.me.sibling()
        )

    def fold_near(self, a):
        self.near_copy(a).wait_recv()
        for b in range(self.sizes[1]):
            add_into(self.own, (a, b), [self.near[a, b]])

    def mid_copy(self, k):
        where, device = self.spot(0, k)
        return far_copy(
            self.own.at[where], self.mid.at[k - 1], (self.mid_s, self.mid_r), k - 1, device
        )

    def send_mid(self):
        for k in range(1, self.sizes[0]):
            self.mid_copy(k).start()

    def fold_mid(self):
        for k in range(1, self.sizes[0]):
            self.mid_copy(k).wait()
        here = self.spot(0, 0)[0]
        for b in range(self.sizes[1]):
            add_into(self.own, (here, b), [self.mid[k - 1, b] for k in range(1, self.sizes[0])])

    def last_copy(self, k):
        here = self.spot(0, 0)[0]
        where, device = self.spot(1, k)
        return far_copy(
            self.own.at[here, where],
            self.last.at[k - 1],
            (self.last_s, self.last_r),
            k - 1,
            device,
        )

    def send_last(self):
        for k in range(1, self.sizes[1]):
            self.last_copy(k).start()

    def fold_last(self):
        me = self.me
        for k in range(1, self.sizes[1]):
            self.last_copy(k).wait()
        total = self.own[self.spot(0, 0)[0], self.spot(1, 0)[0]].astype(f32)
        for k in range(1, self.sizes[1]):
            total = total + self.last[k - 1].astype(f32)
        self.done[me.core, me.chip] = total.astype(bf16)

    def back_copy(self, k):
        me = self.me
        spot = self.done.at[me.core, me.chip]
        return far_copy(spot, spot, (self.back_s, self.back_r), k - 1, me.plane(k))

    def send_back(self):
        for k in range(1, self.done.shape[1]):
            self.back_copy(k).start()

    def side_copy(self):
        spot = self.done.at[self.me.core]
        return far_copy(spot, spot, (self.side_s, self.side_r), 0, self.me.sibling())

    def send_side(self):
        for k in range(1, self.done.shape[1]):
            self.back_copy(k).wait()
        self.side_copy().start()

    def finish(self):
        self.side_copy().wait()


class Sum:
    def __init__(self, me, vec, got, s, r):
        self.me, self.vec, self.got, self.s, self.r = me, vec, got, s, r

    def copies(self, hop):
        me = self.me
        if hop == 0:
            spots = [(0, me.sibling())]
        elif hop == 1:
            spots = [(k, me.plane(k)) for k in range(1, me.chips)]
        else:
            spots = [(me.chips + k - 1, me.tower(k)) for k in range(1, me.depth)]
        return [far_copy(self.vec, self.got.at[n], (self.s, self.r), n, d) for n, d in spots], spots

    def send(self, hop):
        for copy in self.copies(hop)[0]:
            copy.start()

    def fold(self, hop):
        copies, spots = self.copies(hop)
        for copy in copies:
            copy.wait()
        total = self.vec[...]
        for n, _ in spots:
            total = total + self.got[n]
        self.vec[...] = total


def back_kernel(
    chips,
    depth,
    heads,
    q_ref,
    k_ref,
    v_ref,
    p_ref,
    pos_ref,
    x_ref,
    aw_ref,
    ow_ref,
    ew_ref,
    rw_ref,
    vec_ref,
    ctx_ref,
    n1_ref,
    inv_ref,
    ml_ref,
    hid_ref,
    slope_ref,
    lo_ref,
    gb_ref,
    late_ref,
    token_out,
    layer_out,
    aw_out,
    ow_out,
    ew_out,
    rw_out,
    vec_out,
    bias_out,
    dbuf,
    posbuf,
    acc,
    gfar,
    p_mid,
    p_last,
    p_done,
    o_all,
    o_near,
    o_mid,
    o_last,
    o_done,
    e_all,
    e_near,
    e_mid,
    e_last,
    e_done,
    r_all,
    r_near,
    r_mid,
    r_last,
    r_done,
    vbuf,
    vgot,
    bbuf,
    bgot,
    vecs,
    d_s,
    d_r,
    g_s,
    g_r,
    t_s,
    t_r,
    lo_s,
    lo_r,
    load,
    out_sem,
    v_s,
    v_r,
    b_s,
    b_r,
    *sems,
):
    me = Place(chips, depth)
    z, core, chip = me.z, me.core, me.chip
    per, cluster, width = lo_ref.shape[1:]
    half = width // 2
    pairs = heads // 4
    size = half // (2 * pairs)
    blocks = 2 * chips
    share = cluster // blocks
    tile = per * cluster
    hidden = hid_ref.shape[2]
    wide = hidden // blocks
    strip = width // chips
    quarter = width // depth
    eighth = quarter // blocks
    rows = chips * tile
    me.greet()
    groups = [sems[n * 10 : (n + 1) * 10] for n in range(3 + heads // 4)]
    red = Reducer(
        me, r_all.at[core], r_all.at[1 - core], r_near, r_mid, r_last, r_done, groups[0], True
    )
    exp = Reducer(
        me, e_all.at[core], e_all.at[1 - core], e_near, e_mid, e_last, e_done, groups[1], False
    )
    out = Reducer(
        me, o_all.at[core], o_all.at[1 - core], o_near, o_mid, o_last, o_done, groups[2], False
    )
    sums = Sum(me, vbuf, vgot, v_s, v_r)
    biases = Sum(me, bbuf, bgot, b_s, b_r)

    def fetch(src, dst, at):
        return pltpu.make_async_copy(src, dst, load.at[at])

    def lo_copy(k):
        return far_copy(
            lo_ref.at[me.chip_at(k)],
            layer_out.at[pl.ds(chip * per, per)],
            (lo_s, lo_r),
            k - 1,
            me.plane(k),
        )

    lo_keep = pltpu.make_async_copy(
        lo_ref.at[chip], layer_out.at[pl.ds(chip * per, per)], out_sem.at[0]
    )

    block = 2 * wide
    counts = blocks // 2

    def order(n):
        return lax.rem(n + z + chip, counts)

    def fold_red(n):
        at = order(n)
        red.fold_near(at)
        k = lax.rem(at - z + depth, depth)

        @pl.when(k != 0)
        def _():
            red.mid_copy(k).start()

    def fold_exp(n):
        at = order(n)

        @pl.when(lax.div(at, 2) == core)
        def _():
            for side in range(2):
                b = lax.rem(at, 2) * 2 + side
                exp.fold_near(b)
                k = lax.rem(b - chip + chips, chips)

                @pl.when(k != 0)
                def _():
                    exp.mid_copy(k).start()

    def chunks(gb, gbt, mlt, hid, slope, rwc, ewc, gpb):
        def chunk(n, slot):
            at = order(n)
            lanes = pl.ds(multiple(at * block, 128), block)
            return [
                fetch(hid_ref.at[:, :, lanes], hid.at[slot], slot * 4),
                fetch(slope_ref.at[:, :, lanes], slope.at[slot], slot * 4 + 1),
                fetch(rw_ref.at[at], rwc.at[slot], slot * 4 + 2),
                fetch(ew_ref.at[:, :, lanes], ewc.at[slot], slot * 4 + 3),
            ]

        begin = [
            fetch(gb_ref, gb, 8),
            fetch(ml_ref, gpb, 9),
        ]
        later = [
            fetch(vec_ref, vecs, 11),
            fetch(late_ref, vbuf.at[pl.ds(0, 8)], 12),
            fetch(pos_ref, posbuf, 18),
        ]
        for copy in begin[:1] + chunk(0, 0) + begin[1:] + later:
            copy.start()
        for k in range(1, chips):
            lo_copy(k).start()
        lo_keep.start()
        vbuf[8:, :] = jnp.zeros((blocks, width), f32)
        begin[0].wait()
        for j in range(chips):
            gbt[:, j * tile : (j + 1) * tile] = jnp.transpose(gb[j].reshape(tile, width))

        def settle():
            for copy in begin[1:] + later:
                copy.wait()
            for j in range(chips):
                mlt[:, j * tile : (j + 1) * tile] = jnp.transpose(gpb[j].reshape(tile, width))
                acc[j] = gb[j].reshape(tile, width).astype(f32)

        @pl.loop(0, counts)
        def _(n):
            slot = lax.rem(n, 2)
            at = order(n)
            for copy in chunk(n, slot):
                copy.wait()

            @pl.when(n + 1 < counts)
            def _():
                for copy in chunk(n + 1, 1 - slot):
                    copy.start()

            term = dot_rows(gbt[...], hid[slot].reshape(rows, block)).astype(bf16)
            for side in range(2):
                r_all[side, at] = term[:, side * wide : (side + 1) * wide].reshape(
                    chips, strip, wide
                )
            red.near_copy(at).start()

            @pl.when(n == 0)
            def _():
                settle()

            @pl.when(n > 0)
            def _():
                fold_exp(n - 1)

            up = rwc[slot].reshape(block, width)
            down = ewc[slot].reshape(width, block)
            total = jnp.zeros((1, block), f32)
            for j in range(chips):
                grad = dot_lanes(gb[j].reshape(tile, width), up)
                low = (grad * slope[slot, j].astype(f32)).astype(bf16)
                gpb[j] = low.reshape(per, cluster, block)
                acc[j] += dot_lanes(low, down)
                total = total + jnp.sum(low.astype(f32), axis=0, keepdims=True)
            vbuf[pl.ds(8 + at, 1), :block] = total
            fold_red(n)
            term = dot_rows(mlt[...], gpb[...].reshape(rows, block)).astype(bf16)
            for side in range(2):
                e_all[lax.div(at, 2), lax.rem(at, 2) * 2 + side] = term[
                    :, side * wide : (side + 1) * wide
                ].reshape(depth, quarter, wide)

            @pl.when(lax.div(at, 2) != core)
            def _():
                for side in range(2):
                    exp.near_copy(lax.rem(at, 2) * 2 + side).start()

    def first_norm(gb, n1, inv, ctx, ow, dsnd):
        later = [
            fetch(ctx_ref, ctx, 13),
            fetch(ow_ref, ow, 14),
            fetch(inv_ref, inv, 15),
        ]
        def n1_copy(j):
            return fetch(n1_ref.at[j], n1.at[j % 2], 16 + j % 2)

        def d_copy(j):
            return far_copy(dsnd.at[j], dbuf.at[core, j], (d_s, d_r), j, me.sibling())

        n1_copy(0).start()
        for copy in later:
            copy.start()
        fold_exp(counts - 1)
        for copy in later:
            copy.wait()
        gain = vecs[3:4, :]
        for row in range(3, 8):
            vbuf[row : row + 1, :] = jnp.zeros((1, width), f32)
        for j in range(chips):
            n1_copy(j).wait()
            if j + 1 < chips:
                n1_copy(j + 1).start()
            grad = acc[j]
            normed = n1[j % 2]
            vbuf[3:4, :] += jnp.sum(grad * normed, axis=0, keepdims=True)
            vbuf[4:5, :] += jnp.sum(grad, axis=0, keepdims=True)
            scaled = grad * gain
            first = jnp.mean(scaled, axis=1, keepdims=True)
            second = jnp.mean(scaled * normed, axis=1, keepdims=True)
            grad = inv[j][:, :1] * (scaled - first - normed * second)
            acc[j] = grad
            low = grad.astype(bf16)
            gb[j] = low.reshape(per, cluster, width)
            vbuf[5:6, :] += jnp.sum(low.astype(f32), axis=0, keepdims=True)
            back = dot_lanes(low, ow[...].reshape(width, width)).astype(bf16)

            for c in range(2):
                piece = back[:, c * half : (c + 1) * half]

                @pl.when(core == c)
                def _():
                    dbuf[c, j] = piece.reshape(per, cluster, half)

                @pl.when(core != c)
                def _():
                    dsnd[j] = piece.reshape(per, cluster, half)

            d_copy(j).start()
        sums.send(0)
        term = dot_first(ctx[...].reshape(rows, width), gb[...].reshape(rows, width))
        for zz in range(depth):
            for c in range(2):
                for p in range(chips):
                    begin_at = zz * quarter + (c * chips + p) * eighth
                    o_all[c, p, zz] = term[begin_at : begin_at + eighth, :].astype(bf16)
        for p in range(chips):
            out.near_copy(p).start()
        for j in range(chips):
            d_copy(j).wait()
        for a in range(depth):
            red.near_copy(a).wait_send()
        for b in range(chips):
            exp.near_copy(b).wait_send()

    shape = (chips, per, cluster, width)
    vm = pltpu.VMEM

    def feed_back(gb):
        pl.run_scoped(
            functools.partial(chunks, gb),
            vm((width, rows), bf16),
            vm((width, rows), bf16),
            vm((2, chips, tile, block), bf16),
            vm((2, chips, tile, block), bf16),
            vm((2, blocks, block // blocks, width), bf16),
            vm((2, depth, quarter, block), bf16),
            vm(shape[:3] + (block,), bf16),
        )
        pl.run_scoped(
            functools.partial(first_norm, gb),
            vm((2, tile, width), f32),
            vm((chips, tile, 128), f32),
            vm(shape, bf16),
            vm((depth, 2, quarter // 2, width), bf16),
            vm((chips, per, cluster, half), bf16),
        )

    pl.run_scoped(feed_back, vm(shape, bf16))

    def attend_back(qs, ks, vs, ps, xbuf, wbuf, ds, gs, gbuf, tbuf, dw, dwp, turned):
        atts = [
            Reducer(
                me,
                dwp.at[n],
                None,
                None,
                p_mid.at[n],
                p_last.at[n],
                p_done.at[n],
                groups[3 + n],
                n % 2 == 1,
            )
            for n in range(pairs)
        ]

        def loads(i, slot):
            span = pl.ds(i * pairs, pairs)
            pieces = (
                (q_ref.at[span], qs),
                (k_ref.at[span], ks),
                (v_ref.at[span], vs),
                (p_ref.at[span], ps),
            )
            return [fetch(src, dst.at[slot], slot * 4 + n) for n, (src, dst) in enumerate(pieces)]

        def load_x(i):
            return fetch(x_ref.at[:, :, i], xbuf, 8)

        load_w = fetch(aw_ref, wbuf, 9)
        for copy in loads(0, 0) + [load_x(0), load_w]:
            copy.start()
        bbuf[...] = jnp.zeros_like(bbuf)
        slots = lax.broadcasted_iota(jnp.int32, (cluster, cluster), 0)
        low = lax.broadcasted_iota(jnp.int32, (cluster, 128), 1) < size
        scale = size ** (-0.5)

        def tables(jj, i, pair, part):
            begin = part * heads + core * (heads // 2) + 2 * pair
            return [
                one_hot(posbuf[jj // chips, jj % chips, i, pl.ds(begin + h, 1), :], slots)
                for h in range(2)
            ]

        def clusters(i, slot, pair):
            lanes = pl.ds(multiple(pair * 128, 128), 128)
            for jj in range(blocks):
                tq = jnp.concatenate(tables(jj, i, pair, 0), axis=1)
                rows = stack_lanes(dbuf[jj // chips, jj % chips, i, :, lanes], low)
                ds[:, jj * share : (jj + 1) * share, :] = (
                    dot_rows(tq, rows).astype(bf16).reshape(blocks, share, 128)
                )
            for c in range(blocks):
                d = ds[c]
                probs = ps[slot, pair, c]
                slope = dot_lanes(d, stack_lanes(vs[slot, pair, c], low))
                broad = probs.astype(f32)
                halves = []
                for h in range(2):
                    span = slice(h * cluster, (h + 1) * cluster)
                    inner = jnp.sum(broad[:, span] * slope[:, span], axis=1, keepdims=True)
                    halves.append((broad[:, span] * (slope[:, span] - inner)).astype(bf16))
                grads = jnp.concatenate(halves, axis=1)
                gq = dot_rows(grads, stack_lanes(ks[slot, pair, c], low)) * scale
                gk = dot_first(grads, qs[slot, pair, c]) * scale
                gv = dot_first(probs, d)
                gs[0, c] = gq.astype(bf16)
                gs[1, c] = jnp.where(low, gk[:cluster], gk[cluster:]).astype(bf16)
                gs[2, c] = jnp.where(low, gv[:cluster], gv[cluster:]).astype(bf16)
            for jj in range(blocks):
                for part in range(3):
                    if part < 2:
                        table = jnp.concatenate(tables(jj, i, pair, part), axis=0)
                    rows = gs[part, :, jj * share : (jj + 1) * share, :].reshape(cluster, 128)
                    back = dot_first(table, stack_lanes(rows, low))
                    to = pl.ds(multiple(part * half + pair * 128, 128), 128)
                    gbuf[slot, jj // chips, jj % chips, :, to] = back.astype(bf16)

        def give(slot):
            return far_copy(gbuf.at[slot, 1 - core], gfar.at[slot], (g_s, g_r), slot, me.sibling())

        def token_copy(i, slot, k):
            return far_copy(
                tbuf.at[slot, me.chip_at(k)],
                token_out.at[chip * per + i],
                (t_s, t_r),
                i * (chips - 1) + k - 1,
                me.plane(k),
            )

        def token_keep(i, slot):
            return pltpu.make_async_copy(
                tbuf.at[slot, chip], token_out.at[chip * per + i], out_sem.at[1 + i]
            )

        def token_rows(i, slot):
            give(slot).wait()
            near = dot_lanes(gbuf[slot, core].reshape(chips * cluster, 3 * half), wbuf[core])
            distant = dot_lanes(gfar[slot].reshape(chips * cluster, 3 * half), wbuf[1 - core])
            resid = acc[:, i * cluster : (i + 1) * cluster, :].reshape(chips * cluster, width)
            tbuf[slot] = (resid + near + distant).astype(bf16).reshape(chips, cluster, width)
            token_keep(i, slot).start()
            for k in range(1, chips):
                token_copy(i, slot, k).start()

        ready = []

        def emit(src, dst):
            copy = pltpu.make_async_copy(src, dst, out_sem.at[1 + per + len(ready)])
            copy.start()
            ready.append(copy)

        def step_out_near():
            for p in range(chips):
                out.fold_near(p)
            out.send_mid()
            for p in range(chips):
                out.near_copy(p).wait_send()
            sums.fold(0)
            sums.send(1)

        def step_exp_mid():
            exp.fold_mid()
            exp.send_last()

        def step_red_mid():
            red.fold_mid()
            red.send_last()
            sums.fold(1)
            sums.send(2)

        def step_exp_last():
            exp.fold_last()
            exp.send_back()
            out.fold_mid()
            out.send_last()

        def step_red_last():
            red.fold_last()
            red.send_back()
            sums.fold(2)

        def step_out_last():
            out.fold_last()
            out.send_back()
            exp.send_side()

        def step_sides():
            red.send_side()

        def step_out_side():
            out.send_side()

        hooks = {}
        steps = [
            (0, step_out_near),
            (1, step_exp_mid),
            (2, step_red_mid),
            (4, step_exp_last),
            (5, step_red_last),
            (6, step_out_last),
            (7, step_sides),
            (8, step_out_side),
        ]
        for n, step in steps:
            hooks.setdefault(min(n, per * pairs - 1), []).append(step)
        depth_rows = quarter // chips

        def pair_grad(n, slot):
            lanes = [slice(p * half + n * 128, p * half + (n + 1) * 128) for p in range(3)]
            total = jnp.concatenate([dw[:, lane] for lane in lanes], axis=1)
            line = jnp.zeros((1, 384), f32)
            for b in range(2):
                x = jnp.concatenate([xbuf[b, j] for j in range(chips)], axis=0)
                g = jnp.concatenate(
                    [
                        jnp.concatenate([gbuf[slot, b, j, :, lane] for lane in lanes], axis=1)
                        for j in range(chips)
                    ],
                    axis=0,
                )
                total = total + dot_first(x, g)
                line = line + jnp.sum(g.astype(f32), axis=0, keepdims=True)
            for p, lane in enumerate(lanes):
                bbuf[0:1, lane] += line[:, p * 128 : (p + 1) * 128]
            low = total.astype(bf16)
            for a in range(depth):
                for b in range(chips):
                    begin = (a * chips + b) * depth_rows
                    piece = low[begin : begin + depth_rows]
                    if atts[n].tower_first:
                        dwp[n, a, b] = piece
                    else:
                        dwp[n, b, a] = piece
            atts[n].send_mid()

        dw[...] = jnp.zeros_like(dw)
        for i in range(per):
            slot = i % 2
            for copy in loads(i, slot):
                copy.wait()
            if i == min(1, per - 1):
                load_w.wait()
            if i >= 1:
                token_rows(i - 1, 1 - slot)
            if i + 1 < per:
                for copy in loads(i + 1, 1 - slot):
                    copy.start()
            if i == per - 1:
                load_x(i).wait()

            @pl.loop(0, pairs)
            def _(pair):
                clusters(i, slot, pair)
                for n in range(pairs):
                    if hooks.get(i * pairs + n) or i == per - 1:

                        @pl.when(pair == n)
                        def _():
                            if i == per - 1:
                                pair_grad(n, slot)
                            for step in hooks.get(i * pairs + n, ()):
                                step()

            if i >= 2:
                token_keep(i - 2, slot).wait()
                for k in range(1, chips):
                    token_copy(i - 2, slot, k).wait()
            give(slot).start()
            if i + 1 < per:
                load_x(i).wait()
                for b in range(2):
                    x = jnp.concatenate([xbuf[b, j] for j in range(chips)], axis=0)
                    g = jnp.concatenate([gbuf[slot, b, j] for j in range(chips)], axis=0)
                    dw[...] += dot_first(x, g)
                    bbuf[0:1, :] += jnp.sum(g.astype(f32), axis=0, keepdims=True)
                load_x(i + 1).start()

        biases.send(1)
        token_rows(per - 1, (per - 1) % 2)
        emit(vbuf, vec_out)
        for n in range(pairs - 1):
            atts[n].fold_mid()
            atts[n].send_last()
        biases.fold(1)
        biases.send(2)
        exp.finish()
        for c in range(2):
            for p in range(chips):
                emit(e_done.at[c, p], ew_out.at[:, pl.ds((c * chips + p) * wide, wide)])
        for n in range(pairs - 1, pairs):
            atts[n].fold_mid()
            atts[n].send_last()
        for n in range(pairs - 1):
            atts[n].fold_last()
            atts[n].send_back()
        red.finish()
        for c in range(2):
            turned[c] = jnp.transpose(r_done[c].reshape(width, wide))
            emit(turned.at[c], rw_out.at[c])
        out.finish()
        emit(o_done, ow_out)
        biases.fold(2)
        share_bias = far_copy(bbuf, bias_out.at[core], (b_s, b_r), 0, me.sibling())
        share_bias.start()
        emit(bbuf, bias_out.at[core])
        for n in range(pairs - 1, pairs):
            atts[n].fold_last()
            atts[n].send_back()
        for n in range(pairs):
            atts[n].send_side()
        for n in range(pairs):
            atts[n].finish()
            for c in range(2):
                for part in range(3):
                    emit(
                        p_done.at[n, c, :, :, pl.ds(part * 128, 128)],
                        aw_out.at[:, :, pl.ds((2 * part + c) * half + n * 128, 128)],
                    )
        for i in range(max(per - 2, 0), per):
            token_keep(i, i % 2).wait()
            for k in range(1, chips):
                token_copy(i, i % 2, k).wait()
        share_bias.wait()
        for copy in ready:
            copy.wait()
        lo_keep.wait()
        for k in range(1, chips):
            lo_copy(k).wait()

    group = (2, pairs, blocks, cluster)
    pl.run_scoped(
        attend_back,
        vm(group + (128,), bf16),
        vm(group + (128,), bf16),
        vm(group + (128,), bf16),
        vm(group + (2 * cluster,), bf16),
        vm((2, chips, cluster, width), bf16),
        vm(aw_ref.shape, bf16),
        vm((blocks, cluster, 128), bf16),
        vm((3, blocks, cluster, 128), bf16),
        vm((2, 2, chips, cluster, 3 * half), bf16),
        vm((2, chips, cluster, width), bf16),
        vm((width, 3 * half), f32),
        vm((pairs, depth, chips, quarter // chips, 384), bf16),
        vm((2, wide, width), bf16),
    )


def back(arrays, depth, heads):
    chips, per, cluster, width = arrays[17].shape
    half, blocks = width // 2, 2 * chips
    dma = pltpu.SemaphoreType.DMA
    anywhere = pl.BlockSpec(memory_space=pl.ANY)
    quarter = width // depth
    hidden = arrays[15].shape[2]
    eighth, strip, wide = quarter // blocks, width // chips, hidden // blocks
    rows = quarter // chips
    c, t = chips - 1, depth - 1
    pairs = heads // 4
    shapes = [
        ((chips * per, cluster, width), bf16),
        ((chips * per, cluster, width), bf16),
        ((chips, rows, 3 * width), bf16),
        ((2, chips, eighth, width), bf16),
        ((quarter, hidden), bf16),
        ((2, wide, width), bf16),
        ((8 + blocks, width), f32),
        ((2, 8, 3 * half), f32),
    ]
    vm = pltpu.VMEM

    def reducing(near, first, second):
        return [
            dma((near,)), dma((near,)),
            dma((first,)), dma((first,)),
            dma((second,)), dma((second,)),
            dma((c,)), dma((c,)),
            dma((1,)), dma((1,)),
        ]

    return pl.pallas_call(
        functools.partial(back_kernel, chips, depth, heads),
        out_shape=[jax.ShapeDtypeStruct(*s) for s in shapes],
        in_specs=[anywhere] * len(arrays),
        out_specs=[anywhere] * len(shapes),
        scratch_shapes=[
            vm((2, chips, per, cluster, half), bf16),
            vm(arrays[4].shape, jnp.int32),
            vm((chips, per * cluster, width), f32),
            vm((2, chips, cluster, 3 * half), bf16),
            vm((pairs, t, chips, rows, 384), bf16),
            vm((pairs, t, rows, 384), bf16),
            vm((pairs, 2, chips, rows, 384), bf16),
            vm((2, chips, depth, eighth, width), bf16),
            vm((chips, depth, eighth, width), bf16),
            vm((c, depth, eighth, width), bf16),
            vm((t, eighth, width), bf16),
            vm((2, chips, eighth, width), bf16),
            vm((2, chips, depth, quarter, wide), bf16),
            vm((chips, depth, quarter, wide), bf16),
            vm((c, depth, quarter, wide), bf16),
            vm((t, quarter, wide), bf16),
            vm((2, chips, quarter, wide), bf16),
            vm((2, depth, chips, strip, wide), bf16),
            vm((depth, chips, strip, wide), bf16),
            vm((t, chips, strip, wide), bf16),
            vm((c, strip, wide), bf16),
            vm((2, chips, strip, wide), bf16),
            vm((8 + blocks, width), f32),
            vm((chips + t, 8 + blocks, width), f32),
            vm((8, 3 * half), f32),
            vm((chips + t, 8, 3 * half), f32),
            vm((8, width), f32),
            dma((chips,)), dma((chips,)), dma((2,)), dma((2,)),
            dma((per * c,)), dma((per * c,)),
            dma((c,)), dma((c,)),
            dma((19,)), dma((1 + per + 6 + blocks + 6 * pairs,)),
            dma((chips + t,)), dma((chips + t,)), dma((chips + t,)), dma((chips + t,)),
            *reducing(depth, t, c),
            *reducing(chips, c, t),
            *reducing(chips, c, t),
            *[sem for n in range(pairs) for sem in reducing(1, c, t)],
        ],
        compiler_params=pltpu.CompilerParams(
            collective_id=2, has_side_effects=True, vmem_limit_bytes=63 * 2**20
        ),
        name="back",
    )(*arrays)


def places(rank, cluster, share):
    seqs, rows, length = rank.shape
    clusters = cluster // share
    target = rank // cluster
    which = lax.broadcasted_iota(jnp.int32, (1, 1, clusters, 1), 2)
    inside = (target[:, :, None, :] == which).astype(bf16)
    first = lax.broadcasted_iota(jnp.int32, (length, length), 0)
    second = lax.broadcasted_iota(jnp.int32, (length, length), 1)
    before = (first < second).astype(bf16)
    count = lax.dot_general(
        inside.reshape(seqs * rows * clusters, length),
        before,
        (((1,), (0,)), ((), ())),
        preferred_element_type=f32,
    ).reshape(seqs, rows, clusters, length)
    spot = which.astype(f32) * share + count
    return jnp.sum(inside.astype(f32) * spot, axis=2).astype(jnp.int32)


def per_chip(
    tokens,
    attend_weight,
    query_bias,
    value_bias,
    output_weight,
    output_bias,
    first_gain,
    first_shift,
    expand_weight,
    expand_bias,
    reduce_weight,
    reduce_bias,
    second_gain,
    second_shift,
    query_rank,
    key_rank,
    cotangent,
):
    seqs, cluster, width = tokens.shape
    heads = query_rank.shape[1]
    owners = lax.axis_size("seq")
    depth = lax.axis_size("batch")
    chips = owners // 2
    half = width // 2
    share = cluster // owners
    pos = places(jnp.concatenate([query_rank, key_rank], axis=1), cluster, share)
    quarter = width // depth
    lines = [
        query_bias,
        value_bias,
        output_bias,
        first_gain,
        first_shift,
        reduce_bias,
        second_gain,
        second_shift,
    ]
    lines += [
        expand_bias[at : at + quarter] for at in range(0, expand_bias.shape[0], quarter)
    ]
    vectors = jnp.zeros((16 * 256,), f32)
    for row, v in enumerate(lines):
        vectors += jnp.pad(v.astype(f32), (row * 256, (16 - row) * 256 - quarter))
    vectors = vectors.reshape(16, 256)
    (
        x_all,
        context,
        qs,
        ks,
        vs,
        ps,
        pos_all,
        attend_all,
        vecs,
        out_all,
        exp_all,
        red_all,
        normed_one,
        inverse_one,
        middle_low,
        hidden,
        slope,
        layer_out,
        grad_branch_two,
        late_sums,
    ) = forward(
        tokens,
        pos,
        attend_weight,
        vectors,
        output_weight,
        expand_weight,
        reduce_weight,
        cotangent,
        chips,
        depth,
        heads,
    )
    token_grad, layer_out, aw_grad, ow_grad, ew_grad, rw_grad, vec_sum, bias_sum = back(
        (
            qs,
            ks,
            vs,
            ps,
            pos_all,
            x_all,
            attend_all,
            out_all,
            exp_all,
            red_all,
            vecs,
            context,
            normed_one,
            inverse_one,
            middle_low,
            hidden,
            slope,
            layer_out,
            grad_branch_two,
            late_sums,
        ),
        depth,
        heads,
    )
    z = lax.axis_index("batch")
    six = lax.dynamic_slice_in_dim(vec_sum[:6], z * quarter, quarter, 1)
    up = lax.dynamic_index_in_dim(vec_sum[8:], z, 0, keepdims=False)
    both = jnp.concatenate([bias_sum[0, 0], bias_sum[1, 0]]).reshape(2, 3, half)
    query_value = jnp.transpose(both, (1, 0, 2)).reshape(3, width)
    query_value = lax.dynamic_slice_in_dim(query_value, z * quarter, quarter, 1)
    return (
        layer_out,
        token_grad,
        aw_grad.reshape(quarter, 3 * width).astype(f32),
        query_value[0],
        query_value[2],
        ow_grad.reshape(quarter, width).astype(f32),
        six[5],
        six[3],
        six[4],
        ew_grad.astype(f32),
        up,
        rw_grad.reshape(-1, width).astype(f32),
        six[2],
        six[0],
        six[1],
    )


def layer(mesh):
    def run(*arrays):
        seqs, cluster, width = arrays[0].shape
        heads = arrays[14].shape[1]
        owners, depth = mesh.shape["seq"], mesh.shape["batch"]
        chips = owners // 2
        fits = (
            owners % 2 == 0
            and chips > 1
            and depth == chips == 4
            and seqs % chips == 0
            and cluster == 128
            and heads % 4 == 0
            and width == heads * 64
            and cluster == 16 * owners
            and arrays[8].shape[1] == 4 * width
        )
        return (per_chip if fits else per_device)(*arrays)

    return run


def solution(mesh):
    in_specs = (
        P("batch", "seq", None),
        P("batch", None),
        P("batch"),
        P("batch"),
        P("batch", None),
        P("batch"),
        P("batch"),
        P("batch"),
        P("batch", None),
        P("batch"),
        P("batch", None),
        P("batch"),
        P("batch"),
        P("batch"),
        P("batch", None, "seq"),
        P("batch", None, "seq"),
        P("batch", "seq", None),
    )
    out_specs = (
        P("batch", "seq", None),
        P("batch", "seq", None),
        P("batch", None),
        P("batch"),
        P("batch"),
        P("batch", None),
        P("batch"),
        P("batch"),
        P("batch"),
        P("batch", None),
        P("batch"),
        P("batch", None),
        P("batch"),
        P("batch"),
        P("batch"),
    )
    return jax.shard_map(
        layer(mesh), mesh=mesh, in_specs=in_specs, out_specs=out_specs, check_vma=False
    )
```
